32 devices in a mesh: dp: 4 (over z), expert: 8 (over y, x, core).
Axes of the slice: x: 2, y: 2, z: 4, core: 2. Of those that a mesh axis runs over, the one named last changes fastest.
Arguments:
- tokens: bfloat16 [4, 1024, 1024], P('dp', 'expert'), may hold values from -6 to 6
- attn_gain: float32 [1024], replicated, may hold values from 0.5 to 1.5
- w_query: bfloat16 [1024, 1024], replicated, may hold values from -0.5 to 0.5
- w_key: bfloat16 [1024, 512], replicated, may hold values from -0.5 to 0.5
- w_value: bfloat16 [1024, 512], replicated, may hold values from -0.1875 to 0.1875
- w_output: bfloat16 [1024, 1024], replicated, may hold values from -6 to 6
- moe_gain: float32 [1024], replicated, may hold values from 0.5 to 1.5
- w_router: bfloat16 [1024, 32], replicated, may hold values from -0.09375 to 0.09375
- w_gate: bfloat16 [32, 1024, 512], P('expert'), may hold values from -0.1875 to 0.1875
- w_up: bfloat16 [32, 1024, 512], P('expert'), may hold values from -0.1875 to 0.1875
- w_down: bfloat16 [32, 512, 1024], P('expert'), may hold values from -6 to 6
- routes: int32 [4, 1024, 8], P('dp', 'expert'), may hold values from 0 to 31, all different within a row; in each aligned block of 128 rows (0 to 127, 128 to 255, ..., all dimensions but the last counted through in order) at most 48 rows name the same one
- segment_ids: int32 [4, 1024], P('dp', 'expert'), may hold values from 0 to 7, never falling along the last dimension, each value on 1 to 512 neighbouring positions
- out_grad: bfloat16 [4, 1024, 1024], P('dp', 'expert'), may hold values from -6 to 6
Outputs:
- mixed: bfloat16 [4, 1024, 1024], P('dp', 'expert')
- grad_tokens: float32 [4, 1024, 1024], P('dp', 'expert')
- grad_attn_gain: float32 [1024], replicated
- grad_query: float32 [1024, 1024], replicated
- grad_key: float32 [1024, 512], replicated
- grad_value: float32 [1024, 512], replicated
- grad_output: float32 [1024, 1024], replicated
- grad_moe_gain: float32 [1024], replicated
- grad_router: float32 [1024, 32], replicated
- grad_gate: float32 [32, 1024, 512], P('expert', 'dp')
- grad_up: float32 [32, 1024, 512], P('expert', 'dp')
- grad_down: float32 [32, 512, 1024], P('expert', 'dp')
The draws below stay inside these ranges and needn't reach their ends.
Inputs may be any that keep to these rules, and one draw needn't show every extreme that they name: `routes`: each token names 8 different experts. In each aligned block of 128 positions of a packed row no expert is named by more than 48 tokens, and in some block one expert is named by exactly 48. `segment_ids`: along a packed row the document numbers never fall; a document covers one position up to half of 1024, and some document covers exactly half of 1024.
All inputs are finite; a program needn't handle non-finite values.
Results may differ from the reference program's by a relative error of at most 0.018.
Values may be sent and summed in bfloat16 or wider, within the bound.
No kernel may reach another device: no remote copies, remote signals or barrier semaphores. Data moves between devices by JAX's collectives and lax.ppermute only.
A program may use at most 192 MiB of HBM per device.

```python
import math
import jax
import jax.numpy as jnp
import numpy as np
from jax import lax

D = 1024
HEADS = 16
KV_HEADS = 8
HEAD_DIM = 64
EXPERTS = 32
TOP = 8
FE = 512
GROUP = 128
SEGS = 8
PACKED = 4
LENGTH = 1024
MOST = 48


def steps_of(rng, shape, pieces, low, largest):
    def one(position, blocks):
        heights = jax.random.uniform(jax.random.fold_in(jax.random.fold_in(rng, 6), position), (blocks,), jnp.float32, low / len(pieces), largest / len(pieces))
        return jnp.repeat(jnp.exp(heights), shape[position] // blocks).reshape((-1,) + (1,) * (len(shape) - position - 1))

    level = one(*pieces[0])
    for cut in pieces[1:]:
        level = level * one(*cut)
    return level


def profile(count, total, bound, slope):
    loads = [(1 << 20) // math.isqrt(grade ** slope) + 1 for grade in range(2, count + 1)]
    surplus, given = total - bound - (count - 1), [1] * (count - 1)
    while surplus > 0:
        candidates = [i for i in range(count - 1) if given[i] < bound]
        whole, remaining = sum([loads[i] for i in candidates]), surplus
        for i in candidates:
            addition = min(bound - given[i], max(1, remaining * loads[i] // whole), surplus)
            given[i] = given[i] + addition
            surplus = surplus - addition
    return np.array([bound] + given)


def ragged_sizes(key, count, total, limit, skew):
    if count == 2:
        one = jax.random.randint(key, (), max(1, total - limit), min(limit, total - 1) + 1)
        return jnp.stack([one, total - one])
    tallies = jnp.asarray(profile(count, total, limit, skew), jnp.int32)
    twos = (count - 1) // 2
    giver, taker = tallies[1:1 + 2 * twos:2], tallies[2:2 + 2 * twos:2]
    slack = jnp.minimum(giver - 1, limit - taker)
    shifted = jax.random.randint(jax.random.fold_in(key, 1), (twos,), 0, 1 << 20) % (slack + 1)
    tallies = tallies.at[1:1 + 2 * twos:2].set(giver - shifted).at[2:2 + 2 * twos:2].set(taker + shifted)
    return tallies[jax.random.permutation(jax.random.fold_in(key, 2), count)]


def shared_out(own_key, own, number, rows, amount, top, limit, lean):
    ranking = jax.random.permutation(own_key, amount)
    packed, common = portions_of(amount, rows * top, limit, lean, True), portions_of(amount, rows * top, limit, lean, False)
    places = jnp.arange(amount)

    def named(tallies, turn):
        used = int((tallies > 0).sum())
        fixed = max(1, used // 4)
        moved = fixed + (places - fixed + turn * (used - fixed)) % max(1, amount - fixed)
        return jnp.zeros((amount,), jnp.int32).at[ranking[jnp.where(places < fixed, places, moved)]].set(jnp.asarray(tallies, jnp.int32))

    tallies = jnp.where(number % 4 == 0, named(packed, number // 4), named(common, number - number // 4 - 1))
    mixed = jax.random.permutation(jax.random.fold_in(own, 3), amount)
    giver, receiver = mixed[0:amount // 2 * 2:2], mixed[1:amount // 2 * 2:2]
    room = jnp.minimum(tallies[giver] - 1, limit - tallies[receiver]) // 2
    room = jnp.where((giver == ranking[0]) | (receiver == ranking[0]) | (tallies[receiver] == 0), 0, jnp.maximum(room, 0))
    moved = jax.random.randint(jax.random.fold_in(own, 4), (amount // 2,), 0, 1 << 20) % (room + 1)
    tallies = tallies.at[giver].add(-moved).at[receiver].add(moved)
    members = jnp.searchsorted(jnp.cumsum(tallies), jnp.arange(rows * top), side="right").astype(jnp.int32)
    listing = members.reshape(top, rows).T
    listing = listing[jax.random.permutation(jax.random.fold_in(own, 1), rows)]
    turn = jax.random.randint(jax.random.fold_in(own, 2), (rows, 1), 0, top)
    return jnp.take_along_axis(listing, (jnp.arange(top)[None, :] + turn) % top, axis=1)


def portions_of(number_of, total, bound, skew, full):
    weights = [(1 << 20) // math.isqrt(grade ** skew) + 1 for grade in range(1, number_of + 1)]
    largest = bound if full else min(bound, max(-(-total // number_of), total * weights[0] // sum(weights)))
    least = 1 if total - largest >= number_of - 1 else 0
    given, spare = [largest] + [least] * (number_of - 1), total - largest - least * (number_of - 1)
    while spare > 0:
        free = [i for i in range(1, number_of) if given[i] < largest] or [i for i in range(1, number_of) if given[i] < bound]
        whole, remaining = sum([weights[i] for i in free]), spare
        for i in free:
            addition = min(bound - given[i], max(1, remaining * weights[i] // whole), spare)
            given[i] = given[i] + addition
            spare = spare - addition
    return np.array(given)


def bell_draw(own_key, dims, spread, limit, shards=(), kind=jnp.bfloat16):
    drawn = spread * jax.random.normal(own_key, dims, jnp.float32)
    if shards:
        drawn = drawn * steps_of(own_key, dims, shards, -0.22, 0.18)
    return jnp.clip(drawn, -limit, limit).astype(kind)


def setup_inputs(seed: int = 0) -> dict:
    streams_of = jax.random.split(jax.random.key(seed), 15)
    tokens = bell_draw(streams_of[0], (PACKED, LENGTH, D), 1.0, 6.0, ((0, 4), (1, 8)))
    attn_gain = jnp.clip(1.0 + 0.1 * jax.random.normal(streams_of[1], (D,), jnp.float32), 0.5, 1.5)
    w_query = bell_draw(streams_of[2], (D, HEADS * HEAD_DIM), (D // 8) ** -0.5, 0.5)
    w_key = bell_draw(streams_of[3], (D, KV_HEADS * HEAD_DIM), (D // 8) ** -0.5, 0.5)
    w_value = bell_draw(streams_of[4], (D, KV_HEADS * HEAD_DIM), D ** -0.5, 0.1875)
    w_output = bell_draw(streams_of[5], (HEADS * HEAD_DIM, D), 1.0, 6.0)
    moe_gain = jnp.clip(1.0 + 0.1 * jax.random.normal(streams_of[6], (D,), jnp.float32), 0.5, 1.5)
    w_router = bell_draw(streams_of[7], (D, EXPERTS), (4 * D) ** -0.5, 0.09375)
    w_gate = bell_draw(streams_of[8], (EXPERTS, D, FE), D ** -0.5, 0.1875, ((0, 8),))
    w_up = bell_draw(streams_of[9], (EXPERTS, D, FE), D ** -0.5, 0.1875, ((0, 8),))
    w_down = bell_draw(streams_of[10], (EXPERTS, FE, D), 1.0, 6.0, ((0, 8),))
    routes_keys = jax.random.split(jax.random.fold_in(streams_of[11], 1), PACKED * LENGTH // GROUP)
    routes_turns = jax.random.permutation(jax.random.fold_in(streams_of[11], 3), PACKED * LENGTH // GROUP)
    routes = jax.vmap(lambda own, number: shared_out(jax.random.fold_in(streams_of[11], 2), own, number, GROUP, EXPERTS, TOP, MOST, 2))(routes_keys, routes_turns).reshape((PACKED, LENGTH, TOP))
    segment_ids = jax.vmap(lambda own: jnp.searchsorted(jnp.cumsum(ragged_sizes(own, SEGS, LENGTH, LENGTH // 2, 1)), jnp.arange(LENGTH), side="right"))(jax.random.split(streams_of[12], PACKED)).reshape((PACKED, LENGTH)).astype(jnp.int32)
    out_grad = bell_draw(streams_of[13], (PACKED, LENGTH, D), 1.0, 6.0, ((0, 4), (1, 8)))
    return {"tokens": tokens, "attn_gain": attn_gain, "w_query": w_query, "w_key": w_key, "w_value": w_value, "w_output": w_output, "moe_gain": moe_gain, "w_router": w_router, "w_gate": w_gate, "w_up": w_up, "w_down": w_down, "routes": routes, "segment_ids": segment_ids, "out_grad": out_grad}


ATTN_SCALE = 0.015625
RESIDUAL_SCALE = 0.22
NORM_EPS = 1e-06
ROPE_BASE = 10000.0
NEG_FILL = -1e+30

@jax.custom_vjp
def low(v):
    return lax.optimization_barrier(v.astype(jnp.bfloat16)).astype(jnp.float32)

@jax.custom_vjp
def low_back(v):
    return v

def low_keep(v):
    return (low(v), None)

def low_pass(kept, grad):
    return (grad,)

def back_keep(v):
    return (v, None)

def back_low(kept, grad):
    return (low(grad),)
low.defvjp(low_keep, low_pass)
low_back.defvjp(back_keep, back_low)

def matmul_high(left, right):
    return jnp.dot(left, right, precision=lax.Precision.HIGHEST, preferred_element_type=jnp.float32)

def rms_scale(values, gain_vec):
    return values * lax.rsqrt(lax.optimization_barrier(jnp.mean(values * values, axis=-1, keepdims=True)) + NORM_EPS) * gain_vec

def rope_tables(positions):
    half = HEAD_DIM // 2
    freqs = ROPE_BASE ** (-(jnp.arange(half, dtype=jnp.float32) * 2.0) / HEAD_DIM)
    angles = positions.astype(jnp.float32)[..., None] * freqs
    cosine = jnp.concatenate([jnp.cos(angles), jnp.cos(angles)], axis=-1)
    sine = jnp.concatenate([jnp.sin(angles), jnp.sin(angles)], axis=-1)
    return (cosine, sine)

def rotate(vectors, cosine, sine):
    half = vectors.shape[-1] // 2
    turned = jnp.concatenate([-vectors[..., half:], vectors[..., :half]], axis=-1)
    return vectors * cosine + turned * sine

def row_positions(seg_row):
    index = jnp.arange(seg_row.shape[0], dtype=jnp.int32)
    before = lax.optimization_barrier(jnp.sum((seg_row[None, :] < seg_row[:, None]).astype(jnp.int32), axis=1))
    return index - before

def attend_block(row_query, keys_rep, values_rep, row_seg, offset):
    query_block = min(512, LENGTH)
    query_part = lax.dynamic_slice_in_dim(row_query, offset, query_block, 0)
    query_seg = lax.dynamic_slice_in_dim(row_seg, offset, query_block, 0)
    query_index = offset + jnp.arange(query_block, dtype=jnp.int32)
    key_index = jnp.arange(LENGTH, dtype=jnp.int32)
    raw = jnp.einsum('qhd,khd->hqk', query_part, keys_rep, precision=lax.Precision.HIGHEST)
    scores = low_back(raw * ATTN_SCALE)
    allowed = (query_seg[:, None] == row_seg[None, :]) & (key_index[None, :] <= query_index[:, None])
    masked = jnp.where(allowed[None], scores, NEG_FILL)
    probs = low(jax.nn.softmax(masked, axis=-1))
    return jnp.einsum('hqk,khd->qhd', probs, values_rep, precision=lax.Precision.HIGHEST)

def row_attention(packed_row):
    row_query, row_key, row_value, row_seg = packed_row
    repeats = HEADS // KV_HEADS
    keys_rep = jnp.repeat(row_key, repeats, axis=1)
    values_rep = jnp.repeat(row_value, repeats, axis=1)
    query_block = min(512, LENGTH)
    offsets = jnp.arange(0, LENGTH, query_block, dtype=jnp.int32)
    blocks = lax.map(lambda offset: jax.checkpoint(attend_block)(row_query, keys_rep, values_rep, row_seg, offset), offsets)
    return blocks.reshape(LENGTH, HEADS, HEAD_DIM)

def reference(tokens, attn_gain, w_query, w_key, w_value, w_output, moe_gain, w_router, w_gate, w_up, w_down, routes, segment_ids, out_grad):
    tok_total = PACKED * LENGTH
    positions = lax.map(row_positions, segment_ids)
    cosine, sine = rope_tables(positions)
    cos_heads = cosine[:, :, None, :]
    sin_heads = sine[:, :, None, :]
    route_flat = routes.reshape(tok_total, TOP)
    onehot = (route_flat[:, :, None] == jnp.arange(EXPERTS, dtype=jnp.int32)[None, None, :]).astype(jnp.float32)
    routed = lax.optimization_barrier(jnp.sum((route_flat[:, :, None] == jnp.arange(EXPERTS, dtype=jnp.int32)[None, None, :]).astype(jnp.int32), axis=1))
    rank = jnp.cumsum(routed, axis=0) - 1
    capacity = MOST * (tok_total // GROUP)
    target = jnp.where(routed > 0, rank, capacity).astype(jnp.int32)
    expert_ids = jnp.broadcast_to(jnp.arange(EXPERTS, dtype=jnp.int32)[None, :], (tok_total, EXPERTS))
    token_ids = jnp.broadcast_to(jnp.arange(tok_total, dtype=jnp.int32)[:, None], (tok_total, EXPERTS))
    table = jnp.zeros((EXPERTS, capacity), jnp.int32).at[expert_ids, target].set(token_ids, mode='drop')
    filled = jnp.zeros((EXPERTS, capacity), jnp.float32).at[expert_ids, target].set(1.0, mode='drop')

    def forward(inputs, gain_attn, weight_query, weight_key, weight_value, weight_output, gain_moe, weight_router, weight_gate, weight_up, weight_down):
        flat = inputs.reshape(tok_total, D)
        normed = low(rms_scale(flat, gain_attn))
        query_lin = low_back(matmul_high(normed, weight_query)).reshape(PACKED, LENGTH, HEADS, HEAD_DIM)
        key_lin = low_back(matmul_high(normed, weight_key)).reshape(PACKED, LENGTH, KV_HEADS, HEAD_DIM)
        values = low(low_back(matmul_high(normed, weight_value))).reshape(PACKED, LENGTH, KV_HEADS, HEAD_DIM)
        queries = low(rotate(query_lin, cos_heads, sin_heads))
        keys = low(rotate(key_lin, cos_heads, sin_heads))
        attended = lax.map(row_attention, (queries, keys, values, segment_ids))
        attn = low(low_back(attended.reshape(tok_total, HEADS * HEAD_DIM)))
        branch = low_back(matmul_high(attn, weight_output))
        middle = flat + RESIDUAL_SCALE * branch
        normed2 = low(rms_scale(middle, gain_moe))
        logits = low_back(matmul_high(normed2, weight_router))
        picked = lax.optimization_barrier(jnp.sum(onehot * logits[:, None, :], axis=2))
        gates = jax.nn.softmax(picked, axis=-1)
        combine = lax.optimization_barrier(jnp.sum(onehot * gates[:, :, None], axis=1))

        def expert_term(normed_rows, stacked):
            gate_w, up_w, down_w, rows_e, filled_e, weight_col = stacked
            routed_in = low_back(jnp.take(normed_rows, rows_e, axis=0))
            gate_pre = low_back(matmul_high(routed_in, gate_w))
            up_pre = low_back(matmul_high(routed_in, up_w))
            hidden = low(jax.nn.silu(gate_pre) * up_pre)
            expert_out = low(low_back(matmul_high(hidden, down_w)))
            weight_rows = jnp.take(weight_col, rows_e) * filled_e
            return jnp.zeros((tok_total, D), jnp.float32).at[rows_e].add(weight_rows[:, None] * expert_out)

        def expert_step(running, stacked):
            return (running + jax.checkpoint(expert_term)(normed2, stacked), None)
        moe, unused = lax.scan(expert_step, jnp.zeros((tok_total, D), jnp.float32), (weight_gate, weight_up, weight_down, table, filled, jnp.transpose(combine)))
        result = middle + RESIDUAL_SCALE * moe
        return result.reshape(PACKED, LENGTH, D)
    floats = (tokens.astype(jnp.float32), attn_gain.astype(jnp.float32), w_query.astype(jnp.float32), w_key.astype(jnp.float32), w_value.astype(jnp.float32), w_output.astype(jnp.float32), moe_gain.astype(jnp.float32), w_router.astype(jnp.float32), w_gate.astype(jnp.float32), w_up.astype(jnp.float32), w_down.astype(jnp.float32))
    result, pullback = jax.vjp(forward, *floats)
    grads = pullback(out_grad.astype(jnp.float32))
    return (result.astype(jnp.bfloat16), grads[0], grads[1], grads[2], grads[3], grads[4], grads[5], grads[6], grads[7], grads[8], grads[9], grads[10])
```

```python
import jax
import jax.numpy as jnp
from jax import lax
from jax.sharding import PartitionSpec as P

HEADS = 16
KV_HEADS = 8
HEAD_DIM = 64
EXPERTS = 32
TOP = 8
MOST = 48


ATTN_SCALE = 0.015625
RESIDUAL_SCALE = 0.22
NORM_EPS = 1e-06
ROPE_BASE = 10000.0
NEG_FILL = -1e30


def rms_forward(values, gain_vec):
    inverse = lax.rsqrt(jnp.mean(values * values, axis=-1, keepdims=True) + NORM_EPS)
    unit_rows = values * inverse
    return (unit_rows * gain_vec, unit_rows, inverse)


def rms_backward(grad_rows, unit_rows, inverse, gain_vec):
    scaled = grad_rows * gain_vec
    grad_gain = jnp.sum(grad_rows * unit_rows, axis=0)
    grad_in = inverse * (scaled - unit_rows * jnp.mean(scaled * unit_rows, axis=-1, keepdims=True))
    return (grad_in, grad_gain)


def rope_tables(positions):
    half = HEAD_DIM // 2
    freqs = ROPE_BASE ** (-(jnp.arange(half, dtype=jnp.float32) * 2.0) / HEAD_DIM)
    angles = positions.astype(jnp.float32)[..., None] * freqs
    cosine = jnp.concatenate([jnp.cos(angles), jnp.cos(angles)], axis=-1)
    sine = jnp.concatenate([jnp.sin(angles), jnp.sin(angles)], axis=-1)
    return (cosine, sine)


def rotate(vectors, cosine, sine):
    half = vectors.shape[-1] // 2
    turned = jnp.concatenate([-vectors[..., half:], vectors[..., :half]], axis=-1)
    return vectors * cosine + turned * sine


def unrotate(grads, cosine, sine):
    half = grads.shape[-1] // 2
    scaled = grads * sine
    turned = jnp.concatenate([scaled[..., half:], -scaled[..., :half]], axis=-1)
    return grads * cosine + turned


def scaled_scores(query_part, key_part, query_seg, key_seg, query_index, key_index):
    raw = (
        jnp.einsum("qrgjd,krgd->rgjqk", query_part, key_part, preferred_element_type=jnp.float32)
        * ATTN_SCALE
    )
    same = jnp.transpose(query_seg)[:, :, None] == jnp.transpose(key_seg)[:, None, :]
    before = key_index[None, :] <= query_index[:, None]
    return (raw, (same & before[None])[:, None, None])


def probs_and_ds(
    query_part,
    key_part,
    value_part,
    dout_part,
    lse_part,
    delta_part,
    query_seg,
    key_seg,
    query_index,
    key_index,
):
    scores, allowed = scaled_scores(
        query_part, key_part, query_seg, key_seg, query_index, key_index
    )
    lse_rows = jnp.transpose(lse_part, (1, 2, 3, 0))[..., None]
    delta_rows = jnp.transpose(delta_part, (1, 2, 3, 0))[..., None]
    probs = jnp.where(allowed, jnp.exp(scores - lse_rows), 0.0)
    dprobs = jnp.einsum(
        "qrgjd,krgd->rgjqk", dout_part, value_part, preferred_element_type=jnp.float32
    )
    dscore = (probs * (dprobs - delta_rows)).astype(jnp.bfloat16)
    return (probs.astype(jnp.bfloat16), dscore)


def per_device_general(
    tokens,
    attn_gain,
    w_query,
    w_key,
    w_value,
    w_output,
    moe_gain,
    w_router,
    w_gate,
    w_up,
    w_down,
    routes,
    segment_ids,
    out_grad,
):
    row_count, group_len, width = tokens.shape
    devices = lax.axis_size("expert")
    my_index = lax.axis_index("expert")
    length = group_len * devices
    repeats = HEADS // KV_HEADS
    tok_count = group_len * row_count
    slot_rows = row_count * MOST
    seg_local = jnp.transpose(segment_ids)
    seg_all = lax.all_gather(seg_local, "expert", axis=0, tiled=True)
    query_index = my_index * group_len + jnp.arange(group_len, dtype=jnp.int32)
    earlier = jnp.sum((seg_all[None, :, :] < seg_local[:, None, :]).astype(jnp.int32), axis=1)
    cosine, sine = rope_tables(query_index[:, None] - earlier)
    cos_heads = cosine[:, :, None, :]
    sin_heads = sine[:, :, None, :]
    residual = jnp.swapaxes(tokens, 0, 1).astype(jnp.float32).reshape(tok_count, width)
    normed, unit_attn, inv_attn = rms_forward(residual, attn_gain)
    normed_rows = normed.astype(jnp.bfloat16)
    query_lin = jnp.dot(normed_rows, w_query, preferred_element_type=jnp.float32).reshape(
        group_len, row_count, HEADS, HEAD_DIM
    )
    queries = (
        rotate(query_lin, cos_heads, sin_heads)
        .astype(jnp.bfloat16)
        .reshape(group_len, row_count, KV_HEADS, repeats, HEAD_DIM)
    )
    key_lin = jnp.dot(normed_rows, w_key, preferred_element_type=jnp.float32).reshape(
        group_len, row_count, KV_HEADS, HEAD_DIM
    )
    keys = rotate(key_lin, cos_heads, sin_heads).astype(jnp.bfloat16)
    values = (
        jnp.dot(normed_rows, w_value, preferred_element_type=jnp.float32)
        .astype(jnp.bfloat16)
        .reshape(group_len, row_count, KV_HEADS, HEAD_DIM)
    )
    keys_all, values_all = (
        lax.all_gather(keys, "expert", axis=0, tiled=True),
        lax.all_gather(values, "expert", axis=0, tiled=True),
    )
    key_block = min(1024, length)
    block_count = length // key_block
    key_blocks = keys_all.reshape(block_count, key_block, row_count, KV_HEADS, HEAD_DIM)
    value_blocks = values_all.reshape(block_count, key_block, row_count, KV_HEADS, HEAD_DIM)
    seg_blocks = seg_all.reshape(block_count, key_block, row_count)
    index_blocks = jnp.arange(length, dtype=jnp.int32).reshape(block_count, key_block)
    key_inputs = (key_blocks, value_blocks, seg_blocks, index_blocks)

    def max_step(carried, current):
        running, totals = carried
        key_part, value_part, seg_part, index_part = current
        scores, allowed = scaled_scores(
            queries, key_part, seg_local, seg_part, query_index, index_part
        )
        newmax = jnp.maximum(running, jnp.max(jnp.where(allowed, scores, NEG_FILL), axis=-1))
        totals = totals * jnp.exp(running - newmax) + jnp.sum(
            jnp.where(allowed, jnp.exp(scores - newmax[..., None]), 0.0), axis=-1
        )
        return ((newmax, totals), None)

    stat_shape = (row_count, KV_HEADS, repeats, group_len)
    (running, totals), unused = lax.scan(
        max_step,
        (jnp.full(stat_shape, NEG_FILL, jnp.float32), jnp.zeros(stat_shape, jnp.float32)),
        key_inputs,
    )
    logsum = running + jnp.log(totals)
    lse_local = jnp.transpose(logsum, (3, 0, 1, 2))

    def out_step(accum, current):
        key_part, value_part, seg_part, index_part = current
        scores, allowed = scaled_scores(
            queries, key_part, seg_local, seg_part, query_index, index_part
        )
        probs = jnp.where(allowed, jnp.exp(scores - logsum[..., None]), 0.0).astype(jnp.bfloat16)
        return (
            accum
            + jnp.einsum(
                "rgjqk,krgd->qrgjd", probs, value_part, preferred_element_type=jnp.float32
            ),
            None,
        )

    head_shape = (group_len, row_count, KV_HEADS, repeats, HEAD_DIM)
    attended, unused = lax.scan(out_step, jnp.zeros(head_shape, jnp.float32), key_inputs)
    attn_rows = attended.reshape(tok_count, HEADS * HEAD_DIM).astype(jnp.bfloat16)
    branch = jnp.dot(attn_rows, w_output, preferred_element_type=jnp.float32)
    middle = residual + RESIDUAL_SCALE * branch
    normed2, unit_moe, inv_moe = rms_forward(middle, moe_gain)
    moe_rows = normed2.astype(jnp.bfloat16)
    logits = jnp.dot(moe_rows, w_router, preferred_element_type=jnp.float32)
    route_rows = jnp.transpose(routes, (1, 0, 2)).reshape(tok_count, TOP)
    onehot = route_rows[:, :, None] == jnp.arange(EXPERTS, dtype=jnp.int32)[None, None, :]
    picked = jnp.sum(jnp.where(onehot, logits[:, None, :], 0.0), axis=-1)
    gates = jax.nn.softmax(picked, axis=-1)
    by_row = jnp.transpose(
        onehot.reshape(group_len, row_count, TOP, EXPERTS), (1, 0, 2, 3)
    ).reshape(row_count, group_len * TOP, EXPERTS)
    counted = jnp.cumsum(by_row.astype(jnp.int32), axis=1)
    rank = jnp.sum(jnp.where(by_row, counted - 1, 0), axis=-1).reshape(row_count, group_len, TOP)
    rank = jnp.transpose(rank, (1, 0, 2)).reshape(tok_count, TOP)
    row_of = jnp.arange(tok_count, dtype=jnp.int32) % row_count
    target = (route_rows * slot_rows + row_of[:, None] * MOST + rank).reshape(tok_count * TOP)

    def to_slots(route_values):
        placed = (
            jnp.zeros((EXPERTS * slot_rows, width), jnp.bfloat16)
            .at[target]
            .set(route_values.reshape(tok_count * TOP, width))
        )
        return placed.reshape(EXPERTS, slot_rows, width)

    def from_slots(slot_values):
        return (
            slot_values.reshape(EXPERTS * slot_rows, width)[target]
            .reshape(tok_count, TOP, width)
            .astype(jnp.float32)
        )

    sent = to_slots(jnp.broadcast_to(moe_rows[:, None, :], (tok_count, TOP, width)))
    arrived = lax.all_to_all(sent, "expert", split_axis=0, concat_axis=1, tiled=True)
    gate_pre = jnp.einsum("etd,edf->etf", arrived, w_gate, preferred_element_type=jnp.float32)
    up_pre = jnp.einsum("etd,edf->etf", arrived, w_up, preferred_element_type=jnp.float32)
    sigma = jax.nn.sigmoid(gate_pre)
    activated = gate_pre * sigma
    hidden = (activated * up_pre).astype(jnp.bfloat16)
    expert_out = jnp.einsum(
        "etf,efd->etd", hidden, w_down, preferred_element_type=jnp.float32
    ).astype(jnp.bfloat16)
    returned = lax.all_to_all(expert_out, "expert", split_axis=1, concat_axis=0, tiled=True)
    route_out = from_slots(returned)
    moe = jnp.sum(gates[:, :, None] * route_out, axis=1)
    mixed_rows = middle + RESIDUAL_SCALE * moe
    mixed = jnp.swapaxes(mixed_rows.reshape(group_len, row_count, width), 0, 1).astype(jnp.bfloat16)
    upstream = jnp.swapaxes(out_grad, 0, 1).astype(jnp.float32).reshape(tok_count, width)
    dmoe = RESIDUAL_SCALE * upstream
    dgates = jnp.sum(route_out * dmoe[:, None, :], axis=-1)
    dsent = to_slots((gates[:, :, None] * dmoe[:, None, :]).astype(jnp.bfloat16))
    darrived = lax.all_to_all(dsent, "expert", split_axis=0, concat_axis=1, tiled=True)
    dhidden = jnp.einsum("etd,efd->etf", darrived, w_down, preferred_element_type=jnp.float32)
    down_part = jnp.einsum("etf,etd->efd", hidden, darrived, preferred_element_type=jnp.float32)
    dgate_pre = (dhidden * up_pre * sigma * (1.0 + gate_pre * (1.0 - sigma))).astype(jnp.bfloat16)
    dup_pre = (dhidden * activated).astype(jnp.bfloat16)
    gate_part = jnp.einsum("etd,etf->edf", arrived, dgate_pre, preferred_element_type=jnp.float32)
    up_part = jnp.einsum("etd,etf->edf", arrived, dup_pre, preferred_element_type=jnp.float32)
    dinputs = (
        jnp.einsum("etf,edf->etd", dgate_pre, w_gate, preferred_element_type=jnp.float32)
        + jnp.einsum("etf,edf->etd", dup_pre, w_up, preferred_element_type=jnp.float32)
    ).astype(jnp.bfloat16)
    grad_gate, grad_up, grad_down = (
        lax.psum_scatter(
            gate_part.astype(jnp.bfloat16), "dp", scatter_dimension=1, tiled=True
        ).astype(jnp.float32),
        lax.psum_scatter(
            up_part.astype(jnp.bfloat16), "dp", scatter_dimension=1, tiled=True
        ).astype(jnp.float32),
        lax.psum_scatter(
            down_part.astype(jnp.bfloat16), "dp", scatter_dimension=1, tiled=True
        ).astype(jnp.float32),
    )
    dreturned = lax.all_to_all(dinputs, "expert", split_axis=1, concat_axis=0, tiled=True)
    droutes = jnp.sum(from_slots(dreturned), axis=1)
    dpicked = gates * (dgates - jnp.sum(gates * dgates, axis=-1, keepdims=True))
    dlogits = jnp.sum(jnp.where(onehot, dpicked[:, :, None], 0.0), axis=1).astype(jnp.bfloat16)
    router_part = jnp.einsum("nd,ne->de", moe_rows, dlogits, preferred_element_type=jnp.float32)
    dnormed2 = droutes + jnp.einsum(
        "ne,de->nd", dlogits, w_router, preferred_element_type=jnp.float32
    )
    dmiddle_norm, moe_gain_part = rms_backward(dnormed2, unit_moe, inv_moe, moe_gain)
    dmiddle = upstream + dmiddle_norm
    dbranch = (RESIDUAL_SCALE * dmiddle).astype(jnp.bfloat16)
    output_part = jnp.einsum("nh,nd->hd", attn_rows, dbranch, preferred_element_type=jnp.float32)
    dattn = (
        jnp.einsum("nd,hd->nh", dbranch, w_output, preferred_element_type=jnp.float32)
        .astype(jnp.bfloat16)
        .reshape(head_shape)
    )
    delta = jnp.sum(dattn.astype(jnp.float32) * attended, axis=-1)

    def both_step(dq_sum, current):
        key_part, value_part, seg_part, index_part = current
        probs_b, dscore = probs_and_ds(
            queries,
            key_part,
            value_part,
            dattn,
            lse_local,
            delta,
            seg_local,
            seg_part,
            query_index,
            index_part,
        )
        dq_part = (
            jnp.einsum("rgjqk,krgd->qrgjd", dscore, key_part, preferred_element_type=jnp.float32)
            * ATTN_SCALE
        )
        dk_part = (
            jnp.einsum("rgjqk,qrgjd->krgd", dscore, queries, preferred_element_type=jnp.float32)
            * ATTN_SCALE
        )
        dv_part = jnp.einsum(
            "rgjqk,qrgjd->krgd", probs_b, dattn, preferred_element_type=jnp.float32
        )
        return (dq_sum + dq_part, (dk_part, dv_part))

    dq_sum, (dk_stack, dv_stack) = lax.scan(
        both_step, jnp.zeros(head_shape, jnp.float32), key_inputs
    )
    full_shape = (length, row_count, KV_HEADS, HEAD_DIM)
    dkeys, dvalues = (
        lax.psum_scatter(
            dk_stack.reshape(full_shape).astype(jnp.bfloat16),
            "expert",
            scatter_dimension=0,
            tiled=True,
        ).astype(jnp.float32),
        lax.psum_scatter(
            dv_stack.reshape(full_shape).astype(jnp.bfloat16),
            "expert",
            scatter_dimension=0,
            tiled=True,
        ).astype(jnp.float32),
    )
    dquery_lin = (
        unrotate(dq_sum.reshape(group_len, row_count, HEADS, HEAD_DIM), cos_heads, sin_heads)
        .astype(jnp.bfloat16)
        .reshape(tok_count, HEADS * HEAD_DIM)
    )
    dkey_lin = (
        unrotate(dkeys, cos_heads, sin_heads)
        .astype(jnp.bfloat16)
        .reshape(tok_count, KV_HEADS * HEAD_DIM)
    )
    dvalue_rows = dvalues.astype(jnp.bfloat16).reshape(tok_count, KV_HEADS * HEAD_DIM)
    query_part_grad = jnp.einsum(
        "nd,nh->dh", normed_rows, dquery_lin, preferred_element_type=jnp.float32
    )
    key_part_grad = jnp.einsum(
        "nd,nh->dh", normed_rows, dkey_lin, preferred_element_type=jnp.float32
    )
    value_part_grad = jnp.einsum(
        "nd,nh->dh", normed_rows, dvalue_rows, preferred_element_type=jnp.float32
    )
    dnormed = (
        jnp.einsum("nh,dh->nd", dquery_lin, w_query, preferred_element_type=jnp.float32)
        + jnp.einsum("nh,dh->nd", dkey_lin, w_key, preferred_element_type=jnp.float32)
        + jnp.einsum("nh,dh->nd", dvalue_rows, w_value, preferred_element_type=jnp.float32)
    )
    dresid_norm, attn_gain_part = rms_backward(dnormed, unit_attn, inv_attn, attn_gain)
    grad_tokens = jnp.swapaxes((dmiddle + dresid_norm).reshape(group_len, row_count, width), 0, 1)
    query_sum, key_sum, value_sum, output_sum, router_sum, attn_gain_sum, moe_gain_sum = lax.psum(
        (
            query_part_grad,
            key_part_grad,
            value_part_grad,
            output_part,
            router_part,
            attn_gain_part,
            moe_gain_part,
        ),
        ("dp", "expert"),
    )
    return (
        mixed,
        grad_tokens,
        attn_gain_sum,
        query_sum,
        key_sum,
        value_sum,
        output_sum,
        moe_gain_sum,
        router_sum,
        grad_gate,
        grad_up,
        grad_down,
    )


def swap(block, shift, axis, count):
    return lax.ppermute(block, axis, [(i, i ^ shift) for i in range(count)])


def relative_ids(me, devices):
    chips = devices // 2
    return [me ^ (2 * c + core) for core in range(2) for c in range(chips)]


def place_of(distance, devices):
    return (distance >> 1) + (devices // 2) * (distance & 1)


def gather_row(block, devices):
    chips = devices // 2
    same = jnp.stack([block] + [swap(block, 2 * c, "expert", devices) for c in range(1, chips)])
    return jnp.concatenate([same, swap(same, 1, "expert", devices)], axis=0)


def reduce_row(blocks, devices):
    chips = devices // 2
    partner = swap(blocks[chips:], 1, "expert", devices)
    merged = (blocks[:chips].astype(jnp.float32) + partner.astype(jnp.float32)).astype(jnp.bfloat16)
    total = merged[0].astype(jnp.float32)
    for c in range(1, chips):
        total = total + swap(merged[c], 2 * c, "expert", devices).astype(jnp.float32)
    return total


def exchange_row(blocks, devices):
    chips = devices // 2
    shifts = [2 * c + core for core in range(2) for c in range(chips)]
    return jnp.stack(
        [blocks[0]]
        + [swap(blocks[b], shifts[b], "expert", devices) for b in range(1, devices)]
    )


def reduce_z(blocks, copies, me_z):
    total = lax.dynamic_index_in_dim(blocks, me_z, 0, False)
    for s in range(1, copies):
        part = lax.dynamic_index_in_dim(blocks, me_z ^ s, 0, False).astype(jnp.bfloat16)
        total = total + swap(part, s, "dp", copies).astype(jnp.float32)
    return total.astype(jnp.bfloat16)


def gather_z(block, copies):
    return jnp.stack([block] + [swap(block, s, "dp", copies) for s in range(1, copies)])


def absolute(parts, me, place):
    count = parts.shape[0]
    return [lax.dynamic_index_in_dim(parts, place(j ^ me), 0, False) for j in range(count)]


def sum_all(vector, devices, copies):
    for axis, count in (("expert", devices), ("dp", copies)):
        total = vector
        for s in range(1, count):
            total = total + swap(vector, s, axis, count)
        vector = total
    return vector


def masked_gates(logits, mask):
    shown = jnp.where(mask, logits, NEG_FILL)
    weight = jnp.where(mask, jnp.exp(shown - jnp.max(shown, axis=-1, keepdims=True)), 0.0)
    return weight / jnp.sum(weight, axis=-1, keepdims=True)


def slot_table(mask_local, gates_local):
    groups, group_len, held = mask_local.shape
    steps = jnp.arange(group_len, dtype=jnp.int32)
    earlier = (steps[None, :] < steps[:, None]).astype(jnp.bfloat16)
    rank = jnp.einsum("mn,gne->gem", earlier, mask_local, preferred_element_type=jnp.float32)
    mask_turned = jnp.swapaxes(mask_local, 1, 2)
    slot = jnp.where(mask_turned > 0, rank, -1.0).astype(jnp.int32)
    chosen = slot[:, :, None, :] == jnp.arange(MOST, dtype=jnp.int32)[None, None, :, None]
    gates_turned = jnp.swapaxes(gates_local, 1, 2)
    gate_slots = jnp.sum(jnp.where(chosen, gates_turned[:, :, None, :], 0.0), axis=-1)
    return (
        chosen.astype(jnp.bfloat16),
        jnp.swapaxes(gate_slots, 0, 1).reshape(held, groups * MOST),
    )


def to_slots(chosen, rows):
    groups, held, most, group_len = chosen.shape
    picked = jnp.einsum(
        "gmn,gnd->gmd",
        chosen.reshape(groups, held * most, group_len),
        rows,
        preferred_element_type=jnp.float32,
    ).astype(jnp.bfloat16)
    width = rows.shape[-1]
    return jnp.swapaxes(picked.reshape(groups, held, most, width), 0, 1).reshape(
        held, groups * most, width
    )


def from_slots(chosen, slot_rows):
    groups, held, most, group_len = chosen.shape
    width = slot_rows.shape[-1]
    by_group = jnp.swapaxes(slot_rows.reshape(held, groups, most, width), 0, 1)
    return jnp.einsum(
        "gmn,gmd->gnd",
        chosen.reshape(groups, held * most, group_len),
        by_group.reshape(groups, held * most, width),
        preferred_element_type=jnp.float32,
    )


def expert_middle(x_slots, g_slots, gate_slots, w_gate, w_up, w_down):
    gate_pre = jnp.einsum("etd,edf->etf", x_slots, w_gate, preferred_element_type=jnp.float32)
    up_pre = jnp.einsum("etd,edf->etf", x_slots, w_up, preferred_element_type=jnp.float32)
    sigma = jax.nn.sigmoid(gate_pre)
    activated = gate_pre * sigma
    hidden = (activated * up_pre).astype(jnp.bfloat16)
    dexpert_out = (
        gate_slots[:, :, None] * (RESIDUAL_SCALE * g_slots.astype(jnp.float32))
    ).astype(jnp.bfloat16)
    dhidden = jnp.einsum("etd,efd->etf", dexpert_out, w_down, preferred_element_type=jnp.float32)
    dgate_pre = (dhidden * up_pre * sigma * (1.0 + gate_pre * (1.0 - sigma))).astype(jnp.bfloat16)
    dup_pre = (dhidden * activated).astype(jnp.bfloat16)
    return (hidden, dexpert_out, dgate_pre, dup_pre)


def weight_grads(x_slots, hidden, dexpert_out, dgate_pre, dup_pre, me_z, copies):
    width, inner = x_slots.shape[-1], hidden.shape[-1]
    x_part = lax.dynamic_slice_in_dim(x_slots, me_z * (width // copies), width // copies, 2)
    h_part = lax.dynamic_slice_in_dim(hidden, me_z * (inner // copies), inner // copies, 2)
    return (
        jnp.einsum("etd,etf->edf", x_part, dgate_pre, preferred_element_type=jnp.float32),
        jnp.einsum("etd,etf->edf", x_part, dup_pre, preferred_element_type=jnp.float32),
        jnp.einsum("etf,etd->efd", h_part, dexpert_out, preferred_element_type=jnp.float32),
    )


def per_device_heads(
    tokens,
    attn_gain,
    w_query,
    w_key,
    w_value,
    w_output,
    moe_gain,
    w_router,
    w_gate,
    w_up,
    w_down,
    routes,
    segment_ids,
    out_grad,
):
    unused, group_len, width = tokens.shape
    devices, copies = lax.axis_size("expert"), lax.axis_size("dp")
    me, me_z = lax.axis_index("expert"), lax.axis_index("dp")
    length = group_len * devices
    repeats = HEADS // KV_HEADS
    query_cols = repeats * HEAD_DIM
    held = EXPERTS // devices
    lanes = 128
    order = jnp.stack(relative_ids(me, devices))
    bf16 = jnp.bfloat16

    own = tokens[0]
    seg_cols = jnp.broadcast_to(segment_ids[0][:, None], (group_len, lanes)).astype(bf16)
    row_pay = gather_row(jnp.concatenate([own, seg_cols], axis=1), devices)
    row_pay = row_pay.reshape(length, width + lanes)
    seg_row = row_pay[:, width].astype(jnp.int32)
    row_index = (order[:, None] * group_len + jnp.arange(group_len, dtype=jnp.int32)).reshape(length)

    head_weights = jnp.concatenate(
        [
            w_query.reshape(width, devices, query_cols),
            w_key.reshape(width, devices, HEAD_DIM),
            w_value.reshape(width, devices, HEAD_DIM),
        ],
        axis=-1,
    )
    head_weights = jnp.swapaxes(head_weights, 0, 1)[order]
    out_weights = w_output.reshape(devices, query_cols, width)[order]
    mask_own = jnp.any(
        routes[0][:, :, None] == jnp.arange(EXPERTS, dtype=jnp.int32)[None, None, :], axis=1
    )
    grad_pay = jnp.concatenate(
        [out_grad[0], jnp.pad(mask_own.astype(bf16), ((0, 0), (0, lanes - EXPERTS)))], axis=1
    )
    grad_pay, row_pay = lax.optimization_barrier((grad_pay, row_pay))
    grad_row = gather_row(grad_pay, devices)
    grad_mine, unused = lax.optimization_barrier((grad_pay, grad_row[devices // 2]))
    grad_far = gather_row(gather_z(grad_mine, copies)[1:], devices)

    before = jnp.sum((seg_row[None, :] < seg_row[:, None]).astype(jnp.int32), axis=1)
    cosine, sine = rope_tables(row_index - before)
    cos_heads, sin_heads = cosine[:, None, :], sine[:, None, :]
    normed, unused, unused2 = rms_forward(row_pay[:, :width].astype(jnp.float32), attn_gain)
    normed_row = normed.astype(bf16)
    lin = jnp.dot(normed_row, head_weights[0], preferred_element_type=jnp.float32)
    queries = rotate(
        lin[:, :query_cols].reshape(length, repeats, HEAD_DIM), cos_heads, sin_heads
    ).astype(bf16)
    keys = rotate(lin[:, query_cols : query_cols + HEAD_DIM], cosine, sine).astype(bf16)
    values = lin[:, query_cols + HEAD_DIM :].astype(bf16)
    scores = (
        jnp.einsum("qhd,kd->hqk", queries, keys, preferred_element_type=jnp.float32) * ATTN_SCALE
    )
    allowed = (seg_row[:, None] == seg_row[None, :]) & (row_index[None, :] <= row_index[:, None])
    masked = jnp.where(allowed[None], scores, NEG_FILL)
    raised = jnp.exp(masked - jnp.max(masked, axis=-1, keepdims=True))
    probs = raised / jnp.sum(raised, axis=-1, keepdims=True)
    probs_b = probs.astype(bf16)
    attended = jnp.einsum("hqk,kd->qhd", probs_b, values, preferred_element_type=jnp.float32)
    attn_heads = attended.astype(bf16).reshape(length, query_cols)
    attn_back = exchange_row(attn_heads.reshape(devices, group_len, query_cols), devices)
    attn_rows = jnp.swapaxes(attn_back, 0, 1).reshape(group_len, devices * query_cols)

    branch = jnp.dot(
        attn_rows, out_weights.reshape(devices * query_cols, width), preferred_element_type=jnp.float32
    )
    residual = own.astype(jnp.float32)
    middle = residual + RESIDUAL_SCALE * branch
    normed2, unit_moe, inv_moe = rms_forward(middle, moe_gain)
    moe_rows = normed2.astype(bf16)
    gates_own = masked_gates(
        jnp.dot(moe_rows, w_router, preferred_element_type=jnp.float32), mask_own
    )
    moe_row = gather_row(moe_rows, devices)
    moe_mine, unused = lax.optimization_barrier((moe_rows, moe_row[devices // 2]))
    moe_far = gather_row(gather_z(moe_mine, copies)[1:], devices)

    def chosen_slots(x_rows, grads):
        x_rows = x_rows.reshape(-1, group_len, width)
        grads = grads.reshape(-1, group_len, width + lanes)
        mask = grads[:, :, width : width + EXPERTS]
        logits = jnp.einsum("gnd,de->gne", x_rows, w_router, preferred_element_type=jnp.float32)
        gates = masked_gates(logits, mask > 0)
        gates_local = lax.dynamic_slice_in_dim(gates, me * held, held, 2)
        mask_local = lax.dynamic_slice_in_dim(mask, me * held, held, 2)
        chosen, gate_slots = slot_table(mask_local, gates_local)
        return (chosen, gate_slots, to_slots(chosen, x_rows), to_slots(chosen, grads[:, :, :width]))

    chosen, gate_slots, x_slots, g_slots = chosen_slots(moe_row, grad_row)
    hidden, dexpert_out, dgate_pre, dup_pre = expert_middle(
        x_slots, g_slots, gate_slots, w_gate, w_up, w_down
    )
    expert_out = jnp.einsum(
        "etf,efd->etd", hidden, w_down, preferred_element_type=jnp.float32
    ).astype(bf16)
    dgate_slots = jnp.sum(
        RESIDUAL_SCALE * g_slots.astype(jnp.float32) * expert_out.astype(jnp.float32), axis=-1
    )
    dgate_slots = jnp.swapaxes(dgate_slots.reshape(held, devices, MOST), 0, 1)
    dgates_local = jnp.sum(
        jnp.where(chosen > 0, dgate_slots[:, :, :, None], 0.0), axis=2
    )
    spread = (
        jnp.arange(lanes, dtype=jnp.int32)[None, :]
        == me * held + jnp.arange(held, dtype=jnp.int32)[:, None]
    )
    dgates_wide = jnp.sum(
        jnp.where(spread[None, :, None, :], dgates_local[:, :, :, None], 0.0), axis=1
    )
    high = dgates_wide.astype(bf16)
    lower = (dgates_wide - high.astype(jnp.float32)).astype(bf16)
    dinputs = (
        jnp.einsum("etf,edf->etd", dgate_pre, w_gate, preferred_element_type=jnp.float32)
        + jnp.einsum("etf,edf->etd", dup_pre, w_up, preferred_element_type=jnp.float32)
    ).astype(bf16)
    dmoe_part = from_slots(chosen, dinputs).astype(bf16)
    returned = reduce_row(jnp.concatenate([dmoe_part, high, lower], axis=-1), devices)
    dgates = returned[:, width : width + EXPERTS] + returned[:, width + lanes : width + lanes + EXPERTS]

    dpicked = gates_own * (dgates - jnp.sum(gates_own * dgates, axis=-1, keepdims=True))
    dlogits = jnp.where(mask_own, dpicked, 0.0).astype(bf16)
    dnormed2 = returned[:, :width] + jnp.einsum(
        "ne,de->nd", dlogits, w_router, preferred_element_type=jnp.float32
    )
    dmiddle_norm, moe_gain_part = rms_backward(dnormed2, unit_moe, inv_moe, moe_gain)
    dmiddle = out_grad[0].astype(jnp.float32) + dmiddle_norm
    dbranch = (RESIDUAL_SCALE * dmiddle).astype(bf16)
    branch_row = gather_row(
        jnp.concatenate([dbranch, jnp.pad(dlogits, ((0, 0), (0, lanes - EXPERTS)))], axis=1), devices
    ).reshape(length, width + lanes)
    dbranch_row, dlogits_row = branch_row[:, :width], branch_row[:, width:]

    rows_per = width // devices
    output_part = jnp.einsum(
        "nh,nd->hd", attn_heads, dbranch_row, preferred_element_type=jnp.float32
    )
    router_cols = lax.dynamic_slice_in_dim(moe_row.reshape(length, width), me * rows_per, rows_per, 1)
    router_part = jnp.einsum(
        "nd,ne->de", router_cols, dlogits_row, preferred_element_type=jnp.float32
    )
    first_part = jnp.concatenate([output_part, router_part], axis=1).reshape(
        copies, query_cols // copies, width + lanes
    )

    def everywhere(part):
        zed = gather_z(reduce_z(part, copies, me_z), copies)
        zed = jnp.concatenate(absolute(zed, me_z, lambda d: d), axis=0)
        return absolute(gather_row(zed, devices), me, lambda d: place_of(d, devices))

    first_all = jnp.concatenate(everywhere(first_part), axis=0)
    grad_output = first_all[:, :width].astype(jnp.float32)
    grad_router = first_all[:, width : width + EXPERTS].astype(jnp.float32)

    dattn = jnp.einsum(
        "nd,hd->nh", dbranch_row, out_weights[0], preferred_element_type=jnp.float32
    ).astype(bf16).reshape(length, repeats, HEAD_DIM)
    delta = jnp.sum(dattn.astype(jnp.float32) * attended, axis=-1)
    dprobs = jnp.einsum("qhd,kd->hqk", dattn, values, preferred_element_type=jnp.float32)
    dscores = (probs * (dprobs - jnp.swapaxes(delta, 0, 1)[:, :, None])).astype(bf16)
    dqueries = (
        jnp.einsum("hqk,kd->qhd", dscores, keys, preferred_element_type=jnp.float32) * ATTN_SCALE
    )
    dkeys = (
        jnp.einsum("hqk,qhd->kd", dscores, queries, preferred_element_type=jnp.float32) * ATTN_SCALE
    )
    dvalues = jnp.einsum("hqk,qhd->kd", probs_b, dattn, preferred_element_type=jnp.float32)
    dlin = jnp.concatenate(
        [
            unrotate(dqueries, cos_heads, sin_heads).astype(bf16).reshape(length, query_cols),
            unrotate(dkeys, cosine, sine).astype(bf16),
            dvalues.astype(bf16),
        ],
        axis=1,
    )
    head_part = jnp.einsum("nd,nh->dh", normed_row, dlin, preferred_element_type=jnp.float32)
    head_cols = query_cols + 2 * HEAD_DIM
    head_all = everywhere(head_part.reshape(copies, width // copies, head_cols))
    grad_query = jnp.concatenate([h[:, :query_cols] for h in head_all], axis=1).astype(jnp.float32)
    grad_key = jnp.concatenate(
        [h[:, query_cols : query_cols + HEAD_DIM] for h in head_all], axis=1
    ).astype(jnp.float32)
    grad_value = jnp.concatenate(
        [h[:, query_cols + HEAD_DIM :] for h in head_all], axis=1
    ).astype(jnp.float32)

    dlin_back = exchange_row(dlin.reshape(devices, group_len, head_cols), devices)
    dnormed = jnp.einsum("bnh,bdh->nd", dlin_back, head_weights, preferred_element_type=jnp.float32)
    unused, unit_attn, inv_attn = rms_forward(residual, attn_gain)
    dresid_norm, attn_gain_part = rms_backward(dnormed, unit_attn, inv_attn, attn_gain)
    grad_tokens = (dmiddle + dresid_norm)[None]
    gain_sums = sum_all(jnp.stack([attn_gain_part, moe_gain_part]), devices, copies)

    sent_back = from_slots(
        chosen, (gate_slots[:, :, None] * expert_out.astype(jnp.float32)).astype(bf16)
    ).astype(bf16)
    mixed = (middle + RESIDUAL_SCALE * reduce_row(sent_back, devices)).astype(bf16)[None]
    near = weight_grads(x_slots, hidden, dexpert_out, dgate_pre, dup_pre, me_z, copies)
    unused, far_gates, far_x, far_g = chosen_slots(moe_far, grad_far)
    far_hidden, far_dexpert, far_dgate, far_dup = expert_middle(
        far_x, far_g, far_gates, w_gate, w_up, w_down
    )
    far = weight_grads(far_x, far_hidden, far_dexpert, far_dgate, far_dup, me_z, copies)
    grad_gate, grad_up, grad_down = (a + b for a, b in zip(near, far))
    return (
        mixed,
        grad_tokens,
        gain_sums[0],
        grad_query,
        grad_key,
        grad_value,
        grad_output,
        gain_sums[1],
        grad_router,
        grad_gate,
        grad_up,
        grad_down,
    )


def solution(mesh):
    placed = (
        P("dp", "expert", None),
        P(),
        P(),
        P(),
        P(),
        P(),
        P(),
        P(),
        P("expert", None, None),
        P("expert", None, None),
        P("expert", None, None),
        P("dp", "expert", None),
        P("dp", "expert"),
        P("dp", "expert", None),
    )
    whole_heads = mesh.shape["expert"] == KV_HEADS and mesh.shape["dp"] & (mesh.shape["dp"] - 1) == 0
    return jax.shard_map(
        per_device_heads if whole_heads else per_device_general,
        mesh=mesh,
        in_specs=placed,
        out_specs=(
            P("dp", "expert", None),
            P("dp", "expert", None),
            P(),
            P(),
            P(),
            P(),
            P(),
            P(),
            P(),
            P("expert", "dp", None),
            P("expert", "dp", None),
            P("expert", "dp", None),
        ),
        check_vma=False,
    )
```

```python
import jax
import jax.numpy as jnp
from jax import lax
from jax.experimental import pallas as pl
from jax.experimental.pallas import tpu as pltpu
from jax.sharding import PartitionSpec as P

HEADS = 16
KV_HEADS = 8
HEAD_DIM = 64
EXPERTS = 32
TOP = 8
MOST = 48


ATTN_SCALE = 0.015625
RESIDUAL_SCALE = 0.22
NORM_EPS = 1e-06
ROPE_BASE = 10000.0
NEG_FILL = -1e30


def rms_forward(values, gain_vec):
    inverse = lax.rsqrt(jnp.mean(values * values, axis=-1, keepdims=True) + NORM_EPS)
    unit_rows = values * inverse
    return (unit_rows * gain_vec, unit_rows, inverse)


def rms_backward(grad_rows, unit_rows, inverse, gain_vec):
    scaled = grad_rows * gain_vec
    grad_gain = jnp.sum(grad_rows * unit_rows, axis=0)
    grad_in = inverse * (scaled - unit_rows * jnp.mean(scaled * unit_rows, axis=-1, keepdims=True))
    return (grad_in, grad_gain)


def rope_tables(positions):
    half = HEAD_DIM // 2
    freqs = ROPE_BASE ** (-(jnp.arange(half, dtype=jnp.float32) * 2.0) / HEAD_DIM)
    angles = positions.astype(jnp.float32)[..., None] * freqs
    cosine = jnp.concatenate([jnp.cos(angles), jnp.cos(angles)], axis=-1)
    sine = jnp.concatenate([jnp.sin(angles), jnp.sin(angles)], axis=-1)
    return (cosine, sine)


def rotate(vectors, cosine, sine):
    half = vectors.shape[-1] // 2
    turned = jnp.concatenate([-vectors[..., half:], vectors[..., :half]], axis=-1)
    return vectors * cosine + turned * sine


def unrotate(grads, cosine, sine):
    half = grads.shape[-1] // 2
    scaled = grads * sine
    turned = jnp.concatenate([scaled[..., half:], -scaled[..., :half]], axis=-1)
    return grads * cosine + turned


def scaled_scores(query_part, key_part, query_seg, key_seg, query_index, key_index):
    raw = (
        jnp.einsum("qrgjd,krgd->rgjqk", query_part, key_part, preferred_element_type=jnp.float32)
        * ATTN_SCALE
    )
    same = jnp.transpose(query_seg)[:, :, None] == jnp.transpose(key_seg)[:, None, :]
    before = key_index[None, :] <= query_index[:, None]
    return (raw, (same & before[None])[:, None, None])


def probs_and_ds(
    query_part,
    key_part,
    value_part,
    dout_part,
    lse_part,
    delta_part,
    query_seg,
    key_seg,
    query_index,
    key_index,
):
    scores, allowed = scaled_scores(
        query_part, key_part, query_seg, key_seg, query_index, key_index
    )
    lse_rows = jnp.transpose(lse_part, (1, 2, 3, 0))[..., None]
    delta_rows = jnp.transpose(delta_part, (1, 2, 3, 0))[..., None]
    probs = jnp.where(allowed, jnp.exp(scores - lse_rows), 0.0)
    dprobs = jnp.einsum(
        "qrgjd,krgd->rgjqk", dout_part, value_part, preferred_element_type=jnp.float32
    )
    dscore = (probs * (dprobs - delta_rows)).astype(jnp.bfloat16)
    return (probs.astype(jnp.bfloat16), dscore)


def per_device_general(
    tokens,
    attn_gain,
    w_query,
    w_key,
    w_value,
    w_output,
    moe_gain,
    w_router,
    w_gate,
    w_up,
    w_down,
    routes,
    segment_ids,
    out_grad,
):
    row_count, group_len, width = tokens.shape
    devices = lax.axis_size("expert")
    my_index = lax.axis_index("expert")
    length = group_len * devices
    repeats = HEADS // KV_HEADS
    tok_count = group_len * row_count
    slot_rows = row_count * MOST
    seg_local = jnp.transpose(segment_ids)
    seg_all = lax.all_gather(seg_local, "expert", axis=0, tiled=True)
    query_index = my_index * group_len + jnp.arange(group_len, dtype=jnp.int32)
    earlier = jnp.sum((seg_all[None, :, :] < seg_local[:, None, :]).astype(jnp.int32), axis=1)
    cosine, sine = rope_tables(query_index[:, None] - earlier)
    cos_heads = cosine[:, :, None, :]
    sin_heads = sine[:, :, None, :]
    residual = jnp.swapaxes(tokens, 0, 1).astype(jnp.float32).reshape(tok_count, width)
    normed, unit_attn, inv_attn = rms_forward(residual, attn_gain)
    normed_rows = normed.astype(jnp.bfloat16)
    query_lin = jnp.dot(normed_rows, w_query, preferred_element_type=jnp.float32).reshape(
        group_len, row_count, HEADS, HEAD_DIM
    )
    queries = (
        rotate(query_lin, cos_heads, sin_heads)
        .astype(jnp.bfloat16)
        .reshape(group_len, row_count, KV_HEADS, repeats, HEAD_DIM)
    )
    key_lin = jnp.dot(normed_rows, w_key, preferred_element_type=jnp.float32).reshape(
        group_len, row_count, KV_HEADS, HEAD_DIM
    )
    keys = rotate(key_lin, cos_heads, sin_heads).astype(jnp.bfloat16)
    values = (
        jnp.dot(normed_rows, w_value, preferred_element_type=jnp.float32)
        .astype(jnp.bfloat16)
        .reshape(group_len, row_count, KV_HEADS, HEAD_DIM)
    )
    keys_all, values_all = (
        lax.all_gather(keys, "expert", axis=0, tiled=True),
        lax.all_gather(values, "expert", axis=0, tiled=True),
    )
    key_block = min(1024, length)
    block_count = length // key_block
    key_blocks = keys_all.reshape(block_count, key_block, row_count, KV_HEADS, HEAD_DIM)
    value_blocks = values_all.reshape(block_count, key_block, row_count, KV_HEADS, HEAD_DIM)
    seg_blocks = seg_all.reshape(block_count, key_block, row_count)
    index_blocks = jnp.arange(length, dtype=jnp.int32).reshape(block_count, key_block)
    key_inputs = (key_blocks, value_blocks, seg_blocks, index_blocks)

    def max_step(carried, current):
        running, totals = carried
        key_part, value_part, seg_part, index_part = current
        scores, allowed = scaled_scores(
            queries, key_part, seg_local, seg_part, query_index, index_part
        )
        newmax = jnp.maximum(running, jnp.max(jnp.where(allowed, scores, NEG_FILL), axis=-1))
        totals = totals * jnp.exp(running - newmax) + jnp.sum(
            jnp.where(allowed, jnp.exp(scores - newmax[..., None]), 0.0), axis=-1
        )
        return ((newmax, totals), None)

    stat_shape = (row_count, KV_HEADS, repeats, group_len)
    (running, totals), unused = lax.scan(
        max_step,
        (jnp.full(stat_shape, NEG_FILL, jnp.float32), jnp.zeros(stat_shape, jnp.float32)),
        key_inputs,
    )
    logsum = running + jnp.log(totals)
    lse_local = jnp.transpose(logsum, (3, 0, 1, 2))

    def out_step(accum, current):
        key_part, value_part, seg_part, index_part = current
        scores, allowed = scaled_scores(
            queries, key_part, seg_local, seg_part, query_index, index_part
        )
        probs = jnp.where(allowed, jnp.exp(scores - logsum[..., None]), 0.0).astype(jnp.bfloat16)
        return (
            accum
            + jnp.einsum(
                "rgjqk,krgd->qrgjd", probs, value_part, preferred_element_type=jnp.float32
            ),
            None,
        )

    head_shape = (group_len, row_count, KV_HEADS, repeats, HEAD_DIM)
    attended, unused = lax.scan(out_step, jnp.zeros(head_shape, jnp.float32), key_inputs)
    attn_rows = attended.reshape(tok_count, HEADS * HEAD_DIM).astype(jnp.bfloat16)
    branch = jnp.dot(attn_rows, w_output, preferred_element_type=jnp.float32)
    middle = residual + RESIDUAL_SCALE * branch
    normed2, unit_moe, inv_moe = rms_forward(middle, moe_gain)
    moe_rows = normed2.astype(jnp.bfloat16)
    logits = jnp.dot(moe_rows, w_router, preferred_element_type=jnp.float32)
    route_rows = jnp.transpose(routes, (1, 0, 2)).reshape(tok_count, TOP)
    onehot = route_rows[:, :, None] == jnp.arange(EXPERTS, dtype=jnp.int32)[None, None, :]
    picked = jnp.sum(jnp.where(onehot, logits[:, None, :], 0.0), axis=-1)
    gates = jax.nn.softmax(picked, axis=-1)
    by_row = jnp.transpose(
        onehot.reshape(group_len, row_count, TOP, EXPERTS), (1, 0, 2, 3)
    ).reshape(row_count, group_len * TOP, EXPERTS)
    counted = jnp.cumsum(by_row.astype(jnp.int32), axis=1)
    rank = jnp.sum(jnp.where(by_row, counted - 1, 0), axis=-1).reshape(row_count, group_len, TOP)
    rank = jnp.transpose(rank, (1, 0, 2)).reshape(tok_count, TOP)
    row_of = jnp.arange(tok_count, dtype=jnp.int32) % row_count
    target = (route_rows * slot_rows + row_of[:, None] * MOST + rank).reshape(tok_count * TOP)

    def to_slots(route_values):
        placed = (
            jnp.zeros((EXPERTS * slot_rows, width), jnp.bfloat16)
            .at[target]
            .set(route_values.reshape(tok_count * TOP, width))
        )
        return placed.reshape(EXPERTS, slot_rows, width)

    def from_slots(slot_values):
        return (
            slot_values.reshape(EXPERTS * slot_rows, width)[target]
            .reshape(tok_count, TOP, width)
            .astype(jnp.float32)
        )

    sent = to_slots(jnp.broadcast_to(moe_rows[:, None, :], (tok_count, TOP, width)))
    arrived = lax.all_to_all(sent, "expert", split_axis=0, concat_axis=1, tiled=True)
    gate_pre = jnp.einsum("etd,edf->etf", arrived, w_gate, preferred_element_type=jnp.float32)
    up_pre = jnp.einsum("etd,edf->etf", arrived, w_up, preferred_element_type=jnp.float32)
    sigma = jax.nn.sigmoid(gate_pre)
    activated = gate_pre * sigma
    hidden = (activated * up_pre).astype(jnp.bfloat16)
    expert_out = jnp.einsum(
        "etf,efd->etd", hidden, w_down, preferred_element_type=jnp.float32
    ).astype(jnp.bfloat16)
    returned = lax.all_to_all(expert_out, "expert", split_axis=1, concat_axis=0, tiled=True)
    route_out = from_slots(returned)
    moe = jnp.sum(gates[:, :, None] * route_out, axis=1)
    mixed_rows = middle + RESIDUAL_SCALE * moe
    mixed = jnp.swapaxes(mixed_rows.reshape(group_len, row_count, width), 0, 1).astype(jnp.bfloat16)
    upstream = jnp.swapaxes(out_grad, 0, 1).astype(jnp.float32).reshape(tok_count, width)
    dmoe = RESIDUAL_SCALE * upstream
    dgates = jnp.sum(route_out * dmoe[:, None, :], axis=-1)
    dsent = to_slots((gates[:, :, None] * dmoe[:, None, :]).astype(jnp.bfloat16))
    darrived = lax.all_to_all(dsent, "expert", split_axis=0, concat_axis=1, tiled=True)
    dhidden = jnp.einsum("etd,efd->etf", darrived, w_down, preferred_element_type=jnp.float32)
    down_part = jnp.einsum("etf,etd->efd", hidden, darrived, preferred_element_type=jnp.float32)
    dgate_pre = (dhidden * up_pre * sigma * (1.0 + gate_pre * (1.0 - sigma))).astype(jnp.bfloat16)
    dup_pre = (dhidden * activated).astype(jnp.bfloat16)
    gate_part = jnp.einsum("etd,etf->edf", arrived, dgate_pre, preferred_element_type=jnp.float32)
    up_part = jnp.einsum("etd,etf->edf", arrived, dup_pre, preferred_element_type=jnp.float32)
    dinputs = (
        jnp.einsum("etf,edf->etd", dgate_pre, w_gate, preferred_element_type=jnp.float32)
        + jnp.einsum("etf,edf->etd", dup_pre, w_up, preferred_element_type=jnp.float32)
    ).astype(jnp.bfloat16)
    grad_gate, grad_up, grad_down = (
        lax.psum_scatter(
            gate_part.astype(jnp.bfloat16), "dp", scatter_dimension=1, tiled=True
        ).astype(jnp.float32),
        lax.psum_scatter(
            up_part.astype(jnp.bfloat16), "dp", scatter_dimension=1, tiled=True
        ).astype(jnp.float32),
        lax.psum_scatter(
            down_part.astype(jnp.bfloat16), "dp", scatter_dimension=1, tiled=True
        ).astype(jnp.float32),
    )
    dreturned = lax.all_to_all(dinputs, "expert", split_axis=1, concat_axis=0, tiled=True)
    droutes = jnp.sum(from_slots(dreturned), axis=1)
    dpicked = gates * (dgates - jnp.sum(gates * dgates, axis=-1, keepdims=True))
    dlogits = jnp.sum(jnp.where(onehot, dpicked[:, :, None], 0.0), axis=1).astype(jnp.bfloat16)
    router_part = jnp.einsum("nd,ne->de", moe_rows, dlogits, preferred_element_type=jnp.float32)
    dnormed2 = droutes + jnp.einsum(
        "ne,de->nd", dlogits, w_router, preferred_element_type=jnp.float32
    )
    dmiddle_norm, moe_gain_part = rms_backward(dnormed2, unit_moe, inv_moe, moe_gain)
    dmiddle = upstream + dmiddle_norm
    dbranch = (RESIDUAL_SCALE * dmiddle).astype(jnp.bfloat16)
    output_part = jnp.einsum("nh,nd->hd", attn_rows, dbranch, preferred_element_type=jnp.float32)
    dattn = (
        jnp.einsum("nd,hd->nh", dbranch, w_output, preferred_element_type=jnp.float32)
        .astype(jnp.bfloat16)
        .reshape(head_shape)
    )
    delta = jnp.sum(dattn.astype(jnp.float32) * attended, axis=-1)

    def both_step(dq_sum, current):
        key_part, value_part, seg_part, index_part = current
        probs_b, dscore = probs_and_ds(
            queries,
            key_part,
            value_part,
            dattn,
            lse_local,
            delta,
            seg_local,
            seg_part,
            query_index,
            index_part,
        )
        dq_part = (
            jnp.einsum("rgjqk,krgd->qrgjd", dscore, key_part, preferred_element_type=jnp.float32)
            * ATTN_SCALE
        )
        dk_part = (
            jnp.einsum("rgjqk,qrgjd->krgd", dscore, queries, preferred_element_type=jnp.float32)
            * ATTN_SCALE
        )
        dv_part = jnp.einsum(
            "rgjqk,qrgjd->krgd", probs_b, dattn, preferred_element_type=jnp.float32
        )
        return (dq_sum + dq_part, (dk_part, dv_part))

    dq_sum, (dk_stack, dv_stack) = lax.scan(
        both_step, jnp.zeros(head_shape, jnp.float32), key_inputs
    )
    full_shape = (length, row_count, KV_HEADS, HEAD_DIM)
    dkeys, dvalues = (
        lax.psum_scatter(
            dk_stack.reshape(full_shape).astype(jnp.bfloat16),
            "expert",
            scatter_dimension=0,
            tiled=True,
        ).astype(jnp.float32),
        lax.psum_scatter(
            dv_stack.reshape(full_shape).astype(jnp.bfloat16),
            "expert",
            scatter_dimension=0,
            tiled=True,
        ).astype(jnp.float32),
    )
    dquery_lin = (
        unrotate(dq_sum.reshape(group_len, row_count, HEADS, HEAD_DIM), cos_heads, sin_heads)
        .astype(jnp.bfloat16)
        .reshape(tok_count, HEADS * HEAD_DIM)
    )
    dkey_lin = (
        unrotate(dkeys, cos_heads, sin_heads)
        .astype(jnp.bfloat16)
        .reshape(tok_count, KV_HEADS * HEAD_DIM)
    )
    dvalue_rows = dvalues.astype(jnp.bfloat16).reshape(tok_count, KV_HEADS * HEAD_DIM)
    query_part_grad = jnp.einsum(
        "nd,nh->dh", normed_rows, dquery_lin, preferred_element_type=jnp.float32
    )
    key_part_grad = jnp.einsum(
        "nd,nh->dh", normed_rows, dkey_lin, preferred_element_type=jnp.float32
    )
    value_part_grad = jnp.einsum(
        "nd,nh->dh", normed_rows, dvalue_rows, preferred_element_type=jnp.float32
    )
    dnormed = (
        jnp.einsum("nh,dh->nd", dquery_lin, w_query, preferred_element_type=jnp.float32)
        + jnp.einsum("nh,dh->nd", dkey_lin, w_key, preferred_element_type=jnp.float32)
        + jnp.einsum("nh,dh->nd", dvalue_rows, w_value, preferred_element_type=jnp.float32)
    )
    dresid_norm, attn_gain_part = rms_backward(dnormed, unit_attn, inv_attn, attn_gain)
    grad_tokens = jnp.swapaxes((dmiddle + dresid_norm).reshape(group_len, row_count, width), 0, 1)
    query_sum, key_sum, value_sum, output_sum, router_sum, attn_gain_sum, moe_gain_sum = lax.psum(
        (
            query_part_grad,
            key_part_grad,
            value_part_grad,
            output_part,
            router_part,
            attn_gain_part,
            moe_gain_part,
        ),
        ("dp", "expert"),
    )
    return (
        mixed,
        grad_tokens,
        attn_gain_sum,
        query_sum,
        key_sum,
        value_sum,
        output_sum,
        moe_gain_sum,
        router_sum,
        grad_gate,
        grad_up,
        grad_down,
    )


def expert_gather(x_rows, g_rows, mask_rows, slot_rows, router_rows, first, x_scr, g_scr, gate_scr, table_scr, groups):
    held = x_scr.shape[0]
    for g in range(groups):
        rows = x_rows(g)
        logits = lax.dot_general(
            router_rows, rows, (((1,), (1,)), ((), ())), preferred_element_type=jnp.float32
        )
        shown = mask_rows(g) > 0
        raised = jnp.where(
            shown,
            jnp.exp(logits - jnp.max(jnp.where(shown, logits, NEG_FILL), axis=0, keepdims=True)),
            0.0,
        )
        gates = raised / jnp.sum(raised, axis=0, keepdims=True)
        slots = slot_rows(g)
        expert = lax.broadcasted_iota(jnp.int32, gates.shape, 0)
        place = lax.broadcasted_iota(jnp.int32, (MOST, rows.shape[0]), 0)
        tables = []
        for e in range(held):
            gate_row = jnp.sum(jnp.where(expert == first + e, gates, 0.0), axis=0, keepdims=True)
            chosen = place == slots[e : e + 1, :]
            gate_scr[e, g * MOST : (g + 1) * MOST, :] = jnp.sum(
                jnp.where(chosen, gate_row, 0.0), axis=1, keepdims=True
            )
            tables.append(jnp.where(chosen, 1.0, 0.0))
        table = jnp.concatenate(tables, axis=0).astype(jnp.bfloat16)
        if table_scr is not None:
            table_scr[g] = table
        for scr, part in ((x_scr, rows), (g_scr, g_rows(g))):
            picked = jnp.dot(table, part, preferred_element_type=jnp.float32).astype(jnp.bfloat16)
            for e in range(held):
                scr[e, g * MOST : (g + 1) * MOST, :] = picked[e * MOST : (e + 1) * MOST, :]


def nt(left, right):
    return lax.dot_general(
        left, right, (((1,), (1,)), ((), ())), preferred_element_type=jnp.float32
    )


def tn(left, right):
    return lax.dot_general(
        left, right, (((0,), (0,)), ((), ())), preferred_element_type=jnp.float32
    )


def expert_body(x_slots, g_slots, gate_col, gate_w, up_w, down_w):
    gate_pre = jnp.dot(x_slots, gate_w, preferred_element_type=jnp.float32)
    up_pre = jnp.dot(x_slots, up_w, preferred_element_type=jnp.float32)
    sigma = jax.nn.sigmoid(gate_pre)
    activated = gate_pre * sigma
    hidden = (activated * up_pre).astype(jnp.bfloat16)
    dexpert = (gate_col * (RESIDUAL_SCALE * g_slots.astype(jnp.float32))).astype(jnp.bfloat16)
    dhidden = nt(dexpert, down_w)
    dgate_pre = (dhidden * up_pre * sigma * (1.0 + gate_pre * (1.0 - sigma))).astype(jnp.bfloat16)
    dup_pre = (dhidden * activated).astype(jnp.bfloat16)
    return hidden, dexpert, dgate_pre, dup_pre


def near_experts(me, x_near, x_twin, g_row, mask_row, slot_row, router_t, w_gate, w_up, w_down):
    chips, group_len, width = x_near.shape
    held, unused, inner = w_gate.shape
    groups = 2 * chips
    extra = 16
    lanes = 128

    def kernel(me_ref, xn, xt, gr, mr, sr, rt, wg, wu, wd, near_out, twin_out, y_near, y_twin,
               x_scr, g_scr, gate_scr, table_scr, y_scr, d_scr, dg_scr):
        e = pl.program_id(0)
        my = me_ref[0]
        core = my & 1

        def device(g):
            return 2 * (g % chips) + (core ^ (g // chips))

        @pl.when(e == 0)
        def _():
            expert_gather(
                lambda g: (xn if g < chips else xt)[g % chips],
                lambda g: gr[device(g)],
                lambda g: mr[device(g)],
                lambda g: sr[device(g)],
                rt[...],
                my * held,
                x_scr, g_scr, gate_scr, table_scr, groups,
            )

        g_slots = g_scr[e]
        hidden, dexpert, dgate_pre, dup_pre = expert_body(
            x_scr[e], g_slots, gate_scr[e], wg[0], wu[0], wd[0]
        )
        out = jnp.dot(hidden, wd[0], preferred_element_type=jnp.float32).astype(jnp.bfloat16)
        out_wide = out.astype(jnp.float32)
        dgate = jnp.sum(
            RESIDUAL_SCALE * g_slots.astype(jnp.float32) * out_wide, axis=1, keepdims=True
        )
        weighted = (gate_scr[e] * out_wide).astype(jnp.bfloat16)
        dinputs = (nt(dgate_pre, wg[0]) + nt(dup_pre, wu[0])).astype(jnp.bfloat16)
        spot = pl.ds(pl.multiple_of(e * MOST, 16), MOST)
        for g in range(groups):
            part = slice(g * MOST, (g + 1) * MOST)
            y_scr[g, spot, :] = weighted[part]
            d_scr[g, spot, :] = dinputs[part]
            taken = table_scr[g, spot, :].astype(jnp.float32)
            dg_scr[g, e] = jnp.sum(taken * dgate[part], axis=0, keepdims=True)

        @pl.when(e == held - 1)
        def _():
            block = lax.broadcasted_iota(jnp.int32, (held, width), 1) // lanes
            for g in range(groups):
                d_out, y_out = (near_out, y_near) if g < chips else (twin_out, y_twin)
                table = table_scr[g]
                y_out[g % chips] = tn(table, y_scr[g]).astype(jnp.bfloat16)
                d_out[g % chips, :group_len, :] = tn(table, d_scr[g]).astype(jnp.bfloat16)
                rows = jnp.concatenate([dg_scr[g, i] for i in range(held)], axis=0)
                spread = jnp.where(block == my, jnp.concatenate([rows] * groups, axis=1), 0.0)
                high = spread.astype(jnp.bfloat16).astype(jnp.float32)
                tail = jnp.concatenate(
                    [high, spread - high, jnp.zeros((extra - 2 * held, width), jnp.float32)], axis=0
                )
                d_out[g % chips, group_len:, :] = tail.astype(jnp.bfloat16)

    whole = lambda *shape: pl.BlockSpec(shape, lambda e, m: (0,) * len(shape))
    weight = lambda *shape: pl.BlockSpec((1,) + shape, lambda e, m: (e, 0, 0))
    back = jax.ShapeDtypeStruct((chips, group_len + extra, width), jnp.bfloat16)
    forth = jax.ShapeDtypeStruct((chips, group_len, width), jnp.bfloat16)
    slots = groups * MOST
    return pl.pallas_call(
        kernel,
        grid_spec=pltpu.PrefetchScalarGridSpec(
            num_scalar_prefetch=1,
            grid=(held,),
            in_specs=[
                whole(chips, group_len, width),
                whole(chips, group_len, width),
                whole(groups, group_len, width),
                whole(groups, EXPERTS, group_len),
                whole(groups, held, group_len),
                whole(EXPERTS, width),
                weight(width, inner),
                weight(width, inner),
                weight(inner, width),
            ],
            out_specs=[
                whole(chips, group_len + extra, width),
                whole(chips, group_len + extra, width),
                whole(chips, group_len, width),
                whole(chips, group_len, width),
            ],
            scratch_shapes=[
                pltpu.VMEM((held, slots, width), jnp.bfloat16),
                pltpu.VMEM((held, slots, width), jnp.bfloat16),
                pltpu.VMEM((held, slots, 1), jnp.float32),
                pltpu.VMEM((groups, held * MOST, group_len), jnp.bfloat16),
                pltpu.VMEM((groups, held * MOST, width), jnp.bfloat16),
                pltpu.VMEM((groups, held * MOST, width), jnp.bfloat16),
                pltpu.VMEM((groups, held, 1, group_len), jnp.float32),
            ],
        ),
        out_shape=[back, back, forth, forth],
        compiler_params=pltpu.CompilerParams(
            dimension_semantics=("arbitrary",), vmem_limit_bytes=58 * 2**20
        ),
        name="near_experts",
    )(me.reshape(1), x_near, x_twin, g_row, mask_row, slot_row, router_t, w_gate, w_up, w_down)


def expert_weight_grads(ids, x_all, g_all, mask_all, slot_all, router_t, w_gate, w_up, w_down, copies):
    total, group_len, width = x_all.shape
    held, unused, inner = w_gate.shape
    groups = 8
    chunks = total // groups
    slots = groups * MOST
    wide, narrow = width // copies, inner // copies

    def kernel(ids_ref, xr, gr, mr, sr, rt, wg, wu, wd, gate_out, up_out, down_out,
               x_scr, g_scr, gate_scr):
        c, e = pl.program_id(0), pl.program_id(1)
        mine, slab = ids_ref[0], ids_ref[1]

        @pl.when(e == 0)
        def _():
            expert_gather(
                lambda g: xr[g], lambda g: gr[g], lambda g: mr[g], lambda g: sr[g],
                rt[...], mine * held, x_scr, g_scr, gate_scr, None, groups,
            )

        x_slots = x_scr[e]
        hidden, dexpert, dgate_pre, dup_pre = expert_body(
            x_slots, g_scr[e], gate_scr[e], wg[0], wu[0], wd[0]
        )
        x_part, h_part = x_slots[:, :wide], hidden[:, :narrow]
        for k in range(1, copies):
            x_part = jnp.where(slab == k, x_slots[:, k * wide : (k + 1) * wide], x_part)
            h_part = jnp.where(slab == k, hidden[:, k * narrow : (k + 1) * narrow], h_part)
        for out, left, right in (
            (gate_out, x_part, dgate_pre),
            (up_out, x_part, dup_pre),
            (down_out, h_part, dexpert),
        ):
            part = tn(left, right)

            @pl.when(c == 0)
            def _():
                out[e] = part

            @pl.when(c > 0)
            def _():
                out[e] = out[e] + part

    some = lambda *shape: pl.BlockSpec((groups,) + shape, lambda c, e, m: (c, 0, 0))
    weight = lambda *shape: pl.BlockSpec((1,) + shape, lambda c, e, m: (e, 0, 0))
    whole = lambda *shape: pl.BlockSpec(shape, lambda c, e, m: (0,) * len(shape))
    outs = [(held, wide, inner), (held, wide, inner), (held, narrow, width)]
    return pl.pallas_call(
        kernel,
        grid_spec=pltpu.PrefetchScalarGridSpec(
            num_scalar_prefetch=1,
            grid=(chunks, held),
            in_specs=[
                some(group_len, width),
                some(group_len, width),
                some(EXPERTS, group_len),
                some(held, group_len),
                whole(EXPERTS, width),
                weight(width, inner),
                weight(width, inner),
                weight(inner, width),
            ],
            out_specs=[whole(*shape) for shape in outs],
            scratch_shapes=[
                pltpu.VMEM((held, slots, width), jnp.bfloat16),
                pltpu.VMEM((held, slots, width), jnp.bfloat16),
                pltpu.VMEM((held, slots, 1), jnp.float32),
            ],
        ),
        out_shape=[jax.ShapeDtypeStruct(shape, jnp.float32) for shape in outs],
        compiler_params=pltpu.CompilerParams(
            dimension_semantics=("arbitrary", "arbitrary"), vmem_limit_bytes=58 * 2**20
        ),
        name="expert_weight_grads",
    )(ids, x_all, g_all, mask_all, slot_all, router_t, w_gate, w_up, w_down)


def swap_cores(block, devices):
    return lax.ppermute(block, "expert", [(i, i ^ 1) for i in range(devices)])


def across_chips(blocks, devices):
    groups = [[2 * c + core for c in range(devices // 2)] for core in range(2)]
    return lax.all_to_all(blocks, "expert", 0, 0, axis_index_groups=groups, tiled=True)


def spread_row(block, devices):
    near = across_chips(jnp.broadcast_to(block[None], (devices // 2,) + block.shape), devices)
    return near, swap_cores(near, devices)


def reduce_row(near, twin, devices):
    partner = swap_cores(twin, devices)
    merged = (near.astype(jnp.float32) + partner.astype(jnp.float32)).astype(jnp.bfloat16)
    return jnp.sum(across_chips(merged, devices).astype(jnp.float32), axis=0)


def in_order(near, twin, core):
    even = jnp.where(core == 0, near, twin)
    odd = jnp.where(core == 0, twin, near)
    return jnp.stack([even, odd], axis=1).reshape((2 * near.shape[0],) + near.shape[1:])


def exchange(blocks, axis):
    return lax.all_to_all(blocks, axis, 0, 0, tiled=True)


def broadcast(block, count):
    return jnp.broadcast_to(block[None], (count,) + block.shape)


def masked_gates(logits, mask):
    shown = jnp.where(mask, logits, NEG_FILL)
    weight = jnp.where(mask, jnp.exp(shown - jnp.max(shown, axis=-1, keepdims=True)), 0.0)
    return weight / jnp.sum(weight, axis=-1, keepdims=True)


def slot_tables(mask, first, held):
    group_len = mask.shape[1]
    turned = jnp.swapaxes(mask, 1, 2)
    local = lax.dynamic_slice_in_dim(turned, first, held, 1)
    steps = jnp.arange(group_len, dtype=jnp.int32)
    earlier = (steps[:, None] < steps[None, :]).astype(jnp.bfloat16)
    rank = jnp.einsum("gem,mn->gen", local, earlier, preferred_element_type=jnp.float32)
    return turned, jnp.where(local > 0, rank, -1.0).astype(jnp.int32)


def per_device_heads(
    tokens,
    attn_gain,
    w_query,
    w_key,
    w_value,
    w_output,
    moe_gain,
    w_router,
    w_gate,
    w_up,
    w_down,
    routes,
    segment_ids,
    out_grad,
):
    unused, group_len, width = tokens.shape
    devices, copies = lax.axis_size("expert"), lax.axis_size("dp")
    me, me_z = lax.axis_index("expert"), lax.axis_index("dp")
    core = me & 1
    chips = devices // 2
    length = group_len * devices
    repeats = HEADS // KV_HEADS
    query_cols = repeats * HEAD_DIM
    held = EXPERTS // devices
    lanes = 128
    order = jnp.stack([2 * c + (core ^ k) for k in range(2) for c in range(chips)])
    bf16 = jnp.bfloat16

    own = tokens[0]
    seg_cols = jnp.broadcast_to(segment_ids[0][:, None], (group_len, lanes)).astype(bf16)
    near_pay, twin_pay = spread_row(jnp.concatenate([own, seg_cols], axis=1), devices)
    row_pay = jnp.concatenate([near_pay, twin_pay], axis=0).reshape(length, width + lanes)
    seg_row = row_pay[:, width].astype(jnp.int32)
    row_index = (order[:, None] * group_len + jnp.arange(group_len, dtype=jnp.int32)).reshape(length)

    mask_own = jnp.any(
        routes[0][:, :, None] == jnp.arange(EXPERTS, dtype=jnp.int32)[None, None, :], axis=1
    )
    grad_pay = jnp.concatenate(
        [out_grad[0], jnp.pad(mask_own.astype(bf16), ((0, 0), (0, lanes - EXPERTS)))], axis=1
    )
    grad_all = lax.all_gather(grad_pay, ("dp", "expert"), axis=0)
    grad_later, row_pay = lax.optimization_barrier((grad_pay, row_pay))
    grad_row = in_order(*spread_row(grad_later, devices), core)
    mask_row, slot_row = slot_tables(grad_row[:, :, width : width + EXPERTS], me * held, held)
    router_t = jnp.swapaxes(w_router, 0, 1)

    head_weights = jnp.concatenate(
        [
            lax.dynamic_slice_in_dim(w_query, me * query_cols, query_cols, 1),
            lax.dynamic_slice_in_dim(w_key, me * HEAD_DIM, HEAD_DIM, 1),
            lax.dynamic_slice_in_dim(w_value, me * HEAD_DIM, HEAD_DIM, 1),
        ],
        axis=1,
    )
    before = jnp.sum((seg_row[None, :] < seg_row[:, None]).astype(jnp.int32), axis=1)
    cosine, sine = rope_tables(row_index - before)
    cos_heads, sin_heads = cosine[:, None, :], sine[:, None, :]
    normed, unused, unused2 = rms_forward(row_pay[:, :width].astype(jnp.float32), attn_gain)
    normed_row = normed.astype(bf16)
    lin = jnp.dot(normed_row, head_weights, preferred_element_type=jnp.float32)
    queries = rotate(
        lin[:, :query_cols].reshape(length, repeats, HEAD_DIM), cos_heads, sin_heads
    ).astype(bf16)
    keys = rotate(lin[:, query_cols : query_cols + HEAD_DIM], cosine, sine).astype(bf16)
    values = lin[:, query_cols + HEAD_DIM :].astype(bf16)
    scores = (
        jnp.einsum("qhd,kd->hqk", queries, keys, preferred_element_type=jnp.float32) * ATTN_SCALE
    )
    allowed = (seg_row[:, None] == seg_row[None, :]) & (row_index[None, :] <= row_index[:, None])
    masked = jnp.where(allowed[None], scores, NEG_FILL)
    raised = jnp.exp(masked - jnp.max(masked, axis=-1, keepdims=True))
    probs = raised / jnp.sum(raised, axis=-1, keepdims=True)
    probs_b = probs.astype(bf16)
    attended = jnp.einsum("hqk,kd->qhd", probs_b, values, preferred_element_type=jnp.float32)
    attn_heads = attended.astype(bf16).reshape(length, query_cols)

    def to_tokens(rows):
        blocks = rows.reshape(2, chips, group_len, rows.shape[-1])
        return exchange(in_order(blocks[0], blocks[1], core), "expert")

    attn_rows = jnp.swapaxes(to_tokens(attn_heads), 0, 1).reshape(group_len, devices * query_cols)

    branch = jnp.dot(attn_rows, w_output, preferred_element_type=jnp.float32)
    residual = own.astype(jnp.float32)
    middle = residual + RESIDUAL_SCALE * branch
    normed2, unit_moe, inv_moe = rms_forward(middle, moe_gain)
    moe_rows = normed2.astype(bf16)
    gates_own = masked_gates(
        jnp.dot(moe_rows, w_router, preferred_element_type=jnp.float32), mask_own
    )
    x_near, x_twin = spread_row(moe_rows, devices)
    moe_all = lax.all_gather(moe_rows, ("dp", "expert"), axis=0)

    d_near, d_twin, y_near, y_twin = near_experts(
        me, x_near, x_twin, grad_row, mask_row, slot_row, router_t, w_gate, w_up, w_down
    )
    returned = reduce_row(d_near, d_twin, devices)

    parts = returned[group_len : group_len + held] + returned[group_len + held : group_len + 2 * held]
    dgates = jnp.transpose(parts.reshape(held, devices, group_len), (2, 1, 0)).reshape(
        group_len, EXPERTS
    )
    dpicked = gates_own * (dgates - jnp.sum(gates_own * dgates, axis=-1, keepdims=True))
    dlogits = jnp.where(mask_own, dpicked, 0.0).astype(bf16)
    dnormed2 = returned[:group_len] + jnp.einsum(
        "ne,de->nd", dlogits, w_router, preferred_element_type=jnp.float32
    )
    dmiddle_norm, moe_gain_part = rms_backward(dnormed2, unit_moe, inv_moe, moe_gain)
    dmiddle = out_grad[0].astype(jnp.float32) + dmiddle_norm
    dbranch = (RESIDUAL_SCALE * dmiddle).astype(bf16)
    branch_near, branch_twin = spread_row(
        jnp.concatenate([dbranch, jnp.pad(dlogits, ((0, 0), (0, lanes - EXPERTS)))], axis=1), devices
    )
    branch_row = jnp.concatenate([branch_near, branch_twin], axis=0).reshape(length, width + lanes)
    dbranch_row, dlogits_row = branch_row[:, :width], branch_row[:, width:]

    rows_per = width // devices
    output_part = jnp.einsum(
        "nh,nd->hd", attn_heads, dbranch_row, preferred_element_type=jnp.float32
    )
    router_cols = lax.dynamic_slice_in_dim(
        jnp.concatenate([x_near, x_twin], axis=0).reshape(length, width), me * rows_per, rows_per, 1
    )
    router_part = jnp.einsum(
        "nd,ne->de", router_cols, dlogits_row, preferred_element_type=jnp.float32
    )
    first_part = jnp.concatenate([output_part, router_part], axis=1).reshape(
        copies, query_cols // copies, width + lanes
    )

    def everywhere(part):
        summed = jnp.sum(exchange(part.astype(bf16), "dp").astype(jnp.float32), axis=0).astype(bf16)
        column = exchange(broadcast(summed, copies), "dp")
        column = column.reshape((copies * summed.shape[0],) + summed.shape[1:])
        near, twin = spread_row(column, devices)
        return in_order(near, twin, core)

    first_all = everywhere(first_part).reshape(devices * query_cols, width + lanes)
    grad_output = first_all[:, :width].astype(jnp.float32)
    grad_router = first_all[:, width : width + EXPERTS].astype(jnp.float32)

    out_heads = lax.dynamic_slice_in_dim(w_output, me * query_cols, query_cols, 0)
    dattn = jnp.einsum(
        "nd,hd->nh", dbranch_row, out_heads, preferred_element_type=jnp.float32
    ).astype(bf16).reshape(length, repeats, HEAD_DIM)
    delta = jnp.sum(dattn.astype(jnp.float32) * attended, axis=-1)
    dprobs = jnp.einsum("qhd,kd->hqk", dattn, values, preferred_element_type=jnp.float32)
    dscores = (probs * (dprobs - jnp.swapaxes(delta, 0, 1)[:, :, None])).astype(bf16)
    dqueries = (
        jnp.einsum("hqk,kd->qhd", dscores, keys, preferred_element_type=jnp.float32) * ATTN_SCALE
    )
    dkeys = (
        jnp.einsum("hqk,qhd->kd", dscores, queries, preferred_element_type=jnp.float32) * ATTN_SCALE
    )
    dvalues = jnp.einsum("hqk,qhd->kd", probs_b, dattn, preferred_element_type=jnp.float32)
    dlin = jnp.concatenate(
        [
            unrotate(dqueries, cos_heads, sin_heads).astype(bf16).reshape(length, query_cols),
            unrotate(dkeys, cosine, sine).astype(bf16),
            dvalues.astype(bf16),
        ],
        axis=1,
    )
    head_part = jnp.einsum("nd,nh->dh", normed_row, dlin, preferred_element_type=jnp.float32)
    head_cols = query_cols + 2 * HEAD_DIM
    head_all = everywhere(head_part.reshape(copies, width // copies, head_cols))

    def columns(start, count):
        return jnp.swapaxes(head_all[:, :, start : start + count], 0, 1).reshape(
            width, devices * count
        ).astype(jnp.float32)

    grad_query = columns(0, query_cols)
    grad_key = columns(query_cols, HEAD_DIM)
    grad_value = columns(query_cols + HEAD_DIM, HEAD_DIM)

    dlin_back = jnp.swapaxes(to_tokens(dlin), 0, 1)

    def token_grad(start, count, weights):
        rows = dlin_back[:, :, start : start + count].reshape(group_len, devices * count)
        return jnp.einsum("nh,dh->nd", rows, weights, preferred_element_type=jnp.float32)

    dnormed = (
        token_grad(0, query_cols, w_query)
        + token_grad(query_cols, HEAD_DIM, w_key)
        + token_grad(query_cols + HEAD_DIM, HEAD_DIM, w_value)
    )
    unused, unit_attn, inv_attn = rms_forward(residual, attn_gain)
    dresid_norm, attn_gain_part = rms_backward(dnormed, unit_attn, inv_attn, attn_gain)
    grad_tokens = (dmiddle + dresid_norm)[None]
    gain_sums = jnp.stack([attn_gain_part, moe_gain_part])
    for axis, count in (("expert", devices), ("dp", copies)):
        gain_sums = jnp.sum(exchange(broadcast(gain_sums, count), axis), axis=0)

    mixed = (middle + RESIDUAL_SCALE * reduce_row(y_near, y_twin, devices)).astype(bf16)[None]
    mask_all, slot_all = slot_tables(grad_all[:, :, width : width + EXPERTS], me * held, held)
    grad_gate, grad_up, grad_down = expert_weight_grads(
        jnp.stack([me, me_z]), moe_all, grad_all, mask_all, slot_all, router_t, w_gate, w_up, w_down, copies
    )
    return (
        mixed,
        grad_tokens,
        gain_sums[0],
        grad_query,
        grad_key,
        grad_value,
        grad_output,
        gain_sums[1],
        grad_router,
        grad_gate,
        grad_up,
        grad_down,
    )


def solution(mesh):
    placed = (
        P("dp", "expert", None),
        P(),
        P(),
        P(),
        P(),
        P(),
        P(),
        P(),
        P("expert", None, None),
        P("expert", None, None),
        P("expert", None, None),
        P("dp", "expert", None),
        P("dp", "expert"),
        P("dp", "expert", None),
    )
    by_heads = mesh.shape["expert"] == KV_HEADS
    return jax.shard_map(
        per_device_heads if by_heads else per_device_general,
        mesh=mesh,
        in_specs=placed,
        out_specs=(
            P("dp", "expert", None),
            P("dp", "expert", None),
            P(),
            P(),
            P(),
            P(),
            P(),
            P(),
            P(),
            P("expert", "dp", None),
            P("expert", "dp", None),
            P("expert", "dp", None),
        ),
        check_vma=False,
    )
```

```python
import jax
import jax.numpy as jnp
from jax import lax
from jax.experimental import pallas as pl
from jax.experimental.pallas import tpu as pltpu
from jax.sharding import PartitionSpec as P


HEADS = 16
KV_HEADS = 8
HEAD_DIM = 64
EXPERTS = 32
TOP = 8
MOST = 48


ATTN_SCALE = 0.015625
RESIDUAL_SCALE = 0.22
NORM_EPS = 1e-06
ROPE_BASE = 10000.0
NEG_FILL = -1e30
TAIL = 16


def rms_forward(values, gain_vec):
    inverse = lax.rsqrt(jnp.mean(values * values, axis=-1, keepdims=True) + NORM_EPS)
    unit_rows = values * inverse
    return (unit_rows * gain_vec, unit_rows, inverse)


def rms_backward(grad_rows, unit_rows, inverse, gain_vec):
    scaled = grad_rows * gain_vec
    grad_gain = jnp.sum(grad_rows * unit_rows, axis=0)
    grad_in = inverse * (scaled - unit_rows * jnp.mean(scaled * unit_rows, axis=-1, keepdims=True))
    return (grad_in, grad_gain)


def rope_tables(positions):
    half = HEAD_DIM // 2
    freqs = ROPE_BASE ** (-(jnp.arange(half, dtype=jnp.float32) * 2.0) / HEAD_DIM)
    angles = positions.astype(jnp.float32)[..., None] * freqs
    cosine = jnp.concatenate([jnp.cos(angles), jnp.cos(angles)], axis=-1)
    sine = jnp.concatenate([jnp.sin(angles), jnp.sin(angles)], axis=-1)
    return (cosine, sine)


def rotate(vectors, cosine, sine):
    half = vectors.shape[-1] // 2
    turned = jnp.concatenate([-vectors[..., half:], vectors[..., :half]], axis=-1)
    return vectors * cosine + turned * sine


def unrotate(grads, cosine, sine):
    half = grads.shape[-1] // 2
    scaled = grads * sine
    turned = jnp.concatenate([scaled[..., half:], -scaled[..., :half]], axis=-1)
    return grads * cosine + turned


def scaled_scores(query_part, key_part, query_seg, key_seg, query_index, key_index):
    raw = (
        jnp.einsum("qrgjd,krgd->rgjqk", query_part, key_part, preferred_element_type=jnp.float32)
        * ATTN_SCALE
    )
    same = jnp.transpose(query_seg)[:, :, None] == jnp.transpose(key_seg)[:, None, :]
    before = key_index[None, :] <= query_index[:, None]
    return (raw, (same & before[None])[:, None, None])


def probs_and_ds(
    query_part,
    key_part,
    value_part,
    dout_part,
    lse_part,
    delta_part,
    query_seg,
    key_seg,
    query_index,
    key_index,
):
    scores, allowed = scaled_scores(
        query_part, key_part, query_seg, key_seg, query_index, key_index
    )
    lse_rows = jnp.transpose(lse_part, (1, 2, 3, 0))[..., None]
    delta_rows = jnp.transpose(delta_part, (1, 2, 3, 0))[..., None]
    probs = jnp.where(allowed, jnp.exp(scores - lse_rows), 0.0)
    dprobs = jnp.einsum(
        "qrgjd,krgd->rgjqk", dout_part, value_part, preferred_element_type=jnp.float32
    )
    dscore = (probs * (dprobs - delta_rows)).astype(jnp.bfloat16)
    return (probs.astype(jnp.bfloat16), dscore)


def per_device_general(
    tokens,
    attn_gain,
    w_query,
    w_key,
    w_value,
    w_output,
    moe_gain,
    w_router,
    w_gate,
    w_up,
    w_down,
    routes,
    segment_ids,
    out_grad,
):
    row_count, group_len, width = tokens.shape
    devices = lax.axis_size("expert")
    my_index = lax.axis_index("expert")
    length = group_len * devices
    repeats = HEADS // KV_HEADS
    tok_count = group_len * row_count
    slot_rows = row_count * MOST
    seg_local = jnp.transpose(segment_ids)
    seg_all = lax.all_gather(seg_local, "expert", axis=0, tiled=True)
    query_index = my_index * group_len + jnp.arange(group_len, dtype=jnp.int32)
    earlier = jnp.sum((seg_all[None, :, :] < seg_local[:, None, :]).astype(jnp.int32), axis=1)
    cosine, sine = rope_tables(query_index[:, None] - earlier)
    cos_heads = cosine[:, :, None, :]
    sin_heads = sine[:, :, None, :]
    residual = jnp.swapaxes(tokens, 0, 1).astype(jnp.float32).reshape(tok_count, width)
    normed, unit_attn, inv_attn = rms_forward(residual, attn_gain)
    normed_rows = normed.astype(jnp.bfloat16)
    query_lin = jnp.dot(normed_rows, w_query, preferred_element_type=jnp.float32).reshape(
        group_len, row_count, HEADS, HEAD_DIM
    )
    queries = (
        rotate(query_lin, cos_heads, sin_heads)
        .astype(jnp.bfloat16)
        .reshape(group_len, row_count, KV_HEADS, repeats, HEAD_DIM)
    )
    key_lin = jnp.dot(normed_rows, w_key, preferred_element_type=jnp.float32).reshape(
        group_len, row_count, KV_HEADS, HEAD_DIM
    )
    keys = rotate(key_lin, cos_heads, sin_heads).astype(jnp.bfloat16)
    values = (
        jnp.dot(normed_rows, w_value, preferred_element_type=jnp.float32)
        .astype(jnp.bfloat16)
        .reshape(group_len, row_count, KV_HEADS, HEAD_DIM)
    )
    keys_all, values_all = (
        lax.all_gather(keys, "expert", axis=0, tiled=True),
        lax.all_gather(values, "expert", axis=0, tiled=True),
    )
    key_block = min(1024, length)
    block_count = length // key_block
    key_blocks = keys_all.reshape(block_count, key_block, row_count, KV_HEADS, HEAD_DIM)
    value_blocks = values_all.reshape(block_count, key_block, row_count, KV_HEADS, HEAD_DIM)
    seg_blocks = seg_all.reshape(block_count, key_block, row_count)
    index_blocks = jnp.arange(length, dtype=jnp.int32).reshape(block_count, key_block)
    key_inputs = (key_blocks, value_blocks, seg_blocks, index_blocks)

    def max_step(carried, current):
        running, totals = carried
        key_part, _, seg_part, index_part = current
        scores, allowed = scaled_scores(
            queries, key_part, seg_local, seg_part, query_index, index_part
        )
        newmax = jnp.maximum(running, jnp.max(jnp.where(allowed, scores, NEG_FILL), axis=-1))
        totals = totals * jnp.exp(running - newmax) + jnp.sum(
            jnp.where(allowed, jnp.exp(scores - newmax[..., None]), 0.0), axis=-1
        )
        return ((newmax, totals), None)

    stat_shape = (row_count, KV_HEADS, repeats, group_len)
    (running, totals), unused = lax.scan(
        max_step,
        (jnp.full(stat_shape, NEG_FILL, jnp.float32), jnp.zeros(stat_shape, jnp.float32)),
        key_inputs,
    )
    logsum = running + jnp.log(totals)
    lse_local = jnp.transpose(logsum, (3, 0, 1, 2))

    def out_step(accum, current):
        key_part, value_part, seg_part, index_part = current
        scores, allowed = scaled_scores(
            queries, key_part, seg_local, seg_part, query_index, index_part
        )
        probs = jnp.where(allowed, jnp.exp(scores - logsum[..., None]), 0.0).astype(jnp.bfloat16)
        return (
            accum
            + jnp.einsum(
                "rgjqk,krgd->qrgjd", probs, value_part, preferred_element_type=jnp.float32
            ),
            None,
        )

    head_shape = (group_len, row_count, KV_HEADS, repeats, HEAD_DIM)
    attended, unused = lax.scan(out_step, jnp.zeros(head_shape, jnp.float32), key_inputs)
    attn_rows = attended.reshape(tok_count, HEADS * HEAD_DIM).astype(jnp.bfloat16)
    branch = jnp.dot(attn_rows, w_output, preferred_element_type=jnp.float32)
    middle = residual + RESIDUAL_SCALE * branch
    normed2, unit_moe, inv_moe = rms_forward(middle, moe_gain)
    moe_rows = normed2.astype(jnp.bfloat16)
    logits = jnp.dot(moe_rows, w_router, preferred_element_type=jnp.float32)
    route_rows = jnp.transpose(routes, (1, 0, 2)).reshape(tok_count, TOP)
    onehot = route_rows[:, :, None] == jnp.arange(EXPERTS, dtype=jnp.int32)[None, None, :]
    picked = jnp.sum(jnp.where(onehot, logits[:, None, :], 0.0), axis=-1)
    gates = jax.nn.softmax(picked, axis=-1)
    by_row = jnp.transpose(
        onehot.reshape(group_len, row_count, TOP, EXPERTS), (1, 0, 2, 3)
    ).reshape(row_count, group_len * TOP, EXPERTS)
    counted = jnp.cumsum(by_row.astype(jnp.int32), axis=1)
    rank = jnp.sum(jnp.where(by_row, counted - 1, 0), axis=-1).reshape(row_count, group_len, TOP)
    rank = jnp.transpose(rank, (1, 0, 2)).reshape(tok_count, TOP)
    row_of = jnp.arange(tok_count, dtype=jnp.int32) % row_count
    target = (route_rows * slot_rows + row_of[:, None] * MOST + rank).reshape(tok_count * TOP)

    def to_slots(route_values):
        placed = (
            jnp.zeros((EXPERTS * slot_rows, width), jnp.bfloat16)
            .at[target]
            .set(route_values.reshape(tok_count * TOP, width))
        )
        return placed.reshape(EXPERTS, slot_rows, width)

    def from_slots(slot_values):
        return (
            slot_values.reshape(EXPERTS * slot_rows, width)[target]
            .reshape(tok_count, TOP, width)
            .astype(jnp.float32)
        )

    sent = to_slots(jnp.broadcast_to(moe_rows[:, None, :], (tok_count, TOP, width)))
    arrived = lax.all_to_all(sent, "expert", split_axis=0, concat_axis=1, tiled=True)
    gate_pre = jnp.einsum("etd,edf->etf", arrived, w_gate, preferred_element_type=jnp.float32)
    up_pre = jnp.einsum("etd,edf->etf", arrived, w_up, preferred_element_type=jnp.float32)
    sigma = jax.nn.sigmoid(gate_pre)
    activated = gate_pre * sigma
    hidden = (activated * up_pre).astype(jnp.bfloat16)
    expert_out = jnp.einsum(
        "etf,efd->etd", hidden, w_down, preferred_element_type=jnp.float32
    ).astype(jnp.bfloat16)
    returned = lax.all_to_all(expert_out, "expert", split_axis=1, concat_axis=0, tiled=True)
    route_out = from_slots(returned)
    moe = jnp.sum(gates[:, :, None] * route_out, axis=1)
    mixed_rows = middle + RESIDUAL_SCALE * moe
    mixed = jnp.swapaxes(mixed_rows.reshape(group_len, row_count, width), 0, 1).astype(jnp.bfloat16)
    upstream = jnp.swapaxes(out_grad, 0, 1).astype(jnp.float32).reshape(tok_count, width)
    dmoe = RESIDUAL_SCALE * upstream
    dgates = jnp.sum(route_out * dmoe[:, None, :], axis=-1)
    dsent = to_slots((gates[:, :, None] * dmoe[:, None, :]).astype(jnp.bfloat16))
    darrived = lax.all_to_all(dsent, "expert", split_axis=0, concat_axis=1, tiled=True)
    dhidden = jnp.einsum("etd,efd->etf", darrived, w_down, preferred_element_type=jnp.float32)
    down_part = jnp.einsum("etf,etd->efd", hidden, darrived, preferred_element_type=jnp.float32)
    dgate_pre = (dhidden * up_pre * sigma * (1.0 + gate_pre * (1.0 - sigma))).astype(jnp.bfloat16)
    dup_pre = (dhidden * activated).astype(jnp.bfloat16)
    gate_part = jnp.einsum("etd,etf->edf", arrived, dgate_pre, preferred_element_type=jnp.float32)
    up_part = jnp.einsum("etd,etf->edf", arrived, dup_pre, preferred_element_type=jnp.float32)
    dinputs = (
        jnp.einsum("etf,edf->etd", dgate_pre, w_gate, preferred_element_type=jnp.float32)
        + jnp.einsum("etf,edf->etd", dup_pre, w_up, preferred_element_type=jnp.float32)
    ).astype(jnp.bfloat16)
    grad_gate, grad_up, grad_down = (
        lax.psum_scatter(
            gate_part.astype(jnp.bfloat16), "dp", scatter_dimension=1, tiled=True
        ).astype(jnp.float32),
        lax.psum_scatter(
            up_part.astype(jnp.bfloat16), "dp", scatter_dimension=1, tiled=True
        ).astype(jnp.float32),
        lax.psum_scatter(
            down_part.astype(jnp.bfloat16), "dp", scatter_dimension=1, tiled=True
        ).astype(jnp.float32),
    )
    dreturned = lax.all_to_all(dinputs, "expert", split_axis=1, concat_axis=0, tiled=True)
    droutes = jnp.sum(from_slots(dreturned), axis=1)
    dpicked = gates * (dgates - jnp.sum(gates * dgates, axis=-1, keepdims=True))
    dlogits = jnp.sum(jnp.where(onehot, dpicked[:, :, None], 0.0), axis=1).astype(jnp.bfloat16)
    router_part = jnp.einsum("nd,ne->de", moe_rows, dlogits, preferred_element_type=jnp.float32)
    dnormed2 = droutes + jnp.einsum(
        "ne,de->nd", dlogits, w_router, preferred_element_type=jnp.float32
    )
    dmiddle_norm, moe_gain_part = rms_backward(dnormed2, unit_moe, inv_moe, moe_gain)
    dmiddle = upstream + dmiddle_norm
    dbranch = (RESIDUAL_SCALE * dmiddle).astype(jnp.bfloat16)
    output_part = jnp.einsum("nh,nd->hd", attn_rows, dbranch, preferred_element_type=jnp.float32)
    dattn = (
        jnp.einsum("nd,hd->nh", dbranch, w_output, preferred_element_type=jnp.float32)
        .astype(jnp.bfloat16)
        .reshape(head_shape)
    )
    delta = jnp.sum(dattn.astype(jnp.float32) * attended, axis=-1)

    def both_step(dq_sum, current):
        key_part, value_part, seg_part, index_part = current
        probs_b, dscore = probs_and_ds(
            queries,
            key_part,
            value_part,
            dattn,
            lse_local,
            delta,
            seg_local,
            seg_part,
            query_index,
            index_part,
        )
        dq_part = (
            jnp.einsum("rgjqk,krgd->qrgjd", dscore, key_part, preferred_element_type=jnp.float32)
            * ATTN_SCALE
        )
        dk_part = (
            jnp.einsum("rgjqk,qrgjd->krgd", dscore, queries, preferred_element_type=jnp.float32)
            * ATTN_SCALE
        )
        dv_part = jnp.einsum(
            "rgjqk,qrgjd->krgd", probs_b, dattn, preferred_element_type=jnp.float32
        )
        return (dq_sum + dq_part, (dk_part, dv_part))

    dq_sum, (dk_stack, dv_stack) = lax.scan(
        both_step, jnp.zeros(head_shape, jnp.float32), key_inputs
    )
    full_shape = (length, row_count, KV_HEADS, HEAD_DIM)
    dkeys, dvalues = (
        lax.psum_scatter(
            dk_stack.reshape(full_shape).astype(jnp.bfloat16),
            "expert",
            scatter_dimension=0,
            tiled=True,
        ).astype(jnp.float32),
        lax.psum_scatter(
            dv_stack.reshape(full_shape).astype(jnp.bfloat16),
            "expert",
            scatter_dimension=0,
            tiled=True,
        ).astype(jnp.float32),
    )
    dquery_lin = (
        unrotate(dq_sum.reshape(group_len, row_count, HEADS, HEAD_DIM), cos_heads, sin_heads)
        .astype(jnp.bfloat16)
        .reshape(tok_count, HEADS * HEAD_DIM)
    )
    dkey_lin = (
        unrotate(dkeys, cos_heads, sin_heads)
        .astype(jnp.bfloat16)
        .reshape(tok_count, KV_HEADS * HEAD_DIM)
    )
    dvalue_rows = dvalues.astype(jnp.bfloat16).reshape(tok_count, KV_HEADS * HEAD_DIM)
    query_part_grad = jnp.einsum(
        "nd,nh->dh", normed_rows, dquery_lin, preferred_element_type=jnp.float32
    )
    key_part_grad = jnp.einsum(
        "nd,nh->dh", normed_rows, dkey_lin, preferred_element_type=jnp.float32
    )
    value_part_grad = jnp.einsum(
        "nd,nh->dh", normed_rows, dvalue_rows, preferred_element_type=jnp.float32
    )
    dnormed = (
        jnp.einsum("nh,dh->nd", dquery_lin, w_query, preferred_element_type=jnp.float32)
        + jnp.einsum("nh,dh->nd", dkey_lin, w_key, preferred_element_type=jnp.float32)
        + jnp.einsum("nh,dh->nd", dvalue_rows, w_value, preferred_element_type=jnp.float32)
    )
    dresid_norm, attn_gain_part = rms_backward(dnormed, unit_attn, inv_attn, attn_gain)
    grad_tokens = jnp.swapaxes((dmiddle + dresid_norm).reshape(group_len, row_count, width), 0, 1)
    query_sum, key_sum, value_sum, output_sum, router_sum, attn_gain_sum, moe_gain_sum = lax.psum(
        (
            query_part_grad,
            key_part_grad,
            value_part_grad,
            output_part,
            router_part,
            attn_gain_part,
            moe_gain_part,
        ),
        ("dp", "expert"),
    )
    return (
        mixed,
        grad_tokens,
        attn_gain_sum,
        query_sum,
        key_sum,
        value_sum,
        output_sum,
        moe_gain_sum,
        router_sum,
        grad_gate,
        grad_up,
        grad_down,
    )


def expert_gather(x_rows, g_rows, mask_rows, slot_rows, router_rows, first, x_scr, g_scr, gate_scr, table_scr, groups):
    held = x_scr.shape[0]
    for g in range(groups):
        rows = x_rows(g)
        logits = lax.dot_general(
            router_rows, rows, (((1,), (1,)), ((), ())), preferred_element_type=jnp.float32
        )
        shown = mask_rows(g) > 0
        raised = jnp.where(
            shown,
            jnp.exp(logits - jnp.max(jnp.where(shown, logits, NEG_FILL), axis=0, keepdims=True)),
            0.0,
        )
        gates = raised / jnp.sum(raised, axis=0, keepdims=True)
        slots = slot_rows(g)
        expert = lax.broadcasted_iota(jnp.int32, gates.shape, 0)
        place = lax.broadcasted_iota(jnp.int32, (MOST, rows.shape[0]), 0)
        tables = []
        for e in range(held):
            gate_row = jnp.sum(jnp.where(expert == first + e, gates, 0.0), axis=0, keepdims=True)
            chosen = place == slots[e : e + 1, :]
            gate_scr[e, g * MOST : (g + 1) * MOST, :] = jnp.sum(
                jnp.where(chosen, gate_row, 0.0), axis=1, keepdims=True
            )
            tables.append(jnp.where(chosen, 1.0, 0.0))
        table = jnp.concatenate(tables, axis=0).astype(jnp.bfloat16)
        if table_scr is not None:
            table_scr[g] = table
        for scr, part in ((x_scr, rows), (g_scr, g_rows(g))):
            picked = jnp.dot(table, part, preferred_element_type=jnp.float32).astype(jnp.bfloat16)
            for e in range(held):
                scr[e, g * MOST : (g + 1) * MOST, :] = picked[e * MOST : (e + 1) * MOST, :]


def nt(left, right):
    return lax.dot_general(
        left, right, (((1,), (1,)), ((), ())), preferred_element_type=jnp.float32
    )


def tn(left, right):
    return lax.dot_general(
        left, right, (((0,), (0,)), ((), ())), preferred_element_type=jnp.float32
    )


def expert_body(x_slots, g_slots, gate_col, gate_w, up_w, down_w):
    gate_pre = jnp.dot(x_slots, gate_w, preferred_element_type=jnp.float32)
    up_pre = jnp.dot(x_slots, up_w, preferred_element_type=jnp.float32)
    sigma = jax.nn.sigmoid(gate_pre)
    activated = gate_pre * sigma
    hidden = (activated * up_pre).astype(jnp.bfloat16)
    dexpert = (gate_col * (RESIDUAL_SCALE * g_slots.astype(jnp.float32))).astype(jnp.bfloat16)
    dhidden = nt(dexpert, down_w)
    dgate_pre = (dhidden * up_pre * sigma * (1.0 + gate_pre * (1.0 - sigma))).astype(jnp.bfloat16)
    dup_pre = (dhidden * activated).astype(jnp.bfloat16)
    return hidden, dexpert, dgate_pre, dup_pre


def near_experts(me, x_near, x_twin, g_near, g_twin, mask_row, slot_row, router_t, w_gate, w_up, w_down):
    chips, group_len, width = x_near.shape
    held, _, inner = w_gate.shape
    groups = 2 * chips
    extra = 16
    lanes = 128

    def kernel(me_ref, xn, xt, gn, gt, mr, sr, rt, wg, wu, wd, near_out, twin_out, y_near, y_twin,
               x_scr, g_scr, gate_scr, table_scr, y_scr, d_scr, dg_scr):
        e = pl.program_id(0)
        my = me_ref[0]

        @pl.when(e == 0)
        def _():
            expert_gather(
                lambda g: (xn if g < chips else xt)[g % chips],
                lambda g: (gn if g < chips else gt)[g % chips],
                lambda g: mr[g],
                lambda g: sr[g],
                rt[...],
                my * held,
                x_scr, g_scr, gate_scr, table_scr, groups,
            )

        g_slots = g_scr[e]
        hidden, _, dgate_pre, dup_pre = expert_body(
            x_scr[e], g_slots, gate_scr[e], wg[0], wu[0], wd[0]
        )
        out = jnp.dot(hidden, wd[0], preferred_element_type=jnp.float32).astype(jnp.bfloat16)
        out_wide = out.astype(jnp.float32)
        dgate = jnp.sum(
            RESIDUAL_SCALE * g_slots.astype(jnp.float32) * out_wide, axis=1, keepdims=True
        )
        weighted = (gate_scr[e] * out_wide).astype(jnp.bfloat16)
        dinputs = (nt(dgate_pre, wg[0]) + nt(dup_pre, wu[0])).astype(jnp.bfloat16)
        spot = pl.ds(pl.multiple_of(e * MOST, 16), MOST)
        for g in range(groups):
            part = slice(g * MOST, (g + 1) * MOST)
            y_scr[g, spot, :] = weighted[part]
            d_scr[g, spot, :] = dinputs[part]
            taken = table_scr[g, spot, :].astype(jnp.float32)
            dg_scr[g, e] = jnp.sum(taken * dgate[part], axis=0, keepdims=True)

        @pl.when(e == held - 1)
        def _():
            block = lax.broadcasted_iota(jnp.int32, (held, width), 1) // lanes
            for g in range(groups):
                d_out, y_out = (near_out, y_near) if g < chips else (twin_out, y_twin)
                table = table_scr[g]
                y_out[g % chips] = tn(table, y_scr[g]).astype(jnp.bfloat16)
                d_out[g % chips, :group_len, :] = tn(table, d_scr[g]).astype(jnp.bfloat16)
                rows = jnp.concatenate([dg_scr[g, i] for i in range(held)], axis=0)
                spread = jnp.where(block == my, jnp.concatenate([rows] * groups, axis=1), 0.0)
                high = spread.astype(jnp.bfloat16).astype(jnp.float32)
                tail = jnp.concatenate(
                    [high, spread - high, jnp.zeros((extra - 2 * held, width), jnp.float32)], axis=0
                )
                d_out[g % chips, group_len:, :] = tail.astype(jnp.bfloat16)

    whole = lambda *shape: pl.BlockSpec(shape, lambda e, m: (0,) * len(shape))
    weight = lambda *shape: pl.BlockSpec((1,) + shape, lambda e, m: (e, 0, 0))
    back = jax.ShapeDtypeStruct((chips, group_len + extra, width), jnp.bfloat16)
    forth = jax.ShapeDtypeStruct((chips, group_len, width), jnp.bfloat16)
    slots = groups * MOST
    return pl.pallas_call(
        kernel,
        grid_spec=pltpu.PrefetchScalarGridSpec(
            num_scalar_prefetch=1,
            grid=(held,),
            in_specs=[
                whole(chips, group_len, width),
                whole(chips, group_len, width),
                whole(chips, group_len, width),
                whole(chips, group_len, width),
                whole(groups, EXPERTS, group_len),
                whole(groups, held, group_len),
                whole(EXPERTS, width),
                weight(width, inner),
                weight(width, inner),
                weight(inner, width),
            ],
            out_specs=[
                whole(chips, group_len + extra, width),
                whole(chips, group_len + extra, width),
                whole(chips, group_len, width),
                whole(chips, group_len, width),
            ],
            scratch_shapes=[
                pltpu.VMEM((held, slots, width), jnp.bfloat16),
                pltpu.VMEM((held, slots, width), jnp.bfloat16),
                pltpu.VMEM((held, slots, 1), jnp.float32),
                pltpu.VMEM((groups, held * MOST, group_len), jnp.bfloat16),
                pltpu.VMEM((groups, held * MOST, width), jnp.bfloat16),
                pltpu.VMEM((groups, held * MOST, width), jnp.bfloat16),
                pltpu.VMEM((groups, held, 1, group_len), jnp.float32),
            ],
        ),
        out_shape=[back, back, forth, forth],
        compiler_params=pltpu.CompilerParams(
            dimension_semantics=("arbitrary",), vmem_limit_bytes=58 * 2**20
        ),
        cost_estimate=pl.CostEstimate(
            flops=2 * 7 * held * slots * width * inner, transcendentals=0, bytes_accessed=2**24
        ),
        name="near_experts",
    )(me.reshape(1), x_near, x_twin, g_near, g_twin, mask_row, slot_row, router_t, w_gate, w_up, w_down)


def expert_weight_grads(ids, sums, x_near, x_twin, g_near, g_twin, mask_all, slot_all, router_t, weights, copies):
    unused, chips, group_len, width = x_near.shape
    held, unused, inner = weights[0].shape
    groups = 2 * chips
    slots = groups * MOST
    wide, narrow = width // copies, inner // copies

    def kernel(ids_ref, xn, xt, gn, gt, mr, sr, rt, wg, wu, wd, *refs):
        gate_out, up_out, down_out, x_scr, g_scr, gate_scr = refs[-6:]
        befores = refs[:-6] if sums is not None else (None, None, None)
        e = pl.program_id(0)
        mine, slab = ids_ref[0], ids_ref[1]

        @pl.when(e == 0)
        def _():
            expert_gather(
                lambda g: (xn if g < chips else xt)[0, g % chips],
                lambda g: (gn if g < chips else gt)[0, g % chips],
                lambda g: mr[g],
                lambda g: sr[g],
                rt[...], mine * held, x_scr, g_scr, gate_scr, None, groups,
            )

        x_slots = x_scr[e]
        hidden, dexpert, dgate_pre, dup_pre = expert_body(
            x_slots, g_scr[e], gate_scr[e], wg[0], wu[0], wd[0]
        )
        x_part, h_part = x_slots[:, :wide], hidden[:, :narrow]
        for k in range(1, copies):
            x_part = jnp.where(slab == k, x_slots[:, k * wide : (k + 1) * wide], x_part)
            h_part = jnp.where(slab == k, hidden[:, k * narrow : (k + 1) * narrow], h_part)
        for out, before, left, right in zip(
            (gate_out, up_out, down_out),
            befores,
            (x_part, x_part, h_part),
            (dgate_pre, dup_pre, dexpert),
        ):
            part = tn(left, right)
            out[0] = part if before is None else before[0] + part

    some = lambda *shape: pl.BlockSpec((groups,) + shape, lambda e, m: (m[2], 0, 0))
    rows = pl.BlockSpec((1, chips, group_len, width), lambda e, m: (m[2], 0, 0, 0))
    weight = lambda *shape: pl.BlockSpec((1,) + shape, lambda e, m: (e, 0, 0))
    whole = lambda *shape: pl.BlockSpec(shape, lambda e, m: (0,) * len(shape))
    outs = [(held, wide, inner), (held, wide, inner), (held, narrow, width)]
    return pl.pallas_call(
        kernel,
        grid_spec=pltpu.PrefetchScalarGridSpec(
            num_scalar_prefetch=1,
            grid=(held,),
            in_specs=[
                rows,
                rows,
                rows,
                rows,
                some(EXPERTS, group_len),
                some(held, group_len),
                whole(EXPERTS, width),
                weight(width, inner),
                weight(width, inner),
                weight(inner, width),
            ]
            + ([weight(*shape[1:]) for shape in outs] if sums is not None else []),
            out_specs=[weight(*shape[1:]) for shape in outs],
            scratch_shapes=[
                pltpu.VMEM((held, slots, width), jnp.bfloat16),
                pltpu.VMEM((held, slots, width), jnp.bfloat16),
                pltpu.VMEM((held, slots, 1), jnp.float32),
            ],
        ),
        out_shape=[jax.ShapeDtypeStruct(shape, jnp.float32) for shape in outs],
        compiler_params=pltpu.CompilerParams(
            dimension_semantics=("arbitrary",), vmem_limit_bytes=58 * 2**20
        ),
        cost_estimate=pl.CostEstimate(
            flops=2 * 4 * held * slots * width * inner, transcendentals=0, bytes_accessed=2**24
        ),
        input_output_aliases={11 + i: i for i in range(3)} if sums is not None else {},
        name="expert_weight_grads",
    )(ids, x_near, x_twin, g_near, g_twin, mask_all, slot_all, router_t, *weights, *(sums or ()))


def assemble_heads(core, near, twin, query_cols):
    chips, width, _ = near.shape
    devices = 2 * chips
    rows = 128
    pair = 2 * HEAD_DIM

    def kernel(core_ref, near_ref, twin_ref, query_ref, key_ref, value_ref):
        blocks = []
        for j in range(devices):
            mine = near_ref[j // 2].astype(jnp.float32)
            other = twin_ref[j // 2].astype(jnp.float32)
            blocks.append(jnp.where(core_ref[0] == j % 2, mine, other))
            query_ref[:, j * query_cols : (j + 1) * query_cols] = blocks[j][:, :query_cols]
        for c in range(chips):
            for ref, start in ((key_ref, query_cols), (value_ref, query_cols + HEAD_DIM)):
                ref[:, c * pair : (c + 1) * pair] = jnp.concatenate(
                    [blocks[2 * c + k][:, start : start + HEAD_DIM] for k in range(2)], axis=1
                )

    block = pl.BlockSpec((chips, rows, query_cols + pair), lambda r, m: (0, r, 0))
    shapes = [(width, devices * query_cols), (width, devices * HEAD_DIM), (width, devices * HEAD_DIM)]
    return pl.pallas_call(
        kernel,
        grid_spec=pltpu.PrefetchScalarGridSpec(
            num_scalar_prefetch=1,
            grid=(width // rows,),
            in_specs=[block, block],
            out_specs=[pl.BlockSpec((rows, s[1]), lambda r, m: (r, 0)) for s in shapes],
        ),
        out_shape=[jax.ShapeDtypeStruct(s, jnp.float32) for s in shapes],
        name="assemble_heads",
    )(core.reshape(1), near, twin)


def assemble_rows(core, near, twin, width):
    chips, rows, total = near.shape

    def kernel(core_ref, near_ref, twin_ref, output_ref, router_ref):
        mine = core_ref[0] == pl.program_id(0) % 2
        block = jnp.where(mine, near_ref[0].astype(jnp.float32), twin_ref[0].astype(jnp.float32))
        output_ref[...] = block[:, :width]
        router_ref[...] = block[:, width : width + EXPERTS]

    block = pl.BlockSpec((1, rows, total), lambda r, m: (r // 2, 0, 0))
    shapes = [(2 * chips * rows, width), (2 * chips * rows, EXPERTS)]
    return pl.pallas_call(
        kernel,
        grid_spec=pltpu.PrefetchScalarGridSpec(
            num_scalar_prefetch=1,
            grid=(2 * chips,),
            in_specs=[block, block],
            out_specs=[pl.BlockSpec((rows, s[1]), lambda r, m: (r, 0)) for s in shapes],
        ),
        out_shape=[jax.ShapeDtypeStruct(s, jnp.float32) for s in shapes],
        name="assemble_rows",
    )(core.reshape(1), near, twin)


def swap_cores(block, devices):
    return lax.ppermute(block, "expert", [(i, i ^ 1) for i in range(devices)])


def across_chips(blocks, devices):
    groups = [[2 * c + core for c in range(devices // 2)] for core in range(2)]
    return lax.all_to_all(blocks, "expert", 0, 0, axis_index_groups=groups, tiled=True)


def spread_row(block, devices):
    near = across_chips(jnp.broadcast_to(block[None], (devices // 2,) + block.shape), devices)
    return near, swap_cores(near, devices)


def reduce_row(near, twin, devices):
    partner = swap_cores(twin, devices)
    merged = (near.astype(jnp.float32) + partner.astype(jnp.float32)).astype(jnp.bfloat16)
    return jnp.sum(across_chips(merged, devices).astype(jnp.float32), axis=0)


def in_order(near, twin, core):
    even = jnp.where(core == 0, near, twin)
    odd = jnp.where(core == 0, twin, near)
    return jnp.stack([even, odd], axis=1).reshape((2 * near.shape[0],) + near.shape[1:])


def with_tail(rows, tail):
    height, span = tail.shape
    return jnp.concatenate(
        [rows, jnp.pad(tail, ((0, TAIL - height), (0, rows.shape[1] - span)))], axis=0
    )


def exchange(blocks, axis):
    return lax.all_to_all(blocks, axis, 0, 0, tiled=True)


def broadcast(block, count):
    return jnp.broadcast_to(block[None], (count,) + block.shape)


def masked_gates(logits, mask):
    shown = jnp.where(mask, logits, NEG_FILL)
    weight = jnp.where(mask, jnp.exp(shown - jnp.max(shown, axis=-1, keepdims=True)), 0.0)
    return weight / jnp.sum(weight, axis=-1, keepdims=True)


def slot_tables(mask, first, held):
    group_len = mask.shape[2]
    local = lax.dynamic_slice_in_dim(mask, first, held, 1)
    steps = jnp.arange(group_len, dtype=jnp.int32)
    earlier = (steps[:, None] < steps[None, :]).astype(jnp.bfloat16)
    rank = jnp.einsum("gem,mn->gen", local, earlier, preferred_element_type=jnp.float32)
    return mask, jnp.where(local > 0, rank, -1.0).astype(jnp.int32)


def per_device_heads(
    tokens,
    attn_gain,
    w_query,
    w_key,
    w_value,
    w_output,
    moe_gain,
    w_router,
    w_gate,
    w_up,
    w_down,
    routes,
    segment_ids,
    out_grad,
):
    unused, group_len, width = tokens.shape
    devices, copies = lax.axis_size("expert"), lax.axis_size("dp")
    me, me_z = lax.axis_index("expert"), lax.axis_index("dp")
    core = me & 1
    chips = devices // 2
    length = group_len * devices
    repeats = HEADS // KV_HEADS
    query_cols = repeats * HEAD_DIM
    held = EXPERTS // devices
    lanes = 128
    order = jnp.stack([2 * c + (core ^ k) for k in range(2) for c in range(chips)])
    bf16 = jnp.bfloat16

    own = tokens[0]
    near_pay, twin_pay = spread_row(with_tail(own, segment_ids.astype(bf16)), devices)
    row_pay = jnp.concatenate([near_pay, twin_pay], axis=0)
    seg_row = row_pay[:, group_len, :group_len].reshape(length).astype(jnp.int32)
    row_tokens = row_pay[:, :group_len].reshape(length, width)
    row_index = (order[:, None] * group_len + jnp.arange(group_len, dtype=jnp.int32)).reshape(length)

    mask_own = jnp.any(
        routes[0][:, :, None] == jnp.arange(EXPERTS, dtype=jnp.int32)[None, None, :], axis=1
    )
    tail_rows = EXPERTS * group_len // width
    mask_tail = jnp.swapaxes(mask_own.astype(bf16), 0, 1).reshape(tail_rows, width)
    grad_pay, near_pay = lax.optimization_barrier((with_tail(out_grad[0], mask_tail), near_pay))
    g_near, g_twin = spread_row(grad_pay, devices)

    def tables(near, twin, axis):
        tails = [side[..., group_len : group_len + tail_rows, :] for side in (near, twin)]
        return slot_tables(
            jnp.concatenate(tails, axis=axis).reshape(-1, EXPERTS, group_len), me * held, held
        )

    mask_row, slot_row = tables(g_near, g_twin, 0)
    g_near_all = lax.all_gather(g_near, "dp", axis=0)
    router_t = jnp.swapaxes(w_router, 0, 1)

    head_weights = jnp.concatenate(
        [
            lax.dynamic_slice_in_dim(w_query, me * query_cols, query_cols, 1),
            lax.dynamic_slice_in_dim(w_key, me * HEAD_DIM, HEAD_DIM, 1),
            lax.dynamic_slice_in_dim(w_value, me * HEAD_DIM, HEAD_DIM, 1),
        ],
        axis=1,
    )
    before = jnp.sum((seg_row[None, :] < seg_row[:, None]).astype(jnp.int32), axis=1)
    cosine, sine = rope_tables(row_index - before)
    cos_heads, sin_heads = cosine[:, None, :], sine[:, None, :]
    normed, unused, _ = rms_forward(row_tokens.astype(jnp.float32), attn_gain)
    normed_row = normed.astype(bf16)
    lin = jnp.dot(normed_row, head_weights, preferred_element_type=jnp.float32)
    queries = rotate(
        lin[:, :query_cols].reshape(length, repeats, HEAD_DIM), cos_heads, sin_heads
    ).astype(bf16)
    keys = rotate(lin[:, query_cols : query_cols + HEAD_DIM], cosine, sine).astype(bf16)
    values = lin[:, query_cols + HEAD_DIM :].astype(bf16)
    scores = (
        jnp.einsum("qhd,kd->hqk", queries, keys, preferred_element_type=jnp.float32) * ATTN_SCALE
    )
    allowed = (seg_row[:, None] == seg_row[None, :]) & (row_index[None, :] <= row_index[:, None])
    masked = jnp.where(allowed[None], scores, NEG_FILL)
    raised = jnp.exp(masked - jnp.max(masked, axis=-1, keepdims=True))
    probs = raised / jnp.sum(raised, axis=-1, keepdims=True)
    probs_b = probs.astype(bf16)
    attended = jnp.einsum("hqk,kd->qhd", probs_b, values, preferred_element_type=jnp.float32)
    attn_heads = attended.astype(bf16).reshape(length, query_cols)
    attn_heads, g_near, g_twin = lax.optimization_barrier((attn_heads, g_near, g_twin))

    def to_tokens(rows):
        blocks = rows.reshape(2, chips, group_len, rows.shape[-1])
        return exchange(in_order(blocks[0], blocks[1], core), "expert")

    attn_rows = jnp.swapaxes(to_tokens(attn_heads), 0, 1).reshape(group_len, devices * query_cols)

    branch = jnp.dot(attn_rows, w_output, preferred_element_type=jnp.float32)
    residual = own.astype(jnp.float32)
    middle = residual + RESIDUAL_SCALE * branch
    normed2, unit_moe, inv_moe = rms_forward(middle, moe_gain)
    moe_rows = normed2.astype(bf16)
    gates_own = masked_gates(
        jnp.dot(moe_rows, w_router, preferred_element_type=jnp.float32), mask_own
    )
    x_near, x_twin = spread_row(moe_rows, devices)
    x_near_all = lax.all_gather(x_near, "dp", axis=0)

    d_near, d_twin, y_near, y_twin = near_experts(
        me, x_near, x_twin, g_near, g_twin, mask_row, slot_row, router_t, w_gate, w_up, w_down
    )
    returned = reduce_row(d_near, d_twin, devices)

    parts = returned[group_len : group_len + held] + returned[group_len + held : group_len + 2 * held]
    dgates = jnp.transpose(parts.reshape(held, devices, group_len), (2, 1, 0)).reshape(
        group_len, EXPERTS
    )
    dpicked = gates_own * (dgates - jnp.sum(gates_own * dgates, axis=-1, keepdims=True))
    dlogits = jnp.where(mask_own, dpicked, 0.0).astype(bf16)
    dnormed2 = returned[:group_len] + jnp.einsum(
        "ne,de->nd", dlogits, w_router, preferred_element_type=jnp.float32
    )
    dmiddle_norm, moe_gain_part = rms_backward(dnormed2, unit_moe, inv_moe, moe_gain)
    dmiddle = out_grad[0].astype(jnp.float32) + dmiddle_norm
    dbranch = (RESIDUAL_SCALE * dmiddle).astype(bf16)
    branch_near, branch_twin = spread_row(
        with_tail(dbranch, jnp.swapaxes(dlogits, 0, 1).reshape(tail_rows, width)), devices
    )
    y_near, y_twin, branch_near, branch_twin = lax.optimization_barrier(
        (y_near, y_twin, branch_near, branch_twin)
    )
    branch_row = jnp.concatenate([branch_near, branch_twin], axis=0)
    dbranch_row = branch_row[:, :group_len].reshape(length, width)
    dlogits_row = branch_row[:, group_len : group_len + tail_rows].reshape(
        devices, EXPERTS, group_len
    )
    mixed = (middle + RESIDUAL_SCALE * reduce_row(y_near, y_twin, devices)).astype(bf16)[None]

    rows_per = width // devices
    output_part = jnp.einsum(
        "nh,nd->hd", attn_heads, dbranch_row, preferred_element_type=jnp.float32
    )
    router_cols = lax.dynamic_slice_in_dim(
        jnp.concatenate([x_near, x_twin], axis=0).reshape(length, width), me * rows_per, rows_per, 1
    )
    router_part = jnp.einsum(
        "bnd,ben->de",
        router_cols.reshape(devices, group_len, rows_per),
        dlogits_row,
        preferred_element_type=jnp.float32,
    )
    router_part = jnp.pad(router_part, ((0, 0), (0, lanes - EXPERTS)))
    first_part = jnp.concatenate([output_part, router_part], axis=1).reshape(
        copies, query_cols // copies, width + lanes
    )

    def z_sum(part):
        return jnp.sum(exchange(part.astype(bf16), "dp").astype(jnp.float32), axis=0).astype(bf16)

    def z_column(summed):
        column = exchange(broadcast(summed, copies), "dp")
        return column.reshape((copies * summed.shape[0],) + summed.shape[1:])

    first_column = z_column(z_sum(first_part))
    grad_output, grad_router = assemble_rows(core, *spread_row(first_column, devices), width)

    out_heads = lax.dynamic_slice_in_dim(w_output, me * query_cols, query_cols, 0)
    dattn = jnp.einsum(
        "nd,hd->nh", dbranch_row, out_heads, preferred_element_type=jnp.float32
    ).astype(bf16).reshape(length, repeats, HEAD_DIM)
    delta = jnp.sum(dattn.astype(jnp.float32) * attended, axis=-1)
    dprobs = jnp.einsum("qhd,kd->hqk", dattn, values, preferred_element_type=jnp.float32)
    dscores = (probs * (dprobs - jnp.swapaxes(delta, 0, 1)[:, :, None])).astype(bf16)
    dqueries = (
        jnp.einsum("hqk,kd->qhd", dscores, keys, preferred_element_type=jnp.float32) * ATTN_SCALE
    )
    dkeys = (
        jnp.einsum("hqk,qhd->kd", dscores, queries, preferred_element_type=jnp.float32) * ATTN_SCALE
    )
    dvalues = jnp.einsum("hqk,qhd->kd", probs_b, dattn, preferred_element_type=jnp.float32)
    dlin = jnp.concatenate(
        [
            unrotate(dqueries, cos_heads, sin_heads).astype(bf16).reshape(length, query_cols),
            unrotate(dkeys, cosine, sine).astype(bf16),
            dvalues.astype(bf16),
        ],
        axis=1,
    )
    dlin, mixed = lax.optimization_barrier((dlin, mixed))
    head_part = jnp.einsum("nd,nh->dh", normed_row, dlin, preferred_element_type=jnp.float32)
    head_cols = query_cols + 2 * HEAD_DIM
    head_part = head_part.reshape(copies, width // copies, head_cols)
    g_near_all, x_near_all, head_part = lax.optimization_barrier(
        (g_near_all, x_near_all, head_part)
    )
    g_twin_all, x_twin_all = swap_cores(g_near_all, devices), swap_cores(x_near_all, devices)
    mask_all, slot_all = tables(g_near_all, g_twin_all, 1)
    weights = (w_gate, w_up, w_down)

    def far_row(z, sums):
        return expert_weight_grads(
            jnp.stack([me, me_z, jnp.int32(z)]), sums, x_near_all, x_twin_all, g_near_all,
            g_twin_all, mask_all, slot_all, router_t, weights, copies,
        )

    sums = far_row(0, None)
    summed, sums = lax.optimization_barrier((z_sum(head_part), sums))
    sums = far_row(1, sums)
    column, sums = lax.optimization_barrier((z_column(summed), sums))
    sums = far_row(2, sums)
    head_near = across_chips(broadcast(column, chips), devices)
    head_near, sums = lax.optimization_barrier((head_near, sums))
    sums = far_row(3, sums)
    head_twin, sums = lax.optimization_barrier((swap_cores(head_near, devices), sums))
    grad_gate, grad_up, grad_down = sums
    grad_query, grad_key, grad_value = assemble_heads(core, head_near, head_twin, query_cols)

    dlin_back = jnp.swapaxes(to_tokens(dlin), 0, 1)

    def token_grad(start, count, weights):
        rows = dlin_back[:, :, start : start + count].reshape(group_len, devices * count)
        return jnp.einsum("nh,dh->nd", rows, weights, preferred_element_type=jnp.float32)

    dnormed = (
        token_grad(0, query_cols, w_query)
        + token_grad(query_cols, HEAD_DIM, w_key)
        + token_grad(query_cols + HEAD_DIM, HEAD_DIM, w_value)
    )
    unused, unit_attn, inv_attn = rms_forward(residual, attn_gain)
    dresid_norm, attn_gain_part = rms_backward(dnormed, unit_attn, inv_attn, attn_gain)
    grad_tokens = (dmiddle + dresid_norm)[None]
    gain_sums = jnp.stack([attn_gain_part, moe_gain_part])
    for axis, count in (("expert", devices), ("dp", copies)):
        gain_sums = jnp.sum(exchange(broadcast(gain_sums, count), axis), axis=0)

    return (
        mixed,
        grad_tokens,
        gain_sums[0],
        grad_query,
        grad_key,
        grad_value,
        grad_output,
        gain_sums[1],
        grad_router,
        grad_gate,
        grad_up,
        grad_down,
    )


def solution(mesh):
    placed = (
        P("dp", "expert", None),
        P(),
        P(),
        P(),
        P(),
        P(),
        P(),
        P(),
        P("expert", None, None),
        P("expert", None, None),
        P("expert", None, None),
        P("dp", "expert", None),
        P("dp", "expert"),
        P("dp", "expert", None),
    )
    by_heads = mesh.shape["expert"] == KV_HEADS
    return jax.shard_map(
        per_device_heads if by_heads else per_device_general,
        mesh=mesh,
        in_specs=placed,
        out_specs=(
            P("dp", "expert", None),
            P("dp", "expert", None),
            P(),
            P(),
            P(),
            P(),
            P(),
            P(),
            P(),
            P("expert", "dp", None),
            P("expert", "dp", None),
            P("expert", "dp", None),
        ),
        check_vma=False,
    )
```

```python
import jax
import jax.numpy as jnp
from jax import lax
from jax.experimental import pallas as pl
from jax.experimental.pallas import tpu as pltpu
from jax.sharding import PartitionSpec as P


HEADS = 16
KV_HEADS = 8
HEAD_DIM = 64
EXPERTS = 32
TOP = 8
MOST = 48


ATTN_SCALE = 0.015625
RESIDUAL_SCALE = 0.22
NORM_EPS = 1e-06
ROPE_BASE = 10000.0
NEG_FILL = -1e30
TAIL = 16


def rms_forward(values, gain_vec):
    inverse = lax.rsqrt(jnp.mean(values * values, axis=-1, keepdims=True) + NORM_EPS)
    unit_rows = values * inverse
    return (unit_rows * gain_vec, unit_rows, inverse)


def rms_backward(grad_rows, unit_rows, inverse, gain_vec):
    scaled = grad_rows * gain_vec
    grad_gain = jnp.sum(grad_rows * unit_rows, axis=0)
    grad_in = inverse * (scaled - unit_rows * jnp.mean(scaled * unit_rows, axis=-1, keepdims=True))
    return (grad_in, grad_gain)


def rope_tables(positions):
    half = HEAD_DIM // 2
    freqs = ROPE_BASE ** (-(jnp.arange(half, dtype=jnp.float32) * 2.0) / HEAD_DIM)
    angles = positions.astype(jnp.float32)[..., None] * freqs
    cosine = jnp.concatenate([jnp.cos(angles), jnp.cos(angles)], axis=-1)
    sine = jnp.concatenate([jnp.sin(angles), jnp.sin(angles)], axis=-1)
    return (cosine, sine)


def rotate(vectors, cosine, sine):
    half = vectors.shape[-1] // 2
    turned = jnp.concatenate([-vectors[..., half:], vectors[..., :half]], axis=-1)
    return vectors * cosine + turned * sine


def unrotate(grads, cosine, sine):
    half = grads.shape[-1] // 2
    scaled = grads * sine
    turned = jnp.concatenate([scaled[..., half:], -scaled[..., :half]], axis=-1)
    return grads * cosine + turned


def scaled_scores(query_part, key_part, query_seg, key_seg, query_index, key_index):
    raw = (
        jnp.einsum("qrgjd,krgd->rgjqk", query_part, key_part, preferred_element_type=jnp.float32)
        * ATTN_SCALE
    )
    same = jnp.transpose(query_seg)[:, :, None] == jnp.transpose(key_seg)[:, None, :]
    before = key_index[None, :] <= query_index[:, None]
    return (raw, (same & before[None])[:, None, None])


def probs_and_ds(
    query_part,
    key_part,
    value_part,
    dout_part,
    lse_part,
    delta_part,
    query_seg,
    key_seg,
    query_index,
    key_index,
):
    scores, allowed = scaled_scores(
        query_part, key_part, query_seg, key_seg, query_index, key_index
    )
    lse_rows = jnp.transpose(lse_part, (1, 2, 3, 0))[..., None]
    delta_rows = jnp.transpose(delta_part, (1, 2, 3, 0))[..., None]
    probs = jnp.where(allowed, jnp.exp(scores - lse_rows), 0.0)
    dprobs = jnp.einsum(
        "qrgjd,krgd->rgjqk", dout_part, value_part, preferred_element_type=jnp.float32
    )
    dscore = (probs * (dprobs - delta_rows)).astype(jnp.bfloat16)
    return (probs.astype(jnp.bfloat16), dscore)


def per_device_general(
    tokens,
    attn_gain,
    w_query,
    w_key,
    w_value,
    w_output,
    moe_gain,
    w_router,
    w_gate,
    w_up,
    w_down,
    routes,
    segment_ids,
    out_grad,
):
    row_count, group_len, width = tokens.shape
    devices = lax.axis_size("expert")
    my_index = lax.axis_index("expert")
    length = group_len * devices
    repeats = HEADS // KV_HEADS
    tok_count = group_len * row_count
    slot_rows = row_count * MOST
    seg_local = jnp.transpose(segment_ids)
    seg_all = lax.all_gather(seg_local, "expert", axis=0, tiled=True)
    query_index = my_index * group_len + jnp.arange(group_len, dtype=jnp.int32)
    earlier = jnp.sum((seg_all[None, :, :] < seg_local[:, None, :]).astype(jnp.int32), axis=1)
    cosine, sine = rope_tables(query_index[:, None] - earlier)
    cos_heads = cosine[:, :, None, :]
    sin_heads = sine[:, :, None, :]
    residual = jnp.swapaxes(tokens, 0, 1).astype(jnp.float32).reshape(tok_count, width)
    normed, unit_attn, inv_attn = rms_forward(residual, attn_gain)
    normed_rows = normed.astype(jnp.bfloat16)
    query_lin = jnp.dot(normed_rows, w_query, preferred_element_type=jnp.float32).reshape(
        group_len, row_count, HEADS, HEAD_DIM
    )
    queries = (
        rotate(query_lin, cos_heads, sin_heads)
        .astype(jnp.bfloat16)
        .reshape(group_len, row_count, KV_HEADS, repeats, HEAD_DIM)
    )
    key_lin = jnp.dot(normed_rows, w_key, preferred_element_type=jnp.float32).reshape(
        group_len, row_count, KV_HEADS, HEAD_DIM
    )
    keys = rotate(key_lin, cos_heads, sin_heads).astype(jnp.bfloat16)
    values = (
        jnp.dot(normed_rows, w_value, preferred_element_type=jnp.float32)
        .astype(jnp.bfloat16)
        .reshape(group_len, row_count, KV_HEADS, HEAD_DIM)
    )
    keys_all, values_all = (
        lax.all_gather(keys, "expert", axis=0, tiled=True),
        lax.all_gather(values, "expert", axis=0, tiled=True),
    )
    key_block = min(1024, length)
    block_count = length // key_block
    key_blocks = keys_all.reshape(block_count, key_block, row_count, KV_HEADS, HEAD_DIM)
    value_blocks = values_all.reshape(block_count, key_block, row_count, KV_HEADS, HEAD_DIM)
    seg_blocks = seg_all.reshape(block_count, key_block, row_count)
    index_blocks = jnp.arange(length, dtype=jnp.int32).reshape(block_count, key_block)
    key_inputs = (key_blocks, value_blocks, seg_blocks, index_blocks)

    def max_step(carried, current):
        running, totals = carried
        key_part, _, seg_part, index_part = current
        scores, allowed = scaled_scores(
            queries, key_part, seg_local, seg_part, query_index, index_part
        )
        newmax = jnp.maximum(running, jnp.max(jnp.where(allowed, scores, NEG_FILL), axis=-1))
        totals = totals * jnp.exp(running - newmax) + jnp.sum(
            jnp.where(allowed, jnp.exp(scores - newmax[..., None]), 0.0), axis=-1
        )
        return ((newmax, totals), None)

    stat_shape = (row_count, KV_HEADS, repeats, group_len)
    (running, totals), unused = lax.scan(
        max_step,
        (jnp.full(stat_shape, NEG_FILL, jnp.float32), jnp.zeros(stat_shape, jnp.float32)),
        key_inputs,
    )
    logsum = running + jnp.log(totals)
    lse_local = jnp.transpose(logsum, (3, 0, 1, 2))

    def out_step(accum, current):
        key_part, value_part, seg_part, index_part = current
        scores, allowed = scaled_scores(
            queries, key_part, seg_local, seg_part, query_index, index_part
        )
        probs = jnp.where(allowed, jnp.exp(scores - logsum[..., None]), 0.0).astype(jnp.bfloat16)
        return (
            accum
            + jnp.einsum(
                "rgjqk,krgd->qrgjd", probs, value_part, preferred_element_type=jnp.float32
            ),
            None,
        )

    head_shape = (group_len, row_count, KV_HEADS, repeats, HEAD_DIM)
    attended, unused = lax.scan(out_step, jnp.zeros(head_shape, jnp.float32), key_inputs)
    attn_rows = attended.reshape(tok_count, HEADS * HEAD_DIM).astype(jnp.bfloat16)
    branch = jnp.dot(attn_rows, w_output, preferred_element_type=jnp.float32)
    middle = residual + RESIDUAL_SCALE * branch
    normed2, unit_moe, inv_moe = rms_forward(middle, moe_gain)
    moe_rows = normed2.astype(jnp.bfloat16)
    logits = jnp.dot(moe_rows, w_router, preferred_element_type=jnp.float32)
    route_rows = jnp.transpose(routes, (1, 0, 2)).reshape(tok_count, TOP)
    onehot = route_rows[:, :, None] == jnp.arange(EXPERTS, dtype=jnp.int32)[None, None, :]
    picked = jnp.sum(jnp.where(onehot, logits[:, None, :], 0.0), axis=-1)
    gates = jax.nn.softmax(picked, axis=-1)
    by_row = jnp.transpose(
        onehot.reshape(group_len, row_count, TOP, EXPERTS), (1, 0, 2, 3)
    ).reshape(row_count, group_len * TOP, EXPERTS)
    counted = jnp.cumsum(by_row.astype(jnp.int32), axis=1)
    rank = jnp.sum(jnp.where(by_row, counted - 1, 0), axis=-1).reshape(row_count, group_len, TOP)
    rank = jnp.transpose(rank, (1, 0, 2)).reshape(tok_count, TOP)
    row_of = jnp.arange(tok_count, dtype=jnp.int32) % row_count
    target = (route_rows * slot_rows + row_of[:, None] * MOST + rank).reshape(tok_count * TOP)

    def to_slots(route_values):
        placed = (
            jnp.zeros((EXPERTS * slot_rows, width), jnp.bfloat16)
            .at[target]
            .set(route_values.reshape(tok_count * TOP, width))
        )
        return placed.reshape(EXPERTS, slot_rows, width)

    def from_slots(slot_values):
        return (
            slot_values.reshape(EXPERTS * slot_rows, width)[target]
            .reshape(tok_count, TOP, width)
            .astype(jnp.float32)
        )

    sent = to_slots(jnp.broadcast_to(moe_rows[:, None, :], (tok_count, TOP, width)))
    arrived = lax.all_to_all(sent, "expert", split_axis=0, concat_axis=1, tiled=True)
    gate_pre = jnp.einsum("etd,edf->etf", arrived, w_gate, preferred_element_type=jnp.float32)
    up_pre = jnp.einsum("etd,edf->etf", arrived, w_up, preferred_element_type=jnp.float32)
    sigma = jax.nn.sigmoid(gate_pre)
    activated = gate_pre * sigma
    hidden = (activated * up_pre).astype(jnp.bfloat16)
    expert_out = jnp.einsum(
        "etf,efd->etd", hidden, w_down, preferred_element_type=jnp.float32
    ).astype(jnp.bfloat16)
    returned = lax.all_to_all(expert_out, "expert", split_axis=1, concat_axis=0, tiled=True)
    route_out = from_slots(returned)
    moe = jnp.sum(gates[:, :, None] * route_out, axis=1)
    mixed_rows = middle + RESIDUAL_SCALE * moe
    mixed = jnp.swapaxes(mixed_rows.reshape(group_len, row_count, width), 0, 1).astype(jnp.bfloat16)
    upstream = jnp.swapaxes(out_grad, 0, 1).astype(jnp.float32).reshape(tok_count, width)
    dmoe = RESIDUAL_SCALE * upstream
    dgates = jnp.sum(route_out * dmoe[:, None, :], axis=-1)
    dsent = to_slots((gates[:, :, None] * dmoe[:, None, :]).astype(jnp.bfloat16))
    darrived = lax.all_to_all(dsent, "expert", split_axis=0, concat_axis=1, tiled=True)
    dhidden = jnp.einsum("etd,efd->etf", darrived, w_down, preferred_element_type=jnp.float32)
    down_part = jnp.einsum("etf,etd->efd", hidden, darrived, preferred_element_type=jnp.float32)
    dgate_pre = (dhidden * up_pre * sigma * (1.0 + gate_pre * (1.0 - sigma))).astype(jnp.bfloat16)
    dup_pre = (dhidden * activated).astype(jnp.bfloat16)
    gate_part = jnp.einsum("etd,etf->edf", arrived, dgate_pre, preferred_element_type=jnp.float32)
    up_part = jnp.einsum("etd,etf->edf", arrived, dup_pre, preferred_element_type=jnp.float32)
    dinputs = (
        jnp.einsum("etf,edf->etd", dgate_pre, w_gate, preferred_element_type=jnp.float32)
        + jnp.einsum("etf,edf->etd", dup_pre, w_up, preferred_element_type=jnp.float32)
    ).astype(jnp.bfloat16)
    grad_gate, grad_up, grad_down = (
        lax.psum_scatter(
            gate_part.astype(jnp.bfloat16), "dp", scatter_dimension=1, tiled=True
        ).astype(jnp.float32),
        lax.psum_scatter(
            up_part.astype(jnp.bfloat16), "dp", scatter_dimension=1, tiled=True
        ).astype(jnp.float32),
        lax.psum_scatter(
            down_part.astype(jnp.bfloat16), "dp", scatter_dimension=1, tiled=True
        ).astype(jnp.float32),
    )
    dreturned = lax.all_to_all(dinputs, "expert", split_axis=1, concat_axis=0, tiled=True)
    droutes = jnp.sum(from_slots(dreturned), axis=1)
    dpicked = gates * (dgates - jnp.sum(gates * dgates, axis=-1, keepdims=True))
    dlogits = jnp.sum(jnp.where(onehot, dpicked[:, :, None], 0.0), axis=1).astype(jnp.bfloat16)
    router_part = jnp.einsum("nd,ne->de", moe_rows, dlogits, preferred_element_type=jnp.float32)
    dnormed2 = droutes + jnp.einsum(
        "ne,de->nd", dlogits, w_router, preferred_element_type=jnp.float32
    )
    dmiddle_norm, moe_gain_part = rms_backward(dnormed2, unit_moe, inv_moe, moe_gain)
    dmiddle = upstream + dmiddle_norm
    dbranch = (RESIDUAL_SCALE * dmiddle).astype(jnp.bfloat16)
    output_part = jnp.einsum("nh,nd->hd", attn_rows, dbranch, preferred_element_type=jnp.float32)
    dattn = (
        jnp.einsum("nd,hd->nh", dbranch, w_output, preferred_element_type=jnp.float32)
        .astype(jnp.bfloat16)
        .reshape(head_shape)
    )
    delta = jnp.sum(dattn.astype(jnp.float32) * attended, axis=-1)

    def both_step(dq_sum, current):
        key_part, value_part, seg_part, index_part = current
        probs_b, dscore = probs_and_ds(
            queries,
            key_part,
            value_part,
            dattn,
            lse_local,
            delta,
            seg_local,
            seg_part,
            query_index,
            index_part,
        )
        dq_part = (
            jnp.einsum("rgjqk,krgd->qrgjd", dscore, key_part, preferred_element_type=jnp.float32)
            * ATTN_SCALE
        )
        dk_part = (
            jnp.einsum("rgjqk,qrgjd->krgd", dscore, queries, preferred_element_type=jnp.float32)
            * ATTN_SCALE
        )
        dv_part = jnp.einsum(
            "rgjqk,qrgjd->krgd", probs_b, dattn, preferred_element_type=jnp.float32
        )
        return (dq_sum + dq_part, (dk_part, dv_part))

    dq_sum, (dk_stack, dv_stack) = lax.scan(
        both_step, jnp.zeros(head_shape, jnp.float32), key_inputs
    )
    full_shape = (length, row_count, KV_HEADS, HEAD_DIM)
    dkeys, dvalues = (
        lax.psum_scatter(
            dk_stack.reshape(full_shape).astype(jnp.bfloat16),
            "expert",
            scatter_dimension=0,
            tiled=True,
        ).astype(jnp.float32),
        lax.psum_scatter(
            dv_stack.reshape(full_shape).astype(jnp.bfloat16),
            "expert",
            scatter_dimension=0,
            tiled=True,
        ).astype(jnp.float32),
    )
    dquery_lin = (
        unrotate(dq_sum.reshape(group_len, row_count, HEADS, HEAD_DIM), cos_heads, sin_heads)
        .astype(jnp.bfloat16)
        .reshape(tok_count, HEADS * HEAD_DIM)
    )
    dkey_lin = (
        unrotate(dkeys, cos_heads, sin_heads)
        .astype(jnp.bfloat16)
        .reshape(tok_count, KV_HEADS * HEAD_DIM)
    )
    dvalue_rows = dvalues.astype(jnp.bfloat16).reshape(tok_count, KV_HEADS * HEAD_DIM)
    query_part_grad = jnp.einsum(
        "nd,nh->dh", normed_rows, dquery_lin, preferred_element_type=jnp.float32
    )
    key_part_grad = jnp.einsum(
        "nd,nh->dh", normed_rows, dkey_lin, preferred_element_type=jnp.float32
    )
    value_part_grad = jnp.einsum(
        "nd,nh->dh", normed_rows, dvalue_rows, preferred_element_type=jnp.float32
    )
    dnormed = (
        jnp.einsum("nh,dh->nd", dquery_lin, w_query, preferred_element_type=jnp.float32)
        + jnp.einsum("nh,dh->nd", dkey_lin, w_key, preferred_element_type=jnp.float32)
        + jnp.einsum("nh,dh->nd", dvalue_rows, w_value, preferred_element_type=jnp.float32)
    )
    dresid_norm, attn_gain_part = rms_backward(dnormed, unit_attn, inv_attn, attn_gain)
    grad_tokens = jnp.swapaxes((dmiddle + dresid_norm).reshape(group_len, row_count, width), 0, 1)
    query_sum, key_sum, value_sum, output_sum, router_sum, attn_gain_sum, moe_gain_sum = lax.psum(
        (
            query_part_grad,
            key_part_grad,
            value_part_grad,
            output_part,
            router_part,
            attn_gain_part,
            moe_gain_part,
        ),
        ("dp", "expert"),
    )
    return (
        mixed,
        grad_tokens,
        attn_gain_sum,
        query_sum,
        key_sum,
        value_sum,
        output_sum,
        moe_gain_sum,
        router_sum,
        grad_gate,
        grad_up,
        grad_down,
    )


def expert_gather(x_rows, g_rows, mask_rows, slot_rows, router_rows, first, x_scr, g_scr, gate_scr, table_scr, groups):
    held = x_scr.shape[0]
    for g in range(groups):
        rows = x_rows(g)
        logits = lax.dot_general(
            router_rows, rows, (((1,), (1,)), ((), ())), preferred_element_type=jnp.float32
        )
        shown = mask_rows(g) > 0
        raised = jnp.where(
            shown,
            jnp.exp(logits - jnp.max(jnp.where(shown, logits, NEG_FILL), axis=0, keepdims=True)),
            0.0,
        )
        gates = raised / jnp.sum(raised, axis=0, keepdims=True)
        slots = slot_rows(g)
        expert = lax.broadcasted_iota(jnp.int32, gates.shape, 0)
        place = lax.broadcasted_iota(jnp.int32, (MOST, rows.shape[0]), 0)
        tables = []
        for e in range(held):
            gate_row = jnp.sum(jnp.where(expert == first + e, gates, 0.0), axis=0, keepdims=True)
            chosen = place == slots[e : e + 1, :]
            gate_scr[e, g * MOST : (g + 1) * MOST, :] = jnp.sum(
                jnp.where(chosen, gate_row, 0.0), axis=1, keepdims=True
            )
            tables.append(jnp.where(chosen, 1.0, 0.0))
        table = jnp.concatenate(tables, axis=0).astype(jnp.bfloat16)
        if table_scr is not None:
            table_scr[g] = table
        for scr, part in ((x_scr, rows), (g_scr, g_rows(g))):
            picked = jnp.dot(table, part, preferred_element_type=jnp.float32).astype(jnp.bfloat16)
            for e in range(held):
                scr[e, g * MOST : (g + 1) * MOST, :] = picked[e * MOST : (e + 1) * MOST, :]


def nt(left, right):
    return lax.dot_general(
        left, right, (((1,), (1,)), ((), ())), preferred_element_type=jnp.float32
    )


def tn(left, right):
    return lax.dot_general(
        left, right, (((0,), (0,)), ((), ())), preferred_element_type=jnp.float32
    )


def expert_body(x_slots, g_slots, gate_col, gate_w, up_w, down_w):
    gate_pre = jnp.dot(x_slots, gate_w, preferred_element_type=jnp.float32)
    up_pre = jnp.dot(x_slots, up_w, preferred_element_type=jnp.float32)
    sigma = jax.nn.sigmoid(gate_pre)
    activated = gate_pre * sigma
    hidden = (activated * up_pre).astype(jnp.bfloat16)
    dexpert = (gate_col * (RESIDUAL_SCALE * g_slots.astype(jnp.float32))).astype(jnp.bfloat16)
    dhidden = nt(dexpert, down_w)
    dgate_pre = (dhidden * up_pre * sigma * (1.0 + gate_pre * (1.0 - sigma))).astype(jnp.bfloat16)
    dup_pre = (dhidden * activated).astype(jnp.bfloat16)
    return hidden, dexpert, dgate_pre, dup_pre


def near_experts(me, x_near, x_twin, g_near, g_twin, mask_row, slot_row, router_t, w_gate, w_up, w_down):
    chips, group_len, width = x_near.shape
    held, _, inner = w_gate.shape
    groups = 2 * chips
    extra = 16
    lanes = 128

    def kernel(me_ref, xn, xt, gn, gt, mr, sr, rt, wg, wu, wd, near_out, twin_out, y_near, y_twin,
               x_scr, g_scr, gate_scr, table_scr, y_scr, d_scr, dg_scr):
        e = pl.program_id(0)
        my = me_ref[0]

        @pl.when(e == 0)
        def _():
            expert_gather(
                lambda g: (xn if g < chips else xt)[g % chips],
                lambda g: (gn if g < chips else gt)[g % chips],
                lambda g: mr[g],
                lambda g: sr[g],
                rt[...],
                my * held,
                x_scr, g_scr, gate_scr, table_scr, groups,
            )

        g_slots = g_scr[e]
        hidden, _, dgate_pre, dup_pre = expert_body(
            x_scr[e], g_slots, gate_scr[e], wg[0], wu[0], wd[0]
        )
        out = jnp.dot(hidden, wd[0], preferred_element_type=jnp.float32).astype(jnp.bfloat16)
        out_wide = out.astype(jnp.float32)
        dgate = jnp.sum(
            RESIDUAL_SCALE * g_slots.astype(jnp.float32) * out_wide, axis=1, keepdims=True
        )
        weighted = (gate_scr[e] * out_wide).astype(jnp.bfloat16)
        dinputs = (nt(dgate_pre, wg[0]) + nt(dup_pre, wu[0])).astype(jnp.bfloat16)
        spot = pl.ds(pl.multiple_of(e * MOST, 16), MOST)
        for g in range(groups):
            part = slice(g * MOST, (g + 1) * MOST)
            y_scr[g, spot, :] = weighted[part]
            d_scr[g, spot, :] = dinputs[part]
            taken = table_scr[g, spot, :].astype(jnp.float32)
            dg_scr[g, e] = jnp.sum(taken * dgate[part], axis=0, keepdims=True)

        @pl.when(e == held - 1)
        def _():
            block = lax.broadcasted_iota(jnp.int32, (held, width), 1) // lanes
            for g in range(groups):
                d_out, y_out = (near_out, y_near) if g < chips else (twin_out, y_twin)
                table = table_scr[g]
                y_out[g % chips] = tn(table, y_scr[g]).astype(jnp.bfloat16)
                d_out[g % chips, :group_len, :] = tn(table, d_scr[g]).astype(jnp.bfloat16)
                rows = jnp.concatenate([dg_scr[g, i] for i in range(held)], axis=0)
                spread = jnp.where(block == my, jnp.concatenate([rows] * groups, axis=1), 0.0)
                high = spread.astype(jnp.bfloat16).astype(jnp.float32)
                tail = jnp.concatenate(
                    [high, spread - high, jnp.zeros((extra - 2 * held, width), jnp.float32)], axis=0
                )
                d_out[g % chips, group_len:, :] = tail.astype(jnp.bfloat16)

    whole = lambda *shape: pl.BlockSpec(shape, lambda e, m: (0,) * len(shape))
    weight = lambda *shape: pl.BlockSpec((1,) + shape, lambda e, m: (e, 0, 0))
    back = jax.ShapeDtypeStruct((chips, group_len + extra, width), jnp.bfloat16)
    forth = jax.ShapeDtypeStruct((chips, group_len, width), jnp.bfloat16)
    slots = groups * MOST
    return pl.pallas_call(
        kernel,
        grid_spec=pltpu.PrefetchScalarGridSpec(
            num_scalar_prefetch=1,
            grid=(held,),
            in_specs=[
                whole(chips, group_len, width),
                whole(chips, group_len, width),
                whole(chips, group_len, width),
                whole(chips, group_len, width),
                whole(groups, EXPERTS, group_len),
                whole(groups, held, group_len),
                whole(EXPERTS, width),
                weight(width, inner),
                weight(width, inner),
                weight(inner, width),
            ],
            out_specs=[
                whole(chips, group_len + extra, width),
                whole(chips, group_len + extra, width),
                whole(chips, group_len, width),
                whole(chips, group_len, width),
            ],
            scratch_shapes=[
                pltpu.VMEM((held, slots, width), jnp.bfloat16),
                pltpu.VMEM((held, slots, width), jnp.bfloat16),
                pltpu.VMEM((held, slots, 1), jnp.float32),
                pltpu.VMEM((groups, held * MOST, group_len), jnp.bfloat16),
                pltpu.VMEM((groups, held * MOST, width), jnp.bfloat16),
                pltpu.VMEM((groups, held * MOST, width), jnp.bfloat16),
                pltpu.VMEM((groups, held, 1, group_len), jnp.float32),
            ],
        ),
        out_shape=[back, back, forth, forth],
        compiler_params=pltpu.CompilerParams(
            dimension_semantics=("arbitrary",), vmem_limit_bytes=58 * 2**20
        ),
        cost_estimate=pl.CostEstimate(
            flops=2 * 7 * held * slots * width * inner, transcendentals=0, bytes_accessed=2**24
        ),
        name="near_experts",
    )(me.reshape(1), x_near, x_twin, g_near, g_twin, mask_row, slot_row, router_t, w_gate, w_up, w_down)


def expert_weight_grads(ids, sums, x_near, x_twin, g_near, g_twin, mask_all, slot_all, router_t, weights, copies):
    unused, chips, group_len, width = x_near.shape
    held, unused, inner = weights[0].shape
    groups = 2 * chips
    slots = groups * MOST
    wide, narrow = width // copies, inner // copies

    def kernel(ids_ref, xn, xt, gn, gt, mr, sr, rt, wg, wu, wd, *refs):
        gate_out, up_out, down_out, x_scr, g_scr, gate_scr = refs[-6:]
        befores = refs[:-6] if sums is not None else (None, None, None)
        e = pl.program_id(0)
        mine, slab = ids_ref[0], ids_ref[1]

        @pl.when(e == 0)
        def _():
            expert_gather(
                lambda g: (xn if g < chips else xt)[0, g % chips],
                lambda g: (gn if g < chips else gt)[0, g % chips],
                lambda g: mr[g],
                lambda g: sr[g],
                rt[...], mine * held, x_scr, g_scr, gate_scr, None, groups,
            )

        x_slots = x_scr[e]
        hidden, dexpert, dgate_pre, dup_pre = expert_body(
            x_slots, g_scr[e], gate_scr[e], wg[0], wu[0], wd[0]
        )
        x_part, h_part = x_slots[:, :wide], hidden[:, :narrow]
        for k in range(1, copies):
            x_part = jnp.where(slab == k, x_slots[:, k * wide : (k + 1) * wide], x_part)
            h_part = jnp.where(slab == k, hidden[:, k * narrow : (k + 1) * narrow], h_part)
        for out, before, left, right in zip(
            (gate_out, up_out, down_out),
            befores,
            (x_part, x_part, h_part),
            (dgate_pre, dup_pre, dexpert),
        ):
            part = tn(left, right)
            out[0] = part if before is None else before[0] + part

    some = lambda *shape: pl.BlockSpec((groups,) + shape, lambda e, m: (m[2], 0, 0))
    rows = pl.BlockSpec((1, chips, group_len, width), lambda e, m: (m[2], 0, 0, 0))
    weight = lambda *shape: pl.BlockSpec((1,) + shape, lambda e, m: (e, 0, 0))
    whole = lambda *shape: pl.BlockSpec(shape, lambda e, m: (0,) * len(shape))
    outs = [(held, wide, inner), (held, wide, inner), (held, narrow, width)]
    return pl.pallas_call(
        kernel,
        grid_spec=pltpu.PrefetchScalarGridSpec(
            num_scalar_prefetch=1,
            grid=(held,),
            in_specs=[
                rows,
                rows,
                rows,
                rows,
                some(EXPERTS, group_len),
                some(held, group_len),
                whole(EXPERTS, width),
                weight(width, inner),
                weight(width, inner),
                weight(inner, width),
            ]
            + ([weight(*shape[1:]) for shape in outs] if sums is not None else []),
            out_specs=[weight(*shape[1:]) for shape in outs],
            scratch_shapes=[
                pltpu.VMEM((held, slots, width), jnp.bfloat16),
                pltpu.VMEM((held, slots, width), jnp.bfloat16),
                pltpu.VMEM((held, slots, 1), jnp.float32),
            ],
        ),
        out_shape=[jax.ShapeDtypeStruct(shape, jnp.float32) for shape in outs],
        compiler_params=pltpu.CompilerParams(
            dimension_semantics=("arbitrary",), vmem_limit_bytes=58 * 2**20
        ),
        cost_estimate=pl.CostEstimate(
            flops=2 * 4 * held * slots * width * inner, transcendentals=0, bytes_accessed=2**24
        ),
        input_output_aliases={11 + i: i for i in range(3)} if sums is not None else {},
        name="expert_weight_grads",
    )(ids, x_near, x_twin, g_near, g_twin, mask_all, slot_all, router_t, *weights, *(sums or ()))


def assemble_heads(core, near, twin, query_cols):
    chips, width, _ = near.shape
    devices = 2 * chips
    rows = 128
    pair = 2 * HEAD_DIM

    def kernel(core_ref, near_ref, twin_ref, query_ref, key_ref, value_ref):
        blocks = []
        for j in range(devices):
            mine = near_ref[j // 2].astype(jnp.float32)
            other = twin_ref[j // 2].astype(jnp.float32)
            blocks.append(jnp.where(core_ref[0] == j % 2, mine, other))
            query_ref[:, j * query_cols : (j + 1) * query_cols] = blocks[j][:, :query_cols]
        for c in range(chips):
            for ref, start in ((key_ref, query_cols), (value_ref, query_cols + HEAD_DIM)):
                ref[:, c * pair : (c + 1) * pair] = jnp.concatenate(
                    [blocks[2 * c + k][:, start : start + HEAD_DIM] for k in range(2)], axis=1
                )

    block = pl.BlockSpec((chips, rows, query_cols + pair), lambda r, m: (0, r, 0))
    shapes = [(width, devices * query_cols), (width, devices * HEAD_DIM), (width, devices * HEAD_DIM)]
    return pl.pallas_call(
        kernel,
        grid_spec=pltpu.PrefetchScalarGridSpec(
            num_scalar_prefetch=1,
            grid=(width // rows,),
            in_specs=[block, block],
            out_specs=[pl.BlockSpec((rows, s[1]), lambda r, m: (r, 0)) for s in shapes],
        ),
        out_shape=[jax.ShapeDtypeStruct(s, jnp.float32) for s in shapes],
        name="assemble_heads",
    )(core.reshape(1), near, twin)


def assemble_rows(core, near, twin, width):
    chips, rows, total = near.shape

    def kernel(core_ref, near_ref, twin_ref, output_ref, router_ref):
        mine = core_ref[0] == pl.program_id(0) % 2
        block = jnp.where(mine, near_ref[0].astype(jnp.float32), twin_ref[0].astype(jnp.float32))
        output_ref[...] = block[:, :width]
        router_ref[...] = block[:, width : width + EXPERTS]

    block = pl.BlockSpec((1, rows, total), lambda r, m: (r // 2, 0, 0))
    shapes = [(2 * chips * rows, width), (2 * chips * rows, EXPERTS)]
    return pl.pallas_call(
        kernel,
        grid_spec=pltpu.PrefetchScalarGridSpec(
            num_scalar_prefetch=1,
            grid=(2 * chips,),
            in_specs=[block, block],
            out_specs=[pl.BlockSpec((rows, s[1]), lambda r, m: (r, 0)) for s in shapes],
        ),
        out_shape=[jax.ShapeDtypeStruct(s, jnp.float32) for s in shapes],
        name="assemble_rows",
    )(core.reshape(1), near, twin)


def swap_cores(block, devices):
    return lax.ppermute(block, "expert", [(i, i ^ 1) for i in range(devices)])


def across_chips(blocks, devices):
    groups = [[2 * c + core for c in range(devices // 2)] for core in range(2)]
    return lax.all_to_all(blocks, "expert", 0, 0, axis_index_groups=groups, tiled=True)


def spread_row(block, devices):
    near = across_chips(jnp.broadcast_to(block[None], (devices // 2,) + block.shape), devices)
    return near, swap_cores(near, devices)


def merge_cores(near, twin, devices):
    partner = swap_cores(twin, devices)
    return (near.astype(jnp.float32) + partner.astype(jnp.float32)).astype(jnp.bfloat16)


def reduce_chips(merged, devices):
    return jnp.sum(across_chips(merged, devices).astype(jnp.float32), axis=0)


def in_order(near, twin, core):
    even = jnp.where(core == 0, near, twin)
    odd = jnp.where(core == 0, twin, near)
    return jnp.stack([even, odd], axis=1).reshape((2 * near.shape[0],) + near.shape[1:])


def with_tail(rows, tail):
    height, span = tail.shape
    return jnp.concatenate(
        [rows, jnp.pad(tail, ((0, TAIL - height), (0, rows.shape[1] - span)))], axis=0
    )


def exchange(blocks, axis):
    return lax.all_to_all(blocks, axis, 0, 0, tiled=True)


def broadcast(block, count):
    return jnp.broadcast_to(block[None], (count,) + block.shape)


def masked_gates(logits, mask):
    shown = jnp.where(mask, logits, NEG_FILL)
    weight = jnp.where(mask, jnp.exp(shown - jnp.max(shown, axis=-1, keepdims=True)), 0.0)
    return weight / jnp.sum(weight, axis=-1, keepdims=True)


def slot_tables(mask, first, held):
    group_len = mask.shape[2]
    local = lax.dynamic_slice_in_dim(mask, first, held, 1)
    steps = jnp.arange(group_len, dtype=jnp.int32)
    earlier = (steps[:, None] < steps[None, :]).astype(jnp.bfloat16)
    rank = jnp.einsum("gem,mn->gen", local, earlier, preferred_element_type=jnp.float32)
    return mask, jnp.where(local > 0, rank, -1.0).astype(jnp.int32)


def per_device_heads(
    tokens,
    attn_gain,
    w_query,
    w_key,
    w_value,
    w_output,
    moe_gain,
    w_router,
    w_gate,
    w_up,
    w_down,
    routes,
    segment_ids,
    out_grad,
):
    unused, group_len, width = tokens.shape
    devices, copies = lax.axis_size("expert"), lax.axis_size("dp")
    me, me_z = lax.axis_index("expert"), lax.axis_index("dp")
    core = me & 1
    chips = devices // 2
    length = group_len * devices
    repeats = HEADS // KV_HEADS
    query_cols = repeats * HEAD_DIM
    held = EXPERTS // devices
    lanes = 128
    order = jnp.stack([2 * c + (core ^ k) for k in range(2) for c in range(chips)])
    bf16 = jnp.bfloat16

    own = tokens[0]
    near_pay, twin_pay = spread_row(with_tail(own, segment_ids.astype(bf16)), devices)
    row_pay = jnp.concatenate([near_pay, twin_pay], axis=0)
    seg_row = row_pay[:, group_len, :group_len].reshape(length).astype(jnp.int32)
    row_tokens = row_pay[:, :group_len].reshape(length, width)
    row_index = (order[:, None] * group_len + jnp.arange(group_len, dtype=jnp.int32)).reshape(length)

    mask_own = jnp.any(
        routes[0][:, :, None] == jnp.arange(EXPERTS, dtype=jnp.int32)[None, None, :], axis=1
    )
    tail_rows = EXPERTS * group_len // width
    mask_tail = jnp.swapaxes(mask_own.astype(bf16), 0, 1).reshape(tail_rows, width)
    grad_pay, near_pay = lax.optimization_barrier((with_tail(out_grad[0], mask_tail), near_pay))
    g_near, g_twin = spread_row(grad_pay, devices)

    def tables(near, twin, axis):
        tails = [side[..., group_len : group_len + tail_rows, :] for side in (near, twin)]
        return slot_tables(
            jnp.concatenate(tails, axis=axis).reshape(-1, EXPERTS, group_len), me * held, held
        )

    mask_row, slot_row = tables(g_near, g_twin, 0)
    g_near_all = lax.all_gather(g_near, "dp", axis=0)
    router_t = jnp.swapaxes(w_router, 0, 1)

    head_weights = jnp.concatenate(
        [
            lax.dynamic_slice_in_dim(w_query, me * query_cols, query_cols, 1),
            lax.dynamic_slice_in_dim(w_key, me * HEAD_DIM, HEAD_DIM, 1),
            lax.dynamic_slice_in_dim(w_value, me * HEAD_DIM, HEAD_DIM, 1),
        ],
        axis=1,
    )
    before = jnp.sum((seg_row[None, :] < seg_row[:, None]).astype(jnp.int32), axis=1)
    cosine, sine = rope_tables(row_index - before)
    cos_heads, sin_heads = cosine[:, None, :], sine[:, None, :]
    normed, unused, _ = rms_forward(row_tokens.astype(jnp.float32), attn_gain)
    normed_row = normed.astype(bf16)
    lin = jnp.dot(normed_row, head_weights, preferred_element_type=jnp.float32)
    queries = rotate(
        lin[:, :query_cols].reshape(length, repeats, HEAD_DIM), cos_heads, sin_heads
    ).astype(bf16)
    keys = rotate(lin[:, query_cols : query_cols + HEAD_DIM], cosine, sine).astype(bf16)
    values = lin[:, query_cols + HEAD_DIM :].astype(bf16)
    scores = (
        jnp.einsum("qhd,kd->hqk", queries, keys, preferred_element_type=jnp.float32) * ATTN_SCALE
    )
    allowed = (seg_row[:, None] == seg_row[None, :]) & (row_index[None, :] <= row_index[:, None])
    masked = jnp.where(allowed[None], scores, NEG_FILL)
    raised = jnp.exp(masked - jnp.max(masked, axis=-1, keepdims=True))
    probs = raised / jnp.sum(raised, axis=-1, keepdims=True)
    probs_b = probs.astype(bf16)
    attended = jnp.einsum("hqk,kd->qhd", probs_b, values, preferred_element_type=jnp.float32)
    attn_heads = attended.astype(bf16).reshape(length, query_cols)
    attn_heads, g_near, g_twin = lax.optimization_barrier((attn_heads, g_near, g_twin))

    def to_tokens(rows):
        blocks = rows.reshape(2, chips, group_len, rows.shape[-1])
        return exchange(in_order(blocks[0], blocks[1], core), "expert")

    attn_rows = jnp.swapaxes(to_tokens(attn_heads), 0, 1).reshape(group_len, devices * query_cols)

    branch = jnp.dot(attn_rows, w_output, preferred_element_type=jnp.float32)
    residual = own.astype(jnp.float32)
    middle = residual + RESIDUAL_SCALE * branch
    normed2, unit_moe, inv_moe = rms_forward(middle, moe_gain)
    moe_rows = normed2.astype(bf16)
    gates_own = masked_gates(
        jnp.dot(moe_rows, w_router, preferred_element_type=jnp.float32), mask_own
    )
    x_near, x_twin = spread_row(moe_rows, devices)
    x_near_all = lax.all_gather(x_near, "dp", axis=0)

    d_near, d_twin, y_near, y_twin = near_experts(
        me, x_near, x_twin, g_near, g_twin, mask_row, slot_row, router_t, w_gate, w_up, w_down
    )
    d_merged = merge_cores(d_near, d_twin, devices)
    weights = (w_gate, w_up, w_down)

    def expert_row(z, sums, x_rows, g_rows, masks, slots):
        ids = jnp.stack([me, me_z, jnp.int32(z)])
        return expert_weight_grads(
            ids, sums, *x_rows, *g_rows, masks, slots, router_t, weights, copies
        )

    crossed = across_chips(d_merged, devices)
    x_mine, g_mine, d_merged = lax.optimization_barrier(
        ((x_near[None], x_twin[None]), (g_near[None], g_twin[None]), d_merged)
    )
    sums = expert_row(0, None, x_mine, g_mine, mask_row, slot_row)
    crossed, sums = lax.optimization_barrier((crossed, sums))
    returned = jnp.sum(crossed.astype(jnp.float32), axis=0)

    parts = returned[group_len : group_len + held] + returned[group_len + held : group_len + 2 * held]
    dgates = jnp.transpose(parts.reshape(held, devices, group_len), (2, 1, 0)).reshape(
        group_len, EXPERTS
    )
    dpicked = gates_own * (dgates - jnp.sum(gates_own * dgates, axis=-1, keepdims=True))
    dlogits = jnp.where(mask_own, dpicked, 0.0).astype(bf16)
    dnormed2 = returned[:group_len] + jnp.einsum(
        "ne,de->nd", dlogits, w_router, preferred_element_type=jnp.float32
    )
    dmiddle_norm, moe_gain_part = rms_backward(dnormed2, unit_moe, inv_moe, moe_gain)
    dmiddle = out_grad[0].astype(jnp.float32) + dmiddle_norm
    dbranch = (RESIDUAL_SCALE * dmiddle).astype(bf16)
    branch_near, branch_twin = spread_row(
        with_tail(dbranch, jnp.swapaxes(dlogits, 0, 1).reshape(tail_rows, width)), devices
    )
    branch_row = jnp.concatenate([branch_near, branch_twin], axis=0)
    dbranch_row = branch_row[:, :group_len].reshape(length, width)
    dlogits_row = branch_row[:, group_len : group_len + tail_rows].reshape(
        devices, EXPERTS, group_len
    )

    rows_per = width // devices
    output_part = jnp.einsum(
        "nh,nd->hd", attn_heads, dbranch_row, preferred_element_type=jnp.float32
    )
    router_cols = lax.dynamic_slice_in_dim(
        jnp.concatenate([x_near, x_twin], axis=0).reshape(length, width), me * rows_per, rows_per, 1
    )
    router_part = jnp.einsum(
        "bnd,ben->de",
        router_cols.reshape(devices, group_len, rows_per),
        dlogits_row,
        preferred_element_type=jnp.float32,
    )
    router_part = jnp.pad(router_part, ((0, 0), (0, lanes - EXPERTS)))
    first_part = jnp.concatenate([output_part, router_part], axis=1).reshape(
        copies, query_cols // copies, width + lanes
    )

    def z_cross(part):
        return exchange(part.astype(bf16), "dp")

    def z_sum(crossed):
        return jnp.sum(crossed.astype(jnp.float32), axis=0).astype(bf16)

    def z_column(summed):
        column = exchange(broadcast(summed, copies), "dp")
        return column.reshape((copies * summed.shape[0],) + summed.shape[1:])

    first_part = first_part.astype(bf16)
    dbranch_row, first_part = lax.optimization_barrier((dbranch_row, first_part))
    first_crossed = z_cross(first_part)

    out_heads = lax.dynamic_slice_in_dim(w_output, me * query_cols, query_cols, 0)
    dattn = jnp.einsum(
        "nd,hd->nh", dbranch_row, out_heads, preferred_element_type=jnp.float32
    ).astype(bf16).reshape(length, repeats, HEAD_DIM)
    dprobs = jnp.einsum("qhd,kd->hqk", dattn, values, preferred_element_type=jnp.float32)
    delta = jnp.sum(dattn.astype(jnp.float32) * attended, axis=-1)
    dscores = (probs * (dprobs - jnp.swapaxes(delta, 0, 1)[:, :, None])).astype(bf16)
    dqueries = (
        jnp.einsum("hqk,kd->qhd", dscores, keys, preferred_element_type=jnp.float32) * ATTN_SCALE
    )
    dkeys = (
        jnp.einsum("hqk,qhd->kd", dscores, queries, preferred_element_type=jnp.float32) * ATTN_SCALE
    )
    dvalues = jnp.einsum("hqk,qhd->kd", probs_b, dattn, preferred_element_type=jnp.float32)
    dlin = jnp.concatenate(
        [
            unrotate(dqueries, cos_heads, sin_heads).astype(bf16).reshape(length, query_cols),
            unrotate(dkeys, cosine, sine).astype(bf16),
            dvalues.astype(bf16),
        ],
        axis=1,
    )
    dlin, first_crossed = lax.optimization_barrier((dlin, first_crossed))
    head_part = jnp.einsum("nd,nh->dh", normed_row, dlin, preferred_element_type=jnp.float32)
    head_cols = query_cols + 2 * HEAD_DIM
    head_part = head_part.reshape(copies, width // copies, head_cols).astype(bf16)

    head_part, first_crossed, y_near, y_twin = lax.optimization_barrier(
        (head_part, first_crossed, y_near, y_twin)
    )
    head_crossed = z_cross(head_part)
    dlin_back = to_tokens(dlin)
    first_column = z_column(z_sum(first_crossed))
    y_merged = merge_cores(y_near, y_twin, devices)
    g_near_all, x_near_all, head_part = lax.optimization_barrier(
        (g_near_all, x_near_all, head_part)
    )
    g_rows = (g_near_all, swap_cores(g_near_all, devices))
    x_rows = (x_near_all, swap_cores(x_near_all, devices))
    masks, slots = tables(*g_rows, 1)

    def far_row(step, sums):
        return expert_row((me_z + step) % copies, sums, x_rows, g_rows, masks, slots)

    sums = far_row(1, sums)
    head_crossed, first_column, dlin_back, sums = lax.optimization_barrier(
        (head_crossed, first_column, dlin_back, sums)
    )
    column = z_column(z_sum(head_crossed))
    first_near = across_chips(broadcast(first_column, chips), devices)
    for step in range(2, copies - 1):
        sums = far_row(step, sums)
    column, first_near, sums = lax.optimization_barrier((column, first_near, sums))
    head_near = across_chips(broadcast(column, chips), devices)
    grad_output, grad_router = assemble_rows(core, first_near, swap_cores(first_near, devices), width)
    if copies > 2:
        sums = far_row(copies - 1, sums)
    head_near, sums, y_merged = lax.optimization_barrier((head_near, sums, y_merged))
    mixed = (middle + RESIDUAL_SCALE * reduce_chips(y_merged, devices)).astype(bf16)[None]
    head_twin = swap_cores(head_near, devices)
    grad_gate, grad_up, grad_down = sums
    grad_query, grad_key, grad_value = assemble_heads(core, head_near, head_twin, query_cols)

    dlin_back = jnp.swapaxes(dlin_back, 0, 1)

    def token_grad(start, count, weights):
        rows = dlin_back[:, :, start : start + count].reshape(group_len, devices * count)
        return jnp.einsum("nh,dh->nd", rows, weights, preferred_element_type=jnp.float32)

    dnormed = (
        token_grad(0, query_cols, w_query)
        + token_grad(query_cols, HEAD_DIM, w_key)
        + token_grad(query_cols + HEAD_DIM, HEAD_DIM, w_value)
    )
    unused, unit_attn, inv_attn = rms_forward(residual, attn_gain)
    dresid_norm, attn_gain_part = rms_backward(dnormed, unit_attn, inv_attn, attn_gain)
    grad_tokens = (dmiddle + dresid_norm)[None]
    gain_sums = jnp.stack([attn_gain_part, moe_gain_part])
    for axis, count in (("expert", devices), ("dp", copies)):
        gain_sums = jnp.sum(exchange(broadcast(gain_sums, count), axis), axis=0)

    return (
        mixed,
        grad_tokens,
        gain_sums[0],
        grad_query,
        grad_key,
        grad_value,
        grad_output,
        gain_sums[1],
        grad_router,
        grad_gate,
        grad_up,
        grad_down,
    )


def solution(mesh):
    placed = (
        P("dp", "expert", None),
        P(),
        P(),
        P(),
        P(),
        P(),
        P(),
        P(),
        P("expert", None, None),
        P("expert", None, None),
        P("expert", None, None),
        P("dp", "expert", None),
        P("dp", "expert"),
        P("dp", "expert", None),
    )
    by_heads = mesh.shape["expert"] == KV_HEADS
    return jax.shard_map(
        per_device_heads if by_heads else per_device_general,
        mesh=mesh,
        in_specs=placed,
        out_specs=(
            P("dp", "expert", None),
            P("dp", "expert", None),
            P(),
            P(),
            P(),
            P(),
            P(),
            P(),
            P(),
            P("expert", "dp", None),
            P("expert", "dp", None),
            P("expert", "dp", None),
        ),
        check_vma=False,
    )
```

```python
import jax
import jax.numpy as jnp
from jax import lax
from jax.experimental import pallas as pl
from jax.experimental.pallas import tpu as pltpu
from jax.sharding import PartitionSpec as P


HEADS = 16
KV_HEADS = 8
HEAD_DIM = 64
EXPERTS = 32
TOP = 8
MOST = 48


ATTN_SCALE = 0.015625
RESIDUAL_SCALE = 0.22
NORM_EPS = 1e-06
ROPE_BASE = 10000.0
NEG_FILL = -1e30
TAIL = 16


def rms_forward(values, gain_vec):
    inverse = lax.rsqrt(jnp.mean(values * values, axis=-1, keepdims=True) + NORM_EPS)
    unit_rows = values * inverse
    return (unit_rows * gain_vec, unit_rows, inverse)


def rms_backward(grad_rows, unit_rows, inverse, gain_vec):
    scaled = grad_rows * gain_vec
    grad_gain = jnp.sum(grad_rows * unit_rows, axis=0)
    grad_in = inverse * (scaled - unit_rows * jnp.mean(scaled * unit_rows, axis=-1, keepdims=True))
    return (grad_in, grad_gain)


def rope_tables(positions):
    half = HEAD_DIM // 2
    freqs = ROPE_BASE ** (-(jnp.arange(half, dtype=jnp.float32) * 2.0) / HEAD_DIM)
    angles = positions.astype(jnp.float32)[..., None] * freqs
    cosine = jnp.concatenate([jnp.cos(angles), jnp.cos(angles)], axis=-1)
    sine = jnp.concatenate([jnp.sin(angles), jnp.sin(angles)], axis=-1)
    return (cosine, sine)


def rotate(vectors, cosine, sine):
    half = vectors.shape[-1] // 2
    turned = jnp.concatenate([-vectors[..., half:], vectors[..., :half]], axis=-1)
    return vectors * cosine + turned * sine


def unrotate(grads, cosine, sine):
    half = grads.shape[-1] // 2
    scaled = grads * sine
    turned = jnp.concatenate([scaled[..., half:], -scaled[..., :half]], axis=-1)
    return grads * cosine + turned


def scaled_scores(query_part, key_part, query_seg, key_seg, query_index, key_index):
    raw = (
        jnp.einsum("qrgjd,krgd->rgjqk", query_part, key_part, preferred_element_type=jnp.float32)
        * ATTN_SCALE
    )
    same = jnp.transpose(query_seg)[:, :, None] == jnp.transpose(key_seg)[:, None, :]
    before = key_index[None, :] <= query_index[:, None]
    return (raw, (same & before[None])[:, None, None])


def probs_and_ds(
    query_part,
    key_part,
    value_part,
    dout_part,
    lse_part,
    delta_part,
    query_seg,
    key_seg,
    query_index,
    key_index,
):
    scores, allowed = scaled_scores(
        query_part, key_part, query_seg, key_seg, query_index, key_index
    )
    lse_rows = jnp.transpose(lse_part, (1, 2, 3, 0))[..., None]
    delta_rows = jnp.transpose(delta_part, (1, 2, 3, 0))[..., None]
    probs = jnp.where(allowed, jnp.exp(scores - lse_rows), 0.0)
    dprobs = jnp.einsum(
        "qrgjd,krgd->rgjqk", dout_part, value_part, preferred_element_type=jnp.float32
    )
    dscore = (probs * (dprobs - delta_rows)).astype(jnp.bfloat16)
    return (probs.astype(jnp.bfloat16), dscore)


def per_device_general(
    tokens,
    attn_gain,
    w_query,
    w_key,
    w_value,
    w_output,
    moe_gain,
    w_router,
    w_gate,
    w_up,
    w_down,
    routes,
    segment_ids,
    out_grad,
):
    row_count, group_len, width = tokens.shape
    devices = lax.axis_size("expert")
    my_index = lax.axis_index("expert")
    length = group_len * devices
    repeats = HEADS // KV_HEADS
    tok_count = group_len * row_count
    slot_rows = row_count * MOST
    seg_local = jnp.transpose(segment_ids)
    seg_all = lax.all_gather(seg_local, "expert", axis=0, tiled=True)
    query_index = my_index * group_len + jnp.arange(group_len, dtype=jnp.int32)
    earlier = jnp.sum((seg_all[None, :, :] < seg_local[:, None, :]).astype(jnp.int32), axis=1)
    cosine, sine = rope_tables(query_index[:, None] - earlier)
    cos_heads = cosine[:, :, None, :]
    sin_heads = sine[:, :, None, :]
    residual = jnp.swapaxes(tokens, 0, 1).astype(jnp.float32).reshape(tok_count, width)
    normed, unit_attn, inv_attn = rms_forward(residual, attn_gain)
    normed_rows = normed.astype(jnp.bfloat16)
    query_lin = jnp.dot(normed_rows, w_query, preferred_element_type=jnp.float32).reshape(
        group_len, row_count, HEADS, HEAD_DIM
    )
    queries = (
        rotate(query_lin, cos_heads, sin_heads)
        .astype(jnp.bfloat16)
        .reshape(group_len, row_count, KV_HEADS, repeats, HEAD_DIM)
    )
    key_lin = jnp.dot(normed_rows, w_key, preferred_element_type=jnp.float32).reshape(
        group_len, row_count, KV_HEADS, HEAD_DIM
    )
    keys = rotate(key_lin, cos_heads, sin_heads).astype(jnp.bfloat16)
    values = (
        jnp.dot(normed_rows, w_value, preferred_element_type=jnp.float32)
        .astype(jnp.bfloat16)
        .reshape(group_len, row_count, KV_HEADS, HEAD_DIM)
    )
    keys_all, values_all = (
        lax.all_gather(keys, "expert", axis=0, tiled=True),
        lax.all_gather(values, "expert", axis=0, tiled=True),
    )
    key_block = min(1024, length)
    block_count = length // key_block
    key_blocks = keys_all.reshape(block_count, key_block, row_count, KV_HEADS, HEAD_DIM)
    value_blocks = values_all.reshape(block_count, key_block, row_count, KV_HEADS, HEAD_DIM)
    seg_blocks = seg_all.reshape(block_count, key_block, row_count)
    index_blocks = jnp.arange(length, dtype=jnp.int32).reshape(block_count, key_block)
    key_inputs = (key_blocks, value_blocks, seg_blocks, index_blocks)

    def max_step(carried, current):
        running, totals = carried
        key_part, _, seg_part, index_part = current
        scores, allowed = scaled_scores(
            queries, key_part, seg_local, seg_part, query_index, index_part
        )
        newmax = jnp.maximum(running, jnp.max(jnp.where(allowed, scores, NEG_FILL), axis=-1))
        totals = totals * jnp.exp(running - newmax) + jnp.sum(
            jnp.where(allowed, jnp.exp(scores - newmax[..., None]), 0.0), axis=-1
        )
        return ((newmax, totals), None)

    stat_shape = (row_count, KV_HEADS, repeats, group_len)
    (running, totals), unused = lax.scan(
        max_step,
        (jnp.full(stat_shape, NEG_FILL, jnp.float32), jnp.zeros(stat_shape, jnp.float32)),
        key_inputs,
    )
    logsum = running + jnp.log(totals)
    lse_local = jnp.transpose(logsum, (3, 0, 1, 2))

    def out_step(accum, current):
        key_part, value_part, seg_part, index_part = current
        scores, allowed = scaled_scores(
            queries, key_part, seg_local, seg_part, query_index, index_part
        )
        probs = jnp.where(allowed, jnp.exp(scores - logsum[..., None]), 0.0).astype(jnp.bfloat16)
        return (
            accum
            + jnp.einsum(
                "rgjqk,krgd->qrgjd", probs, value_part, preferred_element_type=jnp.float32
            ),
            None,
        )

    head_shape = (group_len, row_count, KV_HEADS, repeats, HEAD_DIM)
    attended, unused = lax.scan(out_step, jnp.zeros(head_shape, jnp.float32), key_inputs)
    attn_rows = attended.reshape(tok_count, HEADS * HEAD_DIM).astype(jnp.bfloat16)
    branch = jnp.dot(attn_rows, w_output, preferred_element_type=jnp.float32)
    middle = residual + RESIDUAL_SCALE * branch
    normed2, unit_moe, inv_moe = rms_forward(middle, moe_gain)
    moe_rows = normed2.astype(jnp.bfloat16)
    logits = jnp.dot(moe_rows, w_router, preferred_element_type=jnp.float32)
    route_rows = jnp.transpose(routes, (1, 0, 2)).reshape(tok_count, TOP)
    onehot = route_rows[:, :, None] == jnp.arange(EXPERTS, dtype=jnp.int32)[None, None, :]
    picked = jnp.sum(jnp.where(onehot, logits[:, None, :], 0.0), axis=-1)
    gates = jax.nn.softmax(picked, axis=-1)
    by_row = jnp.transpose(
        onehot.reshape(group_len, row_count, TOP, EXPERTS), (1, 0, 2, 3)
    ).reshape(row_count, group_len * TOP, EXPERTS)
    counted = jnp.cumsum(by_row.astype(jnp.int32), axis=1)
    rank = jnp.sum(jnp.where(by_row, counted - 1, 0), axis=-1).reshape(row_count, group_len, TOP)
    rank = jnp.transpose(rank, (1, 0, 2)).reshape(tok_count, TOP)
    row_of = jnp.arange(tok_count, dtype=jnp.int32) % row_count
    target = (route_rows * slot_rows + row_of[:, None] * MOST + rank).reshape(tok_count * TOP)

    def to_slots(route_values):
        placed = (
            jnp.zeros((EXPERTS * slot_rows, width), jnp.bfloat16)
            .at[target]
            .set(route_values.reshape(tok_count * TOP, width))
        )
        return placed.reshape(EXPERTS, slot_rows, width)

    def from_slots(slot_values):
        return (
            slot_values.reshape(EXPERTS * slot_rows, width)[target]
            .reshape(tok_count, TOP, width)
            .astype(jnp.float32)
        )

    sent = to_slots(jnp.broadcast_to(moe_rows[:, None, :], (tok_count, TOP, width)))
    arrived = lax.all_to_all(sent, "expert", split_axis=0, concat_axis=1, tiled=True)
    gate_pre = jnp.einsum("etd,edf->etf", arrived, w_gate, preferred_element_type=jnp.float32)
    up_pre = jnp.einsum("etd,edf->etf", arrived, w_up, preferred_element_type=jnp.float32)
    sigma = jax.nn.sigmoid(gate_pre)
    activated = gate_pre * sigma
    hidden = (activated * up_pre).astype(jnp.bfloat16)
    expert_out = jnp.einsum(
        "etf,efd->etd", hidden, w_down, preferred_element_type=jnp.float32
    ).astype(jnp.bfloat16)
    returned = lax.all_to_all(expert_out, "expert", split_axis=1, concat_axis=0, tiled=True)
    route_out = from_slots(returned)
    moe = jnp.sum(gates[:, :, None] * route_out, axis=1)
    mixed_rows = middle + RESIDUAL_SCALE * moe
    mixed = jnp.swapaxes(mixed_rows.reshape(group_len, row_count, width), 0, 1).astype(jnp.bfloat16)
    upstream = jnp.swapaxes(out_grad, 0, 1).astype(jnp.float32).reshape(tok_count, width)
    dmoe = RESIDUAL_SCALE * upstream
    dgates = jnp.sum(route_out * dmoe[:, None, :], axis=-1)
    dsent = to_slots((gates[:, :, None] * dmoe[:, None, :]).astype(jnp.bfloat16))
    darrived = lax.all_to_all(dsent, "expert", split_axis=0, concat_axis=1, tiled=True)
    dhidden = jnp.einsum("etd,efd->etf", darrived, w_down, preferred_element_type=jnp.float32)
    down_part = jnp.einsum("etf,etd->efd", hidden, darrived, preferred_element_type=jnp.float32)
    dgate_pre = (dhidden * up_pre * sigma * (1.0 + gate_pre * (1.0 - sigma))).astype(jnp.bfloat16)
    dup_pre = (dhidden * activated).astype(jnp.bfloat16)
    gate_part = jnp.einsum("etd,etf->edf", arrived, dgate_pre, preferred_element_type=jnp.float32)
    up_part = jnp.einsum("etd,etf->edf", arrived, dup_pre, preferred_element_type=jnp.float32)
    dinputs = (
        jnp.einsum("etf,edf->etd", dgate_pre, w_gate, preferred_element_type=jnp.float32)
        + jnp.einsum("etf,edf->etd", dup_pre, w_up, preferred_element_type=jnp.float32)
    ).astype(jnp.bfloat16)
    grad_gate, grad_up, grad_down = (
        lax.psum_scatter(
            gate_part.astype(jnp.bfloat16), "dp", scatter_dimension=1, tiled=True
        ).astype(jnp.float32),
        lax.psum_scatter(
            up_part.astype(jnp.bfloat16), "dp", scatter_dimension=1, tiled=True
        ).astype(jnp.float32),
        lax.psum_scatter(
            down_part.astype(jnp.bfloat16), "dp", scatter_dimension=1, tiled=True
        ).astype(jnp.float32),
    )
    dreturned = lax.all_to_all(dinputs, "expert", split_axis=1, concat_axis=0, tiled=True)
    droutes = jnp.sum(from_slots(dreturned), axis=1)
    dpicked = gates * (dgates - jnp.sum(gates * dgates, axis=-1, keepdims=True))
    dlogits = jnp.sum(jnp.where(onehot, dpicked[:, :, None], 0.0), axis=1).astype(jnp.bfloat16)
    router_part = jnp.einsum("nd,ne->de", moe_rows, dlogits, preferred_element_type=jnp.float32)
    dnormed2 = droutes + jnp.einsum(
        "ne,de->nd", dlogits, w_router, preferred_element_type=jnp.float32
    )
    dmiddle_norm, moe_gain_part = rms_backward(dnormed2, unit_moe, inv_moe, moe_gain)
    dmiddle = upstream + dmiddle_norm
    dbranch = (RESIDUAL_SCALE * dmiddle).astype(jnp.bfloat16)
    output_part = jnp.einsum("nh,nd->hd", attn_rows, dbranch, preferred_element_type=jnp.float32)
    dattn = (
        jnp.einsum("nd,hd->nh", dbranch, w_output, preferred_element_type=jnp.float32)
        .astype(jnp.bfloat16)
        .reshape(head_shape)
    )
    delta = jnp.sum(dattn.astype(jnp.float32) * attended, axis=-1)

    def both_step(dq_sum, current):
        key_part, value_part, seg_part, index_part = current
        probs_b, dscore = probs_and_ds(
            queries,
            key_part,
            value_part,
            dattn,
            lse_local,
            delta,
            seg_local,
            seg_part,
            query_index,
            index_part,
        )
        dq_part = (
            jnp.einsum("rgjqk,krgd->qrgjd", dscore, key_part, preferred_element_type=jnp.float32)
            * ATTN_SCALE
        )
        dk_part = (
            jnp.einsum("rgjqk,qrgjd->krgd", dscore, queries, preferred_element_type=jnp.float32)
            * ATTN_SCALE
        )
        dv_part = jnp.einsum(
            "rgjqk,qrgjd->krgd", probs_b, dattn, preferred_element_type=jnp.float32
        )
        return (dq_sum + dq_part, (dk_part, dv_part))

    dq_sum, (dk_stack, dv_stack) = lax.scan(
        both_step, jnp.zeros(head_shape, jnp.float32), key_inputs
    )
    full_shape = (length, row_count, KV_HEADS, HEAD_DIM)
    dkeys, dvalues = (
        lax.psum_scatter(
            dk_stack.reshape(full_shape).astype(jnp.bfloat16),
            "expert",
            scatter_dimension=0,
            tiled=True,
        ).astype(jnp.float32),
        lax.psum_scatter(
            dv_stack.reshape(full_shape).astype(jnp.bfloat16),
            "expert",
            scatter_dimension=0,
            tiled=True,
        ).astype(jnp.float32),
    )
    dquery_lin = (
        unrotate(dq_sum.reshape(group_len, row_count, HEADS, HEAD_DIM), cos_heads, sin_heads)
        .astype(jnp.bfloat16)
        .reshape(tok_count, HEADS * HEAD_DIM)
    )
    dkey_lin = (
        unrotate(dkeys, cos_heads, sin_heads)
        .astype(jnp.bfloat16)
        .reshape(tok_count, KV_HEADS * HEAD_DIM)
    )
    dvalue_rows = dvalues.astype(jnp.bfloat16).reshape(tok_count, KV_HEADS * HEAD_DIM)
    query_part_grad = jnp.einsum(
        "nd,nh->dh", normed_rows, dquery_lin, preferred_element_type=jnp.float32
    )
    key_part_grad = jnp.einsum(
        "nd,nh->dh", normed_rows, dkey_lin, preferred_element_type=jnp.float32
    )
    value_part_grad = jnp.einsum(
        "nd,nh->dh", normed_rows, dvalue_rows, preferred_element_type=jnp.float32
    )
    dnormed = (
        jnp.einsum("nh,dh->nd", dquery_lin, w_query, preferred_element_type=jnp.float32)
        + jnp.einsum("nh,dh->nd", dkey_lin, w_key, preferred_element_type=jnp.float32)
        + jnp.einsum("nh,dh->nd", dvalue_rows, w_value, preferred_element_type=jnp.float32)
    )
    dresid_norm, attn_gain_part = rms_backward(dnormed, unit_attn, inv_attn, attn_gain)
    grad_tokens = jnp.swapaxes((dmiddle + dresid_norm).reshape(group_len, row_count, width), 0, 1)
    query_sum, key_sum, value_sum, output_sum, router_sum, attn_gain_sum, moe_gain_sum = lax.psum(
        (
            query_part_grad,
            key_part_grad,
            value_part_grad,
            output_part,
            router_part,
            attn_gain_part,
            moe_gain_part,
        ),
        ("dp", "expert"),
    )
    return (
        mixed,
        grad_tokens,
        attn_gain_sum,
        query_sum,
        key_sum,
        value_sum,
        output_sum,
        moe_gain_sum,
        router_sum,
        grad_gate,
        grad_up,
        grad_down,
    )


def expert_gather(x_rows, g_rows, mask_rows, slot_rows, router_rows, first, x_scr, g_scr, gate_scr, table_scr, groups):
    held = x_scr.shape[0]
    for g in range(groups):
        rows = x_rows(g)
        logits = lax.dot_general(
            router_rows, rows, (((1,), (1,)), ((), ())), preferred_element_type=jnp.float32
        )
        shown = mask_rows(g) > 0
        raised = jnp.where(
            shown,
            jnp.exp(logits - jnp.max(jnp.where(shown, logits, NEG_FILL), axis=0, keepdims=True)),
            0.0,
        )
        gates = raised / jnp.sum(raised, axis=0, keepdims=True)
        slots = slot_rows(g)
        expert = lax.broadcasted_iota(jnp.int32, gates.shape, 0)
        place = lax.broadcasted_iota(jnp.int32, (MOST, rows.shape[0]), 0)
        tables = []
        for e in range(held):
            gate_row = jnp.sum(jnp.where(expert == first + e, gates, 0.0), axis=0, keepdims=True)
            chosen = place == slots[e : e + 1, :]
            gate_scr[e, g * MOST : (g + 1) * MOST, :] = jnp.sum(
                jnp.where(chosen, gate_row, 0.0), axis=1, keepdims=True
            )
            tables.append(jnp.where(chosen, 1.0, 0.0))
        table = jnp.concatenate(tables, axis=0).astype(jnp.bfloat16)
        if table_scr is not None:
            table_scr[g] = table
        for scr, part in ((x_scr, rows), (g_scr, g_rows(g))):
            picked = jnp.dot(table, part, preferred_element_type=jnp.float32).astype(jnp.bfloat16)
            for e in range(held):
                scr[e, g * MOST : (g + 1) * MOST, :] = picked[e * MOST : (e + 1) * MOST, :]


def nt(left, right):
    return lax.dot_general(
        left, right, (((1,), (1,)), ((), ())), preferred_element_type=jnp.float32
    )


def tn(left, right):
    return lax.dot_general(
        left, right, (((0,), (0,)), ((), ())), preferred_element_type=jnp.float32
    )


def expert_body(x_slots, g_slots, gate_col, gate_w, up_w, down_w):
    gate_pre = jnp.dot(x_slots, gate_w, preferred_element_type=jnp.float32)
    up_pre = jnp.dot(x_slots, up_w, preferred_element_type=jnp.float32)
    sigma = jax.nn.sigmoid(gate_pre)
    activated = gate_pre * sigma
    hidden = (activated * up_pre).astype(jnp.bfloat16)
    dexpert = (gate_col * (RESIDUAL_SCALE * g_slots.astype(jnp.float32))).astype(jnp.bfloat16)
    dhidden = nt(dexpert, down_w)
    dgate_pre = (dhidden * up_pre * sigma * (1.0 + gate_pre * (1.0 - sigma))).astype(jnp.bfloat16)
    dup_pre = (dhidden * activated).astype(jnp.bfloat16)
    return hidden, dexpert, dgate_pre, dup_pre


def near_experts(me, x_near, x_twin, g_near, g_twin, mask_row, slot_row, router_t, w_gate, w_up, w_down):
    chips, group_len, width = x_near.shape
    held, _, inner = w_gate.shape
    groups = 2 * chips
    extra = 16
    lanes = 128

    def kernel(me_ref, xn, xt, gn, gt, mr, sr, rt, wg, wu, wd, near_out, twin_out, y_near, y_twin,
               x_scr, g_scr, gate_scr, table_scr, y_scr, d_scr, dg_scr):
        e = pl.program_id(0)
        my = me_ref[0]

        @pl.when(e == 0)
        def _():
            expert_gather(
                lambda g: (xn if g < chips else xt)[g % chips],
                lambda g: (gn if g < chips else gt)[g % chips],
                lambda g: mr[g],
                lambda g: sr[g],
                rt[...],
                my * held,
                x_scr, g_scr, gate_scr, table_scr, groups,
            )

        g_slots = g_scr[e]
        hidden, _, dgate_pre, dup_pre = expert_body(
            x_scr[e], g_slots, gate_scr[e], wg[0], wu[0], wd[0]
        )
        out = jnp.dot(hidden, wd[0], preferred_element_type=jnp.float32).astype(jnp.bfloat16)
        out_wide = out.astype(jnp.float32)
        dgate = jnp.sum(
            RESIDUAL_SCALE * g_slots.astype(jnp.float32) * out_wide, axis=1, keepdims=True
        )
        weighted = (gate_scr[e] * out_wide).astype(jnp.bfloat16)
        dinputs = (nt(dgate_pre, wg[0]) + nt(dup_pre, wu[0])).astype(jnp.bfloat16)
        spot = pl.ds(pl.multiple_of(e * MOST, 16), MOST)
        for g in range(groups):
            part = slice(g * MOST, (g + 1) * MOST)
            y_scr[g, spot, :] = weighted[part]
            d_scr[g, spot, :] = dinputs[part]
            taken = table_scr[g, spot, :].astype(jnp.float32)
            dg_scr[g, e] = jnp.sum(taken * dgate[part], axis=0, keepdims=True)

        @pl.when(e == held - 1)
        def _():
            block = lax.broadcasted_iota(jnp.int32, (held, width), 1) // lanes
            for g in range(groups):
                d_out, y_out = (near_out, y_near) if g < chips else (twin_out, y_twin)
                table = table_scr[g]
                y_out[g % chips] = tn(table, y_scr[g]).astype(jnp.bfloat16)
                d_out[g % chips, :group_len, :] = tn(table, d_scr[g]).astype(jnp.bfloat16)
                rows = jnp.concatenate([dg_scr[g, i] for i in range(held)], axis=0)
                spread = jnp.where(block == my, jnp.concatenate([rows] * groups, axis=1), 0.0)
                high = spread.astype(jnp.bfloat16).astype(jnp.float32)
                tail = jnp.concatenate(
                    [high, spread - high, jnp.zeros((extra - 2 * held, width), jnp.float32)], axis=0
                )
                d_out[g % chips, group_len:, :] = tail.astype(jnp.bfloat16)

    whole = lambda *shape: pl.BlockSpec(shape, lambda e, m: (0,) * len(shape))
    weight = lambda *shape: pl.BlockSpec((1,) + shape, lambda e, m: (e, 0, 0))
    back = jax.ShapeDtypeStruct((chips, group_len + extra, width), jnp.bfloat16)
    forth = jax.ShapeDtypeStruct((chips, group_len, width), jnp.bfloat16)
    slots = groups * MOST
    return pl.pallas_call(
        kernel,
        grid_spec=pltpu.PrefetchScalarGridSpec(
            num_scalar_prefetch=1,
            grid=(held,),
            in_specs=[
                whole(chips, group_len, width),
                whole(chips, group_len, width),
                whole(chips, group_len, width),
                whole(chips, group_len, width),
                whole(groups, EXPERTS, group_len),
                whole(groups, held, group_len),
                whole(EXPERTS, width),
                weight(width, inner),
                weight(width, inner),
                weight(inner, width),
            ],
            out_specs=[
                whole(chips, group_len + extra, width),
                whole(chips, group_len + extra, width),
                whole(chips, group_len, width),
                whole(chips, group_len, width),
            ],
            scratch_shapes=[
                pltpu.VMEM((held, slots, width), jnp.bfloat16),
                pltpu.VMEM((held, slots, width), jnp.bfloat16),
                pltpu.VMEM((held, slots, 1), jnp.float32),
                pltpu.VMEM((groups, held * MOST, group_len), jnp.bfloat16),
                pltpu.VMEM((groups, held * MOST, width), jnp.bfloat16),
                pltpu.VMEM((groups, held * MOST, width), jnp.bfloat16),
                pltpu.VMEM((groups, held, 1, group_len), jnp.float32),
            ],
        ),
        out_shape=[back, back, forth, forth],
        compiler_params=pltpu.CompilerParams(
            dimension_semantics=("arbitrary",), vmem_limit_bytes=58 * 2**20
        ),
        cost_estimate=pl.CostEstimate(
            flops=2 * 7 * held * slots * width * inner, transcendentals=0, bytes_accessed=2**24
        ),
        name="near_experts",
    )(me.reshape(1), x_near, x_twin, g_near, g_twin, mask_row, slot_row, router_t, w_gate, w_up, w_down)


def expert_weight_grads(ids, sums, x_near, x_twin, g_near, g_twin, mask_all, slot_all, router_t, weights, copies):
    unused, chips, group_len, width = x_near.shape
    held, unused, inner = weights[0].shape
    groups = 2 * chips
    slots = groups * MOST
    wide, narrow = width // copies, inner // copies

    def kernel(ids_ref, xn, xt, gn, gt, mr, sr, rt, wg, wu, wd, *refs):
        gate_out, up_out, down_out, x_scr, g_scr, gate_scr = refs[-6:]
        befores = refs[:-6] if sums is not None else (None, None, None)
        e = pl.program_id(0)
        mine, slab = ids_ref[0], ids_ref[1]

        @pl.when(e == 0)
        def _():
            expert_gather(
                lambda g: (xn if g < chips else xt)[0, g % chips],
                lambda g: (gn if g < chips else gt)[0, g % chips],
                lambda g: mr[g],
                lambda g: sr[g],
                rt[...], mine * held, x_scr, g_scr, gate_scr, None, groups,
            )

        x_slots = x_scr[e]
        hidden, dexpert, dgate_pre, dup_pre = expert_body(
            x_slots, g_scr[e], gate_scr[e], wg[0], wu[0], wd[0]
        )
        x_part, h_part = x_slots[:, :wide], hidden[:, :narrow]
        for k in range(1, copies):
            x_part = jnp.where(slab == k, x_slots[:, k * wide : (k + 1) * wide], x_part)
            h_part = jnp.where(slab == k, hidden[:, k * narrow : (k + 1) * narrow], h_part)
        for out, before, left, right in zip(
            (gate_out, up_out, down_out),
            befores,
            (x_part, x_part, h_part),
            (dgate_pre, dup_pre, dexpert),
        ):
            part = tn(left, right)
            out[0] = part if before is None else before[0] + part

    some = lambda *shape: pl.BlockSpec((groups,) + shape, lambda e, m: (m[2], 0, 0))
    rows = pl.BlockSpec((1, chips, group_len, width), lambda e, m: (m[2], 0, 0, 0))
    weight = lambda *shape: pl.BlockSpec((1,) + shape, lambda e, m: (e, 0, 0))
    whole = lambda *shape: pl.BlockSpec(shape, lambda e, m: (0,) * len(shape))
    outs = [(held, wide, inner), (held, wide, inner), (held, narrow, width)]
    return pl.pallas_call(
        kernel,
        grid_spec=pltpu.PrefetchScalarGridSpec(
            num_scalar_prefetch=1,
            grid=(held,),
            in_specs=[
                rows,
                rows,
                rows,
                rows,
                some(EXPERTS, group_len),
                some(held, group_len),
                whole(EXPERTS, width),
                weight(width, inner),
                weight(width, inner),
                weight(inner, width),
            ]
            + ([weight(*shape[1:]) for shape in outs] if sums is not None else []),
            out_specs=[weight(*shape[1:]) for shape in outs],
            scratch_shapes=[
                pltpu.VMEM((held, slots, width), jnp.bfloat16),
                pltpu.VMEM((held, slots, width), jnp.bfloat16),
                pltpu.VMEM((held, slots, 1), jnp.float32),
            ],
        ),
        out_shape=[jax.ShapeDtypeStruct(shape, jnp.float32) for shape in outs],
        compiler_params=pltpu.CompilerParams(
            dimension_semantics=("arbitrary",), vmem_limit_bytes=58 * 2**20
        ),
        cost_estimate=pl.CostEstimate(
            flops=2 * 4 * held * slots * width * inner, transcendentals=0, bytes_accessed=2**24
        ),
        input_output_aliases={11 + i: i for i in range(3)} if sums is not None else {},
        name="expert_weight_grads",
    )(ids, x_near, x_twin, g_near, g_twin, mask_all, slot_all, router_t, *weights, *(sums or ()))


def assemble_heads(core, near, twin, width, query_cols):
    chips = near.shape[0]
    devices = 2 * chips
    rows = 128
    pair = 2 * HEAD_DIM

    def kernel(core_ref, near_ref, twin_ref, query_ref, key_ref, value_ref):
        blocks = []
        for j in range(devices):
            mine = near_ref[j // 2].astype(jnp.float32)
            other = twin_ref[j // 2].astype(jnp.float32)
            blocks.append(jnp.where(core_ref[0] == j % 2, mine, other))
            query_ref[:, j * query_cols : (j + 1) * query_cols] = blocks[j][:, :query_cols]
        for c in range(chips):
            for ref, start in ((key_ref, query_cols), (value_ref, query_cols + HEAD_DIM)):
                ref[:, c * pair : (c + 1) * pair] = jnp.concatenate(
                    [blocks[2 * c + k][:, start : start + HEAD_DIM] for k in range(2)], axis=1
                )

    block = pl.BlockSpec((chips, rows, query_cols + pair), lambda r, m: (0, r, 0))
    shapes = [(width, devices * query_cols), (width, devices * HEAD_DIM), (width, devices * HEAD_DIM)]
    return pl.pallas_call(
        kernel,
        grid_spec=pltpu.PrefetchScalarGridSpec(
            num_scalar_prefetch=1,
            grid=(width // rows,),
            in_specs=[block, block],
            out_specs=[pl.BlockSpec((rows, s[1]), lambda r, m: (r, 0)) for s in shapes],
        ),
        out_shape=[jax.ShapeDtypeStruct(s, jnp.float32) for s in shapes],
        name="assemble_heads",
    )(core.reshape(1), near, twin)


def assemble_rows(me, near, twin, width):
    chips, rows, total = near.shape

    def kernel(me_ref, near_ref, twin_ref, output_ref, router_ref):
        mine = (me_ref[0] & 1) == pl.program_id(0) % 2
        block = jnp.where(mine, near_ref[0].astype(jnp.float32), twin_ref[0].astype(jnp.float32))
        output_ref[...] = block[:, :width]
        router_ref[...] = block[:, width : width + EXPERTS]

    block = pl.BlockSpec((1, rows, total), lambda r, m: ((r // 2) ^ (m[0] >> 1), 0, 0))
    shapes = [(2 * chips * rows, width), (2 * chips * rows, EXPERTS)]
    return pl.pallas_call(
        kernel,
        grid_spec=pltpu.PrefetchScalarGridSpec(
            num_scalar_prefetch=1,
            grid=(2 * chips,),
            in_specs=[block, block],
            out_specs=[pl.BlockSpec((rows, s[1]), lambda r, m: (r, 0)) for s in shapes],
        ),
        out_shape=[jax.ShapeDtypeStruct(s, jnp.float32) for s in shapes],
        name="assemble_rows",
    )(me.reshape(1), near, twin)


def swap_cores(block, devices):
    return lax.ppermute(block, "expert", [(i, i ^ 1) for i in range(devices)])


def across_chips(blocks, devices):
    groups = [[2 * c + core for c in range(devices // 2)] for core in range(2)]
    return lax.all_to_all(blocks, "expert", 0, 0, axis_index_groups=groups, tiled=True)


def permute(block, shift, axis, count):
    return lax.ppermute(block, axis, [(i, i ^ shift) for i in range(count)])


def spread_row(block, devices):
    near = across_chips(jnp.broadcast_to(block[None], (devices // 2,) + block.shape), devices)
    return near, swap_cores(near, devices)


def merge_cores(near, twin, devices):
    partner = swap_cores(twin, devices)
    return (near.astype(jnp.float32) + partner.astype(jnp.float32)).astype(jnp.bfloat16)


def permute_sum(parts, mine, step, axis, count):
    total = lax.dynamic_index_in_dim(parts, mine, 0, False).astype(jnp.float32)
    for s in range(1, parts.shape[0]):
        part = lax.dynamic_index_in_dim(parts, mine ^ s, 0, False)
        total = total + permute(part, s * step, axis, count).astype(jnp.float32)
    return total


def in_order(near, twin, core):
    even = jnp.where(core == 0, near, twin)
    odd = jnp.where(core == 0, twin, near)
    return jnp.stack([even, odd], axis=1).reshape((2 * near.shape[0],) + near.shape[1:])


def with_tail(rows, tail):
    height, span = tail.shape
    return jnp.concatenate(
        [rows, jnp.pad(tail, ((0, TAIL - height), (0, rows.shape[1] - span)))], axis=0
    )


def pack_gains(gains, span):
    high = gains.astype(jnp.bfloat16)
    lower = (gains - high.astype(jnp.float32)).astype(jnp.bfloat16)
    return jnp.concatenate([high, lower], axis=0).reshape(-1, span)


def unpack_gains(packed, width):
    parts = packed.reshape(packed.shape[0], 2, -1, width).astype(jnp.float32)
    return parts[:, 0] + parts[:, 1]


def exchange(blocks, axis):
    return lax.all_to_all(blocks, axis, 0, 0, tiled=True)


def broadcast(block, count):
    return jnp.broadcast_to(block[None], (count,) + block.shape)


def masked_gates(logits, mask):
    shown = jnp.where(mask, logits, NEG_FILL)
    weight = jnp.where(mask, jnp.exp(shown - jnp.max(shown, axis=-1, keepdims=True)), 0.0)
    return weight / jnp.sum(weight, axis=-1, keepdims=True)


def slot_tables(mask, first, held):
    group_len = mask.shape[2]
    local = lax.dynamic_slice_in_dim(mask, first, held, 1)
    steps = jnp.arange(group_len, dtype=jnp.int32)
    earlier = (steps[:, None] < steps[None, :]).astype(jnp.bfloat16)
    rank = jnp.einsum("gem,mn->gen", local, earlier, preferred_element_type=jnp.float32)
    return mask, jnp.where(local > 0, rank, -1.0).astype(jnp.int32)


def per_device_heads(
    tokens,
    attn_gain,
    w_query,
    w_key,
    w_value,
    w_output,
    moe_gain,
    w_router,
    w_gate,
    w_up,
    w_down,
    routes,
    segment_ids,
    out_grad,
):
    unused, group_len, width = tokens.shape
    devices, copies = lax.axis_size("expert"), lax.axis_size("dp")
    me, me_z = lax.axis_index("expert"), lax.axis_index("dp")
    core = me & 1
    chips = devices // 2
    length = group_len * devices
    repeats = HEADS // KV_HEADS
    query_cols = repeats * HEAD_DIM
    held = EXPERTS // devices
    lanes = 128
    order = jnp.stack([2 * c + (core ^ k) for k in range(2) for c in range(chips)])
    bf16 = jnp.bfloat16

    own = tokens[0]
    near_pay, twin_pay = spread_row(with_tail(own, segment_ids.astype(bf16)), devices)
    row_pay = jnp.concatenate([near_pay, twin_pay], axis=0)
    seg_row = row_pay[:, group_len, :group_len].reshape(length).astype(jnp.int32)
    row_tokens = row_pay[:, :group_len].reshape(length, width)
    row_index = (order[:, None] * group_len + jnp.arange(group_len, dtype=jnp.int32)).reshape(length)

    mask_own = jnp.any(
        routes[0][:, :, None] == jnp.arange(EXPERTS, dtype=jnp.int32)[None, None, :], axis=1
    )
    tail_rows = EXPERTS * group_len // width
    mask_tail = jnp.swapaxes(mask_own.astype(bf16), 0, 1).reshape(tail_rows, width)
    grad_pay, near_pay = lax.optimization_barrier((with_tail(out_grad[0], mask_tail), near_pay))
    g_near, g_twin = spread_row(grad_pay, devices)

    def tables(near, twin, axis):
        tails = [side[..., group_len : group_len + tail_rows, :] for side in (near, twin)]
        return slot_tables(
            jnp.concatenate(tails, axis=axis).reshape(-1, EXPERTS, group_len), me * held, held
        )

    mask_row, slot_row = tables(g_near, g_twin, 0)
    g_near_all = lax.all_gather(g_near, "dp", axis=0)
    router_t = jnp.swapaxes(w_router, 0, 1)

    head_weights = jnp.concatenate(
        [
            lax.dynamic_slice_in_dim(w_query, me * query_cols, query_cols, 1),
            lax.dynamic_slice_in_dim(w_key, me * HEAD_DIM, HEAD_DIM, 1),
            lax.dynamic_slice_in_dim(w_value, me * HEAD_DIM, HEAD_DIM, 1),
        ],
        axis=1,
    )
    before = jnp.sum((seg_row[None, :] < seg_row[:, None]).astype(jnp.int32), axis=1)
    cosine, sine = rope_tables(row_index - before)
    cos_heads, sin_heads = cosine[:, None, :], sine[:, None, :]
    normed, unused, _ = rms_forward(row_tokens.astype(jnp.float32), attn_gain)
    normed_row = normed.astype(bf16)
    lin = jnp.dot(normed_row, head_weights, preferred_element_type=jnp.float32)
    queries = rotate(
        lin[:, :query_cols].reshape(length, repeats, HEAD_DIM), cos_heads, sin_heads
    ).astype(bf16)
    keys = rotate(lin[:, query_cols : query_cols + HEAD_DIM], cosine, sine).astype(bf16)
    values = lin[:, query_cols + HEAD_DIM :].astype(bf16)
    scores = (
        jnp.einsum("qhd,kd->hqk", queries, keys, preferred_element_type=jnp.float32) * ATTN_SCALE
    )
    allowed = (seg_row[:, None] == seg_row[None, :]) & (row_index[None, :] <= row_index[:, None])
    masked = jnp.where(allowed[None], scores, NEG_FILL)
    raised = jnp.exp(masked - jnp.max(masked, axis=-1, keepdims=True))
    probs = raised / jnp.sum(raised, axis=-1, keepdims=True)
    probs_b = probs.astype(bf16)
    attended = jnp.einsum("hqk,kd->qhd", probs_b, values, preferred_element_type=jnp.float32)
    attn_heads = attended.astype(bf16).reshape(length, query_cols)
    attn_heads, g_near, g_twin = lax.optimization_barrier((attn_heads, g_near, g_twin))

    def to_tokens(rows):
        blocks = rows.reshape(2, chips, group_len, rows.shape[-1])
        return exchange(in_order(blocks[0], blocks[1], core), "expert")

    attn_rows = jnp.swapaxes(to_tokens(attn_heads), 0, 1).reshape(group_len, devices * query_cols)

    branch = jnp.dot(attn_rows, w_output, preferred_element_type=jnp.float32)
    residual = own.astype(jnp.float32)
    middle = residual + RESIDUAL_SCALE * branch
    normed2, unit_moe, inv_moe = rms_forward(middle, moe_gain)
    moe_rows = normed2.astype(bf16)
    gates_own = masked_gates(
        jnp.dot(moe_rows, w_router, preferred_element_type=jnp.float32), mask_own
    )
    x_near, x_twin = spread_row(moe_rows, devices)
    x_near_all = lax.all_gather(x_near, "dp", axis=0)

    d_near, d_twin, y_near, y_twin = near_experts(
        me, x_near, x_twin, g_near, g_twin, mask_row, slot_row, router_t, w_gate, w_up, w_down
    )
    d_merged = merge_cores(d_near, d_twin, devices)
    weights = (w_gate, w_up, w_down)

    def expert_row(z, sums, x_rows, g_rows, masks, slots):
        ids = jnp.stack([me, me_z, jnp.int32(z)])
        return expert_weight_grads(
            ids, sums, *x_rows, *g_rows, masks, slots, router_t, weights, copies
        )

    crossed = across_chips(d_merged, devices)
    x_mine, g_mine, d_merged = lax.optimization_barrier(
        ((x_near[None], x_twin[None]), (g_near[None], g_twin[None]), d_merged)
    )
    sums = expert_row(0, None, x_mine, g_mine, mask_row, slot_row)
    crossed, sums = lax.optimization_barrier((crossed, sums))
    returned = jnp.sum(crossed.astype(jnp.float32), axis=0)

    parts = returned[group_len : group_len + held] + returned[group_len + held : group_len + 2 * held]
    dgates = jnp.transpose(parts.reshape(held, devices, group_len), (2, 1, 0)).reshape(
        group_len, EXPERTS
    )
    dpicked = gates_own * (dgates - jnp.sum(gates_own * dgates, axis=-1, keepdims=True))
    dlogits = jnp.where(mask_own, dpicked, 0.0).astype(bf16)
    dnormed2 = returned[:group_len] + jnp.einsum(
        "ne,de->nd", dlogits, w_router, preferred_element_type=jnp.float32
    )
    dmiddle_norm, moe_gain_part = rms_backward(dnormed2, unit_moe, inv_moe, moe_gain)
    dmiddle = out_grad[0].astype(jnp.float32) + dmiddle_norm
    dbranch = (RESIDUAL_SCALE * dmiddle).astype(bf16)
    branch_near, branch_twin = spread_row(
        with_tail(dbranch, jnp.swapaxes(dlogits, 0, 1).reshape(tail_rows, width)), devices
    )
    branch_row = jnp.concatenate([branch_near, branch_twin], axis=0)
    dbranch_row = branch_row[:, :group_len].reshape(length, width)
    dlogits_row = branch_row[:, group_len : group_len + tail_rows].reshape(
        devices, EXPERTS, group_len
    )

    rows_per = width // devices
    output_part = jnp.einsum(
        "nh,nd->hd", attn_heads, dbranch_row, preferred_element_type=jnp.float32
    )
    router_cols = lax.dynamic_slice_in_dim(
        jnp.concatenate([x_near, x_twin], axis=0).reshape(length, width), me * rows_per, rows_per, 1
    )
    router_part = jnp.einsum(
        "bnd,ben->de",
        router_cols.reshape(devices, group_len, rows_per),
        dlogits_row,
        preferred_element_type=jnp.float32,
    )
    router_part = jnp.pad(router_part, ((0, 0), (0, lanes - EXPERTS)))
    first_part = jnp.concatenate([output_part, router_part], axis=1).reshape(
        copies, query_cols // copies, width + lanes
    )

    def z_cross(part):
        return exchange(part.astype(bf16), "dp")

    def z_sum(crossed):
        return jnp.sum(crossed.astype(jnp.float32), axis=0).astype(bf16)

    def z_column(summed):
        column = exchange(broadcast(summed, copies), "dp")
        return column.reshape((copies * summed.shape[0],) + summed.shape[1:])

    first_part = first_part.astype(bf16)
    dbranch_row, first_part = lax.optimization_barrier((dbranch_row, first_part))
    first_crossed = z_cross(first_part)

    out_heads = lax.dynamic_slice_in_dim(w_output, me * query_cols, query_cols, 0)
    dattn = jnp.einsum(
        "nd,hd->nh", dbranch_row, out_heads, preferred_element_type=jnp.float32
    ).astype(bf16).reshape(length, repeats, HEAD_DIM)
    dprobs = jnp.einsum("qhd,kd->hqk", dattn, values, preferred_element_type=jnp.float32)
    delta = jnp.sum(dattn.astype(jnp.float32) * attended, axis=-1)
    dscores = (probs * (dprobs - jnp.swapaxes(delta, 0, 1)[:, :, None])).astype(bf16)
    dqueries = (
        jnp.einsum("hqk,kd->qhd", dscores, keys, preferred_element_type=jnp.float32) * ATTN_SCALE
    )
    dkeys = (
        jnp.einsum("hqk,qhd->kd", dscores, queries, preferred_element_type=jnp.float32) * ATTN_SCALE
    )
    dvalues = jnp.einsum("hqk,qhd->kd", probs_b, dattn, preferred_element_type=jnp.float32)
    dlin = jnp.concatenate(
        [
            unrotate(dqueries, cos_heads, sin_heads).astype(bf16).reshape(length, query_cols),
            unrotate(dkeys, cosine, sine).astype(bf16),
            dvalues.astype(bf16),
        ],
        axis=1,
    )
    dlin, first_crossed = lax.optimization_barrier((dlin, first_crossed))
    head_part = jnp.einsum("nd,nh->dh", normed_row, dlin, preferred_element_type=jnp.float32)
    head_cols = query_cols + 2 * HEAD_DIM
    head_part = head_part.reshape(copies, width // copies, head_cols).astype(bf16)

    head_summed = permute_sum(head_part, me_z, 1, "dp", copies).astype(bf16)
    dlin_back = jnp.swapaxes(to_tokens(dlin), 0, 1)
    first_column = z_column(z_sum(first_crossed))

    def token_grad(start, count, weights):
        rows = dlin_back[:, :, start : start + count].reshape(group_len, devices * count)
        return jnp.einsum("nh,dh->nd", rows, weights, preferred_element_type=jnp.float32)

    dnormed = (
        token_grad(0, query_cols, w_query)
        + token_grad(query_cols, HEAD_DIM, w_key)
        + token_grad(query_cols + HEAD_DIM, HEAD_DIM, w_value)
    )
    unused, unit_attn, inv_attn = rms_forward(residual, attn_gain)
    dresid_norm, attn_gain_part = rms_backward(dnormed, unit_attn, inv_attn, attn_gain)
    grad_tokens = (dmiddle + dresid_norm)[None]
    gain_parts = pack_gains(jnp.stack([attn_gain_part, moe_gain_part]), head_cols)
    column = exchange(broadcast(jnp.concatenate([head_summed, gain_parts], axis=0), copies), "dp")

    g_near_all, x_near_all, first_column, y_near, y_twin, gain_parts = lax.optimization_barrier(
        (g_near_all, x_near_all, first_column, y_near, y_twin, gain_parts)
    )
    g_rows = (g_near_all, swap_cores(g_near_all, devices))
    x_rows = (x_near_all, swap_cores(x_near_all, devices))
    masks, slots = tables(*g_rows, 1)
    y_merged = merge_cores(y_near, y_twin, devices)
    first_near = jnp.stack(
        [first_column]
        + [permute(first_column, 2 * s, "expert", devices) for s in range(1, chips)]
    )
    y_sum = permute_sum(y_merged, me >> 1, 2, "expert", devices)

    def far_row(step, sums):
        return expert_row((me_z + step) % copies, sums, x_rows, g_rows, masks, slots)

    sums = far_row(1, sums)
    column, sums = lax.optimization_barrier((column, sums))
    rows = width // copies
    gain_parts = pack_gains(jnp.sum(unpack_gains(column[:, rows:], width), axis=0), head_cols)
    column = jnp.concatenate([column[:, :rows].reshape(width, head_cols), gain_parts], axis=0)
    head_near = across_chips(broadcast(column, chips), devices)
    for step in range(2, copies):
        sums = far_row(step, sums)
    head_near, sums = lax.optimization_barrier((head_near, sums))
    head_twin = swap_cores(head_near, devices)
    mixed = (middle + RESIDUAL_SCALE * y_sum).astype(bf16)[None]
    grad_output, grad_router = assemble_rows(me, first_near, swap_cores(first_near, devices), width)
    grad_gate, grad_up, grad_down = sums
    grad_query, grad_key, grad_value = assemble_heads(core, head_near, head_twin, width, query_cols)
    gain_sums = jnp.sum(unpack_gains(head_near[:, width:], width), axis=0) + jnp.sum(
        unpack_gains(head_twin[:, width:], width), axis=0
    )
    return (
        mixed,
        grad_tokens,
        gain_sums[0],
        grad_query,
        grad_key,
        grad_value,
        grad_output,
        gain_sums[1],
        grad_router,
        grad_gate,
        grad_up,
        grad_down,
    )


def solution(mesh):
    placed = (
        P("dp", "expert", None),
        P(),
        P(),
        P(),
        P(),
        P(),
        P(),
        P(),
        P("expert", None, None),
        P("expert", None, None),
        P("expert", None, None),
        P("dp", "expert", None),
        P("dp", "expert"),
        P("dp", "expert", None),
    )
    by_heads = mesh.shape["expert"] == KV_HEADS
    return jax.shard_map(
        per_device_heads if by_heads else per_device_general,
        mesh=mesh,
        in_specs=placed,
        out_specs=(
            P("dp", "expert", None),
            P("dp", "expert", None),
            P(),
            P(),
            P(),
            P(),
            P(),
            P(),
            P(),
            P("expert", "dp", None),
            P("expert", "dp", None),
            P("expert", "dp", None),
        ),
        check_vma=False,
    )
```

```python
import jax
import jax.numpy as jnp
from jax import lax
from jax.experimental import pallas as pl
from jax.experimental.pallas import tpu as pltpu
from jax.sharding import PartitionSpec as P


HEADS = 16
KV_HEADS = 8
HEAD_DIM = 64
EXPERTS = 32
TOP = 8
MOST = 48


ATTN_SCALE = 0.015625
RESIDUAL_SCALE = 0.22
NORM_EPS = 1e-06
ROPE_BASE = 10000.0
NEG_FILL = -1e30
TAIL = 16
SEGMENTS = 8


def rms_forward(values, gain_vec):
    inverse = lax.rsqrt(jnp.mean(values * values, axis=-1, keepdims=True) + NORM_EPS)
    unit_rows = values * inverse
    return (unit_rows * gain_vec, unit_rows, inverse)


def rms_backward(grad_rows, unit_rows, inverse, gain_vec):
    scaled = grad_rows * gain_vec
    grad_gain = jnp.sum(grad_rows * unit_rows, axis=0)
    grad_in = inverse * (scaled - unit_rows * jnp.mean(scaled * unit_rows, axis=-1, keepdims=True))
    return (grad_in, grad_gain)


def rope_tables(positions):
    half = HEAD_DIM // 2
    freqs = ROPE_BASE ** (-(jnp.arange(half, dtype=jnp.float32) * 2.0) / HEAD_DIM)
    angles = positions.astype(jnp.float32)[..., None] * freqs
    cosine = jnp.concatenate([jnp.cos(angles), jnp.cos(angles)], axis=-1)
    sine = jnp.concatenate([jnp.sin(angles), jnp.sin(angles)], axis=-1)
    return (cosine, sine)


def rotate(vectors, cosine, sine):
    half = vectors.shape[-1] // 2
    turned = jnp.concatenate([-vectors[..., half:], vectors[..., :half]], axis=-1)
    return vectors * cosine + turned * sine


def unrotate(grads, cosine, sine):
    half = grads.shape[-1] // 2
    scaled = grads * sine
    turned = jnp.concatenate([scaled[..., half:], -scaled[..., :half]], axis=-1)
    return grads * cosine + turned


def scaled_scores(query_part, key_part, query_seg, key_seg, query_index, key_index):
    raw = (
        jnp.einsum("qrgjd,krgd->rgjqk", query_part, key_part, preferred_element_type=jnp.float32)
        * ATTN_SCALE
    )
    same = jnp.transpose(query_seg)[:, :, None] == jnp.transpose(key_seg)[:, None, :]
    before = key_index[None, :] <= query_index[:, None]
    return (raw, (same & before[None])[:, None, None])


def probs_and_ds(
    query_part,
    key_part,
    value_part,
    dout_part,
    lse_part,
    delta_part,
    query_seg,
    key_seg,
    query_index,
    key_index,
):
    scores, allowed = scaled_scores(
        query_part, key_part, query_seg, key_seg, query_index, key_index
    )
    lse_rows = jnp.transpose(lse_part, (1, 2, 3, 0))[..., None]
    delta_rows = jnp.transpose(delta_part, (1, 2, 3, 0))[..., None]
    probs = jnp.where(allowed, jnp.exp(scores - lse_rows), 0.0)
    dprobs = jnp.einsum(
        "qrgjd,krgd->rgjqk", dout_part, value_part, preferred_element_type=jnp.float32
    )
    dscore = (probs * (dprobs - delta_rows)).astype(jnp.bfloat16)
    return (probs.astype(jnp.bfloat16), dscore)


def per_device_general(
    tokens,
    attn_gain,
    w_query,
    w_key,
    w_value,
    w_output,
    moe_gain,
    w_router,
    w_gate,
    w_up,
    w_down,
    routes,
    segment_ids,
    out_grad,
):
    row_count, group_len, width = tokens.shape
    devices = lax.axis_size("expert")
    my_index = lax.axis_index("expert")
    length = group_len * devices
    repeats = HEADS // KV_HEADS
    tok_count = group_len * row_count
    slot_rows = row_count * MOST
    seg_local = jnp.transpose(segment_ids)
    seg_all = lax.all_gather(seg_local, "expert", axis=0, tiled=True)
    query_index = my_index * group_len + jnp.arange(group_len, dtype=jnp.int32)
    earlier = jnp.sum((seg_all[None, :, :] < seg_local[:, None, :]).astype(jnp.int32), axis=1)
    cosine, sine = rope_tables(query_index[:, None] - earlier)
    cos_heads = cosine[:, :, None, :]
    sin_heads = sine[:, :, None, :]
    residual = jnp.swapaxes(tokens, 0, 1).astype(jnp.float32).reshape(tok_count, width)
    normed, unit_attn, inv_attn = rms_forward(residual, attn_gain)
    normed_rows = normed.astype(jnp.bfloat16)
    query_lin = jnp.dot(normed_rows, w_query, preferred_element_type=jnp.float32).reshape(
        group_len, row_count, HEADS, HEAD_DIM
    )
    queries = (
        rotate(query_lin, cos_heads, sin_heads)
        .astype(jnp.bfloat16)
        .reshape(group_len, row_count, KV_HEADS, repeats, HEAD_DIM)
    )
    key_lin = jnp.dot(normed_rows, w_key, preferred_element_type=jnp.float32).reshape(
        group_len, row_count, KV_HEADS, HEAD_DIM
    )
    keys = rotate(key_lin, cos_heads, sin_heads).astype(jnp.bfloat16)
    values = (
        jnp.dot(normed_rows, w_value, preferred_element_type=jnp.float32)
        .astype(jnp.bfloat16)
        .reshape(group_len, row_count, KV_HEADS, HEAD_DIM)
    )
    keys_all, values_all = (
        lax.all_gather(keys, "expert", axis=0, tiled=True),
        lax.all_gather(values, "expert", axis=0, tiled=True),
    )
    key_block = min(1024, length)
    block_count = length // key_block
    key_blocks = keys_all.reshape(block_count, key_block, row_count, KV_HEADS, HEAD_DIM)
    value_blocks = values_all.reshape(block_count, key_block, row_count, KV_HEADS, HEAD_DIM)
    seg_blocks = seg_all.reshape(block_count, key_block, row_count)
    index_blocks = jnp.arange(length, dtype=jnp.int32).reshape(block_count, key_block)
    key_inputs = (key_blocks, value_blocks, seg_blocks, index_blocks)

    def max_step(carried, current):
        running, totals = carried
        key_part, _, seg_part, index_part = current
        scores, allowed = scaled_scores(
            queries, key_part, seg_local, seg_part, query_index, index_part
        )
        newmax = jnp.maximum(running, jnp.max(jnp.where(allowed, scores, NEG_FILL), axis=-1))
        totals = totals * jnp.exp(running - newmax) + jnp.sum(
            jnp.where(allowed, jnp.exp(scores - newmax[..., None]), 0.0), axis=-1
        )
        return ((newmax, totals), None)

    stat_shape = (row_count, KV_HEADS, repeats, group_len)
    (running, totals), unused = lax.scan(
        max_step,
        (jnp.full(stat_shape, NEG_FILL, jnp.float32), jnp.zeros(stat_shape, jnp.float32)),
        key_inputs,
    )
    logsum = running + jnp.log(totals)
    lse_local = jnp.transpose(logsum, (3, 0, 1, 2))

    def out_step(accum, current):
        key_part, value_part, seg_part, index_part = current
        scores, allowed = scaled_scores(
            queries, key_part, seg_local, seg_part, query_index, index_part
        )
        probs = jnp.where(allowed, jnp.exp(scores - logsum[..., None]), 0.0).astype(jnp.bfloat16)
        return (
            accum
            + jnp.einsum(
                "rgjqk,krgd->qrgjd", probs, value_part, preferred_element_type=jnp.float32
            ),
            None,
        )

    head_shape = (group_len, row_count, KV_HEADS, repeats, HEAD_DIM)
    attended, unused = lax.scan(out_step, jnp.zeros(head_shape, jnp.float32), key_inputs)
    attn_rows = attended.reshape(tok_count, HEADS * HEAD_DIM).astype(jnp.bfloat16)
    branch = jnp.dot(attn_rows, w_output, preferred_element_type=jnp.float32)
    middle = residual + RESIDUAL_SCALE * branch
    normed2, unit_moe, inv_moe = rms_forward(middle, moe_gain)
    moe_rows = normed2.astype(jnp.bfloat16)
    logits = jnp.dot(moe_rows, w_router, preferred_element_type=jnp.float32)
    route_rows = jnp.transpose(routes, (1, 0, 2)).reshape(tok_count, TOP)
    onehot = route_rows[:, :, None] == jnp.arange(EXPERTS, dtype=jnp.int32)[None, None, :]
    picked = jnp.sum(jnp.where(onehot, logits[:, None, :], 0.0), axis=-1)
    gates = jax.nn.softmax(picked, axis=-1)
    by_row = jnp.transpose(
        onehot.reshape(group_len, row_count, TOP, EXPERTS), (1, 0, 2, 3)
    ).reshape(row_count, group_len * TOP, EXPERTS)
    counted = jnp.cumsum(by_row.astype(jnp.int32), axis=1)
    rank = jnp.sum(jnp.where(by_row, counted - 1, 0), axis=-1).reshape(row_count, group_len, TOP)
    rank = jnp.transpose(rank, (1, 0, 2)).reshape(tok_count, TOP)
    row_of = jnp.arange(tok_count, dtype=jnp.int32) % row_count
    target = (route_rows * slot_rows + row_of[:, None] * MOST + rank).reshape(tok_count * TOP)

    def to_slots(route_values):
        placed = (
            jnp.zeros((EXPERTS * slot_rows, width), jnp.bfloat16)
            .at[target]
            .set(route_values.reshape(tok_count * TOP, width))
        )
        return placed.reshape(EXPERTS, slot_rows, width)

    def from_slots(slot_values):
        return (
            slot_values.reshape(EXPERTS * slot_rows, width)[target]
            .reshape(tok_count, TOP, width)
            .astype(jnp.float32)
        )

    sent = to_slots(jnp.broadcast_to(moe_rows[:, None, :], (tok_count, TOP, width)))
    arrived = lax.all_to_all(sent, "expert", split_axis=0, concat_axis=1, tiled=True)
    gate_pre = jnp.einsum("etd,edf->etf", arrived, w_gate, preferred_element_type=jnp.float32)
    up_pre = jnp.einsum("etd,edf->etf", arrived, w_up, preferred_element_type=jnp.float32)
    sigma = jax.nn.sigmoid(gate_pre)
    activated = gate_pre * sigma
    hidden = (activated * up_pre).astype(jnp.bfloat16)
    expert_out = jnp.einsum(
        "etf,efd->etd", hidden, w_down, preferred_element_type=jnp.float32
    ).astype(jnp.bfloat16)
    returned = lax.all_to_all(expert_out, "expert", split_axis=1, concat_axis=0, tiled=True)
    route_out = from_slots(returned)
    moe = jnp.sum(gates[:, :, None] * route_out, axis=1)
    mixed_rows = middle + RESIDUAL_SCALE * moe
    mixed = jnp.swapaxes(mixed_rows.reshape(group_len, row_count, width), 0, 1).astype(jnp.bfloat16)
    upstream = jnp.swapaxes(out_grad, 0, 1).astype(jnp.float32).reshape(tok_count, width)
    dmoe = RESIDUAL_SCALE * upstream
    dgates = jnp.sum(route_out * dmoe[:, None, :], axis=-1)
    dsent = to_slots((gates[:, :, None] * dmoe[:, None, :]).astype(jnp.bfloat16))
    darrived = lax.all_to_all(dsent, "expert", split_axis=0, concat_axis=1, tiled=True)
    dhidden = jnp.einsum("etd,efd->etf", darrived, w_down, preferred_element_type=jnp.float32)
    down_part = jnp.einsum("etf,etd->efd", hidden, darrived, preferred_element_type=jnp.float32)
    dgate_pre = (dhidden * up_pre * sigma * (1.0 + gate_pre * (1.0 - sigma))).astype(jnp.bfloat16)
    dup_pre = (dhidden * activated).astype(jnp.bfloat16)
    gate_part = jnp.einsum("etd,etf->edf", arrived, dgate_pre, preferred_element_type=jnp.float32)
    up_part = jnp.einsum("etd,etf->edf", arrived, dup_pre, preferred_element_type=jnp.float32)
    dinputs = (
        jnp.einsum("etf,edf->etd", dgate_pre, w_gate, preferred_element_type=jnp.float32)
        + jnp.einsum("etf,edf->etd", dup_pre, w_up, preferred_element_type=jnp.float32)
    ).astype(jnp.bfloat16)
    grad_gate, grad_up, grad_down = (
        lax.psum_scatter(
            gate_part.astype(jnp.bfloat16), "dp", scatter_dimension=1, tiled=True
        ).astype(jnp.float32),
        lax.psum_scatter(
            up_part.astype(jnp.bfloat16), "dp", scatter_dimension=1, tiled=True
        ).astype(jnp.float32),
        lax.psum_scatter(
            down_part.astype(jnp.bfloat16), "dp", scatter_dimension=1, tiled=True
        ).astype(jnp.float32),
    )
    dreturned = lax.all_to_all(dinputs, "expert", split_axis=1, concat_axis=0, tiled=True)
    droutes = jnp.sum(from_slots(dreturned), axis=1)
    dpicked = gates * (dgates - jnp.sum(gates * dgates, axis=-1, keepdims=True))
    dlogits = jnp.sum(jnp.where(onehot, dpicked[:, :, None], 0.0), axis=1).astype(jnp.bfloat16)
    router_part = jnp.einsum("nd,ne->de", moe_rows, dlogits, preferred_element_type=jnp.float32)
    dnormed2 = droutes + jnp.einsum(
        "ne,de->nd", dlogits, w_router, preferred_element_type=jnp.float32
    )
    dmiddle_norm, moe_gain_part = rms_backward(dnormed2, unit_moe, inv_moe, moe_gain)
    dmiddle = upstream + dmiddle_norm
    dbranch = (RESIDUAL_SCALE * dmiddle).astype(jnp.bfloat16)
    output_part = jnp.einsum("nh,nd->hd", attn_rows, dbranch, preferred_element_type=jnp.float32)
    dattn = (
        jnp.einsum("nd,hd->nh", dbranch, w_output, preferred_element_type=jnp.float32)
        .astype(jnp.bfloat16)
        .reshape(head_shape)
    )
    delta = jnp.sum(dattn.astype(jnp.float32) * attended, axis=-1)

    def both_step(dq_sum, current):
        key_part, value_part, seg_part, index_part = current
        probs_b, dscore = probs_and_ds(
            queries,
            key_part,
            value_part,
            dattn,
            lse_local,
            delta,
            seg_local,
            seg_part,
            query_index,
            index_part,
        )
        dq_part = (
            jnp.einsum("rgjqk,krgd->qrgjd", dscore, key_part, preferred_element_type=jnp.float32)
            * ATTN_SCALE
        )
        dk_part = (
            jnp.einsum("rgjqk,qrgjd->krgd", dscore, queries, preferred_element_type=jnp.float32)
            * ATTN_SCALE
        )
        dv_part = jnp.einsum(
            "rgjqk,qrgjd->krgd", probs_b, dattn, preferred_element_type=jnp.float32
        )
        return (dq_sum + dq_part, (dk_part, dv_part))

    dq_sum, (dk_stack, dv_stack) = lax.scan(
        both_step, jnp.zeros(head_shape, jnp.float32), key_inputs
    )
    full_shape = (length, row_count, KV_HEADS, HEAD_DIM)
    dkeys, dvalues = (
        lax.psum_scatter(
            dk_stack.reshape(full_shape).astype(jnp.bfloat16),
            "expert",
            scatter_dimension=0,
            tiled=True,
        ).astype(jnp.float32),
        lax.psum_scatter(
            dv_stack.reshape(full_shape).astype(jnp.bfloat16),
            "expert",
            scatter_dimension=0,
            tiled=True,
        ).astype(jnp.float32),
    )
    dquery_lin = (
        unrotate(dq_sum.reshape(group_len, row_count, HEADS, HEAD_DIM), cos_heads, sin_heads)
        .astype(jnp.bfloat16)
        .reshape(tok_count, HEADS * HEAD_DIM)
    )
    dkey_lin = (
        unrotate(dkeys, cos_heads, sin_heads)
        .astype(jnp.bfloat16)
        .reshape(tok_count, KV_HEADS * HEAD_DIM)
    )
    dvalue_rows = dvalues.astype(jnp.bfloat16).reshape(tok_count, KV_HEADS * HEAD_DIM)
    query_part_grad = jnp.einsum(
        "nd,nh->dh", normed_rows, dquery_lin, preferred_element_type=jnp.float32
    )
    key_part_grad = jnp.einsum(
        "nd,nh->dh", normed_rows, dkey_lin, preferred_element_type=jnp.float32
    )
    value_part_grad = jnp.einsum(
        "nd,nh->dh", normed_rows, dvalue_rows, preferred_element_type=jnp.float32
    )
    dnormed = (
        jnp.einsum("nh,dh->nd", dquery_lin, w_query, preferred_element_type=jnp.float32)
        + jnp.einsum("nh,dh->nd", dkey_lin, w_key, preferred_element_type=jnp.float32)
        + jnp.einsum("nh,dh->nd", dvalue_rows, w_value, preferred_element_type=jnp.float32)
    )
    dresid_norm, attn_gain_part = rms_backward(dnormed, unit_attn, inv_attn, attn_gain)
    grad_tokens = jnp.swapaxes((dmiddle + dresid_norm).reshape(group_len, row_count, width), 0, 1)
    query_sum, key_sum, value_sum, output_sum, router_sum, attn_gain_sum, moe_gain_sum = lax.psum(
        (
            query_part_grad,
            key_part_grad,
            value_part_grad,
            output_part,
            router_part,
            attn_gain_part,
            moe_gain_part,
        ),
        ("dp", "expert"),
    )
    return (
        mixed,
        grad_tokens,
        attn_gain_sum,
        query_sum,
        key_sum,
        value_sum,
        output_sum,
        moe_gain_sum,
        router_sum,
        grad_gate,
        grad_up,
        grad_down,
    )


def expert_gather(x_rows, g_rows, mask_rows, slot_rows, router_rows, first, x_scr, g_scr, gate_scr, table_scr, groups):
    held = x_scr.shape[0]
    for g in range(groups):
        rows = x_rows(g)
        logits = lax.dot_general(
            router_rows, rows, (((1,), (1,)), ((), ())), preferred_element_type=jnp.float32
        )
        shown = mask_rows(g) > 0
        raised = jnp.where(
            shown,
            jnp.exp(logits - jnp.max(jnp.where(shown, logits, NEG_FILL), axis=0, keepdims=True)),
            0.0,
        )
        gates = raised / jnp.sum(raised, axis=0, keepdims=True)
        slots = slot_rows(g)
        expert = lax.broadcasted_iota(jnp.int32, gates.shape, 0)
        place = lax.broadcasted_iota(jnp.int32, (MOST, rows.shape[0]), 0)
        tables = []
        for e in range(held):
            gate_row = jnp.sum(jnp.where(expert == first + e, gates, 0.0), axis=0, keepdims=True)
            chosen = place == slots[e : e + 1, :]
            gate_scr[e, g * MOST : (g + 1) * MOST, :] = jnp.sum(
                jnp.where(chosen, gate_row, 0.0), axis=1, keepdims=True
            )
            tables.append(jnp.where(chosen, 1.0, 0.0))
        table = jnp.concatenate(tables, axis=0).astype(jnp.bfloat16)
        if table_scr is not None:
            table_scr[g] = table
        for scr, part in ((x_scr, rows), (g_scr, g_rows(g))):
            picked = jnp.dot(table, part, preferred_element_type=jnp.float32).astype(jnp.bfloat16)
            for e in range(held):
                scr[e, g * MOST : (g + 1) * MOST, :] = picked[e * MOST : (e + 1) * MOST, :]


def nt(left, right):
    return lax.dot_general(
        left, right, (((1,), (1,)), ((), ())), preferred_element_type=jnp.float32
    )


def tn(left, right):
    return lax.dot_general(
        left, right, (((0,), (0,)), ((), ())), preferred_element_type=jnp.float32
    )


def expert_body(x_slots, g_slots, gate_col, gate_w, up_w, down_w):
    gate_pre = jnp.dot(x_slots, gate_w, preferred_element_type=jnp.float32)
    up_pre = jnp.dot(x_slots, up_w, preferred_element_type=jnp.float32)
    sigma = jax.nn.sigmoid(gate_pre)
    activated = gate_pre * sigma
    hidden = (activated * up_pre).astype(jnp.bfloat16)
    dexpert = (gate_col * (RESIDUAL_SCALE * g_slots.astype(jnp.float32))).astype(jnp.bfloat16)
    dhidden = nt(dexpert, down_w)
    dgate_pre = (dhidden * up_pre * sigma * (1.0 + gate_pre * (1.0 - sigma))).astype(jnp.bfloat16)
    dup_pre = (dhidden * activated).astype(jnp.bfloat16)
    return hidden, dexpert, dgate_pre, dup_pre


def near_experts(me, x_near, x_twin, g_near, g_twin, mask_row, slot_row, router_t, w_gate, w_up, w_down):
    chips, group_len, width = x_near.shape
    held, _, inner = w_gate.shape
    groups = 2 * chips
    extra = 16
    lanes = 128

    def kernel(me_ref, xn, xt, gn, gt, mr, sr, rt, wg, wu, wd, near_out, twin_out, y_near, y_twin,
               x_scr, g_scr, gate_scr, table_scr, y_scr, d_scr, dg_scr):
        e = pl.program_id(0)
        my = me_ref[0]

        @pl.when(e == 0)
        def _():
            expert_gather(
                lambda g: (xn if g < chips else xt)[g % chips],
                lambda g: (gn if g < chips else gt)[g % chips],
                lambda g: mr[g],
                lambda g: sr[g],
                rt[...],
                my * held,
                x_scr, g_scr, gate_scr, table_scr, groups,
            )

        g_slots = g_scr[e]
        hidden, _, dgate_pre, dup_pre = expert_body(
            x_scr[e], g_slots, gate_scr[e], wg[0], wu[0], wd[0]
        )
        out = jnp.dot(hidden, wd[0], preferred_element_type=jnp.float32).astype(jnp.bfloat16)
        out_wide = out.astype(jnp.float32)
        dgate = jnp.sum(
            RESIDUAL_SCALE * g_slots.astype(jnp.float32) * out_wide, axis=1, keepdims=True
        )
        weighted = (gate_scr[e] * out_wide).astype(jnp.bfloat16)
        dinputs = (nt(dgate_pre, wg[0]) + nt(dup_pre, wu[0])).astype(jnp.bfloat16)
        spot = pl.ds(pl.multiple_of(e * MOST, 16), MOST)
        for g in range(groups):
            part = slice(g * MOST, (g + 1) * MOST)
            y_scr[g, spot, :] = weighted[part]
            d_scr[g, spot, :] = dinputs[part]
            taken = table_scr[g, spot, :].astype(jnp.float32)
            dg_scr[g, e] = jnp.sum(taken * dgate[part], axis=0, keepdims=True)

        @pl.when(e == held - 1)
        def _():
            block = lax.broadcasted_iota(jnp.int32, (held, width), 1) // lanes
            for g in range(groups):
                d_out, y_out = (near_out, y_near) if g < chips else (twin_out, y_twin)
                table = table_scr[g]
                y_out[g % chips] = tn(table, y_scr[g]).astype(jnp.bfloat16)
                d_out[g % chips, :group_len, :] = tn(table, d_scr[g]).astype(jnp.bfloat16)
                rows = jnp.concatenate([dg_scr[g, i] for i in range(held)], axis=0)
                spread = jnp.where(block == my, jnp.concatenate([rows] * groups, axis=1), 0.0)
                high = spread.astype(jnp.bfloat16).astype(jnp.float32)
                tail = jnp.concatenate(
                    [high, spread - high, jnp.zeros((extra - 2 * held, width), jnp.float32)], axis=0
                )
                d_out[g % chips, group_len:, :] = tail.astype(jnp.bfloat16)

    whole = lambda *shape: pl.BlockSpec(shape, lambda e, m: (0,) * len(shape))
    weight = lambda *shape: pl.BlockSpec((1,) + shape, lambda e, m: (e, 0, 0))
    back = jax.ShapeDtypeStruct((chips, group_len + extra, width), jnp.bfloat16)
    forth = jax.ShapeDtypeStruct((chips, group_len, width), jnp.bfloat16)
    slots = groups * MOST
    return pl.pallas_call(
        kernel,
        grid_spec=pltpu.PrefetchScalarGridSpec(
            num_scalar_prefetch=1,
            grid=(held,),
            in_specs=[
                whole(chips, group_len, width),
                whole(chips, group_len, width),
                whole(chips, group_len, width),
                whole(chips, group_len, width),
                whole(groups, EXPERTS, group_len),
                whole(groups, held, group_len),
                whole(EXPERTS, width),
                weight(width, inner),
                weight(width, inner),
                weight(inner, width),
            ],
            out_specs=[
                whole(chips, group_len + extra, width),
                whole(chips, group_len + extra, width),
                whole(chips, group_len, width),
                whole(chips, group_len, width),
            ],
            scratch_shapes=[
                pltpu.VMEM((held, slots, width), jnp.bfloat16),
                pltpu.VMEM((held, slots, width), jnp.bfloat16),
                pltpu.VMEM((held, slots, 1), jnp.float32),
                pltpu.VMEM((groups, held * MOST, group_len), jnp.bfloat16),
                pltpu.VMEM((groups, held * MOST, width), jnp.bfloat16),
                pltpu.VMEM((groups, held * MOST, width), jnp.bfloat16),
                pltpu.VMEM((groups, held, 1, group_len), jnp.float32),
            ],
        ),
        out_shape=[back, back, forth, forth],
        compiler_params=pltpu.CompilerParams(
            dimension_semantics=("arbitrary",), vmem_limit_bytes=58 * 2**20
        ),
        cost_estimate=pl.CostEstimate(
            flops=2 * 7 * held * slots * width * inner, transcendentals=0, bytes_accessed=2**24
        ),
        name="near_experts",
    )(me.reshape(1), x_near, x_twin, g_near, g_twin, mask_row, slot_row, router_t, w_gate, w_up, w_down)


def expert_weight_grads(ids, sums, x_near, x_twin, g_near, g_twin, mask_all, slot_all, router_t, weights, copies):
    unused, chips, group_len, width = x_near.shape
    held, unused, inner = weights[0].shape
    groups = 2 * chips
    slots = groups * MOST
    wide, narrow = width // copies, inner // copies

    def kernel(ids_ref, xn, xt, gn, gt, mr, sr, rt, wg, wu, wd, *refs):
        gate_out, up_out, down_out, x_scr, g_scr, gate_scr = refs[-6:]
        befores = refs[:-6] if sums is not None else (None, None, None)
        e = pl.program_id(0)
        mine, slab = ids_ref[0], ids_ref[1]

        @pl.when(e == 0)
        def _():
            expert_gather(
                lambda g: (xn if g < chips else xt)[0, g % chips],
                lambda g: (gn if g < chips else gt)[0, g % chips],
                lambda g: mr[g],
                lambda g: sr[g],
                rt[...], mine * held, x_scr, g_scr, gate_scr, None, groups,
            )

        x_slots = x_scr[e]
        hidden, dexpert, dgate_pre, dup_pre = expert_body(
            x_slots, g_scr[e], gate_scr[e], wg[0], wu[0], wd[0]
        )
        x_part, h_part = x_slots[:, :wide], hidden[:, :narrow]
        for k in range(1, copies):
            x_part = jnp.where(slab == k, x_slots[:, k * wide : (k + 1) * wide], x_part)
            h_part = jnp.where(slab == k, hidden[:, k * narrow : (k + 1) * narrow], h_part)
        for out, before, left, right in zip(
            (gate_out, up_out, down_out),
            befores,
            (x_part, x_part, h_part),
            (dgate_pre, dup_pre, dexpert),
        ):
            part = tn(left, right)
            out[0] = part if before is None else before[0] + part

    some = lambda *shape: pl.BlockSpec((groups,) + shape, lambda e, m: (m[2], 0, 0))
    rows = pl.BlockSpec((1, chips, group_len, width), lambda e, m: (m[2], 0, 0, 0))
    weight = lambda *shape: pl.BlockSpec((1,) + shape, lambda e, m: (e, 0, 0))
    whole = lambda *shape: pl.BlockSpec(shape, lambda e, m: (0,) * len(shape))
    outs = [(held, wide, inner), (held, wide, inner), (held, narrow, width)]
    return pl.pallas_call(
        kernel,
        grid_spec=pltpu.PrefetchScalarGridSpec(
            num_scalar_prefetch=1,
            grid=(held,),
            in_specs=[
                rows,
                rows,
                rows,
                rows,
                some(EXPERTS, group_len),
                some(held, group_len),
                whole(EXPERTS, width),
                weight(width, inner),
                weight(width, inner),
                weight(inner, width),
            ]
            + ([weight(*shape[1:]) for shape in outs] if sums is not None else []),
            out_specs=[weight(*shape[1:]) for shape in outs],
            scratch_shapes=[
                pltpu.VMEM((held, slots, width), jnp.bfloat16),
                pltpu.VMEM((held, slots, width), jnp.bfloat16),
                pltpu.VMEM((held, slots, 1), jnp.float32),
            ],
        ),
        out_shape=[jax.ShapeDtypeStruct(shape, jnp.float32) for shape in outs],
        compiler_params=pltpu.CompilerParams(
            dimension_semantics=("arbitrary",), vmem_limit_bytes=58 * 2**20
        ),
        cost_estimate=pl.CostEstimate(
            flops=2 * 4 * held * slots * width * inner, transcendentals=0, bytes_accessed=2**24
        ),
        input_output_aliases={11 + i: i for i in range(3)} if sums is not None else {},
        name="expert_weight_grads",
    )(ids, x_near, x_twin, g_near, g_twin, mask_all, slot_all, router_t, *weights, *(sums or ()))


def assemble_heads(core, near, twin, width, query_cols):
    chips = near.shape[0]
    devices = 2 * chips
    rows = 128
    pair = 2 * HEAD_DIM

    def kernel(core_ref, near_ref, twin_ref, query_ref, key_ref, value_ref):
        blocks = []
        for j in range(devices):
            mine = near_ref[j // 2].astype(jnp.float32)
            other = twin_ref[j // 2].astype(jnp.float32)
            blocks.append(jnp.where(core_ref[0] == j % 2, mine, other))
            query_ref[:, j * query_cols : (j + 1) * query_cols] = blocks[j][:, :query_cols]
        for c in range(chips):
            for ref, start in ((key_ref, query_cols), (value_ref, query_cols + HEAD_DIM)):
                ref[:, c * pair : (c + 1) * pair] = jnp.concatenate(
                    [blocks[2 * c + k][:, start : start + HEAD_DIM] for k in range(2)], axis=1
                )

    block = pl.BlockSpec((chips, rows, query_cols + pair), lambda r, m: (0, r, 0))
    shapes = [(width, devices * query_cols), (width, devices * HEAD_DIM), (width, devices * HEAD_DIM)]
    return pl.pallas_call(
        kernel,
        grid_spec=pltpu.PrefetchScalarGridSpec(
            num_scalar_prefetch=1,
            grid=(width // rows,),
            in_specs=[block, block],
            out_specs=[pl.BlockSpec((rows, s[1]), lambda r, m: (r, 0)) for s in shapes],
        ),
        out_shape=[jax.ShapeDtypeStruct(s, jnp.float32) for s in shapes],
        name="assemble_heads",
    )(core.reshape(1), near, twin)


def assemble_rows(core, near, twin, start, rows, width):
    chips, _, span = near.shape
    pieces = width // span

    def kernel(core_ref, near_ref, twin_ref, output_ref):
        mine = core_ref[0] == pl.program_id(0) % 2
        block = jnp.where(mine, near_ref[0].astype(jnp.float32), twin_ref[0].astype(jnp.float32))
        for z in range(pieces):
            output_ref[:, z * span : (z + 1) * span] = block[z * rows : (z + 1) * rows]

    block = pl.BlockSpec(
        (1, rows * pieces, span), lambda r, m: (r // 2, start // (rows * pieces), 0)
    )
    return pl.pallas_call(
        kernel,
        grid_spec=pltpu.PrefetchScalarGridSpec(
            num_scalar_prefetch=1,
            grid=(2 * chips,),
            in_specs=[block, block],
            out_specs=pl.BlockSpec((rows, width), lambda r, m: (r, 0)),
        ),
        out_shape=jax.ShapeDtypeStruct((2 * chips * rows, width), jnp.float32),
        name="assemble_rows",
    )(core.reshape(1), near, twin)


def turn(values, sign):
    lanes = lax.broadcasted_iota(jnp.int32, values.shape, 1)
    half = HEAD_DIM // 2
    ahead = pltpu.roll(values, values.shape[1] - half, 1)
    behind = pltpu.roll(values, half, 1)
    return jnp.where(lanes % HEAD_DIM < half, -sign * ahead, sign * behind)


def column_of(row):
    size = row.shape[1]
    diagonal = lax.broadcasted_iota(jnp.int32, (size, size), 0) == lax.broadcasted_iota(
        jnp.int32, (size, size), 1
    )
    return jnp.sum(jnp.where(diagonal, row, 0), axis=1, keepdims=True)


def attend_heads(me, near_pay, twin_pay, gain, head_weights, segs, index):
    chips = near_pay.shape[0]
    blocks, group_len = segs.shape
    width, head_cols = head_weights.shape
    length = blocks * group_len
    pair = 2 * HEAD_DIM

    def device(me, g):
        return 2 * (g % chips) + ((me & 1) ^ (g // chips))

    def kernel(me_ref, near_ref, twin_ref, gain_ref, w_ref, freq_ref, seg_ref, seg_rows, index_ref,
               index_rows, normed_out, qkv_out, cos_out, sin_out, attn_out, attended_out, lse_out,
               k_scr, v_scr, pos_scr):
        step = pl.program_id(0)

        @pl.when(step == 0)
        def _():
            numbers = seg_rows[...]
            start = jnp.zeros(numbers.shape, jnp.float32)
            for s in range(SEGMENTS - 1):
                found = jnp.where(numbers == s, 1.0, 0.0)
                count = jnp.sum(jnp.sum(found, axis=1, keepdims=True), axis=0, keepdims=True)
                start = start + jnp.where(numbers > s, count, 0.0)
            pos_scr[...] = index_rows[...].astype(jnp.float32) - start

        def project(pay_ref, half_row):
            rows = pay_ref[:, :group_len, :].reshape(chips * group_len, width).astype(jnp.float32)
            inverse = lax.rsqrt(jnp.mean(rows * rows, axis=1, keepdims=True) + NORM_EPS)
            normed = (rows * inverse * gain_ref[...]).astype(jnp.bfloat16)
            lin_all = jnp.dot(normed, w_ref[...], preferred_element_type=jnp.float32)
            for c in range(chips):
                g = half_row * chips + c
                here = slice(g * group_len, (g + 1) * group_len)
                normed_out[device(me_ref[0], g)] = normed[c * group_len : (c + 1) * group_len]
                lin = lin_all[c * group_len : (c + 1) * group_len]
                angles = freq_ref[...] * pos_scr[g : g + 1, :]
                cosine = jnp.transpose(jnp.concatenate([jnp.cos(angles)] * 4, axis=0))
                sine = jnp.transpose(jnp.concatenate([jnp.sin(angles)] * 4, axis=0))
                cos_out[here, :] = cosine
                sin_out[here, :] = sine
                query, rest = lin[:, :pair], lin[:, pair:]
                query = query * cosine + turn(query, 1.0) * sine
                key = rest * cosine + turn(rest, 1.0) * sine
                lanes = lax.broadcasted_iota(jnp.int32, rest.shape, 1)
                both = jnp.where(lanes < HEAD_DIM, key, rest).astype(jnp.bfloat16)
                qkv_out[here, :pair] = query.astype(jnp.bfloat16)
                qkv_out[here, pair:] = both
                k_scr[here, :] = both[:, :HEAD_DIM]
                v_scr[here, :] = both[:, HEAD_DIM:]

        @pl.when(step == 0)
        def _():
            project(near_ref, 0)

        @pl.when(step == 1)
        def _():
            project(twin_ref, 1)

        @pl.when(step >= 2)
        def _():
            g = step - 2
            here = pl.ds(pl.multiple_of(g * group_len, group_len), group_len)
            place = device(me_ref[0], g) * group_len + lax.broadcasted_iota(
                jnp.int32, (group_len, 1), 0
            )
            allowed = (seg_ref[...] == column_of(seg_rows[pl.ds(g, 1), :])) & (
                index_ref[...] <= place
            )
            outs, stats = [], []
            for h in range(pair // HEAD_DIM):
                query = qkv_out[here, h * HEAD_DIM : (h + 1) * HEAD_DIM] * jnp.bfloat16(ATTN_SCALE)
                scores = jnp.where(allowed, nt(query, k_scr[...]), NEG_FILL)
                top = jnp.max(scores, axis=1, keepdims=True)
                raised = jnp.exp(scores - top)
                total = jnp.sum(raised, axis=1, keepdims=True)
                probs = (raised * (1.0 / total)).astype(jnp.bfloat16)
                outs.append(jnp.dot(probs, v_scr[...], preferred_element_type=jnp.float32))
                stats.append(jnp.broadcast_to(top + jnp.log(total), (group_len, HEAD_DIM)))
            attended = jnp.concatenate(outs, axis=1)
            attended_out[...] = attended
            attn_out[0] = attended.astype(jnp.bfloat16)
            lse_out[...] = jnp.concatenate(stats, axis=1)

    half = HEAD_DIM // 2
    freqs = ROPE_BASE ** (-(jnp.arange(half, dtype=jnp.float32) * 2.0) / HEAD_DIM)
    whole = lambda *shape: pl.BlockSpec(shape, lambda i, m: (0,) * len(shape))
    second = lambda i: jnp.maximum(i - 2, 0)
    f32, bf16 = jnp.float32, jnp.bfloat16
    return pl.pallas_call(
        kernel,
        grid_spec=pltpu.PrefetchScalarGridSpec(
            num_scalar_prefetch=1,
            grid=(2 + blocks,),
            in_specs=[
                whole(*near_pay.shape),
                whole(*twin_pay.shape),
                whole(1, width),
                whole(width, head_cols),
                whole(half, 1),
                whole(1, length),
                whole(blocks, group_len),
                whole(1, length),
                whole(blocks, group_len),
            ],
            out_specs=[
                whole(blocks, group_len, width),
                whole(length, head_cols),
                whole(length, pair),
                whole(length, pair),
                pl.BlockSpec((1, group_len, pair), lambda i, m: (device(m[0], second(i)), 0, 0)),
                pl.BlockSpec((group_len, pair), lambda i, m: (second(i), 0)),
                pl.BlockSpec((group_len, pair), lambda i, m: (second(i), 0)),
            ],
            scratch_shapes=[
                pltpu.VMEM((length, HEAD_DIM), bf16),
                pltpu.VMEM((length, HEAD_DIM), bf16),
                pltpu.VMEM((blocks, group_len), f32),
            ],
        ),
        out_shape=[
            jax.ShapeDtypeStruct((blocks, group_len, width), bf16),
            jax.ShapeDtypeStruct((length, head_cols), bf16),
            jax.ShapeDtypeStruct((length, pair), f32),
            jax.ShapeDtypeStruct((length, pair), f32),
            jax.ShapeDtypeStruct((blocks, group_len, pair), bf16),
            jax.ShapeDtypeStruct((length, pair), f32),
            jax.ShapeDtypeStruct((length, pair), f32),
        ],
        cost_estimate=pl.CostEstimate(
            flops=2 * length * (width * head_cols + 4 * length * HEAD_DIM) * 2,
            transcendentals=2 * length * length,
            bytes_accessed=2**23,
        ),
        name="attend_heads",
    )(
        me.reshape(1), near_pay, twin_pay, gain[None], head_weights, freqs[:, None],
        segs.reshape(1, length), segs, index.reshape(1, length), index,
    )


def attend_back(me, near_db, twin_db, out_heads, qkv, cosine, sine, attended, lse, segs, index, copies):
    chips = near_db.shape[0]
    span = out_heads.shape[1] // copies
    blocks, group_len = segs.shape
    length, head_cols = qkv.shape
    width = out_heads.shape[1]
    pair = 2 * HEAD_DIM

    def device(me, g):
        return 2 * (g % chips) + ((me & 1) ^ (g // chips))

    def kernel(me_ref, near_ref, twin_ref, w_ref, qkv_ref, cos_ref, sin_ref, att_ref, lse_ref,
               seg_ref, seg_rows, index_ref, dlin_out, part_out, k_scr, v_scr, dk_scr, dv_scr, part_scr):
        g = pl.program_id(0)

        @pl.when(g == 0)
        def _():
            k_scr[...] = qkv_ref[:, pair : pair + HEAD_DIM]
            v_scr[...] = qkv_ref[:, pair + HEAD_DIM :]
            dk_scr[...] = jnp.zeros(dk_scr.shape, jnp.float32)
            dv_scr[...] = jnp.zeros(dv_scr.shape, jnp.float32)
            part_scr[...] = jnp.zeros(part_scr.shape, jnp.float32)

        def block(pay_ref):
            here = pl.ds(pl.multiple_of(g * group_len, group_len), group_len)
            mine = device(me_ref[0], g)
            place = mine * group_len + lax.broadcasted_iota(jnp.int32, (group_len, 1), 0)
            allowed = (seg_ref[...] == column_of(seg_rows[pl.ds(g, 1), :])) & (
                index_ref[...] <= place
            )
            rows = pay_ref[g % chips, :group_len, :]
            dattn = nt(rows, w_ref[...]).astype(jnp.bfloat16)
            attended = att_ref[here, :]
            wide = dattn.astype(jnp.float32) * attended
            part_scr[...] += tn(attended.astype(jnp.bfloat16), rows)
            outs = []
            for h in range(pair // HEAD_DIM):
                part = slice(h * HEAD_DIM, (h + 1) * HEAD_DIM)
                query = qkv_ref[here, part]
                scaled = query * jnp.bfloat16(ATTN_SCALE)
                scores = nt(scaled, k_scr[...])
                level = lse_ref[here, h * HEAD_DIM : h * HEAD_DIM + 1]
                probs = jnp.where(allowed, jnp.exp(scores - level), 0.0)
                delta = jnp.sum(wide[:, part], axis=1, keepdims=True)
                dscores = (probs * (nt(dattn[:, part], v_scr[...]) - delta)).astype(jnp.bfloat16)
                outs.append(jnp.dot(dscores, k_scr[...], preferred_element_type=jnp.float32))
                dk_scr[...] += tn(dscores, scaled)
                dv_scr[...] += tn(probs.astype(jnp.bfloat16), dattn[:, part])
            dquery = jnp.concatenate(outs, axis=1) * ATTN_SCALE
            dlin_out[mine, :, :pair] = (
                dquery * cos_ref[here, :] + turn(dquery * sin_ref[here, :], -1.0)
            ).astype(jnp.bfloat16)

        @pl.when(g < chips)
        def _():
            block(near_ref)

        @pl.when(g >= chips)
        def _():
            block(twin_ref)

        @pl.when(g == blocks - 1)
        def _():
            for z in range(copies):
                part_out[z] = part_scr[:, z * span : (z + 1) * span].astype(jnp.bfloat16)
            for b in range(blocks):
                here = slice(b * group_len, (b + 1) * group_len)
                both = jnp.concatenate([dk_scr[here, :], dv_scr[here, :]], axis=1)
                lanes = lax.broadcasted_iota(jnp.int32, both.shape, 1)
                turned = both * cos_ref[here, :] + turn(both * sin_ref[here, :], -1.0)
                dlin_out[device(me_ref[0], b), :, pair:] = jnp.where(
                    lanes < HEAD_DIM, turned, both
                ).astype(jnp.bfloat16)

    whole = lambda *shape: pl.BlockSpec(shape, lambda i, m: (0,) * len(shape))
    return pl.pallas_call(
        kernel,
        grid_spec=pltpu.PrefetchScalarGridSpec(
            num_scalar_prefetch=1,
            grid=(blocks,),
            in_specs=[
                whole(*near_db.shape),
                whole(*twin_db.shape),
                whole(*out_heads.shape),
                whole(length, head_cols),
                whole(length, pair),
                whole(length, pair),
                whole(length, pair),
                whole(length, pair),
                whole(1, length),
                whole(blocks, group_len),
                whole(1, length),
            ],
            out_specs=[whole(blocks, group_len, head_cols), whole(copies, pair, span)],
            scratch_shapes=[
                pltpu.VMEM((length, HEAD_DIM), jnp.bfloat16),
                pltpu.VMEM((length, HEAD_DIM), jnp.bfloat16),
                pltpu.VMEM((length, HEAD_DIM), jnp.float32),
                pltpu.VMEM((length, HEAD_DIM), jnp.float32),
                pltpu.VMEM((pair, width), jnp.float32),
            ],
        ),
        out_shape=[
            jax.ShapeDtypeStruct((blocks, group_len, head_cols), jnp.bfloat16),
            jax.ShapeDtypeStruct((copies, pair, span), jnp.bfloat16),
        ],
        cost_estimate=pl.CostEstimate(
            flops=2 * length * (width * pair + 10 * length * HEAD_DIM),
            transcendentals=2 * length * length,
            bytes_accessed=2**23,
        ),
        name="attend_back",
    )(
        me.reshape(1), near_db, twin_db, out_heads, qkv, cosine, sine, attended, lse,
        segs.reshape(1, length), segs, index.reshape(1, length),
    )


def swap_cores(block, devices):
    return lax.ppermute(block, "expert", [(i, i ^ 1) for i in range(devices)])


def across_chips(blocks, devices):
    groups = [[2 * c + core for c in range(devices // 2)] for core in range(2)]
    return lax.all_to_all(blocks, "expert", 0, 0, axis_index_groups=groups, tiled=True)


def permute(block, shift, axis, count):
    return lax.ppermute(block, axis, [(i, i ^ shift) for i in range(count)])


def spread_row(block, devices):
    near = across_chips(jnp.broadcast_to(block[None], (devices // 2,) + block.shape), devices)
    return near, swap_cores(near, devices)


def merge_cores(near, twin, devices):
    partner = swap_cores(twin, devices)
    return (near.astype(jnp.float32) + partner.astype(jnp.float32)).astype(jnp.bfloat16)


def permute_sum(parts, mine, step, axis, count):
    total = lax.dynamic_index_in_dim(parts, mine, 0, False).astype(jnp.float32)
    for s in range(1, parts.shape[0]):
        part = lax.dynamic_index_in_dim(parts, mine ^ s, 0, False)
        total = total + permute(part, s * step, axis, count).astype(jnp.float32)
    return total


def in_order(near, twin, core):
    even = jnp.where(core == 0, near, twin)
    odd = jnp.where(core == 0, twin, near)
    return jnp.stack([even, odd], axis=1).reshape((2 * near.shape[0],) + near.shape[1:])


def with_tail(rows, tail):
    height, span = tail.shape
    return jnp.concatenate(
        [rows, jnp.pad(tail, ((0, TAIL - height), (0, rows.shape[1] - span)))], axis=0
    )


def pack_gains(gains, span):
    high = gains.astype(jnp.bfloat16)
    lower = (gains - high.astype(jnp.float32)).astype(jnp.bfloat16)
    return jnp.concatenate([high, lower], axis=0).reshape(-1, span)


def unpack_gains(packed, width):
    parts = packed.reshape(packed.shape[0], 2, -1, width).astype(jnp.float32)
    return parts[:, 0] + parts[:, 1]


def exchange(blocks, axis):
    return lax.all_to_all(blocks, axis, 0, 0, tiled=True)


def broadcast(block, count):
    return jnp.broadcast_to(block[None], (count,) + block.shape)


def masked_gates(logits, mask):
    shown = jnp.where(mask, logits, NEG_FILL)
    weight = jnp.where(mask, jnp.exp(shown - jnp.max(shown, axis=-1, keepdims=True)), 0.0)
    return weight / jnp.sum(weight, axis=-1, keepdims=True)


def slot_tables(mask, first, held):
    group_len = mask.shape[2]
    local = lax.dynamic_slice_in_dim(mask, first, held, 1)
    steps = jnp.arange(group_len, dtype=jnp.int32)
    earlier = (steps[:, None] < steps[None, :]).astype(jnp.bfloat16)
    rank = jnp.einsum("gem,mn->gen", local, earlier, preferred_element_type=jnp.float32)
    return mask, jnp.where(local > 0, rank, -1.0).astype(jnp.int32)


def per_device_heads(
    tokens,
    attn_gain,
    w_query,
    w_key,
    w_value,
    w_output,
    moe_gain,
    w_router,
    w_gate,
    w_up,
    w_down,
    routes,
    segment_ids,
    out_grad,
):
    unused, group_len, width = tokens.shape
    devices, copies = lax.axis_size("expert"), lax.axis_size("dp")
    me, me_z = lax.axis_index("expert"), lax.axis_index("dp")
    core = me & 1
    chips = devices // 2
    length = group_len * devices
    repeats = HEADS // KV_HEADS
    query_cols = repeats * HEAD_DIM
    held = EXPERTS // devices
    order = jnp.stack([2 * c + (core ^ k) for k in range(2) for c in range(chips)])
    bf16 = jnp.bfloat16

    own = tokens[0]
    near_pay, twin_pay = spread_row(with_tail(own, segment_ids.astype(bf16)), devices)
    seg_rows = jnp.concatenate(
        [near_pay[:, group_len, :group_len], twin_pay[:, group_len, :group_len]], axis=0
    ).astype(jnp.int32)
    row_index = order[:, None] * group_len + jnp.arange(group_len, dtype=jnp.int32)

    mask_own = jnp.any(
        routes[0][:, :, None] == jnp.arange(EXPERTS, dtype=jnp.int32)[None, None, :], axis=1
    )
    tail_rows = EXPERTS * group_len // width
    mask_tail = jnp.swapaxes(mask_own.astype(bf16), 0, 1).reshape(tail_rows, width)
    grad_pay, near_pay = lax.optimization_barrier((with_tail(out_grad[0], mask_tail), near_pay))
    g_near, g_twin = spread_row(grad_pay, devices)

    def tables(near, twin, axis):
        tails = [side[..., group_len : group_len + tail_rows, :] for side in (near, twin)]
        return slot_tables(
            jnp.concatenate(tails, axis=axis).reshape(-1, EXPERTS, group_len), me * held, held
        )

    mask_row, slot_row = tables(g_near, g_twin, 0)
    g_near_all = lax.all_gather(g_near, "dp", axis=0)
    router_t = jnp.swapaxes(w_router, 0, 1)

    head_weights = jnp.concatenate(
        [
            lax.dynamic_slice_in_dim(w_query, me * query_cols, query_cols, 1),
            lax.dynamic_slice_in_dim(w_key, me * HEAD_DIM, HEAD_DIM, 1),
            lax.dynamic_slice_in_dim(w_value, me * HEAD_DIM, HEAD_DIM, 1),
        ],
        axis=1,
    )
    normed_row, qkv, cosine, sine, attn_heads, attended, lse = attend_heads(
        me, near_pay, twin_pay, attn_gain, head_weights, seg_rows, row_index
    )
    attn_heads, g_near, g_twin = lax.optimization_barrier((attn_heads, g_near, g_twin))
    attn_rows = jnp.swapaxes(exchange(attn_heads, "expert"), 0, 1).reshape(
        group_len, devices * query_cols
    )

    branch = jnp.dot(attn_rows, w_output, preferred_element_type=jnp.float32)
    residual = own.astype(jnp.float32)
    middle = residual + RESIDUAL_SCALE * branch
    normed2, unit_moe, inv_moe = rms_forward(middle, moe_gain)
    moe_rows = normed2.astype(bf16)
    gates_own = masked_gates(
        jnp.dot(moe_rows, w_router, preferred_element_type=jnp.float32), mask_own
    )
    x_near, x_twin = spread_row(moe_rows, devices)
    x_near_all = lax.all_gather(x_near, "dp", axis=0)

    d_near, d_twin, y_near, y_twin = near_experts(
        me, x_near, x_twin, g_near, g_twin, mask_row, slot_row, router_t, w_gate, w_up, w_down
    )
    d_merged = merge_cores(d_near, d_twin, devices)
    weights = (w_gate, w_up, w_down)

    def expert_row(z, sums, x_rows, g_rows, masks, slots):
        ids = jnp.stack([me, me_z, jnp.int32(z)])
        return expert_weight_grads(
            ids, sums, *x_rows, *g_rows, masks, slots, router_t, weights, copies
        )

    crossed = across_chips(d_merged, devices)
    x_mine, g_mine, d_merged = lax.optimization_barrier(
        ((x_near[None], x_twin[None]), (g_near[None], g_twin[None]), d_merged)
    )
    sums = expert_row(0, None, x_mine, g_mine, mask_row, slot_row)
    crossed, sums = lax.optimization_barrier((crossed, sums))
    returned = jnp.sum(crossed.astype(jnp.float32), axis=0)

    parts = returned[group_len : group_len + held] + returned[group_len + held : group_len + 2 * held]
    dgates = jnp.transpose(parts.reshape(held, devices, group_len), (2, 1, 0)).reshape(
        group_len, EXPERTS
    )
    dpicked = gates_own * (dgates - jnp.sum(gates_own * dgates, axis=-1, keepdims=True))
    dlogits = jnp.where(mask_own, dpicked, 0.0).astype(bf16)
    dnormed2 = returned[:group_len] + jnp.einsum(
        "ne,de->nd", dlogits, w_router, preferred_element_type=jnp.float32
    )
    dmiddle_norm, moe_gain_part = rms_backward(dnormed2, unit_moe, inv_moe, moe_gain)
    dmiddle = out_grad[0].astype(jnp.float32) + dmiddle_norm
    dbranch = (RESIDUAL_SCALE * dmiddle).astype(bf16)
    branch_near, branch_twin = spread_row(
        with_tail(dbranch, jnp.swapaxes(dlogits, 0, 1).reshape(tail_rows, width)), devices
    )
    dlogits_row = jnp.concatenate([branch_near[:, group_len:], branch_twin[:, group_len:]], axis=0)
    dlogits_row = dlogits_row[:, :tail_rows].reshape(devices, EXPERTS, group_len)

    out_heads = lax.dynamic_slice_in_dim(w_output, me * query_cols, query_cols, 0)
    dlin, output_part = attend_back(
        me, branch_near, branch_twin, out_heads, qkv, cosine, sine, attended, lse, seg_rows,
        row_index, copies,
    )
    head_cols = query_cols + 2 * HEAD_DIM
    rows_per = width // devices
    router_cols = lax.dynamic_slice_in_dim(
        jnp.concatenate([x_near, x_twin], axis=0), me * rows_per, rows_per, 2
    )
    router_part = jnp.einsum(
        "bnd,ben->de", router_cols, dlogits_row, preferred_element_type=jnp.float32
    ).astype(bf16)
    router_part = router_part.reshape(copies, -1, head_cols)
    router_rows = router_part.shape[1]
    router_part = jnp.pad(router_part, ((0, 0), (0, TAIL - router_rows), (0, 0)))
    head_part = jnp.einsum(
        "nd,nh->dh",
        normed_row.reshape(length, width),
        dlin.reshape(length, head_cols),
        preferred_element_type=jnp.float32,
    ).astype(bf16)
    rows = width // copies
    shared_part = jnp.concatenate(
        [head_part.reshape(copies, rows, head_cols), output_part, router_part], axis=1
    )

    shared_sum = permute_sum(shared_part, me_z, 1, "dp", copies).astype(bf16)
    dlin_back = jnp.swapaxes(exchange(dlin, "expert"), 0, 1)

    def token_grad(start, count, weights):
        rows = dlin_back[:, :, start : start + count].reshape(group_len, devices * count)
        return jnp.einsum("nh,dh->nd", rows, weights, preferred_element_type=jnp.float32)

    dnormed = (
        token_grad(0, query_cols, w_query)
        + token_grad(query_cols, HEAD_DIM, w_key)
        + token_grad(query_cols + HEAD_DIM, HEAD_DIM, w_value)
    )
    unused, unit_attn, inv_attn = rms_forward(residual, attn_gain)
    dresid_norm, attn_gain_part = rms_backward(dnormed, unit_attn, inv_attn, attn_gain)
    grad_tokens = (dmiddle + dresid_norm)[None]
    gain_parts = pack_gains(jnp.stack([attn_gain_part, moe_gain_part]), head_cols)
    column = exchange(broadcast(jnp.concatenate([shared_sum, gain_parts], axis=0), copies), "dp")

    g_near_all, x_near_all, y_near, y_twin, gain_parts = lax.optimization_barrier(
        (g_near_all, x_near_all, y_near, y_twin, gain_parts)
    )
    g_rows = (g_near_all, swap_cores(g_near_all, devices))
    x_rows = (x_near_all, swap_cores(x_near_all, devices))
    masks, slots = tables(*g_rows, 1)
    y_merged = merge_cores(y_near, y_twin, devices)
    y_sum = permute_sum(y_merged, me >> 1, 2, "expert", devices)

    def far_row(step, sums):
        return expert_row((me_z + step) % copies, sums, x_rows, g_rows, masks, slots)

    sums = far_row(1, sums)
    column, sums = lax.optimization_barrier((column, sums))
    router_start = rows + query_cols
    gain_start = router_start + TAIL
    gain_parts = pack_gains(jnp.sum(unpack_gains(column[:, gain_start:], width), axis=0), head_cols)
    column = jnp.concatenate(
        [
            column[:, :rows].reshape(-1, head_cols),
            column[:, rows:router_start].reshape(-1, head_cols),
            column[:, router_start : router_start + router_rows].reshape(-1, head_cols),
            gain_parts,
        ],
        axis=0,
    )
    head_near = across_chips(broadcast(column, chips), devices)
    for step in range(2, copies):
        sums = far_row(step, sums)
    head_near, sums = lax.optimization_barrier((head_near, sums))
    head_twin = swap_cores(head_near, devices)
    mixed = (middle + RESIDUAL_SCALE * y_sum).astype(bf16)[None]
    grad_gate, grad_up, grad_down = sums
    grad_query, grad_key, grad_value = assemble_heads(core, head_near, head_twin, width, query_cols)
    grad_output = assemble_rows(core, head_near, head_twin, width, query_cols, width)
    router_start = width + query_cols * copies
    gain_start = router_start + router_rows * copies
    grad_router = in_order(
        head_near[:, router_start:gain_start], head_twin[:, router_start:gain_start], core
    ).reshape(width, EXPERTS).astype(jnp.float32)
    gain_sums = jnp.sum(unpack_gains(head_near[:, gain_start:], width), axis=0) + jnp.sum(
        unpack_gains(head_twin[:, gain_start:], width), axis=0
    )
    return (
        mixed,
        grad_tokens,
        gain_sums[0],
        grad_query,
        grad_key,
        grad_value,
        grad_output,
        gain_sums[1],
        grad_router,
        grad_gate,
        grad_up,
        grad_down,
    )


def solution(mesh):
    placed = (
        P("dp", "expert", None),
        P(),
        P(),
        P(),
        P(),
        P(),
        P(),
        P(),
        P("expert", None, None),
        P("expert", None, None),
        P("expert", None, None),
        P("dp", "expert", None),
        P("dp", "expert"),
        P("dp", "expert", None),
    )
    by_heads = mesh.shape["expert"] == KV_HEADS
    return jax.shard_map(
        per_device_heads if by_heads else per_device_general,
        mesh=mesh,
        in_specs=placed,
        out_specs=(
            P("dp", "expert", None),
            P("dp", "expert", None),
            P(),
            P(),
            P(),
            P(),
            P(),
            P(),
            P(),
            P("expert", "dp", None),
            P("expert", "dp", None),
            P("expert", "dp", None),
        ),
        check_vma=False,
    )
```

```python
import jax
import jax.numpy as jnp
from jax import lax
from jax.experimental import pallas as pl
from jax.experimental.pallas import tpu as pltpu
from jax.sharding import PartitionSpec as P


HEADS = 16
KV_HEADS = 8
HEAD_DIM = 64
EXPERTS = 32
TOP = 8
MOST = 48


ATTN_SCALE = 0.015625
RESIDUAL_SCALE = 0.22
NORM_EPS = 1e-06
ROPE_BASE = 10000.0
NEG_FILL = -1e30
TAIL = 16
SEGMENTS = 8


def rms_forward(values, gain_vec):
    inverse = lax.rsqrt(jnp.mean(values * values, axis=-1, keepdims=True) + NORM_EPS)
    unit_rows = values * inverse
    return (unit_rows * gain_vec, unit_rows, inverse)


def rms_backward(grad_rows, unit_rows, inverse, gain_vec):
    scaled = grad_rows * gain_vec
    grad_gain = jnp.sum(grad_rows * unit_rows, axis=0)
    grad_in = inverse * (scaled - unit_rows * jnp.mean(scaled * unit_rows, axis=-1, keepdims=True))
    return (grad_in, grad_gain)


def rope_tables(positions):
    half = HEAD_DIM // 2
    freqs = ROPE_BASE ** (-(jnp.arange(half, dtype=jnp.float32) * 2.0) / HEAD_DIM)
    angles = positions.astype(jnp.float32)[..., None] * freqs
    cosine = jnp.concatenate([jnp.cos(angles), jnp.cos(angles)], axis=-1)
    sine = jnp.concatenate([jnp.sin(angles), jnp.sin(angles)], axis=-1)
    return (cosine, sine)


def rotate(vectors, cosine, sine):
    half = vectors.shape[-1] // 2
    turned = jnp.concatenate([-vectors[..., half:], vectors[..., :half]], axis=-1)
    return vectors * cosine + turned * sine


def unrotate(grads, cosine, sine):
    half = grads.shape[-1] // 2
    scaled = grads * sine
    turned = jnp.concatenate([scaled[..., half:], -scaled[..., :half]], axis=-1)
    return grads * cosine + turned


def scaled_scores(query_part, key_part, query_seg, key_seg, query_index, key_index):
    raw = (
        jnp.einsum("qrgjd,krgd->rgjqk", query_part, key_part, preferred_element_type=jnp.float32)
        * ATTN_SCALE
    )
    same = jnp.transpose(query_seg)[:, :, None] == jnp.transpose(key_seg)[:, None, :]
    before = key_index[None, :] <= query_index[:, None]
    return (raw, (same & before[None])[:, None, None])


def probs_and_ds(
    query_part,
    key_part,
    value_part,
    dout_part,
    lse_part,
    delta_part,
    query_seg,
    key_seg,
    query_index,
    key_index,
):
    scores, allowed = scaled_scores(
        query_part, key_part, query_seg, key_seg, query_index, key_index
    )
    lse_rows = jnp.transpose(lse_part, (1, 2, 3, 0))[..., None]
    delta_rows = jnp.transpose(delta_part, (1, 2, 3, 0))[..., None]
    probs = jnp.where(allowed, jnp.exp(scores - lse_rows), 0.0)
    dprobs = jnp.einsum(
        "qrgjd,krgd->rgjqk", dout_part, value_part, preferred_element_type=jnp.float32
    )
    dscore = (probs * (dprobs - delta_rows)).astype(jnp.bfloat16)
    return (probs.astype(jnp.bfloat16), dscore)


def per_device_general(
    tokens,
    attn_gain,
    w_query,
    w_key,
    w_value,
    w_output,
    moe_gain,
    w_router,
    w_gate,
    w_up,
    w_down,
    routes,
    segment_ids,
    out_grad,
):
    row_count, group_len, width = tokens.shape
    devices = lax.axis_size("expert")
    my_index = lax.axis_index("expert")
    length = group_len * devices
    repeats = HEADS // KV_HEADS
    tok_count = group_len * row_count
    slot_rows = row_count * MOST
    seg_local = jnp.transpose(segment_ids)
    seg_all = lax.all_gather(seg_local, "expert", axis=0, tiled=True)
    query_index = my_index * group_len + jnp.arange(group_len, dtype=jnp.int32)
    earlier = jnp.sum((seg_all[None, :, :] < seg_local[:, None, :]).astype(jnp.int32), axis=1)
    cosine, sine = rope_tables(query_index[:, None] - earlier)
    cos_heads = cosine[:, :, None, :]
    sin_heads = sine[:, :, None, :]
    residual = jnp.swapaxes(tokens, 0, 1).astype(jnp.float32).reshape(tok_count, width)
    normed, unit_attn, inv_attn = rms_forward(residual, attn_gain)
    normed_rows = normed.astype(jnp.bfloat16)
    query_lin = jnp.dot(normed_rows, w_query, preferred_element_type=jnp.float32).reshape(
        group_len, row_count, HEADS, HEAD_DIM
    )
    queries = (
        rotate(query_lin, cos_heads, sin_heads)
        .astype(jnp.bfloat16)
        .reshape(group_len, row_count, KV_HEADS, repeats, HEAD_DIM)
    )
    key_lin = jnp.dot(normed_rows, w_key, preferred_element_type=jnp.float32).reshape(
        group_len, row_count, KV_HEADS, HEAD_DIM
    )
    keys = rotate(key_lin, cos_heads, sin_heads).astype(jnp.bfloat16)
    values = (
        jnp.dot(normed_rows, w_value, preferred_element_type=jnp.float32)
        .astype(jnp.bfloat16)
        .reshape(group_len, row_count, KV_HEADS, HEAD_DIM)
    )
    keys_all, values_all = (
        lax.all_gather(keys, "expert", axis=0, tiled=True),
        lax.all_gather(values, "expert", axis=0, tiled=True),
    )
    key_block = min(1024, length)
    block_count = length // key_block
    key_blocks = keys_all.reshape(block_count, key_block, row_count, KV_HEADS, HEAD_DIM)
    value_blocks = values_all.reshape(block_count, key_block, row_count, KV_HEADS, HEAD_DIM)
    seg_blocks = seg_all.reshape(block_count, key_block, row_count)
    index_blocks = jnp.arange(length, dtype=jnp.int32).reshape(block_count, key_block)
    key_inputs = (key_blocks, value_blocks, seg_blocks, index_blocks)

    def max_step(carried, current):
        running, totals = carried
        key_part, _, seg_part, index_part = current
        scores, allowed = scaled_scores(
            queries, key_part, seg_local, seg_part, query_index, index_part
        )
        newmax = jnp.maximum(running, jnp.max(jnp.where(allowed, scores, NEG_FILL), axis=-1))
        totals = totals * jnp.exp(running - newmax) + jnp.sum(
            jnp.where(allowed, jnp.exp(scores - newmax[..., None]), 0.0), axis=-1
        )
        return ((newmax, totals), None)

    stat_shape = (row_count, KV_HEADS, repeats, group_len)
    (running, totals), unused = lax.scan(
        max_step,
        (jnp.full(stat_shape, NEG_FILL, jnp.float32), jnp.zeros(stat_shape, jnp.float32)),
        key_inputs,
    )
    logsum = running + jnp.log(totals)
    lse_local = jnp.transpose(logsum, (3, 0, 1, 2))

    def out_step(accum, current):
        key_part, value_part, seg_part, index_part = current
        scores, allowed = scaled_scores(
            queries, key_part, seg_local, seg_part, query_index, index_part
        )
        probs = jnp.where(allowed, jnp.exp(scores - logsum[..., None]), 0.0).astype(jnp.bfloat16)
        return (
            accum
            + jnp.einsum(
                "rgjqk,krgd->qrgjd", probs, value_part, preferred_element_type=jnp.float32
            ),
            None,
        )

    head_shape = (group_len, row_count, KV_HEADS, repeats, HEAD_DIM)
    attended, unused = lax.scan(out_step, jnp.zeros(head_shape, jnp.float32), key_inputs)
    attn_rows = attended.reshape(tok_count, HEADS * HEAD_DIM).astype(jnp.bfloat16)
    branch = jnp.dot(attn_rows, w_output, preferred_element_type=jnp.float32)
    middle = residual + RESIDUAL_SCALE * branch
    normed2, unit_moe, inv_moe = rms_forward(middle, moe_gain)
    moe_rows = normed2.astype(jnp.bfloat16)
    logits = jnp.dot(moe_rows, w_router, preferred_element_type=jnp.float32)
    route_rows = jnp.transpose(routes, (1, 0, 2)).reshape(tok_count, TOP)
    onehot = route_rows[:, :, None] == jnp.arange(EXPERTS, dtype=jnp.int32)[None, None, :]
    picked = jnp.sum(jnp.where(onehot, logits[:, None, :], 0.0), axis=-1)
    gates = jax.nn.softmax(picked, axis=-1)
    by_row = jnp.transpose(
        onehot.reshape(group_len, row_count, TOP, EXPERTS), (1, 0, 2, 3)
    ).reshape(row_count, group_len * TOP, EXPERTS)
    counted = jnp.cumsum(by_row.astype(jnp.int32), axis=1)
    rank = jnp.sum(jnp.where(by_row, counted - 1, 0), axis=-1).reshape(row_count, group_len, TOP)
    rank = jnp.transpose(rank, (1, 0, 2)).reshape(tok_count, TOP)
    row_of = jnp.arange(tok_count, dtype=jnp.int32) % row_count
    target = (route_rows * slot_rows + row_of[:, None] * MOST + rank).reshape(tok_count * TOP)

    def to_slots(route_values):
        placed = (
            jnp.zeros((EXPERTS * slot_rows, width), jnp.bfloat16)
            .at[target]
            .set(route_values.reshape(tok_count * TOP, width))
        )
        return placed.reshape(EXPERTS, slot_rows, width)

    def from_slots(slot_values):
        return (
            slot_values.reshape(EXPERTS * slot_rows, width)[target]
            .reshape(tok_count, TOP, width)
            .astype(jnp.float32)
        )

    sent = to_slots(jnp.broadcast_to(moe_rows[:, None, :], (tok_count, TOP, width)))
    arrived = lax.all_to_all(sent, "expert", split_axis=0, concat_axis=1, tiled=True)
    gate_pre = jnp.einsum("etd,edf->etf", arrived, w_gate, preferred_element_type=jnp.float32)
    up_pre = jnp.einsum("etd,edf->etf", arrived, w_up, preferred_element_type=jnp.float32)
    sigma = jax.nn.sigmoid(gate_pre)
    activated = gate_pre * sigma
    hidden = (activated * up_pre).astype(jnp.bfloat16)
    expert_out = jnp.einsum(
        "etf,efd->etd", hidden, w_down, preferred_element_type=jnp.float32
    ).astype(jnp.bfloat16)
    returned = lax.all_to_all(expert_out, "expert", split_axis=1, concat_axis=0, tiled=True)
    route_out = from_slots(returned)
    moe = jnp.sum(gates[:, :, None] * route_out, axis=1)
    mixed_rows = middle + RESIDUAL_SCALE * moe
    mixed = jnp.swapaxes(mixed_rows.reshape(group_len, row_count, width), 0, 1).astype(jnp.bfloat16)
    upstream = jnp.swapaxes(out_grad, 0, 1).astype(jnp.float32).reshape(tok_count, width)
    dmoe = RESIDUAL_SCALE * upstream
    dgates = jnp.sum(route_out * dmoe[:, None, :], axis=-1)
    dsent = to_slots((gates[:, :, None] * dmoe[:, None, :]).astype(jnp.bfloat16))
    darrived = lax.all_to_all(dsent, "expert", split_axis=0, concat_axis=1, tiled=True)
    dhidden = jnp.einsum("etd,efd->etf", darrived, w_down, preferred_element_type=jnp.float32)
    down_part = jnp.einsum("etf,etd->efd", hidden, darrived, preferred_element_type=jnp.float32)
    dgate_pre = (dhidden * up_pre * sigma * (1.0 + gate_pre * (1.0 - sigma))).astype(jnp.bfloat16)
    dup_pre = (dhidden * activated).astype(jnp.bfloat16)
    gate_part = jnp.einsum("etd,etf->edf", arrived, dgate_pre, preferred_element_type=jnp.float32)
    up_part = jnp.einsum("etd,etf->edf", arrived, dup_pre, preferred_element_type=jnp.float32)
    dinputs = (
        jnp.einsum("etf,edf->etd", dgate_pre, w_gate, preferred_element_type=jnp.float32)
        + jnp.einsum("etf,edf->etd", dup_pre, w_up, preferred_element_type=jnp.float32)
    ).astype(jnp.bfloat16)
    grad_gate, grad_up, grad_down = (
        lax.psum_scatter(
            gate_part.astype(jnp.bfloat16), "dp", scatter_dimension=1, tiled=True
        ).astype(jnp.float32),
        lax.psum_scatter(
            up_part.astype(jnp.bfloat16), "dp", scatter_dimension=1, tiled=True
        ).astype(jnp.float32),
        lax.psum_scatter(
            down_part.astype(jnp.bfloat16), "dp", scatter_dimension=1, tiled=True
        ).astype(jnp.float32),
    )
    dreturned = lax.all_to_all(dinputs, "expert", split_axis=1, concat_axis=0, tiled=True)
    droutes = jnp.sum(from_slots(dreturned), axis=1)
    dpicked = gates * (dgates - jnp.sum(gates * dgates, axis=-1, keepdims=True))
    dlogits = jnp.sum(jnp.where(onehot, dpicked[:, :, None], 0.0), axis=1).astype(jnp.bfloat16)
    router_part = jnp.einsum("nd,ne->de", moe_rows, dlogits, preferred_element_type=jnp.float32)
    dnormed2 = droutes + jnp.einsum(
        "ne,de->nd", dlogits, w_router, preferred_element_type=jnp.float32
    )
    dmiddle_norm, moe_gain_part = rms_backward(dnormed2, unit_moe, inv_moe, moe_gain)
    dmiddle = upstream + dmiddle_norm
    dbranch = (RESIDUAL_SCALE * dmiddle).astype(jnp.bfloat16)
    output_part = jnp.einsum("nh,nd->hd", attn_rows, dbranch, preferred_element_type=jnp.float32)
    dattn = (
        jnp.einsum("nd,hd->nh", dbranch, w_output, preferred_element_type=jnp.float32)
        .astype(jnp.bfloat16)
        .reshape(head_shape)
    )
    delta = jnp.sum(dattn.astype(jnp.float32) * attended, axis=-1)

    def both_step(dq_sum, current):
        key_part, value_part, seg_part, index_part = current
        probs_b, dscore = probs_and_ds(
            queries,
            key_part,
            value_part,
            dattn,
            lse_local,
            delta,
            seg_local,
            seg_part,
            query_index,
            index_part,
        )
        dq_part = (
            jnp.einsum("rgjqk,krgd->qrgjd", dscore, key_part, preferred_element_type=jnp.float32)
            * ATTN_SCALE
        )
        dk_part = (
            jnp.einsum("rgjqk,qrgjd->krgd", dscore, queries, preferred_element_type=jnp.float32)
            * ATTN_SCALE
        )
        dv_part = jnp.einsum(
            "rgjqk,qrgjd->krgd", probs_b, dattn, preferred_element_type=jnp.float32
        )
        return (dq_sum + dq_part, (dk_part, dv_part))

    dq_sum, (dk_stack, dv_stack) = lax.scan(
        both_step, jnp.zeros(head_shape, jnp.float32), key_inputs
    )
    full_shape = (length, row_count, KV_HEADS, HEAD_DIM)
    dkeys, dvalues = (
        lax.psum_scatter(
            dk_stack.reshape(full_shape).astype(jnp.bfloat16),
            "expert",
            scatter_dimension=0,
            tiled=True,
        ).astype(jnp.float32),
        lax.psum_scatter(
            dv_stack.reshape(full_shape).astype(jnp.bfloat16),
            "expert",
            scatter_dimension=0,
            tiled=True,
        ).astype(jnp.float32),
    )
    dquery_lin = (
        unrotate(dq_sum.reshape(group_len, row_count, HEADS, HEAD_DIM), cos_heads, sin_heads)
        .astype(jnp.bfloat16)
        .reshape(tok_count, HEADS * HEAD_DIM)
    )
    dkey_lin = (
        unrotate(dkeys, cos_heads, sin_heads)
        .astype(jnp.bfloat16)
        .reshape(tok_count, KV_HEADS * HEAD_DIM)
    )
    dvalue_rows = dvalues.astype(jnp.bfloat16).reshape(tok_count, KV_HEADS * HEAD_DIM)
    query_part_grad = jnp.einsum(
        "nd,nh->dh", normed_rows, dquery_lin, preferred_element_type=jnp.float32
    )
    key_part_grad = jnp.einsum(
        "nd,nh->dh", normed_rows, dkey_lin, preferred_element_type=jnp.float32
    )
    value_part_grad = jnp.einsum(
        "nd,nh->dh", normed_rows, dvalue_rows, preferred_element_type=jnp.float32
    )
    dnormed = (
        jnp.einsum("nh,dh->nd", dquery_lin, w_query, preferred_element_type=jnp.float32)
        + jnp.einsum("nh,dh->nd", dkey_lin, w_key, preferred_element_type=jnp.float32)
        + jnp.einsum("nh,dh->nd", dvalue_rows, w_value, preferred_element_type=jnp.float32)
    )
    dresid_norm, attn_gain_part = rms_backward(dnormed, unit_attn, inv_attn, attn_gain)
    grad_tokens = jnp.swapaxes((dmiddle + dresid_norm).reshape(group_len, row_count, width), 0, 1)
    query_sum, key_sum, value_sum, output_sum, router_sum, attn_gain_sum, moe_gain_sum = lax.psum(
        (
            query_part_grad,
            key_part_grad,
            value_part_grad,
            output_part,
            router_part,
            attn_gain_part,
            moe_gain_part,
        ),
        ("dp", "expert"),
    )
    return (
        mixed,
        grad_tokens,
        attn_gain_sum,
        query_sum,
        key_sum,
        value_sum,
        output_sum,
        moe_gain_sum,
        router_sum,
        grad_gate,
        grad_up,
        grad_down,
    )


def expert_gather(x_rows, g_rows, mask_rows, slot_rows, router_rows, first, x_scr, g_scr, gate_scr, table_scr, groups):
    held = x_scr.shape[0]
    for g in range(groups):
        rows = x_rows(g)
        logits = lax.dot_general(
            router_rows, rows, (((1,), (1,)), ((), ())), preferred_element_type=jnp.float32
        )
        shown = mask_rows(g) > 0
        raised = jnp.where(
            shown,
            jnp.exp(logits - jnp.max(jnp.where(shown, logits, NEG_FILL), axis=0, keepdims=True)),
            0.0,
        )
        gates = raised / jnp.sum(raised, axis=0, keepdims=True)
        slots = slot_rows(g)
        expert = lax.broadcasted_iota(jnp.int32, gates.shape, 0)
        place = lax.broadcasted_iota(jnp.int32, (MOST, rows.shape[0]), 0)
        tables = []
        for e in range(held):
            gate_row = jnp.sum(jnp.where(expert == first + e, gates, 0.0), axis=0, keepdims=True)
            chosen = place == slots[e : e + 1, :]
            gate_scr[e, g * MOST : (g + 1) * MOST, :] = jnp.sum(
                jnp.where(chosen, gate_row, 0.0), axis=1, keepdims=True
            )
            tables.append(jnp.where(chosen, 1.0, 0.0))
        table = jnp.concatenate(tables, axis=0).astype(jnp.bfloat16)
        if table_scr is not None:
            table_scr[g] = table
        for scr, part in ((x_scr, rows), (g_scr, g_rows(g))):
            picked = jnp.dot(table, part, preferred_element_type=jnp.float32).astype(jnp.bfloat16)
            for e in range(held):
                scr[e, g * MOST : (g + 1) * MOST, :] = picked[e * MOST : (e + 1) * MOST, :]


def nt(left, right):
    return lax.dot_general(
        left, right, (((1,), (1,)), ((), ())), preferred_element_type=jnp.float32
    )


def tn(left, right):
    return lax.dot_general(
        left, right, (((0,), (0,)), ((), ())), preferred_element_type=jnp.float32
    )


def expert_body(x_slots, g_slots, gate_col, gate_w, up_w, down_w):
    gate_pre = jnp.dot(x_slots, gate_w, preferred_element_type=jnp.float32)
    up_pre = jnp.dot(x_slots, up_w, preferred_element_type=jnp.float32)
    sigma = jax.nn.sigmoid(gate_pre)
    activated = gate_pre * sigma
    hidden = (activated * up_pre).astype(jnp.bfloat16)
    dexpert = (gate_col * (RESIDUAL_SCALE * g_slots.astype(jnp.float32))).astype(jnp.bfloat16)
    dhidden = nt(dexpert, down_w)
    dgate_pre = (dhidden * up_pre * sigma * (1.0 + gate_pre * (1.0 - sigma))).astype(jnp.bfloat16)
    dup_pre = (dhidden * activated).astype(jnp.bfloat16)
    return hidden, dexpert, dgate_pre, dup_pre


def near_experts(me, x_near, x_twin, g_near, g_twin, mask_row, slot_row, router_t, w_gate, w_up, w_down):
    chips, group_len, width = x_near.shape
    held, _, inner = w_gate.shape
    groups = 2 * chips
    extra = 16
    lanes = 128

    def kernel(me_ref, xn, xt, gn, gt, mr, sr, rt, wg, wu, wd, near_out, twin_out, y_near, y_twin,
               x_scr, g_scr, gate_scr, table_scr, y_scr, d_scr, dg_scr):
        e = pl.program_id(0)
        my = me_ref[0]

        @pl.when(e == 0)
        def _():
            expert_gather(
                lambda g: (xn if g < chips else xt)[g % chips],
                lambda g: (gn if g < chips else gt)[g % chips],
                lambda g: mr[g],
                lambda g: sr[g],
                rt[...],
                my * held,
                x_scr, g_scr, gate_scr, table_scr, groups,
            )

        g_slots = g_scr[e]
        hidden, _, dgate_pre, dup_pre = expert_body(
            x_scr[e], g_slots, gate_scr[e], wg[0], wu[0], wd[0]
        )
        out = jnp.dot(hidden, wd[0], preferred_element_type=jnp.float32).astype(jnp.bfloat16)
        out_wide = out.astype(jnp.float32)
        dgate = jnp.sum(
            RESIDUAL_SCALE * g_slots.astype(jnp.float32) * out_wide, axis=1, keepdims=True
        )
        weighted = (gate_scr[e] * out_wide).astype(jnp.bfloat16)
        dinputs = (nt(dgate_pre, wg[0]) + nt(dup_pre, wu[0])).astype(jnp.bfloat16)
        spot = pl.ds(pl.multiple_of(e * MOST, 16), MOST)
        for g in range(groups):
            part = slice(g * MOST, (g + 1) * MOST)
            y_scr[g, spot, :] = weighted[part]
            d_scr[g, spot, :] = dinputs[part]
            taken = table_scr[g, spot, :].astype(jnp.float32)
            dg_scr[g, e] = jnp.sum(taken * dgate[part], axis=0, keepdims=True)

        @pl.when(e == held - 1)
        def _():
            block = lax.broadcasted_iota(jnp.int32, (held, width), 1) // lanes
            for g in range(groups):
                d_out, y_out = (near_out, y_near) if g < chips else (twin_out, y_twin)
                table = table_scr[g]
                y_out[g % chips] = tn(table, y_scr[g]).astype(jnp.bfloat16)
                d_out[g % chips, :group_len, :] = tn(table, d_scr[g]).astype(jnp.bfloat16)
                rows = jnp.concatenate([dg_scr[g, i] for i in range(held)], axis=0)
                spread = jnp.where(block == my, jnp.concatenate([rows] * groups, axis=1), 0.0)
                high = spread.astype(jnp.bfloat16).astype(jnp.float32)
                tail = jnp.concatenate(
                    [high, spread - high, jnp.zeros((extra - 2 * held, width), jnp.float32)], axis=0
                )
                d_out[g % chips, group_len:, :] = tail.astype(jnp.bfloat16)

    whole = lambda *shape: pl.BlockSpec(shape, lambda e, m: (0,) * len(shape))
    weight = lambda *shape: pl.BlockSpec((1,) + shape, lambda e, m: (e, 0, 0))
    back = jax.ShapeDtypeStruct((chips, group_len + extra, width), jnp.bfloat16)
    forth = jax.ShapeDtypeStruct((chips, group_len, width), jnp.bfloat16)
    slots = groups * MOST
    return pl.pallas_call(
        kernel,
        grid_spec=pltpu.PrefetchScalarGridSpec(
            num_scalar_prefetch=1,
            grid=(held,),
            in_specs=[
                whole(chips, group_len, width),
                whole(chips, group_len, width),
                whole(chips, group_len, width),
                whole(chips, group_len, width),
                whole(groups, EXPERTS, group_len),
                whole(groups, held, group_len),
                whole(EXPERTS, width),
                weight(width, inner),
                weight(width, inner),
                weight(inner, width),
            ],
            out_specs=[
                whole(chips, group_len + extra, width),
                whole(chips, group_len + extra, width),
                whole(chips, group_len, width),
                whole(chips, group_len, width),
            ],
            scratch_shapes=[
                pltpu.VMEM((held, slots, width), jnp.bfloat16),
                pltpu.VMEM((held, slots, width), jnp.bfloat16),
                pltpu.VMEM((held, slots, 1), jnp.float32),
                pltpu.VMEM((groups, held * MOST, group_len), jnp.bfloat16),
                pltpu.VMEM((groups, held * MOST, width), jnp.bfloat16),
                pltpu.VMEM((groups, held * MOST, width), jnp.bfloat16),
                pltpu.VMEM((groups, held, 1, group_len), jnp.float32),
            ],
        ),
        out_shape=[back, back, forth, forth],
        compiler_params=pltpu.CompilerParams(
            dimension_semantics=("arbitrary",), vmem_limit_bytes=58 * 2**20
        ),
        cost_estimate=pl.CostEstimate(
            flops=2 * 7 * held * slots * width * inner, transcendentals=0, bytes_accessed=2**24
        ),
        name="near_experts",
    )(me.reshape(1), x_near, x_twin, g_near, g_twin, mask_row, slot_row, router_t, w_gate, w_up, w_down)


def expert_weight_grads(ids, sums, x_near, x_twin, g_near, g_twin, mask_all, slot_all, router_t, weights, copies):
    chips, unused, group_len, width = x_near.shape
    held, unused, inner = weights[0].shape
    groups = 2 * chips
    slots = groups * MOST
    wide, narrow = width // copies, inner // copies

    def kernel(ids_ref, xn, xt, gn, gt, mr, sr, rt, wg, wu, wd, *refs):
        gate_out, up_out, down_out, x_scr, g_scr, gate_scr = refs[-6:]
        befores = refs[:-6] if sums is not None else (None, None, None)
        e = pl.program_id(0)
        mine, slab = ids_ref[0], ids_ref[1]

        @pl.when(e == 0)
        def _():
            expert_gather(
                lambda g: (xn if g < chips else xt)[g % chips, 0],
                lambda g: (gn if g < chips else gt)[g % chips, 0],
                lambda g: mr[g],
                lambda g: sr[g],
                rt[...], mine * held, x_scr, g_scr, gate_scr, None, groups,
            )

        x_slots = x_scr[e]
        hidden, dexpert, dgate_pre, dup_pre = expert_body(
            x_slots, g_scr[e], gate_scr[e], wg[0], wu[0], wd[0]
        )
        x_part, h_part = x_slots[:, :wide], hidden[:, :narrow]
        for k in range(1, copies):
            x_part = jnp.where(slab == k, x_slots[:, k * wide : (k + 1) * wide], x_part)
            h_part = jnp.where(slab == k, hidden[:, k * narrow : (k + 1) * narrow], h_part)
        for out, before, left, right in zip(
            (gate_out, up_out, down_out),
            befores,
            (x_part, x_part, h_part),
            (dgate_pre, dup_pre, dexpert),
        ):
            part = tn(left, right)
            out[0] = part if before is None else before[0] + part

    some = lambda *shape: pl.BlockSpec((groups,) + shape, lambda e, m: (m[2], 0, 0))
    rows = pl.BlockSpec((chips, 1, group_len, width), lambda e, m: (0, m[2], 0, 0))
    weight = lambda *shape: pl.BlockSpec((1,) + shape, lambda e, m: (e, 0, 0))
    whole = lambda *shape: pl.BlockSpec(shape, lambda e, m: (0,) * len(shape))
    outs = [(held, wide, inner), (held, wide, inner), (held, narrow, width)]
    return pl.pallas_call(
        kernel,
        grid_spec=pltpu.PrefetchScalarGridSpec(
            num_scalar_prefetch=1,
            grid=(held,),
            in_specs=[
                rows,
                rows,
                rows,
                rows,
                some(EXPERTS, group_len),
                some(held, group_len),
                whole(EXPERTS, width),
                weight(width, inner),
                weight(width, inner),
                weight(inner, width),
            ]
            + ([weight(*shape[1:]) for shape in outs] if sums is not None else []),
            out_specs=[weight(*shape[1:]) for shape in outs],
            scratch_shapes=[
                pltpu.VMEM((held, slots, width), jnp.bfloat16),
                pltpu.VMEM((held, slots, width), jnp.bfloat16),
                pltpu.VMEM((held, slots, 1), jnp.float32),
            ],
        ),
        out_shape=[jax.ShapeDtypeStruct(shape, jnp.float32) for shape in outs],
        compiler_params=pltpu.CompilerParams(
            dimension_semantics=("arbitrary",), vmem_limit_bytes=58 * 2**20
        ),
        cost_estimate=pl.CostEstimate(
            flops=2 * 4 * held * slots * width * inner, transcendentals=0, bytes_accessed=2**24
        ),
        input_output_aliases={11 + i: i for i in range(3)} if sums is not None else {},
        name="expert_weight_grads",
    )(ids, x_near, x_twin, g_near, g_twin, mask_all, slot_all, router_t, *weights, *(sums or ()))


def assemble_heads(core, near, twin, width, query_cols):
    chips = near.shape[0]
    devices = 2 * chips
    rows = 128
    pair = 2 * HEAD_DIM

    def kernel(core_ref, near_ref, twin_ref, query_ref, key_ref, value_ref):
        blocks = []
        for j in range(devices):
            mine = near_ref[j // 2].astype(jnp.float32)
            other = twin_ref[j // 2].astype(jnp.float32)
            blocks.append(jnp.where(core_ref[0] == j % 2, mine, other))
            query_ref[:, j * query_cols : (j + 1) * query_cols] = blocks[j][:, :query_cols]
        for c in range(chips):
            for ref, start in ((key_ref, query_cols), (value_ref, query_cols + HEAD_DIM)):
                ref[:, c * pair : (c + 1) * pair] = jnp.concatenate(
                    [blocks[2 * c + k][:, start : start + HEAD_DIM] for k in range(2)], axis=1
                )

    block = pl.BlockSpec((chips, rows, query_cols + pair), lambda r, m: (0, r, 0))
    shapes = [(width, devices * query_cols), (width, devices * HEAD_DIM), (width, devices * HEAD_DIM)]
    return pl.pallas_call(
        kernel,
        grid_spec=pltpu.PrefetchScalarGridSpec(
            num_scalar_prefetch=1,
            grid=(width // rows,),
            in_specs=[block, block],
            out_specs=[pl.BlockSpec((rows, s[1]), lambda r, m: (r, 0)) for s in shapes],
        ),
        out_shape=[jax.ShapeDtypeStruct(s, jnp.float32) for s in shapes],
        name="assemble_heads",
    )(core.reshape(1), near, twin)


def assemble_rows(core, near, twin, start, rows, width):
    chips, _, span = near.shape
    pieces = width // span

    def kernel(core_ref, near_ref, twin_ref, output_ref):
        mine = core_ref[0] == pl.program_id(0) % 2
        block = jnp.where(mine, near_ref[0].astype(jnp.float32), twin_ref[0].astype(jnp.float32))
        for z in range(pieces):
            output_ref[:, z * span : (z + 1) * span] = block[z * rows : (z + 1) * rows]

    block = pl.BlockSpec(
        (1, rows * pieces, span), lambda r, m: (r // 2, start // (rows * pieces), 0)
    )
    return pl.pallas_call(
        kernel,
        grid_spec=pltpu.PrefetchScalarGridSpec(
            num_scalar_prefetch=1,
            grid=(2 * chips,),
            in_specs=[block, block],
            out_specs=pl.BlockSpec((rows, width), lambda r, m: (r, 0)),
        ),
        out_shape=jax.ShapeDtypeStruct((2 * chips * rows, width), jnp.float32),
        name="assemble_rows",
    )(core.reshape(1), near, twin)


def turn(values, sign):
    lanes = lax.broadcasted_iota(jnp.int32, values.shape, 1)
    half = HEAD_DIM // 2
    ahead = pltpu.roll(values, values.shape[1] - half, 1)
    behind = pltpu.roll(values, half, 1)
    return jnp.where(lanes % HEAD_DIM < half, -sign * ahead, sign * behind)


def column_of(row):
    size = row.shape[1]
    diagonal = lax.broadcasted_iota(jnp.int32, (size, size), 0) == lax.broadcasted_iota(
        jnp.int32, (size, size), 1
    )
    return jnp.sum(jnp.where(diagonal, row, 0), axis=1, keepdims=True)


def attend_heads(me, near_pay, twin_pay, gain, head_weights, segs, index):
    chips = near_pay.shape[0]
    blocks, group_len = segs.shape
    width, head_cols = head_weights.shape
    length = blocks * group_len
    pair = 2 * HEAD_DIM

    def device(me, g):
        return 2 * (g % chips) + ((me & 1) ^ (g // chips))

    def kernel(me_ref, near_ref, twin_ref, gain_ref, w_ref, freq_ref, seg_ref, seg_rows, index_ref,
               index_rows, normed_out, qkv_out, cos_out, sin_out, attn_out, attended_out, lse_out,
               k_scr, v_scr, pos_scr):
        step = pl.program_id(0)

        @pl.when(step == 0)
        def _():
            numbers = seg_rows[...]
            start = jnp.zeros(numbers.shape, jnp.float32)
            for s in range(SEGMENTS - 1):
                found = jnp.where(numbers == s, 1.0, 0.0)
                count = jnp.sum(jnp.sum(found, axis=1, keepdims=True), axis=0, keepdims=True)
                start = start + jnp.where(numbers > s, count, 0.0)
            pos_scr[...] = index_rows[...].astype(jnp.float32) - start

        def project(pay_ref, half_row):
            rows = pay_ref[:, :group_len, :].reshape(chips * group_len, width).astype(jnp.float32)
            inverse = lax.rsqrt(jnp.mean(rows * rows, axis=1, keepdims=True) + NORM_EPS)
            normed = (rows * inverse * gain_ref[...]).astype(jnp.bfloat16)
            lin_all = jnp.dot(normed, w_ref[...], preferred_element_type=jnp.float32)
            for c in range(chips):
                g = half_row * chips + c
                here = slice(g * group_len, (g + 1) * group_len)
                normed_out[device(me_ref[0], g)] = normed[c * group_len : (c + 1) * group_len]
                lin = lin_all[c * group_len : (c + 1) * group_len]
                angles = freq_ref[...] * pos_scr[g : g + 1, :]
                cosine = jnp.transpose(jnp.concatenate([jnp.cos(angles)] * 4, axis=0))
                sine = jnp.transpose(jnp.concatenate([jnp.sin(angles)] * 4, axis=0))
                cos_out[here, :] = cosine
                sin_out[here, :] = sine
                query, rest = lin[:, :pair], lin[:, pair:]
                query = query * cosine + turn(query, 1.0) * sine
                key = rest * cosine + turn(rest, 1.0) * sine
                lanes = lax.broadcasted_iota(jnp.int32, rest.shape, 1)
                both = jnp.where(lanes < HEAD_DIM, key, rest).astype(jnp.bfloat16)
                qkv_out[here, :pair] = query.astype(jnp.bfloat16)
                qkv_out[here, pair:] = both
                k_scr[here, :] = both[:, :HEAD_DIM]
                v_scr[here, :] = both[:, HEAD_DIM:]

        @pl.when(step == 0)
        def _():
            project(near_ref, 0)

        @pl.when(step == 1)
        def _():
            project(twin_ref, 1)

        @pl.when(step >= 2)
        def _():
            g = step - 2
            here = pl.ds(pl.multiple_of(g * group_len, group_len), group_len)
            place = device(me_ref[0], g) * group_len + lax.broadcasted_iota(
                jnp.int32, (group_len, 1), 0
            )
            allowed = (seg_ref[...] == column_of(seg_rows[pl.ds(g, 1), :])) & (
                index_ref[...] <= place
            )
            outs, stats = [], []
            for h in range(pair // HEAD_DIM):
                query = qkv_out[here, h * HEAD_DIM : (h + 1) * HEAD_DIM] * jnp.bfloat16(ATTN_SCALE)
                scores = jnp.where(allowed, nt(query, k_scr[...]), NEG_FILL)
                top = jnp.max(scores, axis=1, keepdims=True)
                raised = jnp.exp(scores - top)
                total = jnp.sum(raised, axis=1, keepdims=True)
                probs = (raised * (1.0 / total)).astype(jnp.bfloat16)
                outs.append(jnp.dot(probs, v_scr[...], preferred_element_type=jnp.float32))
                stats.append(jnp.broadcast_to(top + jnp.log(total), (group_len, HEAD_DIM)))
            attended = jnp.concatenate(outs, axis=1)
            attended_out[...] = attended
            attn_out[0] = attended.astype(jnp.bfloat16)
            lse_out[...] = jnp.concatenate(stats, axis=1)

    half = HEAD_DIM // 2
    freqs = ROPE_BASE ** (-(jnp.arange(half, dtype=jnp.float32) * 2.0) / HEAD_DIM)
    whole = lambda *shape: pl.BlockSpec(shape, lambda i, m: (0,) * len(shape))
    second = lambda i: jnp.maximum(i - 2, 0)
    f32, bf16 = jnp.float32, jnp.bfloat16
    return pl.pallas_call(
        kernel,
        grid_spec=pltpu.PrefetchScalarGridSpec(
            num_scalar_prefetch=1,
            grid=(2 + blocks,),
            in_specs=[
                whole(*near_pay.shape),
                whole(*twin_pay.shape),
                whole(1, width),
                whole(width, head_cols),
                whole(half, 1),
                whole(1, length),
                whole(blocks, group_len),
                whole(1, length),
                whole(blocks, group_len),
            ],
            out_specs=[
                whole(blocks, group_len, width),
                whole(length, head_cols),
                whole(length, pair),
                whole(length, pair),
                pl.BlockSpec((1, group_len, pair), lambda i, m: (device(m[0], second(i)), 0, 0)),
                pl.BlockSpec((group_len, pair), lambda i, m: (second(i), 0)),
                pl.BlockSpec((group_len, pair), lambda i, m: (second(i), 0)),
            ],
            scratch_shapes=[
                pltpu.VMEM((length, HEAD_DIM), bf16),
                pltpu.VMEM((length, HEAD_DIM), bf16),
                pltpu.VMEM((blocks, group_len), f32),
            ],
        ),
        out_shape=[
            jax.ShapeDtypeStruct((blocks, group_len, width), bf16),
            jax.ShapeDtypeStruct((length, head_cols), bf16),
            jax.ShapeDtypeStruct((length, pair), f32),
            jax.ShapeDtypeStruct((length, pair), f32),
            jax.ShapeDtypeStruct((blocks, group_len, pair), bf16),
            jax.ShapeDtypeStruct((length, pair), f32),
            jax.ShapeDtypeStruct((length, pair), f32),
        ],
        cost_estimate=pl.CostEstimate(
            flops=2 * length * (width * head_cols + 4 * length * HEAD_DIM) * 2,
            transcendentals=2 * length * length,
            bytes_accessed=2**23,
        ),
        name="attend_heads",
    )(
        me.reshape(1), near_pay, twin_pay, gain[None], head_weights, freqs[:, None],
        segs.reshape(1, length), segs, index.reshape(1, length), index,
    )


def attend_back(me, near_db, twin_db, out_heads, qkv, cosine, sine, attended, lse, segs, index, copies):
    chips = near_db.shape[0]
    span = out_heads.shape[1] // copies
    blocks, group_len = segs.shape
    length, head_cols = qkv.shape
    width = out_heads.shape[1]
    pair = 2 * HEAD_DIM

    def device(me, g):
        return 2 * (g % chips) + ((me & 1) ^ (g // chips))

    def kernel(me_ref, near_ref, twin_ref, w_ref, qkv_ref, cos_ref, sin_ref, att_ref, lse_ref,
               seg_ref, seg_rows, index_ref, dlin_out, part_out, k_scr, v_scr, dk_scr, dv_scr, part_scr):
        g = pl.program_id(0)

        @pl.when(g == 0)
        def _():
            k_scr[...] = qkv_ref[:, pair : pair + HEAD_DIM]
            v_scr[...] = qkv_ref[:, pair + HEAD_DIM :]
            dk_scr[...] = jnp.zeros(dk_scr.shape, jnp.float32)
            dv_scr[...] = jnp.zeros(dv_scr.shape, jnp.float32)
            part_scr[...] = jnp.zeros(part_scr.shape, jnp.float32)

        def block(pay_ref):
            here = pl.ds(pl.multiple_of(g * group_len, group_len), group_len)
            mine = device(me_ref[0], g)
            place = mine * group_len + lax.broadcasted_iota(jnp.int32, (group_len, 1), 0)
            allowed = (seg_ref[...] == column_of(seg_rows[pl.ds(g, 1), :])) & (
                index_ref[...] <= place
            )
            rows = pay_ref[g % chips, :group_len, :]
            dattn = nt(rows, w_ref[...]).astype(jnp.bfloat16)
            attended = att_ref[here, :]
            wide = dattn.astype(jnp.float32) * attended
            part_scr[...] += tn(attended.astype(jnp.bfloat16), rows)
            outs = []
            for h in range(pair // HEAD_DIM):
                part = slice(h * HEAD_DIM, (h + 1) * HEAD_DIM)
                query = qkv_ref[here, part]
                scaled = query * jnp.bfloat16(ATTN_SCALE)
                scores = nt(scaled, k_scr[...])
                level = lse_ref[here, h * HEAD_DIM : h * HEAD_DIM + 1]
                probs = jnp.where(allowed, jnp.exp(scores - level), 0.0)
                delta = jnp.sum(wide[:, part], axis=1, keepdims=True)
                dscores = (probs * (nt(dattn[:, part], v_scr[...]) - delta)).astype(jnp.bfloat16)
                outs.append(jnp.dot(dscores, k_scr[...], preferred_element_type=jnp.float32))
                dk_scr[...] += tn(dscores, scaled)
                dv_scr[...] += tn(probs.astype(jnp.bfloat16), dattn[:, part])
            dquery = jnp.concatenate(outs, axis=1) * ATTN_SCALE
            dlin_out[mine, :, :pair] = (
                dquery * cos_ref[here, :] + turn(dquery * sin_ref[here, :], -1.0)
            ).astype(jnp.bfloat16)

        @pl.when(g < chips)
        def _():
            block(near_ref)

        @pl.when(g >= chips)
        def _():
            block(twin_ref)

        @pl.when(g == blocks - 1)
        def _():
            for z in range(copies):
                part_out[z] = part_scr[:, z * span : (z + 1) * span].astype(jnp.bfloat16)
            for b in range(blocks):
                here = slice(b * group_len, (b + 1) * group_len)
                both = jnp.concatenate([dk_scr[here, :], dv_scr[here, :]], axis=1)
                lanes = lax.broadcasted_iota(jnp.int32, both.shape, 1)
                turned = both * cos_ref[here, :] + turn(both * sin_ref[here, :], -1.0)
                dlin_out[device(me_ref[0], b), :, pair:] = jnp.where(
                    lanes < HEAD_DIM, turned, both
                ).astype(jnp.bfloat16)

    whole = lambda *shape: pl.BlockSpec(shape, lambda i, m: (0,) * len(shape))
    return pl.pallas_call(
        kernel,
        grid_spec=pltpu.PrefetchScalarGridSpec(
            num_scalar_prefetch=1,
            grid=(blocks,),
            in_specs=[
                whole(*near_db.shape),
                whole(*twin_db.shape),
                whole(*out_heads.shape),
                whole(length, head_cols),
                whole(length, pair),
                whole(length, pair),
                whole(length, pair),
                whole(length, pair),
                whole(1, length),
                whole(blocks, group_len),
                whole(1, length),
            ],
            out_specs=[whole(blocks, group_len, head_cols), whole(copies, pair, span)],
            scratch_shapes=[
                pltpu.VMEM((length, HEAD_DIM), jnp.bfloat16),
                pltpu.VMEM((length, HEAD_DIM), jnp.bfloat16),
                pltpu.VMEM((length, HEAD_DIM), jnp.float32),
                pltpu.VMEM((length, HEAD_DIM), jnp.float32),
                pltpu.VMEM((pair, width), jnp.float32),
            ],
        ),
        out_shape=[
            jax.ShapeDtypeStruct((blocks, group_len, head_cols), jnp.bfloat16),
            jax.ShapeDtypeStruct((copies, pair, span), jnp.bfloat16),
        ],
        cost_estimate=pl.CostEstimate(
            flops=2 * length * (width * pair + 10 * length * HEAD_DIM),
            transcendentals=2 * length * length,
            bytes_accessed=2**23,
        ),
        name="attend_back",
    )(
        me.reshape(1), near_db, twin_db, out_heads, qkv, cosine, sine, attended, lse,
        segs.reshape(1, length), segs, index.reshape(1, length),
    )


def swap_cores(block, devices):
    return lax.ppermute(block, "expert", [(i, i ^ 1) for i in range(devices)])


def across_chips(blocks, devices):
    groups = [[2 * c + core for c in range(devices // 2)] for core in range(2)]
    return lax.all_to_all(blocks, "expert", 0, 0, axis_index_groups=groups, tiled=True)


def permute(block, shift, axis, count):
    return lax.ppermute(block, axis, [(i, i ^ shift) for i in range(count)])


def spread_row(block, devices):
    near = across_chips(jnp.broadcast_to(block[None], (devices // 2,) + block.shape), devices)
    return near, swap_cores(near, devices)


def far_rows_of(block, copies):
    return jnp.stack([permute(block, s, "dp", copies) for s in range(1, copies)])


def spread_far(rows, devices):
    return jnp.stack(
        [rows] + [permute(rows, 2 * c, "expert", devices) for c in range(1, devices // 2)]
    )


def merge_cores(near, twin, devices):
    partner = swap_cores(twin, devices)
    return (near.astype(jnp.float32) + partner.astype(jnp.float32)).astype(jnp.bfloat16)


def permute_sum(parts, mine, step, axis, count):
    total = lax.dynamic_index_in_dim(parts, mine, 0, False).astype(jnp.float32)
    for s in range(1, parts.shape[0]):
        part = lax.dynamic_index_in_dim(parts, mine ^ s, 0, False)
        total = total + permute(part, s * step, axis, count).astype(jnp.float32)
    return total


def in_order(near, twin, core):
    even = jnp.where(core == 0, near, twin)
    odd = jnp.where(core == 0, twin, near)
    return jnp.stack([even, odd], axis=1).reshape((2 * near.shape[0],) + near.shape[1:])


def with_tail(rows, tail):
    height, span = tail.shape
    return jnp.concatenate(
        [rows, jnp.pad(tail, ((0, TAIL - height), (0, rows.shape[1] - span)))], axis=0
    )


def pack_gains(gains, span):
    high = gains.astype(jnp.bfloat16)
    lower = (gains - high.astype(jnp.float32)).astype(jnp.bfloat16)
    return jnp.concatenate([high, lower], axis=0).reshape(-1, span)


def unpack_gains(packed, width):
    parts = packed.reshape(packed.shape[0], 2, -1, width).astype(jnp.float32)
    return parts[:, 0] + parts[:, 1]


def exchange(blocks, axis):
    return lax.all_to_all(blocks, axis, 0, 0, tiled=True)


def broadcast(block, count):
    return jnp.broadcast_to(block[None], (count,) + block.shape)


def masked_gates(logits, mask):
    shown = jnp.where(mask, logits, NEG_FILL)
    weight = jnp.where(mask, jnp.exp(shown - jnp.max(shown, axis=-1, keepdims=True)), 0.0)
    return weight / jnp.sum(weight, axis=-1, keepdims=True)


def slot_tables(mask, first, held):
    group_len = mask.shape[2]
    local = lax.dynamic_slice_in_dim(mask, first, held, 1)
    steps = jnp.arange(group_len, dtype=jnp.int32)
    earlier = (steps[:, None] < steps[None, :]).astype(jnp.bfloat16)
    rank = jnp.einsum("gem,mn->gen", local, earlier, preferred_element_type=jnp.float32)
    return mask, jnp.where(local > 0, rank, -1.0).astype(jnp.int32)


def per_device_heads(
    tokens,
    attn_gain,
    w_query,
    w_key,
    w_value,
    w_output,
    moe_gain,
    w_router,
    w_gate,
    w_up,
    w_down,
    routes,
    segment_ids,
    out_grad,
):
    unused, group_len, width = tokens.shape
    devices, copies = lax.axis_size("expert"), lax.axis_size("dp")
    me, me_z = lax.axis_index("expert"), lax.axis_index("dp")
    core = me & 1
    chips = devices // 2
    length = group_len * devices
    repeats = HEADS // KV_HEADS
    query_cols = repeats * HEAD_DIM
    held = EXPERTS // devices
    order = jnp.stack([2 * c + (core ^ k) for k in range(2) for c in range(chips)])
    bf16 = jnp.bfloat16

    own = tokens[0]
    near_pay, twin_pay = spread_row(with_tail(own, segment_ids.astype(bf16)), devices)
    seg_rows = jnp.concatenate(
        [near_pay[:, group_len, :group_len], twin_pay[:, group_len, :group_len]], axis=0
    ).astype(jnp.int32)
    row_index = order[:, None] * group_len + jnp.arange(group_len, dtype=jnp.int32)

    mask_own = jnp.any(
        routes[0][:, :, None] == jnp.arange(EXPERTS, dtype=jnp.int32)[None, None, :], axis=1
    )
    tail_rows = EXPERTS * group_len // width
    mask_tail = jnp.swapaxes(mask_own.astype(bf16), 0, 1).reshape(tail_rows, width)
    grad_pay = with_tail(out_grad[0], mask_tail)
    g_far_own = far_rows_of(grad_pay, copies)
    grad_pay, near_pay = lax.optimization_barrier((grad_pay, near_pay))
    g_near, g_twin = spread_row(grad_pay, devices)

    def tables(tails):
        return slot_tables(tails.reshape(-1, EXPERTS, group_len), me * held, held)

    tail_span = slice(group_len, group_len + tail_rows)
    mask_row, slot_row = tables(
        jnp.concatenate([g_near[:, tail_span], g_twin[:, tail_span]], axis=0)
    )
    router_t = jnp.swapaxes(w_router, 0, 1)

    head_weights = jnp.concatenate(
        [
            lax.dynamic_slice_in_dim(w_query, me * query_cols, query_cols, 1),
            lax.dynamic_slice_in_dim(w_key, me * HEAD_DIM, HEAD_DIM, 1),
            lax.dynamic_slice_in_dim(w_value, me * HEAD_DIM, HEAD_DIM, 1),
        ],
        axis=1,
    )
    normed_row, qkv, cosine, sine, attn_heads, attended, lse = attend_heads(
        me, near_pay, twin_pay, attn_gain, head_weights, seg_rows, row_index
    )
    attn_heads, g_near, g_twin = lax.optimization_barrier((attn_heads, g_near, g_twin))
    attn_rows = jnp.swapaxes(exchange(attn_heads, "expert"), 0, 1).reshape(
        group_len, devices * query_cols
    )

    branch = jnp.dot(attn_rows, w_output, preferred_element_type=jnp.float32)
    residual = own.astype(jnp.float32)
    middle = residual + RESIDUAL_SCALE * branch
    normed2, unit_moe, inv_moe = rms_forward(middle, moe_gain)
    moe_rows = normed2.astype(bf16)
    gates_own = masked_gates(
        jnp.dot(moe_rows, w_router, preferred_element_type=jnp.float32), mask_own
    )
    x_near, x_twin = spread_row(moe_rows, devices)
    x_far_own = far_rows_of(moe_rows, copies)
    x_near, g_far_own = lax.optimization_barrier((x_near, g_far_own))
    g_far = spread_far(g_far_own, devices)

    d_near, d_twin, y_near, y_twin = near_experts(
        me, x_near, x_twin, g_near, g_twin, mask_row, slot_row, router_t, w_gate, w_up, w_down
    )
    d_merged = merge_cores(d_near, d_twin, devices)
    weights = (w_gate, w_up, w_down)

    def expert_row(z, sums, x_rows, g_rows, masks, slots):
        ids = jnp.stack([me, me_z, jnp.int32(z)])
        return expert_weight_grads(
            ids, sums, *x_rows, *g_rows, masks, slots, router_t, weights, copies
        )

    crossed = across_chips(d_merged, devices)
    x_mine, g_mine, d_merged = lax.optimization_barrier(
        ((x_near[:, None], x_twin[:, None]), (g_near[:, None], g_twin[:, None]), d_merged)
    )
    sums = expert_row(0, None, x_mine, g_mine, mask_row, slot_row)
    crossed, sums = lax.optimization_barrier((crossed, sums))
    returned = jnp.sum(crossed.astype(jnp.float32), axis=0)

    parts = returned[group_len : group_len + held] + returned[group_len + held : group_len + 2 * held]
    dgates = jnp.transpose(parts.reshape(held, devices, group_len), (2, 1, 0)).reshape(
        group_len, EXPERTS
    )
    dpicked = gates_own * (dgates - jnp.sum(gates_own * dgates, axis=-1, keepdims=True))
    dlogits = jnp.where(mask_own, dpicked, 0.0).astype(bf16)
    dnormed2 = returned[:group_len] + jnp.einsum(
        "ne,de->nd", dlogits, w_router, preferred_element_type=jnp.float32
    )
    dmiddle_norm, moe_gain_part = rms_backward(dnormed2, unit_moe, inv_moe, moe_gain)
    dmiddle = out_grad[0].astype(jnp.float32) + dmiddle_norm
    dbranch = (RESIDUAL_SCALE * dmiddle).astype(bf16)
    branch_near, branch_twin = spread_row(
        with_tail(dbranch, jnp.swapaxes(dlogits, 0, 1).reshape(tail_rows, width)), devices
    )
    branch_near, x_far_own = lax.optimization_barrier((branch_near, x_far_own))
    x_far = spread_far(x_far_own, devices)
    dlogits_row = jnp.concatenate([branch_near[:, group_len:], branch_twin[:, group_len:]], axis=0)
    dlogits_row = dlogits_row[:, :tail_rows].reshape(devices, EXPERTS, group_len)

    out_heads = lax.dynamic_slice_in_dim(w_output, me * query_cols, query_cols, 0)
    dlin, output_part = attend_back(
        me, branch_near, branch_twin, out_heads, qkv, cosine, sine, attended, lse, seg_rows,
        row_index, copies,
    )
    head_cols = query_cols + 2 * HEAD_DIM
    rows_per = width // devices
    router_cols = lax.dynamic_slice_in_dim(
        jnp.concatenate([x_near, x_twin], axis=0), me * rows_per, rows_per, 2
    )
    router_part = jnp.einsum(
        "bnd,ben->de", router_cols, dlogits_row, preferred_element_type=jnp.float32
    ).astype(bf16)
    router_part = router_part.reshape(copies, -1, head_cols)
    router_rows = router_part.shape[1]
    router_part = jnp.pad(router_part, ((0, 0), (0, TAIL - router_rows), (0, 0)))
    head_part = jnp.einsum(
        "nd,nh->dh",
        normed_row.reshape(length, width),
        dlin.reshape(length, head_cols),
        preferred_element_type=jnp.float32,
    ).astype(bf16)
    rows = width // copies
    shared_part = jnp.concatenate(
        [head_part.reshape(copies, rows, head_cols), output_part, router_part], axis=1
    )

    shared_sum = permute_sum(shared_part, me_z, 1, "dp", copies).astype(bf16)
    dlin_back = jnp.swapaxes(exchange(dlin, "expert"), 0, 1)

    def token_grad(start, count, weights):
        rows = dlin_back[:, :, start : start + count].reshape(group_len, devices * count)
        return jnp.einsum("nh,dh->nd", rows, weights, preferred_element_type=jnp.float32)

    dnormed = (
        token_grad(0, query_cols, w_query)
        + token_grad(query_cols, HEAD_DIM, w_key)
        + token_grad(query_cols + HEAD_DIM, HEAD_DIM, w_value)
    )
    unused, unit_attn, inv_attn = rms_forward(residual, attn_gain)
    dresid_norm, attn_gain_part = rms_backward(dnormed, unit_attn, inv_attn, attn_gain)
    grad_tokens = (dmiddle + dresid_norm)[None]
    gain_parts = pack_gains(jnp.stack([attn_gain_part, moe_gain_part]), head_cols)
    column = exchange(broadcast(jnp.concatenate([shared_sum, gain_parts], axis=0), copies), "dp")

    g_far, x_far, y_near, y_twin, gain_parts = lax.optimization_barrier(
        (g_far, x_far, y_near, y_twin, gain_parts)
    )
    g_rows, x_rows = (g_far, swap_cores(g_far, devices)), (x_far, swap_cores(x_far, devices))
    masks, slots = tables(
        jnp.transpose(jnp.stack([rows_of[:, :, tail_span] for rows_of in g_rows]), (2, 0, 1, 3, 4))
    )
    y_merged = merge_cores(y_near, y_twin, devices)
    y_sum = permute_sum(y_merged, me >> 1, 2, "expert", devices)

    def far_row(step, sums):
        return expert_row(step - 1, sums, x_rows, g_rows, masks, slots)

    sums = far_row(1, sums)
    column, sums = lax.optimization_barrier((column, sums))
    router_start = rows + query_cols
    gain_start = router_start + TAIL
    gain_parts = pack_gains(jnp.sum(unpack_gains(column[:, gain_start:], width), axis=0), head_cols)
    column = jnp.concatenate(
        [
            column[:, :rows].reshape(-1, head_cols),
            column[:, rows:router_start].reshape(-1, head_cols),
            column[:, router_start : router_start + router_rows].reshape(-1, head_cols),
            gain_parts,
        ],
        axis=0,
    )
    head_near = across_chips(broadcast(column, chips), devices)
    for step in range(2, copies):
        sums = far_row(step, sums)
    head_near, sums = lax.optimization_barrier((head_near, sums))
    head_twin = swap_cores(head_near, devices)
    mixed = (middle + RESIDUAL_SCALE * y_sum).astype(bf16)[None]
    grad_gate, grad_up, grad_down = sums
    grad_query, grad_key, grad_value = assemble_heads(core, head_near, head_twin, width, query_cols)
    grad_output = assemble_rows(core, head_near, head_twin, width, query_cols, width)
    router_start = width + query_cols * copies
    gain_start = router_start + router_rows * copies
    grad_router = in_order(
        head_near[:, router_start:gain_start], head_twin[:, router_start:gain_start], core
    ).reshape(width, EXPERTS).astype(jnp.float32)
    gain_sums = jnp.sum(unpack_gains(head_near[:, gain_start:], width), axis=0) + jnp.sum(
        unpack_gains(head_twin[:, gain_start:], width), axis=0
    )
    return (
        mixed,
        grad_tokens,
        gain_sums[0],
        grad_query,
        grad_key,
        grad_value,
        grad_output,
        gain_sums[1],
        grad_router,
        grad_gate,
        grad_up,
        grad_down,
    )


def solution(mesh):
    placed = (
        P("dp", "expert", None),
        P(),
        P(),
        P(),
        P(),
        P(),
        P(),
        P(),
        P("expert", None, None),
        P("expert", None, None),
        P("expert", None, None),
        P("dp", "expert", None),
        P("dp", "expert"),
        P("dp", "expert", None),
    )
    by_heads = mesh.shape["expert"] == KV_HEADS
    return jax.shard_map(
        per_device_heads if by_heads else per_device_general,
        mesh=mesh,
        in_specs=placed,
        out_specs=(
            P("dp", "expert", None),
            P("dp", "expert", None),
            P(),
            P(),
            P(),
            P(),
            P(),
            P(),
            P(),
            P("expert", "dp", None),
            P("expert", "dp", None),
            P("expert", "dp", None),
        ),
        check_vma=False,
    )
```

```python
import jax
import jax.numpy as jnp
from jax import lax
from jax.experimental import pallas as pl
from jax.experimental.pallas import tpu as pltpu
from jax.sharding import PartitionSpec as P


HEADS = 16
KV_HEADS = 8
HEAD_DIM = 64
EXPERTS = 32
TOP = 8
MOST = 48


ATTN_SCALE = 0.015625
RESIDUAL_SCALE = 0.22
NORM_EPS = 1e-06
ROPE_BASE = 10000.0
NEG_FILL = -1e30
TAIL = 16
SEGMENTS = 8


def rms_forward(values, gain_vec):
    inverse = lax.rsqrt(jnp.mean(values * values, axis=-1, keepdims=True) + NORM_EPS)
    unit_rows = values * inverse
    return (unit_rows * gain_vec, unit_rows, inverse)


def rms_backward(grad_rows, unit_rows, inverse, gain_vec):
    scaled = grad_rows * gain_vec
    grad_gain = jnp.sum(grad_rows * unit_rows, axis=0)
    grad_in = inverse * (scaled - unit_rows * jnp.mean(scaled * unit_rows, axis=-1, keepdims=True))
    return (grad_in, grad_gain)


def rope_tables(positions):
    half = HEAD_DIM // 2
    freqs = ROPE_BASE ** (-(jnp.arange(half, dtype=jnp.float32) * 2.0) / HEAD_DIM)
    angles = positions.astype(jnp.float32)[..., None] * freqs
    cosine = jnp.concatenate([jnp.cos(angles), jnp.cos(angles)], axis=-1)
    sine = jnp.concatenate([jnp.sin(angles), jnp.sin(angles)], axis=-1)
    return (cosine, sine)


def rotate(vectors, cosine, sine):
    half = vectors.shape[-1] // 2
    turned = jnp.concatenate([-vectors[..., half:], vectors[..., :half]], axis=-1)
    return vectors * cosine + turned * sine


def unrotate(grads, cosine, sine):
    half = grads.shape[-1] // 2
    scaled = grads * sine
    turned = jnp.concatenate([scaled[..., half:], -scaled[..., :half]], axis=-1)
    return grads * cosine + turned


def scaled_scores(query_part, key_part, query_seg, key_seg, query_index, key_index):
    raw = (
        jnp.einsum("qrgjd,krgd->rgjqk", query_part, key_part, preferred_element_type=jnp.float32)
        * ATTN_SCALE
    )
    same = jnp.transpose(query_seg)[:, :, None] == jnp.transpose(key_seg)[:, None, :]
    before = key_index[None, :] <= query_index[:, None]
    return (raw, (same & before[None])[:, None, None])


def probs_and_ds(
    query_part,
    key_part,
    value_part,
    dout_part,
    lse_part,
    delta_part,
    query_seg,
    key_seg,
    query_index,
    key_index,
):
    scores, allowed = scaled_scores(
        query_part, key_part, query_seg, key_seg, query_index, key_index
    )
    lse_rows = jnp.transpose(lse_part, (1, 2, 3, 0))[..., None]
    delta_rows = jnp.transpose(delta_part, (1, 2, 3, 0))[..., None]
    probs = jnp.where(allowed, jnp.exp(scores - lse_rows), 0.0)
    dprobs = jnp.einsum(
        "qrgjd,krgd->rgjqk", dout_part, value_part, preferred_element_type=jnp.float32
    )
    dscore = (probs * (dprobs - delta_rows)).astype(jnp.bfloat16)
    return (probs.astype(jnp.bfloat16), dscore)


def per_device_general(
    tokens,
    attn_gain,
    w_query,
    w_key,
    w_value,
    w_output,
    moe_gain,
    w_router,
    w_gate,
    w_up,
    w_down,
    routes,
    segment_ids,
    out_grad,
):
    row_count, group_len, width = tokens.shape
    devices = lax.axis_size("expert")
    my_index = lax.axis_index("expert")
    length = group_len * devices
    repeats = HEADS // KV_HEADS
    tok_count = group_len * row_count
    slot_rows = row_count * MOST
    seg_local = jnp.transpose(segment_ids)
    seg_all = lax.all_gather(seg_local, "expert", axis=0, tiled=True)
    query_index = my_index * group_len + jnp.arange(group_len, dtype=jnp.int32)
    earlier = jnp.sum((seg_all[None, :, :] < seg_local[:, None, :]).astype(jnp.int32), axis=1)
    cosine, sine = rope_tables(query_index[:, None] - earlier)
    cos_heads = cosine[:, :, None, :]
    sin_heads = sine[:, :, None, :]
    residual = jnp.swapaxes(tokens, 0, 1).astype(jnp.float32).reshape(tok_count, width)
    normed, unit_attn, inv_attn = rms_forward(residual, attn_gain)
    normed_rows = normed.astype(jnp.bfloat16)
    query_lin = jnp.dot(normed_rows, w_query, preferred_element_type=jnp.float32).reshape(
        group_len, row_count, HEADS, HEAD_DIM
    )
    queries = (
        rotate(query_lin, cos_heads, sin_heads)
        .astype(jnp.bfloat16)
        .reshape(group_len, row_count, KV_HEADS, repeats, HEAD_DIM)
    )
    key_lin = jnp.dot(normed_rows, w_key, preferred_element_type=jnp.float32).reshape(
        group_len, row_count, KV_HEADS, HEAD_DIM
    )
    keys = rotate(key_lin, cos_heads, sin_heads).astype(jnp.bfloat16)
    values = (
        jnp.dot(normed_rows, w_value, preferred_element_type=jnp.float32)
        .astype(jnp.bfloat16)
        .reshape(group_len, row_count, KV_HEADS, HEAD_DIM)
    )
    keys_all, values_all = (
        lax.all_gather(keys, "expert", axis=0, tiled=True),
        lax.all_gather(values, "expert", axis=0, tiled=True),
    )
    key_block = min(1024, length)
    block_count = length // key_block
    key_blocks = keys_all.reshape(block_count, key_block, row_count, KV_HEADS, HEAD_DIM)
    value_blocks = values_all.reshape(block_count, key_block, row_count, KV_HEADS, HEAD_DIM)
    seg_blocks = seg_all.reshape(block_count, key_block, row_count)
    index_blocks = jnp.arange(length, dtype=jnp.int32).reshape(block_count, key_block)
    key_inputs = (key_blocks, value_blocks, seg_blocks, index_blocks)

    def max_step(carried, current):
        running, totals = carried
        key_part, _, seg_part, index_part = current
        scores, allowed = scaled_scores(
            queries, key_part, seg_local, seg_part, query_index, index_part
        )
        newmax = jnp.maximum(running, jnp.max(jnp.where(allowed, scores, NEG_FILL), axis=-1))
        totals = totals * jnp.exp(running - newmax) + jnp.sum(
            jnp.where(allowed, jnp.exp(scores - newmax[..., None]), 0.0), axis=-1
        )
        return ((newmax, totals), None)

    stat_shape = (row_count, KV_HEADS, repeats, group_len)
    (running, totals), unused = lax.scan(
        max_step,
        (jnp.full(stat_shape, NEG_FILL, jnp.float32), jnp.zeros(stat_shape, jnp.float32)),
        key_inputs,
    )
    logsum = running + jnp.log(totals)
    lse_local = jnp.transpose(logsum, (3, 0, 1, 2))

    def out_step(accum, current):
        key_part, value_part, seg_part, index_part = current
        scores, allowed = scaled_scores(
            queries, key_part, seg_local, seg_part, query_index, index_part
        )
        probs = jnp.where(allowed, jnp.exp(scores - logsum[..., None]), 0.0).astype(jnp.bfloat16)
        return (
            accum
            + jnp.einsum(
                "rgjqk,krgd->qrgjd", probs, value_part, preferred_element_type=jnp.float32
            ),
            None,
        )

    head_shape = (group_len, row_count, KV_HEADS, repeats, HEAD_DIM)
    attended, unused = lax.scan(out_step, jnp.zeros(head_shape, jnp.float32), key_inputs)
    attn_rows = attended.reshape(tok_count, HEADS * HEAD_DIM).astype(jnp.bfloat16)
    branch = jnp.dot(attn_rows, w_output, preferred_element_type=jnp.float32)
    middle = residual + RESIDUAL_SCALE * branch
    normed2, unit_moe, inv_moe = rms_forward(middle, moe_gain)
    moe_rows = normed2.astype(jnp.bfloat16)
    logits = jnp.dot(moe_rows, w_router, preferred_element_type=jnp.float32)
    route_rows = jnp.transpose(routes, (1, 0, 2)).reshape(tok_count, TOP)
    onehot = route_rows[:, :, None] == jnp.arange(EXPERTS, dtype=jnp.int32)[None, None, :]
    picked = jnp.sum(jnp.where(onehot, logits[:, None, :], 0.0), axis=-1)
    gates = jax.nn.softmax(picked, axis=-1)
    by_row = jnp.transpose(
        onehot.reshape(group_len, row_count, TOP, EXPERTS), (1, 0, 2, 3)
    ).reshape(row_count, group_len * TOP, EXPERTS)
    counted = jnp.cumsum(by_row.astype(jnp.int32), axis=1)
    rank = jnp.sum(jnp.where(by_row, counted - 1, 0), axis=-1).reshape(row_count, group_len, TOP)
    rank = jnp.transpose(rank, (1, 0, 2)).reshape(tok_count, TOP)
    row_of = jnp.arange(tok_count, dtype=jnp.int32) % row_count
    target = (route_rows * slot_rows + row_of[:, None] * MOST + rank).reshape(tok_count * TOP)

    def to_slots(route_values):
        placed = (
            jnp.zeros((EXPERTS * slot_rows, width), jnp.bfloat16)
            .at[target]
            .set(route_values.reshape(tok_count * TOP, width))
        )
        return placed.reshape(EXPERTS, slot_rows, width)

    def from_slots(slot_values):
        return (
            slot_values.reshape(EXPERTS * slot_rows, width)[target]
            .reshape(tok_count, TOP, width)
            .astype(jnp.float32)
        )

    sent = to_slots(jnp.broadcast_to(moe_rows[:, None, :], (tok_count, TOP, width)))
    arrived = lax.all_to_all(sent, "expert", split_axis=0, concat_axis=1, tiled=True)
    gate_pre = jnp.einsum("etd,edf->etf", arrived, w_gate, preferred_element_type=jnp.float32)
    up_pre = jnp.einsum("etd,edf->etf", arrived, w_up, preferred_element_type=jnp.float32)
    sigma = jax.nn.sigmoid(gate_pre)
    activated = gate_pre * sigma
    hidden = (activated * up_pre).astype(jnp.bfloat16)
    expert_out = jnp.einsum(
        "etf,efd->etd", hidden, w_down, preferred_element_type=jnp.float32
    ).astype(jnp.bfloat16)
    returned = lax.all_to_all(expert_out, "expert", split_axis=1, concat_axis=0, tiled=True)
    route_out = from_slots(returned)
    moe = jnp.sum(gates[:, :, None] * route_out, axis=1)
    mixed_rows = middle + RESIDUAL_SCALE * moe
    mixed = jnp.swapaxes(mixed_rows.reshape(group_len, row_count, width), 0, 1).astype(jnp.bfloat16)
    upstream = jnp.swapaxes(out_grad, 0, 1).astype(jnp.float32).reshape(tok_count, width)
    dmoe = RESIDUAL_SCALE * upstream
    dgates = jnp.sum(route_out * dmoe[:, None, :], axis=-1)
    dsent = to_slots((gates[:, :, None] * dmoe[:, None, :]).astype(jnp.bfloat16))
    darrived = lax.all_to_all(dsent, "expert", split_axis=0, concat_axis=1, tiled=True)
    dhidden = jnp.einsum("etd,efd->etf", darrived, w_down, preferred_element_type=jnp.float32)
    down_part = jnp.einsum("etf,etd->efd", hidden, darrived, preferred_element_type=jnp.float32)
    dgate_pre = (dhidden * up_pre * sigma * (1.0 + gate_pre * (1.0 - sigma))).astype(jnp.bfloat16)
    dup_pre = (dhidden * activated).astype(jnp.bfloat16)
    gate_part = jnp.einsum("etd,etf->edf", arrived, dgate_pre, preferred_element_type=jnp.float32)
    up_part = jnp.einsum("etd,etf->edf", arrived, dup_pre, preferred_element_type=jnp.float32)
    dinputs = (
        jnp.einsum("etf,edf->etd", dgate_pre, w_gate, preferred_element_type=jnp.float32)
        + jnp.einsum("etf,edf->etd", dup_pre, w_up, preferred_element_type=jnp.float32)
    ).astype(jnp.bfloat16)
    grad_gate, grad_up, grad_down = (
        lax.psum_scatter(
            gate_part.astype(jnp.bfloat16), "dp", scatter_dimension=1, tiled=True
        ).astype(jnp.float32),
        lax.psum_scatter(
            up_part.astype(jnp.bfloat16), "dp", scatter_dimension=1, tiled=True
        ).astype(jnp.float32),
        lax.psum_scatter(
            down_part.astype(jnp.bfloat16), "dp", scatter_dimension=1, tiled=True
        ).astype(jnp.float32),
    )
    dreturned = lax.all_to_all(dinputs, "expert", split_axis=1, concat_axis=0, tiled=True)
    droutes = jnp.sum(from_slots(dreturned), axis=1)
    dpicked = gates * (dgates - jnp.sum(gates * dgates, axis=-1, keepdims=True))
    dlogits = jnp.sum(jnp.where(onehot, dpicked[:, :, None], 0.0), axis=1).astype(jnp.bfloat16)
    router_part = jnp.einsum("nd,ne->de", moe_rows, dlogits, preferred_element_type=jnp.float32)
    dnormed2 = droutes + jnp.einsum(
        "ne,de->nd", dlogits, w_router, preferred_element_type=jnp.float32
    )
    dmiddle_norm, moe_gain_part = rms_backward(dnormed2, unit_moe, inv_moe, moe_gain)
    dmiddle = upstream + dmiddle_norm
    dbranch = (RESIDUAL_SCALE * dmiddle).astype(jnp.bfloat16)
    output_part = jnp.einsum("nh,nd->hd", attn_rows, dbranch, preferred_element_type=jnp.float32)
    dattn = (
        jnp.einsum("nd,hd->nh", dbranch, w_output, preferred_element_type=jnp.float32)
        .astype(jnp.bfloat16)
        .reshape(head_shape)
    )
    delta = jnp.sum(dattn.astype(jnp.float32) * attended, axis=-1)

    def both_step(dq_sum, current):
        key_part, value_part, seg_part, index_part = current
        probs_b, dscore = probs_and_ds(
            queries,
            key_part,
            value_part,
            dattn,
            lse_local,
            delta,
            seg_local,
            seg_part,
            query_index,
            index_part,
        )
        dq_part = (
            jnp.einsum("rgjqk,krgd->qrgjd", dscore, key_part, preferred_element_type=jnp.float32)
            * ATTN_SCALE
        )
        dk_part = (
            jnp.einsum("rgjqk,qrgjd->krgd", dscore, queries, preferred_element_type=jnp.float32)
            * ATTN_SCALE
        )
        dv_part = jnp.einsum(
            "rgjqk,qrgjd->krgd", probs_b, dattn, preferred_element_type=jnp.float32
        )
        return (dq_sum + dq_part, (dk_part, dv_part))

    dq_sum, (dk_stack, dv_stack) = lax.scan(
        both_step, jnp.zeros(head_shape, jnp.float32), key_inputs
    )
    full_shape = (length, row_count, KV_HEADS, HEAD_DIM)
    dkeys, dvalues = (
        lax.psum_scatter(
            dk_stack.reshape(full_shape).astype(jnp.bfloat16),
            "expert",
            scatter_dimension=0,
            tiled=True,
        ).astype(jnp.float32),
        lax.psum_scatter(
            dv_stack.reshape(full_shape).astype(jnp.bfloat16),
            "expert",
            scatter_dimension=0,
            tiled=True,
        ).astype(jnp.float32),
    )
    dquery_lin = (
        unrotate(dq_sum.reshape(group_len, row_count, HEADS, HEAD_DIM), cos_heads, sin_heads)
        .astype(jnp.bfloat16)
        .reshape(tok_count, HEADS * HEAD_DIM)
    )
    dkey_lin = (
        unrotate(dkeys, cos_heads, sin_heads)
        .astype(jnp.bfloat16)
        .reshape(tok_count, KV_HEADS * HEAD_DIM)
    )
    dvalue_rows = dvalues.astype(jnp.bfloat16).reshape(tok_count, KV_HEADS * HEAD_DIM)
    query_part_grad = jnp.einsum(
        "nd,nh->dh", normed_rows, dquery_lin, preferred_element_type=jnp.float32
    )
    key_part_grad = jnp.einsum(
        "nd,nh->dh", normed_rows, dkey_lin, preferred_element_type=jnp.float32
    )
    value_part_grad = jnp.einsum(
        "nd,nh->dh", normed_rows, dvalue_rows, preferred_element_type=jnp.float32
    )
    dnormed = (
        jnp.einsum("nh,dh->nd", dquery_lin, w_query, preferred_element_type=jnp.float32)
        + jnp.einsum("nh,dh->nd", dkey_lin, w_key, preferred_element_type=jnp.float32)
        + jnp.einsum("nh,dh->nd", dvalue_rows, w_value, preferred_element_type=jnp.float32)
    )
    dresid_norm, attn_gain_part = rms_backward(dnormed, unit_attn, inv_attn, attn_gain)
    grad_tokens = jnp.swapaxes((dmiddle + dresid_norm).reshape(group_len, row_count, width), 0, 1)
    query_sum, key_sum, value_sum, output_sum, router_sum, attn_gain_sum, moe_gain_sum = lax.psum(
        (
            query_part_grad,
            key_part_grad,
            value_part_grad,
            output_part,
            router_part,
            attn_gain_part,
            moe_gain_part,
        ),
        ("dp", "expert"),
    )
    return (
        mixed,
        grad_tokens,
        attn_gain_sum,
        query_sum,
        key_sum,
        value_sum,
        output_sum,
        moe_gain_sum,
        router_sum,
        grad_gate,
        grad_up,
        grad_down,
    )


def expert_gather(x_rows, g_rows, mask_rows, slot_rows, router_rows, first, x_scr, g_scr, gate_scr, table_scr, groups):
    held = x_scr.shape[0]
    for g in range(groups):
        rows = x_rows(g)
        logits = lax.dot_general(
            router_rows, rows, (((1,), (1,)), ((), ())), preferred_element_type=jnp.float32
        )
        shown = mask_rows(g) > 0
        raised = jnp.where(
            shown,
            jnp.exp(logits - jnp.max(jnp.where(shown, logits, NEG_FILL), axis=0, keepdims=True)),
            0.0,
        )
        gates = raised / jnp.sum(raised, axis=0, keepdims=True)
        slots = slot_rows(g)
        expert = lax.broadcasted_iota(jnp.int32, gates.shape, 0)
        place = lax.broadcasted_iota(jnp.int32, (MOST, rows.shape[0]), 0)
        tables = []
        for e in range(held):
            gate_row = jnp.sum(jnp.where(expert == first + e, gates, 0.0), axis=0, keepdims=True)
            chosen = place == slots[e : e + 1, :]
            gate_scr[e, g * MOST : (g + 1) * MOST, :] = jnp.sum(
                jnp.where(chosen, gate_row, 0.0), axis=1, keepdims=True
            )
            tables.append(jnp.where(chosen, 1.0, 0.0))
        table = jnp.concatenate(tables, axis=0).astype(jnp.bfloat16)
        if table_scr is not None:
            table_scr[g] = table
        for scr, part in ((x_scr, rows), (g_scr, g_rows(g))):
            picked = jnp.dot(table, part, preferred_element_type=jnp.float32).astype(jnp.bfloat16)
            for e in range(held):
                scr[e, g * MOST : (g + 1) * MOST, :] = picked[e * MOST : (e + 1) * MOST, :]


def nt(left, right):
    return lax.dot_general(
        left, right, (((1,), (1,)), ((), ())), preferred_element_type=jnp.float32
    )


def tn(left, right):
    return lax.dot_general(
        left, right, (((0,), (0,)), ((), ())), preferred_element_type=jnp.float32
    )


def expert_body(x_slots, g_slots, gate_col, gate_w, up_w, down_w):
    gate_pre = jnp.dot(x_slots, gate_w, preferred_element_type=jnp.float32)
    up_pre = jnp.dot(x_slots, up_w, preferred_element_type=jnp.float32)
    sigma = jax.nn.sigmoid(gate_pre)
    activated = gate_pre * sigma
    hidden = (activated * up_pre).astype(jnp.bfloat16)
    dexpert = (gate_col * (RESIDUAL_SCALE * g_slots.astype(jnp.float32))).astype(jnp.bfloat16)
    dhidden = nt(dexpert, down_w)
    dgate_pre = (dhidden * up_pre * sigma * (1.0 + gate_pre * (1.0 - sigma))).astype(jnp.bfloat16)
    dup_pre = (dhidden * activated).astype(jnp.bfloat16)
    return hidden, dexpert, dgate_pre, dup_pre


def near_experts(me, x_near, x_twin, g_near, g_twin, mask_row, slot_row, router_t, w_gate, w_up, w_down):
    chips, group_len, width = x_near.shape
    held, _, inner = w_gate.shape
    groups = 2 * chips
    extra = 16
    lanes = 128

    def kernel(me_ref, xn, xt, gn, gt, mr, sr, rt, wg, wu, wd, near_out, twin_out, y_near, y_twin,
               x_scr, g_scr, gate_scr, table_scr, y_scr, d_scr, dg_scr):
        e = pl.program_id(0)
        my = me_ref[0]

        @pl.when(e == 0)
        def _():
            expert_gather(
                lambda g: (xn if g < chips else xt)[g % chips],
                lambda g: (gn if g < chips else gt)[g % chips],
                lambda g: mr[g],
                lambda g: sr[g],
                rt[...],
                my * held,
                x_scr, g_scr, gate_scr, table_scr, groups,
            )

        g_slots = g_scr[e]
        hidden, _, dgate_pre, dup_pre = expert_body(
            x_scr[e], g_slots, gate_scr[e], wg[0], wu[0], wd[0]
        )
        out = jnp.dot(hidden, wd[0], preferred_element_type=jnp.float32).astype(jnp.bfloat16)
        out_wide = out.astype(jnp.float32)
        dgate = jnp.sum(
            RESIDUAL_SCALE * g_slots.astype(jnp.float32) * out_wide, axis=1, keepdims=True
        )
        weighted = (gate_scr[e] * out_wide).astype(jnp.bfloat16)
        dinputs = (nt(dgate_pre, wg[0]) + nt(dup_pre, wu[0])).astype(jnp.bfloat16)
        spot = pl.ds(pl.multiple_of(e * MOST, 16), MOST)
        for g in range(groups):
            part = slice(g * MOST, (g + 1) * MOST)
            y_scr[g, spot, :] = weighted[part]
            d_scr[g, spot, :] = dinputs[part]
            taken = table_scr[g, spot, :].astype(jnp.float32)
            dg_scr[g, e] = jnp.sum(taken * dgate[part], axis=0, keepdims=True)

        @pl.when(e == held - 1)
        def _():
            block = lax.broadcasted_iota(jnp.int32, (held, width), 1) // lanes
            for g in range(groups):
                d_out, y_out = (near_out, y_near) if g < chips else (twin_out, y_twin)
                table = table_scr[g]
                y_out[g % chips] = tn(table, y_scr[g]).astype(jnp.bfloat16)
                d_out[g % chips, :group_len, :] = tn(table, d_scr[g]).astype(jnp.bfloat16)
                rows = jnp.concatenate([dg_scr[g, i] for i in range(held)], axis=0)
                spread = jnp.where(block == my, jnp.concatenate([rows] * groups, axis=1), 0.0)
                high = spread.astype(jnp.bfloat16).astype(jnp.float32)
                tail = jnp.concatenate(
                    [high, spread - high, jnp.zeros((extra - 2 * held, width), jnp.float32)], axis=0
                )
                d_out[g % chips, group_len:, :] = tail.astype(jnp.bfloat16)

    whole = lambda *shape: pl.BlockSpec(shape, lambda e, m: (0,) * len(shape))
    weight = lambda *shape: pl.BlockSpec((1,) + shape, lambda e, m: (e, 0, 0))
    back = jax.ShapeDtypeStruct((chips, group_len + extra, width), jnp.bfloat16)
    forth = jax.ShapeDtypeStruct((chips, group_len, width), jnp.bfloat16)
    slots = groups * MOST
    return pl.pallas_call(
        kernel,
        grid_spec=pltpu.PrefetchScalarGridSpec(
            num_scalar_prefetch=1,
            grid=(held,),
            in_specs=[
                whole(chips, group_len, width),
                whole(chips, group_len, width),
                whole(chips, group_len, width),
                whole(chips, group_len, width),
                whole(groups, EXPERTS, group_len),
                whole(groups, held, group_len),
                whole(EXPERTS, width),
                weight(width, inner),
                weight(width, inner),
                weight(inner, width),
            ],
            out_specs=[
                whole(chips, group_len + extra, width),
                whole(chips, group_len + extra, width),
                whole(chips, group_len, width),
                whole(chips, group_len, width),
            ],
            scratch_shapes=[
                pltpu.VMEM((held, slots, width), jnp.bfloat16),
                pltpu.VMEM((held, slots, width), jnp.bfloat16),
                pltpu.VMEM((held, slots, 1), jnp.float32),
                pltpu.VMEM((groups, held * MOST, group_len), jnp.bfloat16),
                pltpu.VMEM((groups, held * MOST, width), jnp.bfloat16),
                pltpu.VMEM((groups, held * MOST, width), jnp.bfloat16),
                pltpu.VMEM((groups, held, 1, group_len), jnp.float32),
            ],
        ),
        out_shape=[back, back, forth, forth],
        compiler_params=pltpu.CompilerParams(
            dimension_semantics=("arbitrary",), vmem_limit_bytes=58 * 2**20
        ),
        cost_estimate=pl.CostEstimate(
            flops=2 * 7 * held * slots * width * inner, transcendentals=0, bytes_accessed=2**24
        ),
        name="near_experts",
    )(me.reshape(1), x_near, x_twin, g_near, g_twin, mask_row, slot_row, router_t, w_gate, w_up, w_down)


def expert_weight_grads(ids, sums, x_near, x_twin, g_near, g_twin, mask_all, slot_all, router_t, weights, copies):
    chips, count, group_len, width = x_near.shape
    held, _, inner = weights[0].shape
    groups = 2 * chips
    slots = groups * MOST
    wide, narrow = width // copies, inner // copies

    def kernel(ids_ref, xn, xt, gn, gt, mr, sr, rt, wg, wu, wd, *refs):
        gate_out, up_out, down_out, x_scr, g_scr, gate_scr = refs[-6:]
        befores = refs[:-6] if sums is not None else (None, None, None)
        step = pl.program_id(0)
        mine, slab = ids_ref[0], ids_ref[1]

        @pl.when(step < count)
        def _():
            expert_gather(
                lambda g: (xn if g < chips else xt)[g % chips, 0],
                lambda g: (gn if g < chips else gt)[g % chips, 0],
                lambda g: mr[g],
                lambda g: sr[g],
                rt[...], mine * held, x_scr.at[step], g_scr.at[step], gate_scr.at[step], None, groups,
            )

        @pl.when(step >= count)
        def _():
            e, row = (step - count) // count, (step - count) % count
            x_slots = x_scr[row, e]
            hidden, dexpert, dgate_pre, dup_pre = expert_body(
                x_slots, g_scr[row, e], gate_scr[row, e], wg[0], wu[0], wd[0]
            )
            x_part, h_part = x_slots[:, :wide], hidden[:, :narrow]
            for k in range(1, copies):
                x_part = jnp.where(slab == k, x_slots[:, k * wide : (k + 1) * wide], x_part)
                h_part = jnp.where(slab == k, hidden[:, k * narrow : (k + 1) * narrow], h_part)
            for out, before, left, right in zip(
                (gate_out, up_out, down_out),
                befores,
                (x_part, x_part, h_part),
                (dgate_pre, dup_pre, dexpert),
            ):
                part = tn(left, right)

                @pl.when(row == 0)
                def _():
                    out[0] = part if before is None else before[0] + part

                @pl.when(row > 0)
                def _():
                    out[0] = out[0] + part

    some = lambda *shape: pl.BlockSpec((groups,) + shape, lambda i, m: (jnp.minimum(i, count - 1), 0, 0))
    rows = pl.BlockSpec((chips, 1, group_len, width), lambda i, m: (0, jnp.minimum(i, count - 1), 0, 0))
    weight = lambda *shape: pl.BlockSpec((1,) + shape, lambda i, m: (jnp.maximum(i - count, 0) // count, 0, 0))
    whole = lambda *shape: pl.BlockSpec(shape, lambda i, m: (0,) * len(shape))
    outs = [(held, wide, inner), (held, wide, inner), (held, narrow, width)]
    return pl.pallas_call(
        kernel,
        grid_spec=pltpu.PrefetchScalarGridSpec(
            num_scalar_prefetch=1,
            grid=(count + held * count,),
            in_specs=[
                rows,
                rows,
                rows,
                rows,
                some(EXPERTS, group_len),
                some(held, group_len),
                whole(EXPERTS, width),
                weight(width, inner),
                weight(width, inner),
                weight(inner, width),
            ]
            + ([weight(*shape[1:]) for shape in outs] if sums is not None else []),
            out_specs=[weight(*shape[1:]) for shape in outs],
            scratch_shapes=[
                pltpu.VMEM((count, held, slots, width), jnp.bfloat16),
                pltpu.VMEM((count, held, slots, width), jnp.bfloat16),
                pltpu.VMEM((count, held, slots, 1), jnp.float32),
            ],
        ),
        out_shape=[jax.ShapeDtypeStruct(shape, jnp.float32) for shape in outs],
        compiler_params=pltpu.CompilerParams(
            dimension_semantics=("arbitrary",), vmem_limit_bytes=58 * 2**20
        ),
        cost_estimate=pl.CostEstimate(
            flops=2 * 4 * count * held * slots * width * inner, transcendentals=0, bytes_accessed=2**24
        ),
        input_output_aliases={11 + i: i for i in range(3)} if sums is not None else {},
        name="expert_weight_grads",
    )(ids, x_near, x_twin, g_near, g_twin, mask_all, slot_all, router_t, *weights, *(sums or ()))


def assemble_heads(core, near, twin, width, query_cols):
    chips = near.shape[0]
    devices = 2 * chips
    rows = 128
    pair = 2 * HEAD_DIM

    def kernel(core_ref, near_ref, twin_ref, query_ref, key_ref, value_ref):
        blocks = []
        for j in range(devices):
            mine = near_ref[j // 2].astype(jnp.float32)
            other = twin_ref[j // 2].astype(jnp.float32)
            blocks.append(jnp.where(core_ref[0] == j % 2, mine, other))
            query_ref[:, j * query_cols : (j + 1) * query_cols] = blocks[j][:, :query_cols]
        for c in range(chips):
            for ref, start in ((key_ref, query_cols), (value_ref, query_cols + HEAD_DIM)):
                ref[:, c * pair : (c + 1) * pair] = jnp.concatenate(
                    [blocks[2 * c + k][:, start : start + HEAD_DIM] for k in range(2)], axis=1
                )

    block = pl.BlockSpec((chips, rows, query_cols + pair), lambda r, m: (0, r, 0))
    shapes = [(width, devices * query_cols), (width, devices * HEAD_DIM), (width, devices * HEAD_DIM)]
    return pl.pallas_call(
        kernel,
        grid_spec=pltpu.PrefetchScalarGridSpec(
            num_scalar_prefetch=1,
            grid=(width // rows,),
            in_specs=[block, block],
            out_specs=[pl.BlockSpec((rows, s[1]), lambda r, m: (r, 0)) for s in shapes],
        ),
        out_shape=[jax.ShapeDtypeStruct(s, jnp.float32) for s in shapes],
        name="assemble_heads",
    )(core.reshape(1), near, twin)


def assemble_rows(core, near, twin, start, rows, width):
    chips, _, span = near.shape
    pieces = width // span

    def kernel(core_ref, near_ref, twin_ref, output_ref):
        mine = core_ref[0] == pl.program_id(0) % 2
        block = jnp.where(mine, near_ref[0].astype(jnp.float32), twin_ref[0].astype(jnp.float32))
        for z in range(pieces):
            output_ref[:, z * span : (z + 1) * span] = block[z * rows : (z + 1) * rows]

    block = pl.BlockSpec(
        (1, rows * pieces, span), lambda r, m: (r // 2, start // (rows * pieces), 0)
    )
    return pl.pallas_call(
        kernel,
        grid_spec=pltpu.PrefetchScalarGridSpec(
            num_scalar_prefetch=1,
            grid=(2 * chips,),
            in_specs=[block, block],
            out_specs=pl.BlockSpec((rows, width), lambda r, m: (r, 0)),
        ),
        out_shape=jax.ShapeDtypeStruct((2 * chips * rows, width), jnp.float32),
        name="assemble_rows",
    )(core.reshape(1), near, twin)


def turn(values, sign):
    lanes = lax.broadcasted_iota(jnp.int32, values.shape, 1)
    half = HEAD_DIM // 2
    ahead = pltpu.roll(values, values.shape[1] - half, 1)
    behind = pltpu.roll(values, half, 1)
    return jnp.where(lanes % HEAD_DIM < half, -sign * ahead, sign * behind)


def column_of(row):
    size = row.shape[1]
    diagonal = lax.broadcasted_iota(jnp.int32, (size, size), 0) == lax.broadcasted_iota(
        jnp.int32, (size, size), 1
    )
    return jnp.sum(jnp.where(diagonal, row, 0), axis=1, keepdims=True)


def attend_heads(me, near_pay, twin_pay, gain, head_weights, index):
    chips = near_pay.shape[0]
    blocks, group_len = index.shape
    width, head_cols = head_weights.shape
    length = blocks * group_len
    pair = 2 * HEAD_DIM

    def device(me, g):
        return 2 * (g % chips) + ((me & 1) ^ (g // chips))

    def kernel(me_ref, near_ref, twin_ref, gain_ref, w_ref, freq_ref, index_ref, index_rows,
               normed_out, qkv_out, cos_out, sin_out, attn_out, attended_out, lse_out,
               seg_rows, seg_ref, k_scr, v_scr, pos_scr):
        step = pl.program_id(0)

        @pl.when(step == 0)
        def _():
            numbers = jnp.concatenate(
                [
                    (near_ref if g < chips else twin_ref)[
                        g % chips, group_len : group_len + 1, :group_len
                    ].astype(jnp.float32)
                    for g in range(blocks)
                ],
                axis=0,
            ).astype(jnp.int32)
            seg_rows[...] = numbers
            for g in range(blocks):
                seg_ref[:, g * group_len : (g + 1) * group_len] = numbers[g : g + 1, :]
            start = jnp.zeros(numbers.shape, jnp.float32)
            for s in range(SEGMENTS - 1):
                found = jnp.where(numbers == s, 1.0, 0.0)
                count = jnp.sum(jnp.sum(found, axis=1, keepdims=True), axis=0, keepdims=True)
                start = start + jnp.where(numbers > s, count, 0.0)
            pos_scr[...] = index_rows[...].astype(jnp.float32) - start

        def project(pay_ref, half_row):
            rows = pay_ref[:, :group_len, :].reshape(chips * group_len, width).astype(jnp.float32)
            inverse = lax.rsqrt(jnp.mean(rows * rows, axis=1, keepdims=True) + NORM_EPS)
            normed = (rows * inverse * gain_ref[...]).astype(jnp.bfloat16)
            lin_all = jnp.dot(normed, w_ref[...], preferred_element_type=jnp.float32)
            for c in range(chips):
                g = half_row * chips + c
                here = slice(g * group_len, (g + 1) * group_len)
                normed_out[device(me_ref[0], g)] = normed[c * group_len : (c + 1) * group_len]
                lin = lin_all[c * group_len : (c + 1) * group_len]
                angles = freq_ref[...] * pos_scr[g : g + 1, :]
                cosine = jnp.transpose(jnp.concatenate([jnp.cos(angles)] * 4, axis=0))
                sine = jnp.transpose(jnp.concatenate([jnp.sin(angles)] * 4, axis=0))
                cos_out[here, :] = cosine
                sin_out[here, :] = sine
                query, rest = lin[:, :pair], lin[:, pair:]
                query = query * cosine + turn(query, 1.0) * sine
                key = rest * cosine + turn(rest, 1.0) * sine
                lanes = lax.broadcasted_iota(jnp.int32, rest.shape, 1)
                both = jnp.where(lanes < HEAD_DIM, key, rest).astype(jnp.bfloat16)
                qkv_out[here, :pair] = query.astype(jnp.bfloat16)
                qkv_out[here, pair:] = both
                k_scr[here, :] = both[:, :HEAD_DIM]
                v_scr[here, :] = both[:, HEAD_DIM:]

        @pl.when(step == 0)
        def _():
            project(near_ref, 0)

        @pl.when(step == 1)
        def _():
            project(twin_ref, 1)

        @pl.when(step >= 2)
        def _():
            g = step - 2
            here = pl.ds(pl.multiple_of(g * group_len, group_len), group_len)
            place = device(me_ref[0], g) * group_len + lax.broadcasted_iota(
                jnp.int32, (group_len, 1), 0
            )
            allowed = (seg_ref[...] == column_of(seg_rows[pl.ds(g, 1), :])) & (
                index_ref[...] <= place
            )
            outs, stats = [], []
            for h in range(pair // HEAD_DIM):
                query = qkv_out[here, h * HEAD_DIM : (h + 1) * HEAD_DIM] * jnp.bfloat16(ATTN_SCALE)
                scores = jnp.where(allowed, nt(query, k_scr[...]), NEG_FILL)
                top = jnp.max(scores, axis=1, keepdims=True)
                raised = jnp.exp(scores - top)
                total = jnp.sum(raised, axis=1, keepdims=True)
                probs = (raised * (1.0 / total)).astype(jnp.bfloat16)
                outs.append(jnp.dot(probs, v_scr[...], preferred_element_type=jnp.float32))
                stats.append(jnp.broadcast_to(top + jnp.log(total), (group_len, HEAD_DIM)))
            attended = jnp.concatenate(outs, axis=1)
            attended_out[...] = attended
            attn_out[0] = attended.astype(jnp.bfloat16)
            lse_out[...] = jnp.concatenate(stats, axis=1)

    half = HEAD_DIM // 2
    freqs = ROPE_BASE ** (-(jnp.arange(half, dtype=jnp.float32) * 2.0) / HEAD_DIM)
    whole = lambda *shape: pl.BlockSpec(shape, lambda i, m: (0,) * len(shape))
    second = lambda i: jnp.maximum(i - 2, 0)
    f32, bf16 = jnp.float32, jnp.bfloat16
    return pl.pallas_call(
        kernel,
        grid_spec=pltpu.PrefetchScalarGridSpec(
            num_scalar_prefetch=1,
            grid=(2 + blocks,),
            in_specs=[
                whole(*near_pay.shape),
                whole(*twin_pay.shape),
                whole(1, width),
                whole(width, head_cols),
                whole(half, 1),
                whole(1, length),
                whole(blocks, group_len),
            ],
            out_specs=[
                whole(blocks, group_len, width),
                whole(length, head_cols),
                whole(length, pair),
                whole(length, pair),
                pl.BlockSpec((1, group_len, pair), lambda i, m: (device(m[0], second(i)), 0, 0)),
                pl.BlockSpec((group_len, pair), lambda i, m: (second(i), 0)),
                pl.BlockSpec((group_len, pair), lambda i, m: (second(i), 0)),
                whole(blocks, group_len),
                whole(1, length),
            ],
            scratch_shapes=[
                pltpu.VMEM((length, HEAD_DIM), bf16),
                pltpu.VMEM((length, HEAD_DIM), bf16),
                pltpu.VMEM((blocks, group_len), f32),
            ],
        ),
        out_shape=[
            jax.ShapeDtypeStruct((blocks, group_len, width), bf16),
            jax.ShapeDtypeStruct((length, head_cols), bf16),
            jax.ShapeDtypeStruct((length, pair), f32),
            jax.ShapeDtypeStruct((length, pair), f32),
            jax.ShapeDtypeStruct((blocks, group_len, pair), bf16),
            jax.ShapeDtypeStruct((length, pair), f32),
            jax.ShapeDtypeStruct((length, pair), f32),
            jax.ShapeDtypeStruct((blocks, group_len), jnp.int32),
            jax.ShapeDtypeStruct((1, length), jnp.int32),
        ],
        cost_estimate=pl.CostEstimate(
            flops=2 * length * (width * head_cols + 4 * length * HEAD_DIM) * 2,
            transcendentals=2 * length * length,
            bytes_accessed=2**23,
        ),
        name="attend_heads",
    )(
        me.reshape(1), near_pay, twin_pay, gain[None], head_weights, freqs[:, None],
        index.reshape(1, length), index,
    )


def attend_back(me, near_db, twin_db, out_heads, qkv, cosine, sine, attended, lse, segs, seg_lane, index, copies):
    chips = near_db.shape[0]
    span = out_heads.shape[1] // copies
    blocks, group_len = segs.shape
    length, head_cols = qkv.shape
    width = out_heads.shape[1]
    pair = 2 * HEAD_DIM

    def device(me, g):
        return 2 * (g % chips) + ((me & 1) ^ (g // chips))

    def kernel(me_ref, near_ref, twin_ref, w_ref, qkv_ref, cos_ref, sin_ref, att_ref, lse_ref,
               seg_ref, seg_rows, index_ref, dlin_out, part_out, k_scr, v_scr, dk_scr, dv_scr, part_scr):
        g = pl.program_id(0)

        @pl.when(g == 0)
        def _():
            k_scr[...] = qkv_ref[:, pair : pair + HEAD_DIM]
            v_scr[...] = qkv_ref[:, pair + HEAD_DIM :]
            dk_scr[...] = jnp.zeros(dk_scr.shape, jnp.float32)
            dv_scr[...] = jnp.zeros(dv_scr.shape, jnp.float32)
            part_scr[...] = jnp.zeros(part_scr.shape, jnp.float32)

        def block(pay_ref):
            here = pl.ds(pl.multiple_of(g * group_len, group_len), group_len)
            mine = device(me_ref[0], g)
            place = mine * group_len + lax.broadcasted_iota(jnp.int32, (group_len, 1), 0)
            allowed = (seg_ref[...] == column_of(seg_rows[pl.ds(g, 1), :])) & (
                index_ref[...] <= place
            )
            rows = pay_ref[g % chips, :group_len, :]
            dattn = nt(rows, w_ref[...]).astype(jnp.bfloat16)
            attended = att_ref[here, :]
            wide = dattn.astype(jnp.float32) * attended
            part_scr[...] += tn(attended.astype(jnp.bfloat16), rows)
            outs = []
            for h in range(pair // HEAD_DIM):
                part = slice(h * HEAD_DIM, (h + 1) * HEAD_DIM)
                query = qkv_ref[here, part]
                scaled = query * jnp.bfloat16(ATTN_SCALE)
                scores = nt(scaled, k_scr[...])
                level = lse_ref[here, h * HEAD_DIM : h * HEAD_DIM + 1]
                probs = jnp.where(allowed, jnp.exp(scores - level), 0.0)
                delta = jnp.sum(wide[:, part], axis=1, keepdims=True)
                dscores = (probs * (nt(dattn[:, part], v_scr[...]) - delta)).astype(jnp.bfloat16)
                outs.append(jnp.dot(dscores, k_scr[...], preferred_element_type=jnp.float32))
                dk_scr[...] += tn(dscores, scaled)
                dv_scr[...] += tn(probs.astype(jnp.bfloat16), dattn[:, part])
            dquery = jnp.concatenate(outs, axis=1) * ATTN_SCALE
            dlin_out[mine, :, :pair] = (
                dquery * cos_ref[here, :] + turn(dquery * sin_ref[here, :], -1.0)
            ).astype(jnp.bfloat16)

        @pl.when(g < chips)
        def _():
            block(near_ref)

        @pl.when(g >= chips)
        def _():
            block(twin_ref)

        @pl.when(g == blocks - 1)
        def _():
            for z in range(copies):
                part_out[z] = part_scr[:, z * span : (z + 1) * span].astype(jnp.bfloat16)
            for b in range(blocks):
                here = slice(b * group_len, (b + 1) * group_len)
                both = jnp.concatenate([dk_scr[here, :], dv_scr[here, :]], axis=1)
                lanes = lax.broadcasted_iota(jnp.int32, both.shape, 1)
                turned = both * cos_ref[here, :] + turn(both * sin_ref[here, :], -1.0)
                dlin_out[device(me_ref[0], b), :, pair:] = jnp.where(
                    lanes < HEAD_DIM, turned, both
                ).astype(jnp.bfloat16)

    whole = lambda *shape: pl.BlockSpec(shape, lambda i, m: (0,) * len(shape))
    return pl.pallas_call(
        kernel,
        grid_spec=pltpu.PrefetchScalarGridSpec(
            num_scalar_prefetch=1,
            grid=(blocks,),
            in_specs=[
                whole(*near_db.shape),
                whole(*twin_db.shape),
                whole(*out_heads.shape),
                whole(length, head_cols),
                whole(length, pair),
                whole(length, pair),
                whole(length, pair),
                whole(length, pair),
                whole(1, length),
                whole(blocks, group_len),
                whole(1, length),
            ],
            out_specs=[whole(blocks, group_len, head_cols), whole(copies, pair, span)],
            scratch_shapes=[
                pltpu.VMEM((length, HEAD_DIM), jnp.bfloat16),
                pltpu.VMEM((length, HEAD_DIM), jnp.bfloat16),
                pltpu.VMEM((length, HEAD_DIM), jnp.float32),
                pltpu.VMEM((length, HEAD_DIM), jnp.float32),
                pltpu.VMEM((pair, width), jnp.float32),
            ],
        ),
        out_shape=[
            jax.ShapeDtypeStruct((blocks, group_len, head_cols), jnp.bfloat16),
            jax.ShapeDtypeStruct((copies, pair, span), jnp.bfloat16),
        ],
        cost_estimate=pl.CostEstimate(
            flops=2 * length * (width * pair + 10 * length * HEAD_DIM),
            transcendentals=2 * length * length,
            bytes_accessed=2**23,
        ),
        name="attend_back",
    )(
        me.reshape(1), near_db, twin_db, out_heads, qkv, cosine, sine, attended, lse,
        seg_lane, segs, index.reshape(1, length),
    )


def token_back(dlin, w_query, w_key, w_value, tokens, dmiddle, gain):
    devices, group_len, head_cols = dlin.shape
    width = tokens.shape[1]
    pair = head_cols - 2 * HEAD_DIM

    def kernel(dlin_ref, wq_ref, wk_ref, wv_ref, tokens_ref, dmid_ref, gain_ref, out_ref, part_ref,
               sum_scr):
        j = pl.program_id(0)
        here = dlin_ref[...]
        total = nt(jnp.concatenate([here[0][:, :pair], here[1][:, :pair]], axis=1), wq_ref[...])
        for start, ref in ((pair, wk_ref), (pair + HEAD_DIM, wv_ref)):
            both = jnp.concatenate(
                [here[0][:, start : start + HEAD_DIM], here[1][:, start : start + HEAD_DIM]], axis=1
            )
            total = total + nt(both, ref[...])

        @pl.when(j == 0)
        def _():
            sum_scr[...] = total

        @pl.when(j > 0)
        def _():
            sum_scr[...] += total

        @pl.when(j == devices // 2 - 1)
        def _():
            rows = tokens_ref[...].astype(jnp.float32)
            dnormed = sum_scr[...]
            inverse = lax.rsqrt(jnp.mean(rows * rows, axis=1, keepdims=True) + NORM_EPS)
            unit = rows * inverse
            scaled = dnormed * gain_ref[...]
            mean = jnp.mean(scaled * unit, axis=1, keepdims=True)
            out_ref[...] = dmid_ref[...] + inverse * (scaled - unit * mean)
            part_ref[...] = jnp.sum(dnormed * unit, axis=0, keepdims=True)

    whole = lambda *shape: pl.BlockSpec(shape, lambda j: (0,) * len(shape))
    return pl.pallas_call(
        kernel,
        grid=(devices // 2,),
        in_specs=[
            pl.BlockSpec((2, group_len, head_cols), lambda j: (j, 0, 0)),
            pl.BlockSpec((width, 2 * pair), lambda j: (0, j)),
            pl.BlockSpec((width, 2 * HEAD_DIM), lambda j: (0, j)),
            pl.BlockSpec((width, 2 * HEAD_DIM), lambda j: (0, j)),
            whole(group_len, width),
            whole(group_len, width),
            whole(1, width),
        ],
        out_specs=[whole(group_len, width), whole(1, width)],
        scratch_shapes=[pltpu.VMEM((group_len, width), jnp.float32)],
        out_shape=[
            jax.ShapeDtypeStruct((group_len, width), jnp.float32),
            jax.ShapeDtypeStruct((1, width), jnp.float32),
        ],
        cost_estimate=pl.CostEstimate(
            flops=2 * group_len * width * head_cols * devices, transcendentals=0,
            bytes_accessed=2**22,
        ),
        name="token_back",
    )(dlin, w_query, w_key, w_value, tokens, dmiddle, gain[None])


def swap_cores(block, devices):
    return lax.ppermute(block, "expert", [(i, i ^ 1) for i in range(devices)])


def across_chips(blocks, devices):
    groups = [[2 * c + core for c in range(devices // 2)] for core in range(2)]
    return lax.all_to_all(blocks, "expert", 0, 0, axis_index_groups=groups, tiled=True)


def permute(block, shift, axis, count):
    return lax.ppermute(block, axis, [(i, i ^ shift) for i in range(count)])


def spread_row(block, devices):
    near = across_chips(jnp.broadcast_to(block[None], (devices // 2,) + block.shape), devices)
    return near, swap_cores(near, devices)


def far_rows_of(block, copies):
    return jnp.stack([permute(block, s, "dp", copies) for s in range(1, copies)])


def spread_far(rows, devices):
    return jnp.stack(
        [rows] + [permute(rows, 2 * c, "expert", devices) for c in range(1, devices // 2)]
    )


def merge_cores(near, twin, devices):
    partner = swap_cores(twin, devices)
    return (near.astype(jnp.float32) + partner.astype(jnp.float32)).astype(jnp.bfloat16)


def permute_sum(parts, mine, step, axis, count):
    total = lax.dynamic_index_in_dim(parts, mine, 0, False).astype(jnp.float32)
    for s in range(1, parts.shape[0]):
        part = lax.dynamic_index_in_dim(parts, mine ^ s, 0, False)
        total = total + permute(part, s * step, axis, count).astype(jnp.float32)
    return total


def in_order(near, twin, core):
    even = jnp.where(core == 0, near, twin)
    odd = jnp.where(core == 0, twin, near)
    return jnp.stack([even, odd], axis=1).reshape((2 * near.shape[0],) + near.shape[1:])


def with_tail(rows, tail):
    height, span = tail.shape
    return jnp.concatenate(
        [rows, jnp.pad(tail, ((0, TAIL - height), (0, rows.shape[1] - span)))], axis=0
    )


def pack_gains(gains, span):
    high = gains.astype(jnp.bfloat16)
    lower = (gains - high.astype(jnp.float32)).astype(jnp.bfloat16)
    return jnp.concatenate([high, lower], axis=0).reshape(-1, span)


def unpack_gains(packed, width):
    parts = packed.reshape(packed.shape[0], 2, -1, width).astype(jnp.float32)
    return parts[:, 0] + parts[:, 1]


def exchange(blocks, axis):
    return lax.all_to_all(blocks, axis, 0, 0, tiled=True)


def broadcast(block, count):
    return jnp.broadcast_to(block[None], (count,) + block.shape)


def masked_gates(logits, mask):
    shown = jnp.where(mask, logits, NEG_FILL)
    weight = jnp.where(mask, jnp.exp(shown - jnp.max(shown, axis=-1, keepdims=True)), 0.0)
    return weight / jnp.sum(weight, axis=-1, keepdims=True)


def slot_tables(mask, first, held):
    group_len = mask.shape[2]
    local = lax.dynamic_slice_in_dim(mask, first, held, 1)
    steps = jnp.arange(group_len, dtype=jnp.int32)
    earlier = (steps[:, None] < steps[None, :]).astype(jnp.bfloat16)
    rank = jnp.einsum("gem,mn->gen", local, earlier, preferred_element_type=jnp.float32)
    return mask, jnp.where(local > 0, rank, -1.0).astype(jnp.int32)


def per_device_heads(
    tokens,
    attn_gain,
    w_query,
    w_key,
    w_value,
    w_output,
    moe_gain,
    w_router,
    w_gate,
    w_up,
    w_down,
    routes,
    segment_ids,
    out_grad,
):
    _, group_len, width = tokens.shape
    devices, copies = lax.axis_size("expert"), lax.axis_size("dp")
    me, me_z = lax.axis_index("expert"), lax.axis_index("dp")
    core = me & 1
    chips = devices // 2
    length = group_len * devices
    repeats = HEADS // KV_HEADS
    query_cols = repeats * HEAD_DIM
    held = EXPERTS // devices
    order = jnp.stack([2 * c + (core ^ k) for k in range(2) for c in range(chips)])
    bf16 = jnp.bfloat16

    own = tokens[0]
    near_pay, twin_pay = spread_row(with_tail(own, segment_ids.astype(bf16)), devices)
    row_index = order[:, None] * group_len + jnp.arange(group_len, dtype=jnp.int32)

    mask_own = jnp.any(
        routes[0][:, :, None] == jnp.arange(EXPERTS, dtype=jnp.int32)[None, None, :], axis=1
    )
    tail_rows = EXPERTS * group_len // width
    mask_tail = jnp.swapaxes(mask_own.astype(bf16), 0, 1).reshape(tail_rows, width)
    grad_pay = with_tail(out_grad[0], mask_tail)
    g_far_own = far_rows_of(grad_pay, copies)
    grad_pay, near_pay = lax.optimization_barrier((grad_pay, near_pay))
    g_near, g_twin = spread_row(grad_pay, devices)

    def tables(tails):
        return slot_tables(tails.reshape(-1, EXPERTS, group_len), me * held, held)

    tail_span = slice(group_len, group_len + tail_rows)
    mask_row, slot_row = tables(
        jnp.concatenate([g_near[:, tail_span], g_twin[:, tail_span]], axis=0)
    )
    router_t = jnp.swapaxes(w_router, 0, 1)

    head_weights = jnp.concatenate(
        [
            lax.dynamic_slice_in_dim(w_query, me * query_cols, query_cols, 1),
            lax.dynamic_slice_in_dim(w_key, me * HEAD_DIM, HEAD_DIM, 1),
            lax.dynamic_slice_in_dim(w_value, me * HEAD_DIM, HEAD_DIM, 1),
        ],
        axis=1,
    )
    normed_row, qkv, cosine, sine, attn_heads, attended, lse, seg_rows, seg_lane = attend_heads(
        me, near_pay, twin_pay, attn_gain, head_weights, row_index
    )
    attn_heads, g_near, g_twin = lax.optimization_barrier((attn_heads, g_near, g_twin))
    attn_rows = jnp.swapaxes(exchange(attn_heads, "expert"), 0, 1).reshape(
        group_len, devices * query_cols
    )

    branch = jnp.dot(attn_rows, w_output, preferred_element_type=jnp.float32)
    residual = own.astype(jnp.float32)
    middle = residual + RESIDUAL_SCALE * branch
    normed2, unit_moe, inv_moe = rms_forward(middle, moe_gain)
    moe_rows = normed2.astype(bf16)
    gates_own = masked_gates(
        jnp.dot(moe_rows, w_router, preferred_element_type=jnp.float32), mask_own
    )
    x_near, x_twin = spread_row(moe_rows, devices)
    x_far_own = far_rows_of(moe_rows, copies)
    x_near, g_far_own = lax.optimization_barrier((x_near, g_far_own))
    g_far = spread_far(g_far_own, devices)

    d_near, d_twin, y_near, y_twin = near_experts(
        me, x_near, x_twin, g_near, g_twin, mask_row, slot_row, router_t, w_gate, w_up, w_down
    )
    d_merged = merge_cores(d_near, d_twin, devices)
    weights = (w_gate, w_up, w_down)

    def expert_rows(sums, x_rows, g_rows, masks, slots):
        ids = jnp.stack([me, me_z])
        return expert_weight_grads(
            ids, sums, *x_rows, *g_rows, masks, slots, router_t, weights, copies
        )

    crossed = across_chips(d_merged, devices)
    x_mine, g_mine, d_merged = lax.optimization_barrier(
        ((x_near[:, None], x_twin[:, None]), (g_near[:, None], g_twin[:, None]), d_merged)
    )
    sums = expert_rows(None, x_mine, g_mine, mask_row, slot_row)
    crossed, sums = lax.optimization_barrier((crossed, sums))
    returned = jnp.sum(crossed.astype(jnp.float32), axis=0)

    parts = returned[group_len : group_len + held] + returned[group_len + held : group_len + 2 * held]
    dgates = jnp.transpose(parts.reshape(held, devices, group_len), (2, 1, 0)).reshape(
        group_len, EXPERTS
    )
    dpicked = gates_own * (dgates - jnp.sum(gates_own * dgates, axis=-1, keepdims=True))
    dlogits = jnp.where(mask_own, dpicked, 0.0).astype(bf16)
    dnormed2 = returned[:group_len] + jnp.einsum(
        "ne,de->nd", dlogits, w_router, preferred_element_type=jnp.float32
    )
    dmiddle_norm, moe_gain_part = rms_backward(dnormed2, unit_moe, inv_moe, moe_gain)
    dmiddle = out_grad[0].astype(jnp.float32) + dmiddle_norm
    dbranch = (RESIDUAL_SCALE * dmiddle).astype(bf16)
    branch_near, branch_twin = spread_row(
        with_tail(dbranch, jnp.swapaxes(dlogits, 0, 1).reshape(tail_rows, width)), devices
    )
    branch_near, x_far_own = lax.optimization_barrier((branch_near, x_far_own))
    x_far = spread_far(x_far_own, devices)
    dlogits_row = jnp.concatenate([branch_near[:, group_len:], branch_twin[:, group_len:]], axis=0)
    dlogits_row = dlogits_row[:, :tail_rows].reshape(devices, EXPERTS, group_len)

    out_heads = lax.dynamic_slice_in_dim(w_output, me * query_cols, query_cols, 0)
    dlin, output_part = attend_back(
        me, branch_near, branch_twin, out_heads, qkv, cosine, sine, attended, lse, seg_rows,
        seg_lane, row_index, copies,
    )
    head_cols = query_cols + 2 * HEAD_DIM
    rows_per = width // devices
    router_cols = lax.dynamic_slice_in_dim(
        jnp.concatenate([x_near, x_twin], axis=0), me * rows_per, rows_per, 2
    )
    router_part = jnp.einsum(
        "bnd,ben->de", router_cols, dlogits_row, preferred_element_type=jnp.float32
    ).astype(bf16)
    router_part = router_part.reshape(copies, -1, head_cols)
    router_rows = router_part.shape[1]
    router_part = jnp.pad(router_part, ((0, 0), (0, TAIL - router_rows), (0, 0)))
    head_part = jnp.einsum(
        "nd,nh->dh",
        normed_row.reshape(length, width),
        dlin.reshape(length, head_cols),
        preferred_element_type=jnp.float32,
    ).astype(bf16)
    rows = width // copies
    shared_part = jnp.concatenate(
        [head_part.reshape(copies, rows, head_cols), output_part, router_part], axis=1
    )

    shared_sum = permute_sum(shared_part, me_z, 1, "dp", copies).astype(bf16)
    grad_tokens, attn_gain_part = token_back(
        exchange(dlin, "expert"), w_query, w_key, w_value, own, dmiddle, attn_gain
    )
    grad_tokens = grad_tokens[None]
    gain_parts = pack_gains(jnp.stack([attn_gain_part[0], moe_gain_part]), head_cols)
    column = exchange(broadcast(jnp.concatenate([shared_sum, gain_parts], axis=0), copies), "dp")

    g_far, x_far, y_near, y_twin, gain_parts = lax.optimization_barrier(
        (g_far, x_far, y_near, y_twin, gain_parts)
    )
    g_rows, x_rows = (g_far, swap_cores(g_far, devices)), (x_far, swap_cores(x_far, devices))
    masks, slots = tables(
        jnp.transpose(jnp.stack([rows_of[:, :, tail_span] for rows_of in g_rows]), (2, 0, 1, 3, 4))
    )
    y_merged = merge_cores(y_near, y_twin, devices)
    y_sum = permute_sum(y_merged, me >> 1, 2, "expert", devices)

    router_start = rows + query_cols
    gain_start = router_start + TAIL
    gain_parts = pack_gains(jnp.sum(unpack_gains(column[:, gain_start:], width), axis=0), head_cols)
    column = jnp.concatenate(
        [
            column[:, :rows].reshape(-1, head_cols),
            column[:, rows:router_start].reshape(-1, head_cols),
            column[:, router_start : router_start + router_rows].reshape(-1, head_cols),
            gain_parts,
        ],
        axis=0,
    )
    head_near = across_chips(broadcast(column, chips), devices)
    sums = expert_rows(sums, x_rows, g_rows, masks, slots)
    head_near, sums = lax.optimization_barrier((head_near, sums))
    head_twin = swap_cores(head_near, devices)
    mixed = (middle + RESIDUAL_SCALE * y_sum).astype(bf16)[None]
    grad_gate, grad_up, grad_down = sums
    grad_query, grad_key, grad_value = assemble_heads(core, head_near, head_twin, width, query_cols)
    grad_output = assemble_rows(core, head_near, head_twin, width, query_cols, width)
    router_start = width + query_cols * copies
    gain_start = router_start + router_rows * copies
    grad_router = in_order(
        head_near[:, router_start:gain_start], head_twin[:, router_start:gain_start], core
    ).reshape(width, EXPERTS).astype(jnp.float32)
    gain_sums = jnp.sum(unpack_gains(head_near[:, gain_start:], width), axis=0) + jnp.sum(
        unpack_gains(head_twin[:, gain_start:], width), axis=0
    )
    return (
        mixed,
        grad_tokens,
        gain_sums[0],
        grad_query,
        grad_key,
        grad_value,
        grad_output,
        gain_sums[1],
        grad_router,
        grad_gate,
        grad_up,
        grad_down,
    )


def solution(mesh):
    placed = (
        P("dp", "expert", None),
        P(),
        P(),
        P(),
        P(),
        P(),
        P(),
        P(),
        P("expert", None, None),
        P("expert", None, None),
        P("expert", None, None),
        P("dp", "expert", None),
        P("dp", "expert"),
        P("dp", "expert", None),
    )
    by_heads = mesh.shape["expert"] == KV_HEADS
    return jax.shard_map(
        per_device_heads if by_heads else per_device_general,
        mesh=mesh,
        in_specs=placed,
        out_specs=(
            P("dp", "expert", None),
            P("dp", "expert", None),
            P(),
            P(),
            P(),
            P(),
            P(),
            P(),
            P(),
            P("expert", "dp", None),
            P("expert", "dp", None),
            P("expert", "dp", None),
        ),
        check_vma=False,
    )
```
